32 devices in a mesh: img: 4 (over z), band: 8 (over y, x, core).
Axes of the slice: x: 2, y: 2, z: 4, core: 2. Of those that a mesh axis runs over, the one named last changes fastest.
Arguments:
- pixels: bfloat16 [4, 4, 1024, 192], P(None, 'img', 'band'), may hold values from -4 to 4
- valid: int32 [4, 4, 1024, 192], P(None, 'img', 'band'), may hold values from 0 to 1, as said below
- codes: int32 [4, 4, 1024], P(None, 'img', 'band'), may hold values from 0 to 8191
- image_kind: int32 [4, 4], P(None, 'img'), may hold values from 0 to 1
- w_wide: float32 [3584, 2, 512], P(('img', 'band')), may hold values from -0.25 to 0.25
- w_narrow: float32 [2560, 2, 512], P(('img', 'band')), may hold values from -0.25 to 0.25
- w_edge: float32 [512, 448], P(('img', 'band')), may hold values from -0.25 to 0.25
- codebook: float32 [8192, 32], P(('img', 'band')), may hold values from -5 to 5
- norms: float32 [10, 512], replicated, may hold values from 0.25 to 1.75
- bases: float32 [4, 512, 512], replicated, may hold values from -0.25 to 0.25
- basis_edge: float32 [448, 448], replicated, may hold values from -0.25 to 0.25
- m_wide: float32 [3584, 2, 512], P(('img', 'band')), may hold values from -2.3841858e-06 to 2.3841858e-06
- v_wide: float32 [3584, 2, 512], P(('img', 'band')), may hold values from 1.4731672e-13 to 5.8926686e-13
- m_narrow: float32 [2560, 2, 512], P(('img', 'band')), may hold values from -2.3841858e-06 to 2.3841858e-06
- v_narrow: float32 [2560, 2, 512], P(('img', 'band')), may hold values from 1.4731672e-13 to 5.8926686e-13
- m_edge: float32 [512, 448], P(('img', 'band')), may hold values from -2.3841858e-06 to 2.3841858e-06
- v_edge: float32 [512, 448], P(('img', 'band')), may hold values from 1.4731672e-13 to 5.8926686e-13
- m_code: float32 [8192, 32], P(('img', 'band')), may hold values from -5.9604645e-07 to 5.9604645e-07
- v_code: float32 [8192, 32], P(('img', 'band')), may hold values from 9.207295e-15 to 3.682918e-14
- m_norm: float32 [10, 512], replicated, may hold values from -6.67572e-06 to 6.67572e-06
- v_norm: float32 [10, 512], replicated, may hold values from 1.3258505e-12 to 5.303402e-12
Outputs:
- new_wide: float32 [3584, 2, 512], P(('img', 'band'))
- new_m_wide: float32 [3584, 2, 512], P(('img', 'band'))
- new_v_wide: float32 [3584, 2, 512], P(('img', 'band'))
- new_narrow: float32 [2560, 2, 512], P(('img', 'band'))
- new_m_narrow: float32 [2560, 2, 512], P(('img', 'band'))
- new_v_narrow: float32 [2560, 2, 512], P(('img', 'band'))
- new_edge: float32 [512, 448], P(('img', 'band'))
- new_m_edge: float32 [512, 448], P(('img', 'band'))
- new_v_edge: float32 [512, 448], P(('img', 'band'))
- new_codebook: float32 [8192, 32], P(('img', 'band'))
- new_m_code: float32 [8192, 32], P(('img', 'band'))
- new_v_code: float32 [8192, 32], P(('img', 'band'))
- new_norms: float32 [10, 512], replicated
- new_m_norm: float32 [10, 512], replicated
- new_v_norm: float32 [10, 512], replicated
- grad_norm: float32 [], replicated
- loss: float32 [], replicated
The draws below stay inside these ranges and needn't reach their ends.
Inputs may be any that keep to these rules, and one draw needn't show every extreme that they name: `valid`: 1 where a pixel counts; rows hold more counted pixels towards their end. `image_kind`: 0: the row is one image of 1024 tokens; 1: the row is four images of 256 tokens in order.
All inputs are finite; a program needn't handle non-finite values.
Results may differ from the reference program's by a relative error of at most 0.00075.
The reference program's roundings to bfloat16 on the way count: a program that leaves them out, or rounds other values in their place, can miss the bound.
Values may be sent and summed in bfloat16 or wider, within the bound.
A program may use at most 512 MiB of HBM per device.

```python
import math
import jax
import jax.numpy as jnp
import numpy as np
from jax import lax

D = 512
HEADS = 8
HDIM = 64
CODES = 8192
CDIM = 32
PATCH = 192
MB = 4
LAYERS = 2
NORMS = 10
L = 1024
IMGS = 4
WIDE = 3584
NARROW = 2560
EDGE = 448
PARAMS = 6788096


def draw_valid(key, part):
    position = jnp.arange(L, dtype=jnp.int32)[None, None, :, None]
    rolled = jax.random.randint(key, (MB, IMGS, L, PATCH), 0, 4 * L)
    return (rolled < L + 2 * position).astype(jnp.int32)


def set_ends(entries, key, low, top_value):
    index_at = [jax.random.randint(jax.random.fold_in(key, axis), (), 0, length) for axis, length in enumerate(entries.shape)]
    main_axis = entries.shape.index(max(entries.shape))
    neighbour = index_at[:main_axis] + [(index_at[main_axis] + 1) % entries.shape[main_axis]] + index_at[main_axis + 1:]
    return entries.at[tuple(index_at)].set(low).at[tuple(neighbour)].set(top_value)


def levels(stream_key, extent, split, least, largest):
    gain = 1.0
    for axis_at, parts in split:
        draws = jax.random.uniform(jax.random.fold_in(jax.random.fold_in(stream_key, 6), axis_at), (parts,), jnp.float32, least / len(split), largest / len(split))
        gain = gain * jnp.repeat(jnp.exp(draws), extent[axis_at] // parts).reshape((-1,) + (1,) * (len(extent) - 1 - axis_at))
    return gain


def rank_table(number_of, slope):
    portions = [(1 << 20) // math.isqrt(standing ** slope) + 1 for standing in range(1, number_of + 1)]
    scale = 1 + sum(portions) // (1 << 30)
    return np.cumsum(np.array([max(1, weight // scale) for weight in portions]))


def ranked_ids(own_key, dims, count, lean):
    grid = rank_table(count, lean)
    ticket = jax.random.randint(jax.random.fold_in(own_key, 1), dims, 0, int(grid[count - 1]))
    rank = jnp.searchsorted(jnp.asarray(grid, jnp.int32), ticket, side="right")
    return jax.random.permutation(jax.random.fold_in(own_key, 2), count)[rank].astype(jnp.int32)


def bell_draw(own_key, dims, scale, most, pieces=(), kind=jnp.bfloat16):
    factor_of = levels(own_key, dims, pieces, -0.22, 0.18) if pieces else 1.0
    values = jax.random.normal(own_key, dims, jnp.float32) * scale * factor_of
    return jnp.minimum(jnp.maximum(values, -most), most).astype(kind)


def setup_inputs(seed: int = 0) -> dict:
    streams_of = jax.random.split(jax.random.key(seed), 22)
    return {
        "pixels": bell_draw(streams_of[0], (MB, IMGS, L, PATCH), 1.0, 4.0, ((1, 4), (2, 8))),
        "valid": draw_valid(jax.random.fold_in(streams_of[21], 71), 0),
        "codes": set_ends(ranked_ids(streams_of[2], (MB, IMGS, L), CODES, 2), jax.random.fold_in(streams_of[2], 3), 0, CODES - 1).astype(jnp.int32),
        "image_kind": set_ends(jax.random.randint(streams_of[3], (MB, IMGS), 0, 2), jax.random.fold_in(streams_of[3], 1), 0, 1).astype(jnp.int32),
        "w_wide": bell_draw(streams_of[4], (WIDE, LAYERS, D), D ** -0.5, 0.25, ((0, 32),), jnp.float32),
        "w_narrow": bell_draw(streams_of[5], (NARROW, LAYERS, D), D ** -0.5, 0.25, ((0, 32),), jnp.float32),
        "w_edge": bell_draw(streams_of[6], (D, EDGE), D ** -0.5, 0.25, ((0, 32),), jnp.float32),
        "codebook": bell_draw(streams_of[7], (CODES, CDIM), 1.0, 5.0, ((0, 32),), jnp.float32),
        "norms": jnp.clip(1.0 + 0.15 * jax.random.normal(streams_of[8], (NORMS, D), jnp.float32), 0.25, 1.75),
        "bases": bell_draw(streams_of[9], (2 * LAYERS, D, D), D ** -0.5, 0.25, (), jnp.float32),
        "basis_edge": bell_draw(streams_of[10], (EDGE, EDGE), EDGE ** -0.5, 0.25, (), jnp.float32),
        "m_wide": bell_draw(streams_of[11], (WIDE, LAYERS, D), (0.001 / PARAMS ** 0.5), 2.384185791015625e-06, ((0, 32),), jnp.float32),
        "v_wide": jnp.clip(jnp.exp(math.log(5.89266862301846e-13) - 1.3862944 * jax.random.uniform(streams_of[12], (WIDE, LAYERS, D), jnp.float32) ** levels(streams_of[12], (WIDE, LAYERS, D), ((0, 32),), -0.2, 0.2)), 1.473167155754615e-13, 5.89266862301846e-13),
        "m_narrow": bell_draw(streams_of[13], (NARROW, LAYERS, D), (0.001 / PARAMS ** 0.5), 2.384185791015625e-06, ((0, 32),), jnp.float32),
        "v_narrow": jnp.clip(jnp.exp(math.log(5.89266862301846e-13) - 1.3862944 * jax.random.uniform(streams_of[14], (NARROW, LAYERS, D), jnp.float32) ** levels(streams_of[14], (NARROW, LAYERS, D), ((0, 32),), -0.2, 0.2)), 1.473167155754615e-13, 5.89266862301846e-13),
        "m_edge": bell_draw(streams_of[15], (D, EDGE), (0.001 / PARAMS ** 0.5), 2.384185791015625e-06, ((0, 32),), jnp.float32),
        "v_edge": jnp.clip(jnp.exp(math.log(5.89266862301846e-13) - 1.3862944 * jax.random.uniform(streams_of[16], (D, EDGE), jnp.float32) ** levels(streams_of[16], (D, EDGE), ((0, 32),), -0.2, 0.2)), 1.473167155754615e-13, 5.89266862301846e-13),
        "m_code": bell_draw(streams_of[17], (CODES, CDIM), (0.00025 / PARAMS ** 0.5), 5.960464477539062e-07, ((0, 32),), jnp.float32),
        "v_code": jnp.clip(jnp.exp(math.log(3.6829178893865375e-14) - 1.3862944 * jax.random.uniform(streams_of[18], (CODES, CDIM), jnp.float32) ** levels(streams_of[18], (CODES, CDIM), ((0, 32),), -0.2, 0.2)), 9.207294723466344e-15, 3.6829178893865375e-14),
        "m_norm": bell_draw(streams_of[19], (NORMS, D), (0.003 / PARAMS ** 0.5), 6.67572021484375e-06, (), jnp.float32),
        "v_norm": jnp.clip(jnp.exp(jax.random.uniform(streams_of[20], (NORMS, D), jnp.float32, math.log(1.3258504537316806e-12), math.log(5.3034018149267226e-12))), 1.3258504537316806e-12, 5.3034018149267226e-12),
    }


@jax.custom_vjp
def low(v):
    return lax.optimization_barrier(v.astype(jnp.bfloat16)).astype(jnp.float32)

@jax.custom_vjp
def low_back(v):
    return v

def low_keep(v):
    return (low(v), None)

def low_pass(kept, grad):
    return (grad,)

def back_keep(v):
    return (v, None)

def back_low(kept, grad):
    return (low(grad),)
low.defvjp(low_keep, low_pass)
low_back.defvjp(back_keep, back_low)
norm_eps = 1e-05
adam_eps = 1e-08
clip_level = 0.001
beta_first = 0.5
beta_second = 0.6
rate_matrix = 0.02
rate_vector = 0.3
weight_decay = 0.01
commitment = 0.25
masked_score = -1000000000.0
highest = lax.Precision.HIGHEST

def matmul(first_op, second_op):
    return jnp.dot(first_op, second_op, precision=highest)

def layer_norm(hidden, scale_gain, offset):
    centred = hidden - lax.optimization_barrier(jnp.mean(hidden, axis=-1, keepdims=True))
    spread = lax.optimization_barrier(jnp.mean(centred * centred, axis=-1, keepdims=True))
    return centred * lax.rsqrt(spread + norm_eps) * scale_gain + offset

def gelu_tanh(inputs):
    return 0.5 * inputs * (1.0 + jnp.tanh(0.7978845608028654 * (inputs + 0.044715 * inputs * inputs * inputs)))

def block(hidden, wide_rows, narrow_rows, gain_rows, segment):
    model_width = hidden.shape[1]
    row_count = hidden.shape[0]
    normed = low(layer_norm(hidden, gain_rows[0], gain_rows[1]))
    projected = low_back(low(matmul(normed, wide_rows[:3 * model_width].T)))
    queries = projected[:, :model_width].reshape(row_count, HEADS, HDIM)
    key_rows = projected[:, model_width:2 * model_width].reshape(row_count, HEADS, HDIM)
    value_rows = projected[:, 2 * model_width:].reshape(row_count, HEADS, HDIM)
    scores = low_back(jnp.einsum('qhd,khd->hqk', queries, key_rows, precision=highest) * HDIM ** (-0.5))
    allowed = segment[:, None] == segment[None, :]
    scores = jnp.where(allowed[None], scores, masked_score)
    softmaxed = low(jax.nn.softmax(scores, axis=-1))
    attended = low_back(low(jnp.einsum('hqk,khd->qhd', softmaxed, value_rows, precision=highest).reshape(row_count, model_width)))
    middle = hidden + low_back(matmul(attended, narrow_rows[:model_width]))
    second = low(layer_norm(middle, gain_rows[2], gain_rows[3]))
    upper_in = low_back(matmul(second, wide_rows[3 * model_width:].T))
    active = low(gelu_tanh(upper_in))
    return middle + low_back(matmul(active, narrow_rows[model_width:]))

def encode(w_wide, w_narrow, w_edge, norms, pixel_rows, segments):
    wide_low = low(w_wide)
    narrow_low = low(w_narrow)
    edge_low = low(w_edge)

    def one_row(pixel_row, segment):
        hidden = low_back(matmul(pixel_row, edge_low[:, :PATCH].T))
        hidden = block(hidden, wide_low[:, 0], narrow_low[:, 0], norms[0:4], segment)
        return low_back(matmul(low(hidden), edge_low[:, 2 * PATCH:2 * PATCH + CDIM]))
    checked = jax.checkpoint(one_row)
    return lax.map(lambda row_pair: checked(row_pair[0], row_pair[1]), (pixel_rows, segments))

def decode(w_wide, w_narrow, w_edge, norms, quantized, segments, targets, pixel_mask, count):
    wide_low = low(w_wide)
    narrow_low = low(w_narrow)
    edge_low = low(w_edge)

    def one_row(total, row_data):
        code_row, segment, target_row, mask_row = row_data
        hidden = low_back(matmul(code_row, edge_low[:, 2 * PATCH + CDIM:].T))
        hidden = block(hidden, wide_low[:, 1], narrow_low[:, 1], norms[4:8], segment)
        final = low(layer_norm(hidden, norms[8], norms[9]))
        predict = low_back(matmul(final, edge_low[:, PATCH:2 * PATCH]))
        error = predict - target_row
        return (total + jnp.sum(mask_row * (error * error + jnp.abs(error))), None)
    total, _ = lax.scan(jax.checkpoint(one_row), jnp.zeros((), jnp.float32), (quantized, segments, targets, pixel_mask))
    return total / count

def quant_loss(codebook, latent, code_rows, latent_fixed, chosen_fixed):
    chosen = low(codebook)[code_rows]
    gap_book = chosen - latent_fixed
    gap_commit = latent - chosen_fixed
    return (jnp.sum(gap_book * gap_book) + commitment * jnp.sum(gap_commit * gap_commit)) / (MB * IMGS * L * CDIM)

def moments(gradient, first_old, second_old):
    first_new = beta_first * first_old + (1.0 - beta_first) * gradient
    second_new = beta_second * second_old + (1.0 - beta_second) * gradient * gradient
    return (first_new, second_new, first_new / (jnp.sqrt(second_new) + adam_eps))

def rotated_update(weight, gradient, first_old, second_old, basis_stack):
    turned = jnp.einsum('rld,lde->rle', gradient, basis_stack, precision=highest)
    first_new, second_new, direction = moments(turned, first_old, second_old)
    turned_back = jnp.einsum('rle,lde->rld', direction, basis_stack, precision=highest)
    return (weight - rate_matrix * (turned_back + weight_decay * weight), first_new, second_new)

def plain_update(weight, gradient, first_old, second_old):
    first_new, second_new, direction = moments(gradient, first_old, second_old)
    return (weight - rate_vector * (direction + weight_decay * weight), first_new, second_new)

def reference(pixels, valid, codes, image_kind, w_wide, w_narrow, w_edge, codebook, norms, bases, basis_edge, m_wide, v_wide, m_narrow, v_narrow, m_edge, v_edge, m_code, v_code, m_norm, v_norm):
    row_total = MB * IMGS
    pixel_rows = pixels.astype(jnp.float32).reshape(row_total, L, PATCH)
    pixel_mask = valid.astype(jnp.float32).reshape(row_total, L, PATCH)
    code_rows = codes.reshape(row_total, L)
    spans = jnp.where(image_kind.reshape(row_total) == 0, L, L // 4).astype(jnp.int32)
    segments = jnp.arange(L, dtype=jnp.int32)[None, :] // spans[:, None]
    count = jnp.sum(pixel_mask)
    latent, enc_back = jax.vjp(lambda wa, wb, wc, wd: encode(wa, wb, wc, wd, pixel_rows, segments), w_wide, w_narrow, w_edge, norms)
    chosen = low(codebook)[code_rows]
    recon, dec_back = jax.vjp(lambda wa, wb, wc, wd, quant: decode(wa, wb, wc, wd, quant, segments, pixel_rows, pixel_mask, count), w_wide, w_narrow, w_edge, norms, chosen)
    dec_grads = dec_back(jnp.ones_like(recon))
    vq_value, vq_back = jax.vjp(lambda book, lat: quant_loss(book, lat, code_rows, latent, chosen), codebook, latent)
    grad_book, grad_latent = vq_back(jnp.ones_like(vq_value))
    enc_grads = enc_back(dec_grads[4] + grad_latent)
    grad_wide = enc_grads[0] + dec_grads[0]
    grad_narrow = enc_grads[1] + dec_grads[1]
    grad_edge = enc_grads[2] + dec_grads[2]
    grad_norms = enc_grads[3] + dec_grads[3]
    squares = jnp.sum(grad_wide * grad_wide) + jnp.sum(grad_narrow * grad_narrow) + jnp.sum(grad_edge * grad_edge) + jnp.sum(grad_book * grad_book) + jnp.sum(grad_norms * grad_norms)
    grad_norm = jnp.sqrt(squares)
    factor = jnp.minimum(1.0, clip_level / grad_norm)
    new_wide, new_m_wide, new_v_wide = rotated_update(w_wide, factor * grad_wide, m_wide, v_wide, bases[:LAYERS])
    new_narrow, new_m_narrow, new_v_narrow = rotated_update(w_narrow, factor * grad_narrow, m_narrow, v_narrow, bases[LAYERS:])
    new_edge, new_m_edge, new_v_edge = rotated_update(w_edge[:, None], factor * grad_edge[:, None], m_edge[:, None], v_edge[:, None], basis_edge[None])
    new_book, new_m_code, new_v_code = plain_update(codebook, factor * grad_book, m_code, v_code)
    new_norms, new_m_norm, new_v_norm = plain_update(norms, factor * grad_norms, m_norm, v_norm)
    return (new_wide, new_m_wide, new_v_wide, new_narrow, new_m_narrow, new_v_narrow, new_edge[:, 0], new_m_edge[:, 0], new_v_edge[:, 0], new_book, new_m_code, new_v_code, new_norms, new_m_norm, new_v_norm, grad_norm, recon + vq_value)
```

```python
import functools

import jax
import jax.numpy as jnp
from jax import lax
from jax.experimental import pallas as pl
from jax.experimental.pallas import tpu as pltpu
from jax.sharding import PartitionSpec as P

HEADS = 8
HDIM = 64
MESH = pl.DeviceIdType.MESH


norm_eps = 1e-05
adam_eps = 1e-08
clip_level = 0.001
beta_first = 0.5
beta_second = 0.6
rate_matrix = 0.02
rate_vector = 0.3
weight_decay = 0.01
commitment = 0.25
masked_score = -1000000000.0
highest = lax.Precision.HIGHEST


def matmul_plain(first_op, second_op):
    return jnp.dot(first_op, second_op, preferred_element_type=jnp.float32)


def matmul_trans(first_op, second_op):
    return lax.dot_general(
        first_op, second_op, (((1,), (1,)), ((), ())), preferred_element_type=jnp.float32
    )


def matmul_outer(first_op, second_op):
    return lax.dot_general(
        first_op, second_op, (((0,), (0,)), ((), ())), preferred_element_type=jnp.float32
    )


def layer_norm(hidden, scale_gain, offset):
    centred = hidden - jnp.mean(hidden, axis=-1, keepdims=True)
    spread = jnp.mean(centred * centred, axis=-1, keepdims=True)
    return centred * lax.rsqrt(spread + norm_eps) * scale_gain + offset


def gelu_tanh(inputs):
    return (
        0.5
        * inputs
        * (1.0 + jnp.tanh(0.7978845608028654 * (inputs + 0.044715 * inputs * inputs * inputs)))
    )


def split_heads(matrix):
    return matrix.reshape(matrix.shape[0], HEADS, HDIM)


def head_scores(q_heads, k_heads, allowed):
    scores = jnp.einsum(
        "qhd,khd->hqk", q_heads, k_heads, preferred_element_type=jnp.float32
    ) * HDIM ** (-0.5)
    return jnp.where(allowed[None], scores, masked_score)


def attend(queries, key_rows, value_rows, allowed):
    scores = head_scores(split_heads(queries), split_heads(key_rows), allowed)
    score_peak = jnp.max(scores, axis=-1, keepdims=True)
    expo = jnp.exp(scores - score_peak)
    total = jnp.sum(expo, axis=-1, keepdims=True)
    softmaxed = (expo / total).astype(jnp.bfloat16)
    attended = jnp.einsum(
        "hqk,khd->qhd", softmaxed, split_heads(value_rows), preferred_element_type=jnp.float32
    )
    return (
        attended.reshape(queries.shape[0], -1).astype(jnp.bfloat16),
        score_peak + jnp.log(total),
    )


def attend_back(queries, key_rows, value_rows, allowed, log_total, grad_out):
    q_heads = split_heads(queries)
    k_heads = split_heads(key_rows)
    v_heads = split_heads(value_rows)
    g_heads = split_heads(grad_out)
    softmaxed = jnp.exp(head_scores(q_heads, k_heads, allowed) - log_total)
    grad_soft = jnp.einsum("qhd,khd->hqk", g_heads, v_heads, preferred_element_type=jnp.float32)
    row_dot = jnp.sum(softmaxed * grad_soft, axis=-1, keepdims=True)
    grad_scores = (softmaxed * (grad_soft - row_dot)).astype(jnp.bfloat16)
    scale = HDIM ** (-0.5)
    grad_q = (
        jnp.einsum("hqk,khd->qhd", grad_scores, k_heads, preferred_element_type=jnp.float32) * scale
    )
    grad_k = (
        jnp.einsum("hqk,qhd->khd", grad_scores, q_heads, preferred_element_type=jnp.float32) * scale
    )
    grad_v = jnp.einsum(
        "hqk,qhd->khd", softmaxed.astype(jnp.bfloat16), g_heads, preferred_element_type=jnp.float32
    )
    return (
        grad_q.reshape(queries.shape[0], -1),
        grad_k.reshape(key_rows.shape[0], -1),
        grad_v.reshape(key_rows.shape[0], -1),
    )


def block_forward(hidden_all, part, wide_rows, narrow_rows, gain_rows, allowed):
    model_width = hidden_all.shape[1]
    own_rows = allowed.shape[0]
    normed_all = layer_norm(hidden_all, gain_rows[0], gain_rows[1]).astype(jnp.bfloat16)
    hidden = lax.dynamic_slice_in_dim(hidden_all, part * own_rows, own_rows, 0)
    normed = lax.dynamic_slice_in_dim(normed_all, part * own_rows, own_rows, 0)
    queries = matmul_trans(normed, wide_rows[:model_width]).astype(jnp.bfloat16)
    key_rows = matmul_trans(normed_all, wide_rows[model_width : 2 * model_width]).astype(jnp.bfloat16)
    value_rows = matmul_trans(normed_all, wide_rows[2 * model_width : 3 * model_width]).astype(jnp.bfloat16)
    attended, log_total = attend(queries, key_rows, value_rows, allowed)
    middle = hidden + matmul_plain(attended, narrow_rows[:model_width])
    second = layer_norm(middle, gain_rows[2], gain_rows[3]).astype(jnp.bfloat16)
    upper_in = matmul_trans(second, wide_rows[3 * model_width :])
    active = gelu_tanh(upper_in).astype(jnp.bfloat16)
    result = middle + matmul_plain(active, narrow_rows[model_width:])
    return (
        result,
        (hidden, normed, queries, key_rows, value_rows, attended, log_total, middle, second, upper_in, active),
    )


def block_backward(grad_out, wide_rows, narrow_rows, gain_rows, allowed, saved, groups):
    (hidden, normed, queries, key_rows, value_rows, attended, log_total, middle, second, upper_in, active) = saved
    model_width = hidden.shape[1]
    grad_y = grad_out.astype(jnp.bfloat16)
    grad_down = matmul_outer(active, grad_y)
    grad_active = matmul_trans(grad_y, narrow_rows[model_width:])
    grad_upper = jax.vjp(gelu_tanh, upper_in)[1](grad_active)[0].astype(jnp.bfloat16)
    grad_up = matmul_outer(grad_upper, second)
    _, second_back = jax.vjp(layer_norm, middle, gain_rows[2], gain_rows[3])
    grad_mid, gain_two, offset_two = second_back(
        matmul_plain(grad_upper, wide_rows[3 * model_width :])
    )
    grad_mid = grad_mid + grad_out
    grad_attn = grad_mid.astype(jnp.bfloat16)
    grad_outproj = matmul_outer(attended, grad_attn)
    grad_att = matmul_trans(grad_attn, narrow_rows[:model_width]).astype(jnp.bfloat16)
    grad_q, grad_keys, grad_values = attend_back(
        queries, key_rows, value_rows, allowed, log_total, grad_att
    )
    grad_k = lax.psum_scatter(grad_keys, "band", scatter_dimension=0, tiled=True, axis_index_groups=groups)
    grad_v = lax.psum_scatter(grad_values, "band", scatter_dimension=0, tiled=True, axis_index_groups=groups)
    grad_mixed = jnp.concatenate([grad_q, grad_k, grad_v], axis=1).astype(jnp.bfloat16)
    grad_qkv = matmul_outer(grad_mixed, normed)
    _, first_back = jax.vjp(layer_norm, hidden, gain_rows[0], gain_rows[1])
    grad_in, gain_one, offset_one = first_back(
        matmul_plain(grad_mixed, wide_rows[: 3 * model_width])
    )
    gain_grads = jnp.stack([gain_one, offset_one, gain_two, offset_two], axis=0)
    return (
        grad_in + grad_mid,
        jnp.concatenate([grad_qkv, grad_up], axis=0),
        jnp.concatenate([grad_outproj, grad_down], axis=0),
        gain_grads,
    )


def pick_codes(code_rows, book_wide, code_width):
    fold = book_wide.shape[1] // code_width
    one_hot = (
        (code_rows // fold)[:, None] == jnp.arange(book_wide.shape[0], dtype=jnp.int32)[None, :]
    ).astype(jnp.bfloat16)
    lane_fold = jnp.arange(book_wide.shape[1], dtype=jnp.int32)[None, :] // code_width
    lane_mask = (code_rows % fold)[:, None] == lane_fold
    spread = jnp.where(lane_mask, matmul_plain(one_hot, book_wide), 0.0)
    chosen = sum(spread[:, k * code_width : (k + 1) * code_width] for k in range(fold))
    return chosen, one_hot, lane_mask


def row_step(gathered, norms, pixel_all, valid_rows, code_all, part, allowed, count, latent_total, groups):
    wide_all, narrow_all, edge_all, book_wide = gathered
    patch_size = pixel_all.shape[1]
    code_width = edge_all.shape[1] // 2 - patch_size
    own_rows = allowed.shape[0]
    edge_in = edge_all[:, :patch_size]
    edge_pix = edge_all[:, patch_size : 2 * patch_size]
    edge_qin = edge_all[:, 2 * patch_size : 2 * patch_size + code_width]
    edge_qout = edge_all[:, 2 * patch_size + code_width :]
    pixel_rows = lax.dynamic_slice_in_dim(pixel_all, part * own_rows, own_rows, 0)
    chosen_all, one_hot_all, lane_mask_all = pick_codes(code_all, book_wide, code_width)
    chosen_low_all = chosen_all.astype(jnp.bfloat16)
    chosen = lax.dynamic_slice_in_dim(chosen_all, part * own_rows, own_rows, 0)
    one_hot = lax.dynamic_slice_in_dim(one_hot_all, part * own_rows, own_rows, 0)
    lane_mask = lax.dynamic_slice_in_dim(lane_mask_all, part * own_rows, own_rows, 0)
    chosen_low = chosen.astype(jnp.bfloat16)
    begin = matmul_trans(chosen_low_all, edge_qout)
    decoded, dec_saved = block_forward(begin, part, wide_all[1], narrow_all[1], norms[4:8], allowed)
    final = layer_norm(decoded, norms[8], norms[9]).astype(jnp.bfloat16)
    predict = matmul_plain(final, edge_pix)
    error = predict - pixel_rows.astype(jnp.float32)
    pixel_mask = valid_rows.astype(jnp.float32)
    loss_pix = jnp.sum(pixel_mask * (error * error + jnp.abs(error))) / count
    grad_pred = (pixel_mask * (2.0 * error + jnp.sign(error)) / count).astype(jnp.bfloat16)
    grad_pixw = matmul_outer(final, grad_pred)
    _, final_back = jax.vjp(layer_norm, decoded, norms[8], norms[9])
    grad_dec, gain_last, offset_last = final_back(matmul_trans(grad_pred, edge_pix))
    grad_begin, dec_wide, dec_narrow, dec_gains = block_backward(
        grad_dec, wide_all[1], narrow_all[1], norms[4:8], allowed, dec_saved, groups
    )
    grad_begin_low = grad_begin.astype(jnp.bfloat16)
    grad_qout = matmul_outer(grad_begin_low, chosen_low)
    start = matmul_trans(pixel_all, edge_in)
    encoded, enc_saved = block_forward(start, part, wide_all[0], narrow_all[0], norms[0:4], allowed)
    encoded_low = encoded.astype(jnp.bfloat16)
    latent = matmul_plain(encoded_low, edge_qin)
    gap = chosen - latent
    loss_part = loss_pix + (1.0 + commitment) * jnp.sum(gap * gap) / latent_total
    grad_latent = (
        matmul_plain(grad_begin_low, edge_qout) - 2.0 * commitment * gap / latent_total
    ).astype(jnp.bfloat16)
    fold = lane_mask.shape[1] // code_width
    gap_wide = jnp.where(lane_mask, jnp.tile(2.0 * gap / latent_total, (1, fold)), 0.0)
    gap_high = gap_wide.astype(jnp.bfloat16)
    gap_rest = gap_wide - gap_high.astype(jnp.float32)
    gap_middle = gap_rest.astype(jnp.bfloat16)
    gap_low = (gap_rest - gap_middle.astype(jnp.float32)).astype(jnp.bfloat16)
    grad_book = (
        matmul_outer(one_hot, gap_high) + matmul_outer(one_hot, gap_middle)
    ) + matmul_outer(one_hot, gap_low)
    grad_qin = matmul_outer(encoded_low, grad_latent)
    grad_start, enc_wide, enc_narrow, enc_gains = block_backward(
        matmul_trans(grad_latent, edge_qin), wide_all[0], narrow_all[0], norms[0:4], allowed, enc_saved, groups
    )
    grad_inw = matmul_outer(grad_start.astype(jnp.bfloat16), pixel_rows)
    grads = (
        enc_wide, dec_wide, enc_narrow, dec_narrow,
        jnp.concatenate([grad_inw, grad_pixw, grad_qin, grad_qout], axis=1),
        grad_book,
    )
    norm_grad = jnp.concatenate([enc_gains, dec_gains, gain_last[None], offset_last[None]], axis=0)
    return (grads, norm_grad, loss_part)


def place():
    img_at = lax.axis_index("img")
    band_at = lax.axis_index("band")
    return img_at, band_at, band_at // 4, (band_at // 2) % 2, band_at % 2


def peers(img_at, band_at):
    found = [((img_at + step) % 4, band_at) for step in range(1, 4)]
    return found + [(img_at, (band_at + step) % 8) for step in range(1, 8)]


def meet(img_at, band_at):
    barrier = pltpu.get_barrier_semaphore()
    for peer in peers(img_at, band_at):
        pl.semaphore_signal(barrier, inc=1, device_id=peer, device_id_type=MESH)
    pl.semaphore_wait(barrier, 10)


def far_copy(src, dst, send, recv, target):
    return pltpu.make_async_remote_copy(
        src_ref=src, dst_ref=dst, send_sem=send, recv_sem=recv, device_id=target, device_id_type=MESH
    )


def sum_everywhere(own_ref, img_buf, band_buf, send, recv, img_at, band_at, result_ref):
    img_buf[img_at] = own_ref[...]
    first = [
        far_copy(own_ref, img_buf.at[img_at], send.at[step], recv.at[step], ((img_at + step) % 4, band_at))
        for step in range(1, 4)
    ]
    for copy in first:
        copy.start()
    for copy in first:
        copy.wait()
    result_ref[...] = (img_buf[0] + img_buf[1]) + (img_buf[2] + img_buf[3])
    band_buf[band_at] = result_ref[...]
    second = [
        far_copy(
            result_ref, band_buf.at[band_at], send.at[3 + step], recv.at[3 + step], (img_at, (band_at + step) % 8)
        )
        for step in range(1, 8)
    ]
    for copy in second:
        copy.start()
    for copy in second:
        copy.wait()
    total = band_buf[0]
    for k in range(1, 8):
        total = total + band_buf[k]
    result_ref[...] = total


def gather_kernel(cuts, *refs):
    count = len(cuts)
    shards, (slab, code, tally) = refs[:count], refs[count : count + 3]
    wholes = refs[count + 3 : 2 * count + 3]
    slab_all, code_all, tally_all = refs[2 * count + 3 : 2 * count + 6]
    (img_buf, band_buf, near, z_send, z_recv, p_send, p_recv, e_send, e_recv, t_send, t_recv) = refs[2 * count + 6 :]
    img_at, band_at, y_at, x_at, c_at = place()
    chip_at = band_at // 2
    over_y = (img_at, band_at + 4 - 8 * y_at)
    over_x = (img_at, band_at + 2 - 4 * x_at)
    over_c = (img_at, band_at + 1 - 2 * c_at)
    meet(img_at, band_at)
    exchange = []
    for step in range(1, 4):
        chip = (chip_at + step) % 4
        for k, (src, dst) in enumerate(((slab, slab_all), (code, code_all))):
            exchange.append(
                far_copy(
                    src.at[chip], dst.at[chip_at, c_at], e_send.at[k, step], e_recv.at[k, step],
                    (img_at, 2 * chip + c_at),
                )
            )
    for k, (src, dst) in enumerate(((slab, slab_all), (code, code_all))):
        exchange.append(pltpu.make_async_copy(src.at[chip_at], dst.at[chip_at, c_at], near.at[count + k]))
    for copy in exchange:
        copy.start()

    def along_z(p):
        here = wholes[p].at[img_at, y_at, x_at, c_at]
        copies = [
            far_copy(shards[p], here, z_send.at[p, step], z_recv.at[p, step], ((img_at + step) % 4, band_at))
            for step in range(1, 4)
        ]
        return copies + [pltpu.make_async_copy(shards[p], here, near.at[p])]

    def along_first(p):
        cut, rows = cuts[p], shards[p].shape[0]
        copies = []
        if cut > 0:
            part = wholes[p].at[:, y_at, x_at, c_at, pl.ds(0, cut)]
            copies.append(far_copy(part, part, p_send.at[p, 0], p_recv.at[p, 0], over_y))
        if cut < rows:
            part = wholes[p].at[:, y_at, x_at, c_at, pl.ds(cut, rows - cut)]
            copies.append(far_copy(part, part, p_send.at[p, 1], p_recv.at[p, 1], over_x))
        return copies

    def along_second(p):
        cut, rows = cuts[p], shards[p].shape[0]
        copies = []
        if cut > 0:
            part = wholes[p].at[:, :, x_at, c_at, pl.ds(0, cut)]
            copies.append(far_copy(part, part, p_send.at[p, 2], p_recv.at[p, 2], over_x))
        if cut < rows:
            part = wholes[p].at[:, y_at, :, c_at, pl.ds(cut, rows - cut)]
            copies.append(far_copy(part, part, p_send.at[p, 3], p_recv.at[p, 3], over_y))
        return copies

    def along_core(p):
        part = wholes[p].at[:, :, :, c_at]
        return [far_copy(part, part, p_send.at[p, 4], p_recv.at[p, 4], over_c)]

    stages = (along_z, along_first, along_second, along_core)
    flying = {}

    def launch(p, k):
        flying[p, k] = stages[k](p)
        for copy in flying[p, k]:
            copy.start()

    def land(p, k):
        for copy in flying.pop((p, k)):
            copy.wait()

    for p in range(count):
        launch(p, 0)
    for copy in exchange:
        copy.wait()
    late = []
    for k, dst in enumerate((slab_all, code_all)):
        part = dst.at[:, c_at]
        late.append(far_copy(part, part, e_send.at[k, 0], e_recv.at[k, 0], over_c))
    for copy in late:
        copy.start()
    sum_everywhere(tally, img_buf, band_buf, t_send, t_recv, img_at, band_at, tally_all)
    for beat in range(count + 3):
        for k in range(4):
            p = beat - k
            if 0 <= p < count:
                land(p, k)
                if k < 3:
                    launch(p, k + 1)
    for copy in late:
        copy.wait()


def gather_all(shards, cuts, slab, code, tally):
    any_space = pl.BlockSpec(memory_space=pl.ANY)
    vmem_space = pl.BlockSpec(memory_space=pltpu.VMEM)
    count = len(shards)
    out_shape = [jax.ShapeDtypeStruct((4, 2, 2, 2) + s.shape, s.dtype) for s in shards]
    out_shape += [
        jax.ShapeDtypeStruct((4, 2) + slab.shape[1:], slab.dtype),
        jax.ShapeDtypeStruct((4, 2) + code.shape[1:], code.dtype),
        jax.ShapeDtypeStruct(tally.shape, tally.dtype),
    ]
    dma = pltpu.SemaphoreType.DMA
    return pl.pallas_call(
        functools.partial(gather_kernel, cuts),
        out_shape=out_shape,
        in_specs=[any_space] * (count + 2) + [vmem_space],
        out_specs=[any_space] * (count + 2) + [vmem_space],
        scratch_shapes=[
            pltpu.VMEM((4,) + tally.shape, tally.dtype),
            pltpu.VMEM((8,) + tally.shape, tally.dtype),
            dma((count + 2,)),
            dma((count, 4)), dma((count, 4)),
            dma((count, 5)), dma((count, 5)),
            dma((2, 4)), dma((2, 4)),
            dma((11,)), dma((11,)),
        ],
        compiler_params=pltpu.CompilerParams(collective_id=0, has_side_effects=True),
        name="gather_all",
    )(*shards, slab, code, tally)


def reduce_kernel(cuts, *refs):
    count = len(cuts)
    grads, small = refs[:count], refs[count]
    shares = refs[count + 1 : 2 * count + 1]
    small_all = refs[2 * count + 1]
    rest = refs[2 * count + 2 :]
    own, pair = rest[:count], rest[count : 2 * count]
    first_a, first_b = rest[2 * count : 3 * count], rest[3 * count : 4 * count]
    second_a, second_b = rest[4 * count : 5 * count], rest[5 * count : 6 * count]
    last = rest[6 * count : 7 * count]
    (img_buf, band_buf, small_own, near, p_send, p_recv, z_send, z_recv, t_send, t_recv) = rest[7 * count :]
    img_at, band_at, y_at, x_at, c_at = place()
    over_y = (img_at, band_at + 4 - 8 * y_at)
    over_x = (img_at, band_at + 2 - 4 * x_at)
    over_c = (img_at, band_at + 1 - 2 * c_at)
    meet(img_at, band_at)

    def along_core(p):
        return [
            far_copy(grads[p].at[:, :, :, 1 - c_at], pair[p], p_send.at[p, 0], p_recv.at[p, 0], over_c),
            pltpu.make_async_copy(grads[p].at[:, :, :, c_at], own[p], near.at[p]),
        ]

    def add_core(p):
        def step(k, carry):
            z, yx = k // 4, k % 4
            own[p][z, yx // 2, yx % 2] += pair[p][z, yx // 2, yx % 2]
            return carry
        lax.fori_loop(0, 16, step, 0)

    def spans(p):
        rows = own[p].shape[3]
        return pl.ds(0, cuts[p]), pl.ds(cuts[p], rows - cuts[p])

    def along_first(p):
        rows_a, rows_b = spans(p)
        return [
            far_copy(own[p].at[:, :, 1 - x_at, rows_a], first_a[p], p_send.at[p, 1], p_recv.at[p, 1], over_x),
            far_copy(own[p].at[:, 1 - y_at, :, rows_b], first_b[p], p_send.at[p, 2], p_recv.at[p, 2], over_y),
        ]

    def add_first(p):
        rows_a, rows_b = spans(p)
        def step(k, carry):
            z, w = k // 2, k % 2
            own[p][z, w, x_at, rows_a] += first_a[p][z, w]
            own[p][z, y_at, w, rows_b] += first_b[p][z, w]
            return carry
        lax.fori_loop(0, 8, step, 0)

    def along_second(p):
        rows_a, rows_b = spans(p)
        return [
            far_copy(own[p].at[:, 1 - y_at, x_at, rows_a], second_a[p], p_send.at[p, 3], p_recv.at[p, 3], over_y),
            far_copy(own[p].at[:, y_at, 1 - x_at, rows_b], second_b[p], p_send.at[p, 4], p_recv.at[p, 4], over_x),
        ]

    def add_second(p):
        rows_a, rows_b = spans(p)
        def step(z, carry):
            own[p][z, y_at, x_at, rows_a] += second_a[p][z]
            own[p][z, y_at, x_at, rows_b] += second_b[p][z]
            return carry
        lax.fori_loop(0, 4, step, 0)

    def along_z(p):
        copies = []
        for step in range(1, 4):
            target = (img_at + step) % 4
            copies.append(
                far_copy(
                    own[p].at[target, y_at, x_at], last[p].at[step - 1],
                    z_send.at[p, step], z_recv.at[p, step], (target, band_at),
                )
            )
        return copies

    def add_z(p):
        shares[p][...] = (own[p][img_at, y_at, x_at] + last[p][0]) + (last[p][1] + last[p][2])

    stages = (along_core, along_first, along_second, along_z)
    adds = (add_core, add_first, add_second, add_z)
    flying = {}

    def launch(p, k):
        flying[p, k] = stages[k](p)
        for copy in flying[p, k]:
            copy.start()

    def land(p, k):
        for copy in flying.pop((p, k)):
            copy.wait()
        adds[k](p)

    for p in range(count):
        launch(p, 0)
    for beat in range(count + 3):
        for k in range(4):
            p = beat - k
            if 0 <= p < count:
                land(p, k)
                if k < 3:
                    launch(p, k + 1)
    squares = sum(jnp.sum(share[...] * share[...]) for share in shares)
    shape = small.shape
    at_spot = (lax.broadcasted_iota(jnp.int32, shape, 0) == 11) & (lax.broadcasted_iota(jnp.int32, shape, 1) == 0)
    small_own[...] = small[...] + jnp.where(at_spot, squares, 0.0)
    sum_everywhere(small_own, img_buf, band_buf, t_send, t_recv, img_at, band_at, small_all)


def reduce_all(grads, cuts, small):
    any_space = pl.BlockSpec(memory_space=pl.ANY)
    vmem_space = pl.BlockSpec(memory_space=pltpu.VMEM)
    count = len(grads)
    rows = [g.shape[4] for g in grads]
    wide = [g.shape[5] for g in grads]
    f32 = jnp.float32
    dma = pltpu.SemaphoreType.DMA
    scratch = [pltpu.VMEM((4, 2, 2, r, w), f32) for r, w in zip(rows, wide)]
    scratch += [pltpu.VMEM((4, 2, 2, r, w), f32) for r, w in zip(rows, wide)]
    scratch += [pltpu.VMEM((4, 2, a, w), f32) for a, w in zip(cuts, wide)]
    scratch += [pltpu.VMEM((4, 2, r - a, w), f32) for a, r, w in zip(cuts, rows, wide)]
    scratch += [pltpu.VMEM((4, a, w), f32) for a, w in zip(cuts, wide)]
    scratch += [pltpu.VMEM((4, r - a, w), f32) for a, r, w in zip(cuts, rows, wide)]
    scratch += [pltpu.VMEM((3, r, w), f32) for r, w in zip(rows, wide)]
    scratch += [
        pltpu.VMEM((4,) + small.shape, f32),
        pltpu.VMEM((8,) + small.shape, f32),
        pltpu.VMEM(small.shape, f32),
        dma((count,)),
        dma((count, 5)), dma((count, 5)),
        dma((count, 4)), dma((count, 4)),
        dma((11,)), dma((11,)),
    ]
    return pl.pallas_call(
        functools.partial(reduce_kernel, cuts),
        out_shape=[jax.ShapeDtypeStruct((r, w), f32) for r, w in zip(rows, wide)]
        + [jax.ShapeDtypeStruct(small.shape, f32)],
        in_specs=[any_space] * count + [vmem_space],
        out_specs=[vmem_space] * (count + 1),
        scratch_shapes=scratch,
        compiler_params=pltpu.CompilerParams(collective_id=1, has_side_effects=True, vmem_limit_bytes=56 << 20),
        name="reduce_all",
    )(*grads, small)


def moments(gradient, first_old, second_old):
    first_new = beta_first * first_old + (1.0 - beta_first) * gradient
    second_new = beta_second * second_old + (1.0 - beta_second) * gradient * gradient
    return (first_new, second_new, first_new / (jnp.sqrt(second_new) + adam_eps))


def rotated_update(weight, gradient, first_old, second_old, basis_stack):
    turned = jnp.einsum("rld,lde->rle", gradient, basis_stack, precision=highest)
    first_new, second_new, direction = moments(turned, first_old, second_old)
    turned_back = jnp.einsum("rle,lde->rld", direction, basis_stack, precision=highest)
    return (weight - rate_matrix * (turned_back + weight_decay * weight), first_new, second_new)


def plain_update(weight, gradient, first_old, second_old):
    first_new, second_new, direction = moments(gradient, first_old, second_old)
    return (weight - rate_vector * (direction + weight_decay * weight), first_new, second_new)


def body(
    pixels,
    valid,
    codes,
    image_kind,
    w_wide,
    w_narrow,
    w_edge,
    codebook,
    norms,
    bases,
    basis_edge,
    m_wide,
    v_wide,
    m_narrow,
    v_narrow,
    m_edge,
    v_edge,
    m_code,
    v_code,
    m_norm,
    v_norm,
):
    band_count = lax.axis_size("band")
    band_index = lax.axis_index("band")
    row_count = pixels.shape[2]
    length = row_count * band_count
    batch_count = pixels.shape[0]
    group = band_count // batch_count
    row = band_index // group
    part = band_index % group
    own_rows = length // group
    groups = [[k * group + j for j in range(group)] for k in range(batch_count)]
    layer_count = w_wide.shape[1]
    code_width = codebook.shape[1]
    latent_total = batch_count * lax.axis_size("img") * length * code_width
    both = ("img", "band")

    direct = band_count == 8 and lax.axis_size("img") == 4 and batch_count == 4
    shards = [w_wide[:, l].astype(jnp.bfloat16) for l in range(layer_count)]
    shards += [w_narrow[:, l].astype(jnp.bfloat16) for l in range(layer_count)]
    shards += [w_edge.astype(jnp.bfloat16), codebook.astype(jnp.bfloat16).reshape(-1, 4 * code_width)]
    slab = jnp.concatenate([pixels[:, 0], valid[:, 0].astype(jnp.bfloat16)], axis=2)
    local_count = jnp.sum(valid.astype(jnp.float32))
    patch_size = pixels.shape[3]
    if direct:
        order = (5, 4, 1, 3, 0, 2)
        cuts = tuple({112: 64, 80: 32, 16: 16, 64: 0}[shards[k].shape[0]] for k in order)
        moved = gather_all([shards[k] for k in order], cuts, slab, codes, jnp.full((8, 128), local_count))
        wholes = [None] * 6
        for k, value in zip(order, moved):
            wholes[k] = value.reshape((-1, value.shape[-1]))
        slab_all = moved[6].reshape(length, -1)
        code_all = moved[7].reshape(length)
        count = moved[8][0, 0]
    else:
        wholes = [lax.all_gather(shard, both, axis=0, tiled=True) for shard in shards]
        count = lax.psum(local_count, both)

        def whole_row(local):
            everywhere = lax.all_gather(local, "band", axis=0)
            chosen_row = lax.dynamic_index_in_dim(everywhere, row, axis=1, keepdims=False)
            return chosen_row.reshape((length,) + local.shape[2:])

        slab_all = whole_row(slab)
        code_all = whole_row(codes[:, 0])
    gathered = (wholes[:2], wholes[2:4], wholes[4], wholes[5])
    pixel_all = slab_all[:, :patch_size]
    valid_rows = lax.dynamic_slice_in_dim(slab_all, part * own_rows, own_rows, 0)[:, patch_size:]
    positions = jnp.arange(length, dtype=jnp.int32)
    own_positions = part * own_rows + jnp.arange(own_rows, dtype=jnp.int32)
    kind = lax.dynamic_index_in_dim(image_kind[:, 0], row, 0, keepdims=False)
    span = jnp.where(kind == 0, length, length // 4)
    allowed = (own_positions // span)[:, None] == (positions // span)[None, :]
    local_grads, norm_sum, loss_sum = row_step(
        gathered, norms, pixel_all, valid_rows, code_all, part, allowed, count, latent_total, groups
    )
    if direct:
        blocks = [g.reshape((4, 2, 2, 2, g.shape[0] // 32, g.shape[1])) for g in local_grads]
        order = (1, 3, 0, 2, 4, 5)
        cuts = tuple(blocks[k].shape[4] // 2 for k in order)
        small = jnp.zeros((16, norm_sum.shape[1]), jnp.float32)
        small = small.at[:10].set(norm_sum).at[10, 0].set(loss_sum)
        reduced = reduce_all([blocks[k] for k in order], cuts, small)
        shares = [None] * 6
        for k, value in zip(order, reduced):
            shares[k] = value
        norm_total = reduced[6][:10]
        loss_total = reduced[6][10, 0]
        square_total = reduced[6][11, 0]
    else:
        shares = [lax.psum_scatter(g, both, scatter_dimension=0, tiled=True) for g in local_grads]
        squares = sum(jnp.sum(share * share) for share in shares)
        norm_total, square_total, loss_total = lax.psum((norm_sum, squares, loss_sum), both)
    grad_sum = (
        jnp.stack([shares[0], shares[1]], axis=1),
        jnp.stack([shares[2], shares[3]], axis=1),
        shares[4],
        shares[5].reshape(-1, code_width),
    )
    grad_norm = jnp.sqrt(square_total + jnp.sum(norm_total * norm_total))
    factor = jnp.minimum(1.0, clip_level / grad_norm)
    grad_wide, grad_narrow, grad_edge, grad_book = grad_sum
    new_wide, new_m_wide, new_v_wide = rotated_update(
        w_wide, factor * grad_wide, m_wide, v_wide, bases[:layer_count]
    )
    new_narrow, new_m_narrow, new_v_narrow = rotated_update(
        w_narrow, factor * grad_narrow, m_narrow, v_narrow, bases[layer_count:]
    )
    new_edge, new_m_edge, new_v_edge = rotated_update(
        w_edge[:, None],
        factor * grad_edge[:, None],
        m_edge[:, None],
        v_edge[:, None],
        basis_edge[None],
    )
    new_book, new_m_code, new_v_code = plain_update(codebook, factor * grad_book, m_code, v_code)
    new_norms, new_m_norm, new_v_norm = plain_update(norms, factor * norm_total, m_norm, v_norm)
    return (
        new_wide,
        new_m_wide,
        new_v_wide,
        new_narrow,
        new_m_narrow,
        new_v_narrow,
        new_edge[:, 0],
        new_m_edge[:, 0],
        new_v_edge[:, 0],
        new_book,
        new_m_code,
        new_v_code,
        new_norms,
        new_m_norm,
        new_v_norm,
        grad_norm,
        loss_total,
    )


def solution(mesh):
    in_specs = (
        P(None, "img", "band", None),
        P(None, "img", "band", None),
        P(None, "img", "band"),
        P(None, "img"),
        P(("img", "band"), None, None),
        P(("img", "band"), None, None),
        P(("img", "band"), None),
        P(("img", "band"), None),
        P(),
        P(),
        P(),
        P(("img", "band"), None, None),
        P(("img", "band"), None, None),
        P(("img", "band"), None, None),
        P(("img", "band"), None, None),
        P(("img", "band"), None),
        P(("img", "band"), None),
        P(("img", "band"), None),
        P(("img", "band"), None),
        P(),
        P(),
    )
    out_specs = (
        P(("img", "band"), None, None),
        P(("img", "band"), None, None),
        P(("img", "band"), None, None),
        P(("img", "band"), None, None),
        P(("img", "band"), None, None),
        P(("img", "band"), None, None),
        P(("img", "band"), None),
        P(("img", "band"), None),
        P(("img", "band"), None),
        P(("img", "band"), None),
        P(("img", "band"), None),
        P(("img", "band"), None),
        P(),
        P(),
        P(),
        P(),
        P(),
    )
    return jax.shard_map(body, mesh=mesh, in_specs=in_specs, out_specs=out_specs, check_vma=False)
```

```python
import functools

import jax
import jax.numpy as jnp
from jax import lax
from jax.experimental import pallas as pl
from jax.experimental.pallas import tpu as pltpu
from jax.sharding import PartitionSpec as P

HEADS = 8
HDIM = 64
MESH = pl.DeviceIdType.MESH


norm_eps = 1e-05
adam_eps = 1e-08
clip_level = 0.001
beta_first = 0.5
beta_second = 0.6
rate_matrix = 0.02
rate_vector = 0.3
weight_decay = 0.01
commitment = 0.25
masked_score = -1000000000.0
highest = lax.Precision.HIGHEST


def matmul_plain(first_op, second_op):
    return jnp.dot(first_op, second_op, preferred_element_type=jnp.float32)


def matmul_trans(first_op, second_op):
    return lax.dot_general(
        first_op, second_op, (((1,), (1,)), ((), ())), preferred_element_type=jnp.float32
    )


def matmul_outer(first_op, second_op):
    return lax.dot_general(
        first_op, second_op, (((0,), (0,)), ((), ())), preferred_element_type=jnp.float32
    )


def layer_norm(hidden, scale_gain, offset):
    centred = hidden - jnp.mean(hidden, axis=-1, keepdims=True)
    spread = jnp.mean(centred * centred, axis=-1, keepdims=True)
    return centred * lax.rsqrt(spread + norm_eps) * scale_gain + offset


def gelu_tanh(inputs):
    return (
        0.5
        * inputs
        * (1.0 + jnp.tanh(0.7978845608028654 * (inputs + 0.044715 * inputs * inputs * inputs)))
    )


def split_heads(matrix):
    return matrix.reshape(matrix.shape[0], HEADS, HDIM)


def head_scores(q_heads, k_heads, allowed):
    scores = jnp.einsum(
        "qhd,khd->hqk", q_heads, k_heads, preferred_element_type=jnp.float32
    ) * HDIM ** (-0.5)
    return jnp.where(allowed[None], scores, masked_score)


def attend(queries, key_rows, value_rows, allowed):
    scores = head_scores(split_heads(queries), split_heads(key_rows), allowed)
    score_peak = jnp.max(scores, axis=-1, keepdims=True)
    expo = jnp.exp(scores - score_peak)
    total = jnp.sum(expo, axis=-1, keepdims=True)
    softmaxed = (expo / total).astype(jnp.bfloat16)
    attended = jnp.einsum(
        "hqk,khd->qhd", softmaxed, split_heads(value_rows), preferred_element_type=jnp.float32
    )
    return (
        attended.reshape(queries.shape[0], -1).astype(jnp.bfloat16),
        score_peak + jnp.log(total),
    )


def attend_back(queries, key_rows, value_rows, allowed, log_total, grad_out):
    q_heads = split_heads(queries)
    k_heads = split_heads(key_rows)
    v_heads = split_heads(value_rows)
    g_heads = split_heads(grad_out)
    softmaxed = jnp.exp(head_scores(q_heads, k_heads, allowed) - log_total)
    grad_soft = jnp.einsum("qhd,khd->hqk", g_heads, v_heads, preferred_element_type=jnp.float32)
    row_dot = jnp.sum(softmaxed * grad_soft, axis=-1, keepdims=True)
    grad_scores = (softmaxed * (grad_soft - row_dot)).astype(jnp.bfloat16)
    scale = HDIM ** (-0.5)
    grad_q = (
        jnp.einsum("hqk,khd->qhd", grad_scores, k_heads, preferred_element_type=jnp.float32) * scale
    )
    grad_k = (
        jnp.einsum("hqk,qhd->khd", grad_scores, q_heads, preferred_element_type=jnp.float32) * scale
    )
    grad_v = jnp.einsum(
        "hqk,qhd->khd", softmaxed.astype(jnp.bfloat16), g_heads, preferred_element_type=jnp.float32
    )
    return (
        grad_q.reshape(queries.shape[0], -1),
        grad_k.reshape(key_rows.shape[0], -1),
        grad_v.reshape(key_rows.shape[0], -1),
    )


def block_forward(hidden_all, part, wide_rows, narrow_rows, gain_rows, allowed):
    model_width = hidden_all.shape[1]
    own_rows = allowed.shape[0]
    normed_all = layer_norm(hidden_all, gain_rows[0], gain_rows[1]).astype(jnp.bfloat16)
    hidden = lax.dynamic_slice_in_dim(hidden_all, part * own_rows, own_rows, 0)
    normed = lax.dynamic_slice_in_dim(normed_all, part * own_rows, own_rows, 0)
    queries = matmul_trans(normed, wide_rows[:model_width]).astype(jnp.bfloat16)
    key_rows = matmul_trans(normed_all, wide_rows[model_width : 2 * model_width]).astype(jnp.bfloat16)
    value_rows = matmul_trans(normed_all, wide_rows[2 * model_width : 3 * model_width]).astype(jnp.bfloat16)
    attended, log_total = attend(queries, key_rows, value_rows, allowed)
    middle = hidden + matmul_plain(attended, narrow_rows[:model_width])
    second = layer_norm(middle, gain_rows[2], gain_rows[3]).astype(jnp.bfloat16)
    upper_in = matmul_trans(second, wide_rows[3 * model_width :])
    active = gelu_tanh(upper_in).astype(jnp.bfloat16)
    result = middle + matmul_plain(active, narrow_rows[model_width:])
    return (
        result,
        (hidden, normed, queries, key_rows, value_rows, attended, log_total, middle, second, upper_in, active),
    )


def block_backward(grad_out, wide_rows, narrow_rows, gain_rows, allowed, saved, groups):
    (hidden, normed, queries, key_rows, value_rows, attended, log_total, middle, second, upper_in, active) = saved
    model_width = hidden.shape[1]
    grad_y = grad_out.astype(jnp.bfloat16)
    grad_down = matmul_outer(active, grad_y)
    grad_active = matmul_trans(grad_y, narrow_rows[model_width:])
    grad_upper = jax.vjp(gelu_tanh, upper_in)[1](grad_active)[0].astype(jnp.bfloat16)
    grad_up = matmul_outer(grad_upper, second)
    _, second_back = jax.vjp(layer_norm, middle, gain_rows[2], gain_rows[3])
    grad_mid, gain_two, offset_two = second_back(
        matmul_plain(grad_upper, wide_rows[3 * model_width :])
    )
    grad_mid = grad_mid + grad_out
    grad_attn = grad_mid.astype(jnp.bfloat16)
    grad_outproj = matmul_outer(attended, grad_attn)
    grad_att = matmul_trans(grad_attn, narrow_rows[:model_width]).astype(jnp.bfloat16)
    grad_q, grad_keys, grad_values = attend_back(
        queries, key_rows, value_rows, allowed, log_total, grad_att
    )
    grad_k = lax.psum_scatter(grad_keys, "band", scatter_dimension=0, tiled=True, axis_index_groups=groups)
    grad_v = lax.psum_scatter(grad_values, "band", scatter_dimension=0, tiled=True, axis_index_groups=groups)
    grad_mixed = jnp.concatenate([grad_q, grad_k, grad_v], axis=1).astype(jnp.bfloat16)
    grad_qkv = matmul_outer(grad_mixed, normed)
    _, first_back = jax.vjp(layer_norm, hidden, gain_rows[0], gain_rows[1])
    grad_in, gain_one, offset_one = first_back(
        matmul_plain(grad_mixed, wide_rows[: 3 * model_width])
    )
    gain_grads = jnp.stack([gain_one, offset_one, gain_two, offset_two], axis=0)
    return (
        grad_in + grad_mid,
        jnp.concatenate([grad_qkv, grad_up], axis=0),
        jnp.concatenate([grad_outproj, grad_down], axis=0),
        gain_grads,
    )


def pick_codes(code_rows, book_wide, code_width):
    fold = book_wide.shape[1] // code_width
    one_hot = (
        (code_rows // fold)[:, None] == jnp.arange(book_wide.shape[0], dtype=jnp.int32)[None, :]
    ).astype(jnp.bfloat16)
    lane_fold = jnp.arange(book_wide.shape[1], dtype=jnp.int32)[None, :] // code_width
    lane_mask = (code_rows % fold)[:, None] == lane_fold
    spread = jnp.where(lane_mask, matmul_plain(one_hot, book_wide), 0.0)
    chosen = sum(spread[:, k * code_width : (k + 1) * code_width] for k in range(fold))
    return chosen, one_hot, lane_mask


def row_step(gathered, norms, pixel_all, valid_rows, code_all, part, allowed, count, latent_total, groups):
    wide_all, narrow_all, edge_all, book_wide = gathered
    patch_size = pixel_all.shape[1]
    code_width = edge_all.shape[1] // 2 - patch_size
    own_rows = allowed.shape[0]
    edge_in = edge_all[:, :patch_size]
    edge_pix = edge_all[:, patch_size : 2 * patch_size]
    edge_qin = edge_all[:, 2 * patch_size : 2 * patch_size + code_width]
    edge_qout = edge_all[:, 2 * patch_size + code_width :]
    pixel_rows = lax.dynamic_slice_in_dim(pixel_all, part * own_rows, own_rows, 0)
    chosen_all, one_hot_all, lane_mask_all = pick_codes(code_all, book_wide, code_width)
    chosen_low_all = chosen_all.astype(jnp.bfloat16)
    chosen = lax.dynamic_slice_in_dim(chosen_all, part * own_rows, own_rows, 0)
    one_hot = lax.dynamic_slice_in_dim(one_hot_all, part * own_rows, own_rows, 0)
    lane_mask = lax.dynamic_slice_in_dim(lane_mask_all, part * own_rows, own_rows, 0)
    chosen_low = chosen.astype(jnp.bfloat16)
    begin = matmul_trans(chosen_low_all, edge_qout)
    decoded, dec_saved = block_forward(begin, part, wide_all[1], narrow_all[1], norms[4:8], allowed)
    final = layer_norm(decoded, norms[8], norms[9]).astype(jnp.bfloat16)
    predict = matmul_plain(final, edge_pix)
    error = predict - pixel_rows.astype(jnp.float32)
    pixel_mask = valid_rows.astype(jnp.float32)
    loss_pix = jnp.sum(pixel_mask * (error * error + jnp.abs(error))) / count
    grad_pred = (pixel_mask * (2.0 * error + jnp.sign(error)) / count).astype(jnp.bfloat16)
    grad_pixw = matmul_outer(final, grad_pred)
    _, final_back = jax.vjp(layer_norm, decoded, norms[8], norms[9])
    grad_dec, gain_last, offset_last = final_back(matmul_trans(grad_pred, edge_pix))
    grad_begin, dec_wide, dec_narrow, dec_gains = block_backward(
        grad_dec, wide_all[1], narrow_all[1], norms[4:8], allowed, dec_saved, groups
    )
    grad_begin_low = grad_begin.astype(jnp.bfloat16)
    grad_qout = matmul_outer(grad_begin_low, chosen_low)
    start = matmul_trans(pixel_all, edge_in)
    encoded, enc_saved = block_forward(start, part, wide_all[0], narrow_all[0], norms[0:4], allowed)
    encoded_low = encoded.astype(jnp.bfloat16)
    latent = matmul_plain(encoded_low, edge_qin)
    gap = chosen - latent
    loss_part = loss_pix + (1.0 + commitment) * jnp.sum(gap * gap) / latent_total
    grad_latent = (
        matmul_plain(grad_begin_low, edge_qout) - 2.0 * commitment * gap / latent_total
    ).astype(jnp.bfloat16)
    fold = lane_mask.shape[1] // code_width
    gap_wide = jnp.where(lane_mask, jnp.tile(2.0 * gap / latent_total, (1, fold)), 0.0)
    gap_high = gap_wide.astype(jnp.bfloat16)
    gap_rest = gap_wide - gap_high.astype(jnp.float32)
    gap_middle = gap_rest.astype(jnp.bfloat16)
    gap_low = (gap_rest - gap_middle.astype(jnp.float32)).astype(jnp.bfloat16)
    grad_book = (
        matmul_outer(one_hot, gap_high) + matmul_outer(one_hot, gap_middle)
    ) + matmul_outer(one_hot, gap_low)
    grad_qin = matmul_outer(encoded_low, grad_latent)
    grad_start, enc_wide, enc_narrow, enc_gains = block_backward(
        matmul_trans(grad_latent, edge_qin), wide_all[0], narrow_all[0], norms[0:4], allowed, enc_saved, groups
    )
    grad_inw = matmul_outer(grad_start.astype(jnp.bfloat16), pixel_rows)
    grads = (
        enc_wide, dec_wide, enc_narrow, dec_narrow,
        jnp.concatenate([grad_inw, grad_pixw, grad_qin, grad_qout], axis=1),
        grad_book,
    )
    norm_grad = jnp.concatenate([enc_gains, dec_gains, gain_last[None], offset_last[None]], axis=0)
    return (grads, norm_grad, loss_part)


def place():
    img_at = lax.axis_index("img")
    band_at = lax.axis_index("band")
    return img_at, band_at, band_at // 4, (band_at // 2) % 2, band_at % 2


def peers(img_at, band_at):
    found = [((img_at + step) % 4, band_at) for step in range(1, 4)]
    return found + [(img_at, (band_at + step) % 8) for step in range(1, 8)]


def meet(img_at, band_at):
    barrier = pltpu.get_barrier_semaphore()
    for peer in peers(img_at, band_at):
        pl.semaphore_signal(barrier, inc=1, device_id=peer, device_id_type=MESH)
    pl.semaphore_wait(barrier, 10)


def far_copy(src, dst, send, recv, target):
    return pltpu.make_async_remote_copy(
        src_ref=src, dst_ref=dst, send_sem=send, recv_sem=recv, device_id=target, device_id_type=MESH
    )


def sum_everywhere(own_ref, img_buf, band_buf, send, recv, img_at, band_at, result_ref):
    img_buf[img_at] = own_ref[...]
    first = [
        far_copy(own_ref, img_buf.at[img_at], send.at[step], recv.at[step], ((img_at + step) % 4, band_at))
        for step in range(1, 4)
    ]
    for copy in first:
        copy.start()
    for copy in first:
        copy.wait()
    result_ref[...] = (img_buf[0] + img_buf[1]) + (img_buf[2] + img_buf[3])
    band_buf[band_at] = result_ref[...]
    second = [
        far_copy(
            result_ref, band_buf.at[band_at], send.at[3 + step], recv.at[3 + step], (img_at, (band_at + step) % 8)
        )
        for step in range(1, 8)
    ]
    for copy in second:
        copy.start()
    for copy in second:
        copy.wait()
    total = band_buf[0]
    for k in range(1, 8):
        total = total + band_buf[k]
    result_ref[...] = total


def gather_kernel(cuts, *refs):
    count = len(cuts)
    shards, (slab, code, tally) = refs[:count], refs[count : count + 3]
    wholes = refs[count + 3 : 2 * count + 3]
    slab_all, code_all, tally_all = refs[2 * count + 3 : 2 * count + 6]
    (img_buf, band_buf, near, z_send, z_recv, p_send, p_recv, e_send, e_recv, t_send, t_recv) = refs[2 * count + 6 :]
    img_at, band_at, y_at, x_at, c_at = place()
    chip_at = band_at // 2
    over_y = (img_at, band_at + 4 - 8 * y_at)
    over_x = (img_at, band_at + 2 - 4 * x_at)
    over_c = (img_at, band_at + 1 - 2 * c_at)
    meet(img_at, band_at)
    exchange = []
    for step in range(1, 4):
        chip = (chip_at + step) % 4
        for k, (src, dst) in enumerate(((slab, slab_all), (code, code_all))):
            exchange.append(
                far_copy(
                    src.at[chip], dst.at[chip_at, c_at], e_send.at[k, step], e_recv.at[k, step],
                    (img_at, 2 * chip + c_at),
                )
            )
    for k, (src, dst) in enumerate(((slab, slab_all), (code, code_all))):
        exchange.append(pltpu.make_async_copy(src.at[chip_at], dst.at[chip_at, c_at], near.at[count + k]))
    for copy in exchange:
        copy.start()

    def along_z(p):
        here = wholes[p].at[img_at, y_at, x_at, c_at]
        copies = [
            far_copy(shards[p], here, z_send.at[p, step], z_recv.at[p, step], ((img_at + step) % 4, band_at))
            for step in range(1, 4)
        ]
        return copies + [pltpu.make_async_copy(shards[p], here, near.at[p])]

    def along_first(p):
        cut, rows = cuts[p], shards[p].shape[0]
        copies = []
        if cut > 0:
            part = wholes[p].at[:, y_at, x_at, c_at, pl.ds(0, cut)]
            copies.append(far_copy(part, part, p_send.at[p, 0], p_recv.at[p, 0], over_y))
        if cut < rows:
            part = wholes[p].at[:, y_at, x_at, c_at, pl.ds(cut, rows - cut)]
            copies.append(far_copy(part, part, p_send.at[p, 1], p_recv.at[p, 1], over_x))
        return copies

    def along_second(p):
        cut, rows = cuts[p], shards[p].shape[0]
        copies = []
        if cut > 0:
            part = wholes[p].at[:, :, x_at, c_at, pl.ds(0, cut)]
            copies.append(far_copy(part, part, p_send.at[p, 2], p_recv.at[p, 2], over_x))
        if cut < rows:
            part = wholes[p].at[:, y_at, :, c_at, pl.ds(cut, rows - cut)]
            copies.append(far_copy(part, part, p_send.at[p, 3], p_recv.at[p, 3], over_y))
        return copies

    def along_core(p):
        part = wholes[p].at[:, :, :, c_at]
        return [far_copy(part, part, p_send.at[p, 4], p_recv.at[p, 4], over_c)]

    stages = (along_z, along_first, along_second, along_core)
    flying = {}

    def launch(p, k):
        flying[p, k] = stages[k](p)
        for copy in flying[p, k]:
            copy.start()

    def land(p, k):
        for copy in flying.pop((p, k)):
            copy.wait()

    for p in range(count):
        launch(p, 0)
    for copy in exchange:
        copy.wait()
    late = []
    for k, dst in enumerate((slab_all, code_all)):
        part = dst.at[:, c_at]
        late.append(far_copy(part, part, e_send.at[k, 0], e_recv.at[k, 0], over_c))
    for copy in late:
        copy.start()
    sum_everywhere(tally, img_buf, band_buf, t_send, t_recv, img_at, band_at, tally_all)
    for beat in range(count + 3):
        for k in range(4):
            p = beat - k
            if 0 <= p < count:
                land(p, k)
                if k < 3:
                    launch(p, k + 1)
    for copy in late:
        copy.wait()


def gather_all(shards, cuts, slab, code, tally):
    any_space = pl.BlockSpec(memory_space=pl.ANY)
    vmem_space = pl.BlockSpec(memory_space=pltpu.VMEM)
    count = len(shards)
    out_shape = [jax.ShapeDtypeStruct((4, 2, 2, 2) + s.shape, s.dtype) for s in shards]
    out_shape += [
        jax.ShapeDtypeStruct((4, 2) + slab.shape[1:], slab.dtype),
        jax.ShapeDtypeStruct((4, 2) + code.shape[1:], code.dtype),
        jax.ShapeDtypeStruct(tally.shape, tally.dtype),
    ]
    dma = pltpu.SemaphoreType.DMA
    return pl.pallas_call(
        functools.partial(gather_kernel, cuts),
        out_shape=out_shape,
        in_specs=[any_space] * (count + 2) + [vmem_space],
        out_specs=[any_space] * (count + 2) + [vmem_space],
        scratch_shapes=[
            pltpu.VMEM((4,) + tally.shape, tally.dtype),
            pltpu.VMEM((8,) + tally.shape, tally.dtype),
            dma((count + 2,)),
            dma((count, 4)), dma((count, 4)),
            dma((count, 5)), dma((count, 5)),
            dma((2, 4)), dma((2, 4)),
            dma((11,)), dma((11,)),
        ],
        compiler_params=pltpu.CompilerParams(collective_id=0, has_side_effects=True),
        name="gather_all",
    )(*shards, slab, code, tally)


def dot_nn(a, b):
    return lax.dot_general(a, b, (((1,), (0,)), ((), ())), preferred_element_type=jnp.float32)


def dot_nt(a, b):
    return lax.dot_general(a, b, (((1,), (1,)), ((), ())), preferred_element_type=jnp.float32)


def dot_tn(a, b):
    return lax.dot_general(a, b, (((0,), (0,)), ((), ())), preferred_element_type=jnp.float32)


def norm_parts(h):
    centred = h - jnp.mean(h, axis=-1, keepdims=True)
    rate = lax.rsqrt(jnp.mean(centred * centred, axis=-1, keepdims=True) + norm_eps)
    return centred * rate, rate


def norm_back(grad, h, gain):
    shape, rate = norm_parts(h)
    inner = grad * gain
    back = rate * (
        inner
        - jnp.mean(inner, axis=-1, keepdims=True)
        - shape * jnp.mean(inner * shape, axis=-1, keepdims=True)
    )
    return (
        back,
        jnp.sum(grad * shape, axis=0, keepdims=True),
        jnp.sum(grad, axis=0, keepdims=True),
    )


STEP = 256


def block_kernel(decoder, latent_total, *refs):
    n_in = 12 if decoder else 13
    if decoder:
        (code_col, book, first_w, wide, narrow, norms, q_extra, k_extra, e_pix, pix_own, mask_own, tally) = refs[:n_in]
        (g_wide, g_narrow, small, g_head, g_first, chosen_out, cross_out) = refs[n_in : n_in + 7]
        rest = refs[n_in + 7 :]
    else:
        (source, first_w, wide, narrow, norms, q_extra, k_extra, e_qin, pix_own, chosen, cross, code_col, code_row) = refs[:n_in]
        (g_wide, g_narrow, small, g_head, g_first, g_book) = refs[n_in : n_in + 6]
        rest = refs[n_in + 6 :]
    (hidden, normed, q_buf, kv, probs, att, middle, second, slope, active, grad_out, grad_low, gup, gatt,
     dkv, dkv_in, dqkv, stage, stage_sem, x_send, x_recv) = rest[:21]
    if decoder:
        spread, = rest[21:22]
        source = spread
    img_at, band_at, y_at, x_at, part = place()
    barrier = pltpu.get_barrier_semaphore()
    sibling = (img_at, band_at + 1 - 2 * part)
    pl.semaphore_signal(barrier, inc=1, device_id=sibling, device_id_type=MESH)
    pl.semaphore_wait(barrier, 1)
    total_rows, width = hidden.shape
    own_rows = q_buf.shape[0]
    own = pl.multiple_of(part * own_rows, own_rows)
    base = 4 if decoder else 0
    chunks_all, chunks_own = total_rows // STEP, own_rows // STEP
    f32, bf16 = jnp.float32, jnp.bfloat16

    def at(k):
        return pl.ds(pl.multiple_of(k * STEP, STEP), STEP)

    def at_own(k):
        return pl.ds(pl.multiple_of(own + k * STEP, STEP), STEP)

    def gain(k):
        return norms[pl.ds(base + k, 1), :]

    small[...] = jnp.zeros(small.shape, f32)

    def enter(k, carry):
        rows = at(k)
        if decoder:
            code = code_col[rows]
            fold = book.shape[1] // 32
            picks = lax.broadcasted_iota(jnp.int32, (STEP, book.shape[0]), 1)
            hot = jnp.where(picks == code // fold, 1.0, 0.0).astype(bf16)
            lanes = lax.broadcasted_iota(jnp.int32, (STEP, book.shape[1]), 1) // 32
            spread[rows] = jnp.where(lanes == code % fold, dot_nn(hot, book[...]), 0.0).astype(bf16)
        h = dot_nt(source[rows], first_w[...])
        hidden[rows] = h
        shape, _ = norm_parts(h)
        low = (shape * gain(0) + gain(1)).astype(bf16)
        normed[rows] = low
        kv[rows] = dot_nt(low, wide[width : 3 * width]).astype(bf16)
        return carry

    lax.fori_loop(0, chunks_all, enter, 0)

    def make_q(k, carry):
        q_buf[at(k)] = (dot_nt(normed[at_own(k)], wide[:width]).astype(bf16).astype(f32) * HDIM**-0.5).astype(bf16)
        return carry

    lax.fori_loop(0, chunks_own, make_q, 0)
    lane_head = lax.broadcasted_iota(jnp.int32, (1, 128), 1) // HDIM
    picks_head = [jnp.where(lane_head == k, 1.0, 0.0).astype(bf16) for k in range(2)]

    def pair_lanes(p, offset=0):
        return pl.ds(pl.multiple_of(offset + p * 128, 128), 128)

    def attend_pair(p, carry):
        k_cat = jnp.concatenate([kv[:, pair_lanes(p)], k_extra[...]], axis=1)
        v_pair = kv[:, pair_lanes(p, width)]

        def rows_step(j, inner):
            rows = at(j)
            q_pair = q_buf[rows, pair_lanes(p)]
            mixed = None
            for k in range(2):
                q_cat = jnp.concatenate([q_pair * picks_head[k], q_extra[rows]], axis=1)
                scores = dot_nt(q_cat, k_cat)
                expo = jnp.exp(scores - jnp.max(scores, axis=-1, keepdims=True))
                prob = expo * (1.0 / jnp.sum(expo, axis=-1, keepdims=True))
                probs[2 * p + k, rows] = prob
                term = dot_nn(prob.astype(bf16), v_pair * picks_head[k])
                mixed = term if mixed is None else mixed + term
            att[rows, pair_lanes(p)] = mixed.astype(bf16)
            return inner

        return lax.fori_loop(0, chunks_own, rows_step, carry)

    lax.fori_loop(0, width // 128, attend_pair, 0)

    def after_attention(k, carry):
        rows = at(k)
        mid = hidden[at_own(k)] + dot_nn(att[rows], narrow[:width])
        middle[rows] = mid
        shape, _ = norm_parts(mid)
        second[rows] = (shape * gain(2) + gain(3)).astype(bf16)
        grad_out[rows] = mid
        return carry

    lax.fori_loop(0, chunks_own, after_attention, 0)

    def mlp(n, carry):
        f = n // chunks_own
        rows = at(n % chunks_own)
        feature = pl.ds(pl.multiple_of(f * width, width), width)
        u = dot_nt(second[rows], wide[pl.ds(pl.multiple_of((3 + f) * width, width), width)])
        squared = u * u
        bend = jnp.tanh(0.7978845608028654 * (u + 0.044715 * squared * u))
        low = (0.5 * u * (1.0 + bend)).astype(bf16)
        active[rows, feature] = low
        slope[rows, feature] = 0.5 * (1.0 + bend) + (0.5 * u) * (1.0 - bend * bend) * (
            0.7978845608028654 * (1.0 + (3.0 * 0.044715) * squared)
        )
        grad_out[rows] += dot_nn(low, narrow[pl.ds(pl.multiple_of((1 + f) * width, width), width)])
        return carry

    lax.fori_loop(0, 4 * chunks_own, mlp, 0)

    def add_small(row, value):
        small[pl.ds(row, 1), :] += value

    first_lane = lax.broadcasted_iota(jnp.int32, (1, width), 1) == 0

    def add_loss(value):
        add_small(6, jnp.where(first_lane, value, 0.0))

    def head(k, carry):
        rows = at(k)
        out = grad_out[rows]
        if decoder:
            shape, _ = norm_parts(out)
            final = (shape * norms[pl.ds(8, 1), :] + norms[pl.ds(9, 1), :]).astype(bf16)
            error = dot_nn(final, e_pix[...]) - pix_own[rows].astype(f32)
            counted = mask_own[rows].astype(f32)
            number = tally[0:1, 0:1]
            add_loss(jnp.sum(counted * (error * error + jnp.abs(error))) / number)
            sign = jnp.where(error > 0.0, 1.0, jnp.where(error < 0.0, -1.0, 0.0))
            grad_pred = (counted * (2.0 * error + sign) / number).astype(bf16)
            g_head[...] += dot_tn(final, grad_pred)
            back, g_gain, g_offset = norm_back(dot_nt(grad_pred, e_pix[...]), out, norms[pl.ds(8, 1), :])
            add_small(4, g_gain)
            add_small(5, g_offset)
        else:
            low = out.astype(bf16)
            lanes = lax.broadcasted_iota(jnp.int32, (STEP, 128), 1) // 32
            mine = lanes == code_col[at_own(k)] % 4
            gap = jnp.where(mine, chosen[rows].astype(f32) - dot_nn(low, e_qin[...]), 0.0)
            add_loss((1.0 + commitment) * jnp.sum(gap * gap) / latent_total)
            grad_latent = jnp.where(mine, cross[rows] - 2.0 * commitment * gap / latent_total, 0.0).astype(bf16)
            g_head[...] += dot_tn(low, grad_latent)
            back = dot_nt(grad_latent, e_qin[...])
            gap = 2.0 * gap / latent_total
            high = gap.astype(bf16)
            left = gap - high.astype(f32)
            between = left.astype(bf16)
            parts = jnp.concatenate([high, between, (left - between.astype(f32)).astype(bf16)], axis=1)
            split[rows] = parts
        grad_out[rows] = back
        grad_low[rows] = back.astype(bf16)
        return carry

    g_head[...] = jnp.zeros(g_head.shape, f32)
    if not decoder:
        split = rest[21]
    lax.fori_loop(0, chunks_own, head, 0)

    if not decoder:
        def book_rows(k, carry):
            picks = lax.broadcasted_iota(jnp.int32, (STEP, own_rows), 0) + k * STEP
            hot = jnp.where(picks == code_row[...] // 4, 1.0, 0.0).astype(bf16)
            summed = dot_nn(hot, split[...])
            g_book[at(k)] = (summed[:, :128] + summed[:, 128:256]) + summed[:, 256:]
            return carry
        lax.fori_loop(0, g_book.shape[0] // STEP, book_rows, 0)

    def mlp_back(k, carry):
        rows = at(k)
        gy = grad_low[rows]

        def feature_step(f, acc):
            feature = pl.ds(pl.multiple_of(f * width, width), width)
            ga = dot_nt(gy, narrow[pl.ds(pl.multiple_of((1 + f) * width, width), width)])
            low = (ga * slope[rows, feature]).astype(bf16)
            gup[rows, feature] = low
            return acc + dot_nn(low, wide[pl.ds(pl.multiple_of((3 + f) * width, width), width)])

        gsec = lax.fori_loop(0, 4, feature_step, jnp.zeros((STEP, width), f32))
        back, g_gain, g_offset = norm_back(gsec, middle[rows], gain(2))
        add_small(2, g_gain)
        add_small(3, g_offset)
        grad_mid = back + grad_out[rows]
        grad_out[rows] = grad_mid
        low = grad_mid.astype(bf16)
        mid_low[rows] = low
        gatt[rows] = dot_nt(low, narrow[:width]).astype(bf16)
        return carry

    mid_low = rest[22]
    lax.fori_loop(0, chunks_own, mlp_back, 0)

    def attend_back_pair(p, carry):
        k_pair = kv[:, pair_lanes(p)]
        v_pair = kv[:, pair_lanes(p, width)]
        dkv[:, pair_lanes(p)] = jnp.zeros((total_rows, 128), f32)
        dkv[:, pair_lanes(p, width)] = jnp.zeros((total_rows, 128), f32)

        def rows_step(j, inner):
            rows = at(j)
            q_pair = q_buf[rows, pair_lanes(p)]
            g_pair = gatt[rows, pair_lanes(p)]
            dq = None
            for k in range(2):
                g_head_rows = g_pair * picks_head[k]
                prob = probs[2 * p + k, rows]
                d_prob = dot_nt(g_head_rows, v_pair)
                dot_row = jnp.sum(prob * d_prob, axis=-1, keepdims=True)
                d_score = (prob * (d_prob - dot_row)).astype(bf16)
                term = dot_nn(d_score, k_pair * picks_head[k])
                dq = term if dq is None else dq + term
                dkv[:, pair_lanes(p)] += dot_tn(d_score, q_pair * picks_head[k])
                dkv[:, pair_lanes(p, width)] += dot_tn(prob.astype(bf16), g_head_rows)
            dqkv[rows, pair_lanes(p)] = (dq * HDIM**-0.5).astype(bf16)
            return inner

        return lax.fori_loop(0, chunks_own, rows_step, carry)

    lax.fori_loop(0, width // 128, attend_back_pair, 0)
    theirs = pl.ds(pl.multiple_of((1 - part) * own_rows, own_rows), own_rows)
    swap = far_copy(dkv.at[theirs], dkv_in, x_send, x_recv, sibling)
    swap.start()

    def emit(lhs, rhs, rhs_rows, out, out_row, count):
        def copy_of(k):
            slot = k % 2
            return pltpu.make_async_copy(
                stage.at[slot], out.at[pl.ds(pl.multiple_of((out_row + k) * width, width), width)], stage_sem.at[slot]
            )

        def step(k, carry):
            value = dot_tn(lhs[:, pl.ds(pl.multiple_of(k * width, width), width)], rhs[rhs_rows])

            @pl.when(k >= 2)
            def _():
                copy_of(k - 2).wait()

            stage[k % 2] = value
            copy_of(k).start()
            return carry

        lax.fori_loop(0, count, step, 0)
        for k in range(max(0, count - 2), count):
            copy_of(k).wait()

    every = slice(None)
    emit(active, grad_low, every, g_narrow, 1, 4)
    emit(gup, second, every, g_wide, 3, 4)
    emit(att, mid_low, every, g_narrow, 0, 1)
    swap.wait()

    def join(k, carry):
        rows = at(k)
        dqkv[rows, width:] = (dkv[at_own(k)] + dkv_in[rows]).astype(bf16)
        return carry

    lax.fori_loop(0, chunks_own, join, 0)
    emit(dqkv, normed, pl.ds(own, own_rows), g_wide, 0, 3)
    g_first[...] = jnp.zeros(g_first.shape, f32)

    def leave(k, carry):
        rows = at(k)
        grad_normed = dot_nn(dqkv[rows], wide[: 3 * width])
        back, g_gain, g_offset = norm_back(grad_normed, hidden[at_own(k)], gain(0))
        add_small(0, g_gain)
        add_small(1, g_offset)
        low = (back + grad_out[rows]).astype(bf16)
        if decoder:
            mine = spread[at_own(k)]
            chosen_out[rows] = mine
            cross_out[rows] = dot_nn(low, first_w[...])
            g_first[...] += dot_tn(low, mine)
        else:
            g_first[...] += dot_tn(low, pix_own[rows])
        return carry

    lax.fori_loop(0, chunks_own, leave, 0)


def run_block(decoder, latent_total, inputs, total_rows, own_rows):
    width = 512
    f32, bf16 = jnp.float32, jnp.bfloat16
    any_space = pl.BlockSpec(memory_space=pl.ANY)
    vmem = pl.BlockSpec(memory_space=pltpu.VMEM)
    shape = jax.ShapeDtypeStruct
    out_shape = [shape((7 * width, width), f32), shape((5 * width, width), f32), shape((8, width), f32)]
    if decoder:
        out_shape += [shape((width, 192), f32), shape((width, 128), f32)]
        out_shape += [shape((own_rows, 128), bf16), shape((own_rows, 128), f32)]
    else:
        out_shape += [shape((width, 128), f32), shape((width, 192), f32), shape((2048, 128), f32)]
    scratch = [
        pltpu.VMEM((total_rows, width), f32),
        pltpu.VMEM((total_rows, width), bf16),
        pltpu.VMEM((own_rows, width), bf16),
        pltpu.VMEM((total_rows, 2 * width), bf16),
        pltpu.VMEM((HEADS, own_rows, total_rows), f32),
        pltpu.VMEM((own_rows, width), bf16),
        pltpu.VMEM((own_rows, width), f32),
        pltpu.VMEM((own_rows, width), bf16),
        pltpu.VMEM((own_rows, 4 * width), f32),
        pltpu.VMEM((own_rows, 4 * width), bf16),
        pltpu.VMEM((own_rows, width), f32),
        pltpu.VMEM((own_rows, width), bf16),
        pltpu.VMEM((own_rows, 4 * width), bf16),
        pltpu.VMEM((own_rows, width), bf16),
        pltpu.VMEM((total_rows, 2 * width), f32),
        pltpu.VMEM((own_rows, 2 * width), f32),
        pltpu.VMEM((own_rows, 3 * width), bf16),
        pltpu.VMEM((2, width, width), f32),
        pltpu.SemaphoreType.DMA((2,)),
        pltpu.SemaphoreType.DMA,
        pltpu.SemaphoreType.DMA,
        pltpu.VMEM((total_rows, 128), bf16) if decoder else pltpu.VMEM((own_rows, 384), bf16),
        pltpu.VMEM((own_rows, width), bf16),
    ]
    return pl.pallas_call(
        functools.partial(block_kernel, decoder, latent_total),
        out_shape=out_shape,
        in_specs=[vmem] * len(inputs),
        out_specs=[any_space] * 2 + [vmem] * (len(out_shape) - 2),
        scratch_shapes=scratch,
        compiler_params=pltpu.CompilerParams(
            collective_id=2 if decoder else 3, has_side_effects=True, vmem_limit_bytes=60 << 20
        ),
        name="decoder_step" if decoder else "encoder_step",
    )(*inputs)


def reduce_kernel(cuts, *refs):
    count = len(cuts)
    grads, small = refs[:count], refs[count]
    shares = refs[count + 1 : 2 * count + 1]
    small_all = refs[2 * count + 1]
    rest = refs[2 * count + 2 :]
    own, pair = rest[:count], rest[count : 2 * count]
    first_a, first_b = rest[2 * count : 3 * count], rest[3 * count : 4 * count]
    second_a, second_b = rest[4 * count : 5 * count], rest[5 * count : 6 * count]
    last = rest[6 * count : 7 * count]
    (img_buf, band_buf, small_own, near, p_send, p_recv, z_send, z_recv, t_send, t_recv) = rest[7 * count :]
    img_at, band_at, y_at, x_at, c_at = place()
    over_y = (img_at, band_at + 4 - 8 * y_at)
    over_x = (img_at, band_at + 2 - 4 * x_at)
    over_c = (img_at, band_at + 1 - 2 * c_at)
    meet(img_at, band_at)

    def along_core(p):
        return [
            far_copy(grads[p].at[:, :, :, 1 - c_at], pair[p], p_send.at[p, 0], p_recv.at[p, 0], over_c),
            pltpu.make_async_copy(grads[p].at[:, :, :, c_at], own[p], near.at[p]),
        ]

    def add_core(p):
        def step(k, carry):
            z, yx = k // 4, k % 4
            own[p][z, yx // 2, yx % 2] += pair[p][z, yx // 2, yx % 2]
            return carry
        lax.fori_loop(0, 16, step, 0)

    def spans(p):
        rows = own[p].shape[3]
        return pl.ds(0, cuts[p]), pl.ds(cuts[p], rows - cuts[p])

    def along_first(p):
        rows_a, rows_b = spans(p)
        return [
            far_copy(own[p].at[:, :, 1 - x_at, rows_a], first_a[p], p_send.at[p, 1], p_recv.at[p, 1], over_x),
            far_copy(own[p].at[:, 1 - y_at, :, rows_b], first_b[p], p_send.at[p, 2], p_recv.at[p, 2], over_y),
        ]

    def add_first(p):
        rows_a, rows_b = spans(p)
        def step(k, carry):
            z, w = k // 2, k % 2
            own[p][z, w, x_at, rows_a] += first_a[p][z, w]
            own[p][z, y_at, w, rows_b] += first_b[p][z, w]
            return carry
        lax.fori_loop(0, 8, step, 0)

    def along_second(p):
        rows_a, rows_b = spans(p)
        return [
            far_copy(own[p].at[:, 1 - y_at, x_at, rows_a], second_a[p], p_send.at[p, 3], p_recv.at[p, 3], over_y),
            far_copy(own[p].at[:, y_at, 1 - x_at, rows_b], second_b[p], p_send.at[p, 4], p_recv.at[p, 4], over_x),
        ]

    def add_second(p):
        rows_a, rows_b = spans(p)
        def step(z, carry):
            own[p][z, y_at, x_at, rows_a] += second_a[p][z]
            own[p][z, y_at, x_at, rows_b] += second_b[p][z]
            return carry
        lax.fori_loop(0, 4, step, 0)

    def along_z(p):
        copies = []
        for step in range(1, 4):
            target = (img_at + step) % 4
            copies.append(
                far_copy(
                    own[p].at[target, y_at, x_at], last[p].at[step - 1],
                    z_send.at[p, step], z_recv.at[p, step], (target, band_at),
                )
            )
        return copies

    def add_z(p):
        shares[p][...] = (own[p][img_at, y_at, x_at] + last[p][0]) + (last[p][1] + last[p][2])

    stages = (along_core, along_first, along_second, along_z)
    adds = (add_core, add_first, add_second, add_z)
    flying = {}

    def launch(p, k):
        flying[p, k] = stages[k](p)
        for copy in flying[p, k]:
            copy.start()

    def land(p, k):
        for copy in flying.pop((p, k)):
            copy.wait()
        adds[k](p)

    for p in range(count):
        launch(p, 0)
    for beat in range(count + 3):
        for k in range(4):
            p = beat - k
            if 0 <= p < count:
                land(p, k)
                if k < 3:
                    launch(p, k + 1)
    squares = sum(jnp.sum(share[...] * share[...]) for share in shares)
    shape = small.shape
    at_spot = (lax.broadcasted_iota(jnp.int32, shape, 0) == 11) & (lax.broadcasted_iota(jnp.int32, shape, 1) == 0)
    small_own[...] = small[...] + jnp.where(at_spot, squares, 0.0)
    sum_everywhere(small_own, img_buf, band_buf, t_send, t_recv, img_at, band_at, small_all)


def reduce_all(grads, cuts, small):
    any_space = pl.BlockSpec(memory_space=pl.ANY)
    vmem_space = pl.BlockSpec(memory_space=pltpu.VMEM)
    count = len(grads)
    rows = [g.shape[4] for g in grads]
    wide = [g.shape[5] for g in grads]
    f32 = jnp.float32
    dma = pltpu.SemaphoreType.DMA
    scratch = [pltpu.VMEM((4, 2, 2, r, w), f32) for r, w in zip(rows, wide)]
    scratch += [pltpu.VMEM((4, 2, 2, r, w), f32) for r, w in zip(rows, wide)]
    scratch += [pltpu.VMEM((4, 2, a, w), f32) for a, w in zip(cuts, wide)]
    scratch += [pltpu.VMEM((4, 2, r - a, w), f32) for a, r, w in zip(cuts, rows, wide)]
    scratch += [pltpu.VMEM((4, a, w), f32) for a, w in zip(cuts, wide)]
    scratch += [pltpu.VMEM((4, r - a, w), f32) for a, r, w in zip(cuts, rows, wide)]
    scratch += [pltpu.VMEM((3, r, w), f32) for r, w in zip(rows, wide)]
    scratch += [
        pltpu.VMEM((4,) + small.shape, f32),
        pltpu.VMEM((8,) + small.shape, f32),
        pltpu.VMEM(small.shape, f32),
        dma((count,)),
        dma((count, 5)), dma((count, 5)),
        dma((count, 4)), dma((count, 4)),
        dma((11,)), dma((11,)),
    ]
    return pl.pallas_call(
        functools.partial(reduce_kernel, cuts),
        out_shape=[jax.ShapeDtypeStruct((r, w), f32) for r, w in zip(rows, wide)]
        + [jax.ShapeDtypeStruct(small.shape, f32)],
        in_specs=[any_space] * count + [vmem_space],
        out_specs=[vmem_space] * (count + 1),
        scratch_shapes=scratch,
        compiler_params=pltpu.CompilerParams(collective_id=1, has_side_effects=True, vmem_limit_bytes=56 << 20),
        name="reduce_all",
    )(*grads, small)


def moments(gradient, first_old, second_old):
    first_new = beta_first * first_old + (1.0 - beta_first) * gradient
    second_new = beta_second * second_old + (1.0 - beta_second) * gradient * gradient
    return (first_new, second_new, first_new / (jnp.sqrt(second_new) + adam_eps))


def rotated_update(weight, gradient, first_old, second_old, basis_stack):
    turned = jnp.einsum("rld,lde->rle", gradient, basis_stack, precision=highest)
    first_new, second_new, direction = moments(turned, first_old, second_old)
    turned_back = jnp.einsum("rle,lde->rld", direction, basis_stack, precision=highest)
    return (weight - rate_matrix * (turned_back + weight_decay * weight), first_new, second_new)


def plain_update(weight, gradient, first_old, second_old):
    first_new, second_new, direction = moments(gradient, first_old, second_old)
    return (weight - rate_vector * (direction + weight_decay * weight), first_new, second_new)


def body(
    pixels,
    valid,
    codes,
    image_kind,
    w_wide,
    w_narrow,
    w_edge,
    codebook,
    norms,
    bases,
    basis_edge,
    m_wide,
    v_wide,
    m_narrow,
    v_narrow,
    m_edge,
    v_edge,
    m_code,
    v_code,
    m_norm,
    v_norm,
):
    band_count = lax.axis_size("band")
    band_index = lax.axis_index("band")
    row_count = pixels.shape[2]
    length = row_count * band_count
    batch_count = pixels.shape[0]
    group = band_count // batch_count
    row = band_index // group
    part = band_index % group
    own_rows = length // group
    groups = [[k * group + j for j in range(group)] for k in range(batch_count)]
    layer_count = w_wide.shape[1]
    code_width = codebook.shape[1]
    latent_total = batch_count * lax.axis_size("img") * length * code_width
    both = ("img", "band")

    direct = band_count == 8 and lax.axis_size("img") == 4 and batch_count == 4
    shards = [w_wide[:, l].astype(jnp.bfloat16) for l in range(layer_count)]
    shards += [w_narrow[:, l].astype(jnp.bfloat16) for l in range(layer_count)]
    shards += [w_edge.astype(jnp.bfloat16), codebook.astype(jnp.bfloat16).reshape(-1, 4 * code_width)]
    slab = jnp.concatenate([pixels[:, 0], valid[:, 0].astype(jnp.bfloat16)], axis=2)
    local_count = jnp.sum(valid.astype(jnp.float32))
    patch_size = pixels.shape[3]
    if direct:
        order = (5, 4, 1, 3, 0, 2)
        cuts = tuple({112: 64, 80: 32, 16: 16, 64: 0}[shards[k].shape[0]] for k in order)
        moved = gather_all([shards[k] for k in order], cuts, slab, codes, jnp.full((8, 128), local_count))
        wholes = [None] * 6
        for k, value in zip(order, moved):
            wholes[k] = value.reshape((-1, value.shape[-1]))
        slab_all = moved[6].reshape(length, -1)
        code_all = moved[7].reshape(length)
        count = moved[8][0, 0]
    else:
        wholes = [lax.all_gather(shard, both, axis=0, tiled=True) for shard in shards]
        count = lax.psum(local_count, both)

        def whole_row(local):
            everywhere = lax.all_gather(local, "band", axis=0)
            chosen_row = lax.dynamic_index_in_dim(everywhere, row, axis=1, keepdims=False)
            return chosen_row.reshape((length,) + local.shape[2:])

        slab_all = whole_row(slab)
        code_all = whole_row(codes[:, 0])
    kind = lax.dynamic_index_in_dim(image_kind[:, 0], row, 0, keepdims=False)
    span = jnp.where(kind == 0, length, length // 4)
    positions = jnp.arange(length, dtype=jnp.int32)
    if direct:
        own = functools.partial(lax.dynamic_slice_in_dim, start_index=part * own_rows, slice_size=own_rows, axis=0)
        edge_all = wholes[4]
        pixel_all = slab_all[:, :patch_size]
        slab_own = own(slab_all)
        pix_own, mask_own = slab_own[:, :patch_size], slab_own[:, patch_size:]
        edge_in = edge_all[:, :patch_size]
        edge_pix = edge_all[:, patch_size : 2 * patch_size]
        edge_qin = jnp.tile(edge_all[:, 2 * patch_size : 2 * patch_size + code_width], (1, 4))
        edge_qout = jnp.tile(edge_all[:, 2 * patch_size + code_width :], (1, 4))
        lanes = jnp.arange(128, dtype=jnp.int32)[None, :]
        segment = (positions // span)[:, None]
        k_extra = (lanes == segment).astype(jnp.bfloat16)
        q_extra = own(jnp.where((lanes < 4) & (lanes != segment), -(2.0**30), 0.0).astype(jnp.bfloat16))
        code_col = code_all[:, None]
        dec = run_block(
            True,
            latent_total,
            (code_col, wholes[5], edge_qout, wholes[1], wholes[3], norms, q_extra, k_extra, edge_pix, pix_own,
             mask_own, moved[8]),
            length,
            own_rows,
        )
        enc = run_block(
            False,
            latent_total,
            (pixel_all, edge_in, wholes[0], wholes[2], norms, q_extra, k_extra, edge_qin, pix_own, dec[5], dec[6],
             code_col, own(code_all)[None, :]),
            length,
            own_rows,
        )

        def fold(g):
            return sum(g[:, k * code_width : (k + 1) * code_width] for k in range(4))

        local_grads = (
            enc[0], dec[0], enc[1], dec[1],
            jnp.concatenate([enc[4], dec[3], fold(enc[3]), fold(dec[4])], axis=1),
            enc[5],
        )
        norm_sum = jnp.concatenate([enc[2][:4], dec[2][:6]], axis=0)
        loss_sum = enc[2][6, 0] + dec[2][6, 0]
    else:
        gathered = (wholes[:2], wholes[2:4], wholes[4], wholes[5])
        pixel_all = slab_all[:, :patch_size]
        valid_rows = lax.dynamic_slice_in_dim(slab_all, part * own_rows, own_rows, 0)[:, patch_size:]
        own_positions = part * own_rows + jnp.arange(own_rows, dtype=jnp.int32)
        allowed = (own_positions // span)[:, None] == (positions // span)[None, :]
        local_grads, norm_sum, loss_sum = row_step(
            gathered, norms, pixel_all, valid_rows, code_all, part, allowed, count, latent_total, groups
        )
    if direct:
        blocks = [g.reshape((4, 2, 2, 2, g.shape[0] // 32, g.shape[1])) for g in local_grads]
        order = (1, 3, 0, 2, 4, 5)
        cuts = tuple(blocks[k].shape[4] // 2 for k in order)
        small = jnp.zeros((16, norm_sum.shape[1]), jnp.float32)
        small = small.at[:10].set(norm_sum).at[10, 0].set(loss_sum)
        reduced = reduce_all([blocks[k] for k in order], cuts, small)
        shares = [None] * 6
        for k, value in zip(order, reduced):
            shares[k] = value
        norm_total = reduced[6][:10]
        loss_total = reduced[6][10, 0]
        square_total = reduced[6][11, 0]
    else:
        shares = [lax.psum_scatter(g, both, scatter_dimension=0, tiled=True) for g in local_grads]
        squares = sum(jnp.sum(share * share) for share in shares)
        norm_total, square_total, loss_total = lax.psum((norm_sum, squares, loss_sum), both)
    grad_sum = (
        jnp.stack([shares[0], shares[1]], axis=1),
        jnp.stack([shares[2], shares[3]], axis=1),
        shares[4],
        shares[5].reshape(-1, code_width),
    )
    grad_norm = jnp.sqrt(square_total + jnp.sum(norm_total * norm_total))
    factor = jnp.minimum(1.0, clip_level / grad_norm)
    grad_wide, grad_narrow, grad_edge, grad_book = grad_sum
    new_wide, new_m_wide, new_v_wide = rotated_update(
        w_wide, factor * grad_wide, m_wide, v_wide, bases[:layer_count]
    )
    new_narrow, new_m_narrow, new_v_narrow = rotated_update(
        w_narrow, factor * grad_narrow, m_narrow, v_narrow, bases[layer_count:]
    )
    new_edge, new_m_edge, new_v_edge = rotated_update(
        w_edge[:, None],
        factor * grad_edge[:, None],
        m_edge[:, None],
        v_edge[:, None],
        basis_edge[None],
    )
    new_book, new_m_code, new_v_code = plain_update(codebook, factor * grad_book, m_code, v_code)
    new_norms, new_m_norm, new_v_norm = plain_update(norms, factor * norm_total, m_norm, v_norm)
    return (
        new_wide,
        new_m_wide,
        new_v_wide,
        new_narrow,
        new_m_narrow,
        new_v_narrow,
        new_edge[:, 0],
        new_m_edge[:, 0],
        new_v_edge[:, 0],
        new_book,
        new_m_code,
        new_v_code,
        new_norms,
        new_m_norm,
        new_v_norm,
        grad_norm,
        loss_total,
    )


def solution(mesh):
    in_specs = (
        P(None, "img", "band", None),
        P(None, "img", "band", None),
        P(None, "img", "band"),
        P(None, "img"),
        P(("img", "band"), None, None),
        P(("img", "band"), None, None),
        P(("img", "band"), None),
        P(("img", "band"), None),
        P(),
        P(),
        P(),
        P(("img", "band"), None, None),
        P(("img", "band"), None, None),
        P(("img", "band"), None, None),
        P(("img", "band"), None, None),
        P(("img", "band"), None),
        P(("img", "band"), None),
        P(("img", "band"), None),
        P(("img", "band"), None),
        P(),
        P(),
    )
    out_specs = (
        P(("img", "band"), None, None),
        P(("img", "band"), None, None),
        P(("img", "band"), None, None),
        P(("img", "band"), None, None),
        P(("img", "band"), None, None),
        P(("img", "band"), None, None),
        P(("img", "band"), None),
        P(("img", "band"), None),
        P(("img", "band"), None),
        P(("img", "band"), None),
        P(("img", "band"), None),
        P(("img", "band"), None),
        P(),
        P(),
        P(),
        P(),
        P(),
    )
    return jax.shard_map(body, mesh=mesh, in_specs=in_specs, out_specs=out_specs, check_vma=False)
```

```python
import functools

import jax
import jax.numpy as jnp
from jax import lax
from jax.experimental import pallas as pl
from jax.experimental.pallas import tpu as pltpu
from jax.sharding import PartitionSpec as P

HEADS = 8
HDIM = 64
MESH = pl.DeviceIdType.MESH


norm_eps = 1e-05
adam_eps = 1e-08
clip_level = 0.001
beta_first = 0.5
beta_second = 0.6
rate_matrix = 0.02
rate_vector = 0.3
weight_decay = 0.01
commitment = 0.25
masked_score = -1000000000.0
highest = lax.Precision.HIGHEST


def matmul_plain(first_op, second_op):
    return jnp.dot(first_op, second_op, preferred_element_type=jnp.float32)


def matmul_trans(first_op, second_op):
    return lax.dot_general(
        first_op, second_op, (((1,), (1,)), ((), ())), preferred_element_type=jnp.float32
    )


def matmul_outer(first_op, second_op):
    return lax.dot_general(
        first_op, second_op, (((0,), (0,)), ((), ())), preferred_element_type=jnp.float32
    )


def layer_norm(hidden, scale_gain, offset):
    centred = hidden - jnp.mean(hidden, axis=-1, keepdims=True)
    spread = jnp.mean(centred * centred, axis=-1, keepdims=True)
    return centred * lax.rsqrt(spread + norm_eps) * scale_gain + offset


def gelu_tanh(inputs):
    return (
        0.5
        * inputs
        * (1.0 + jnp.tanh(0.7978845608028654 * (inputs + 0.044715 * inputs * inputs * inputs)))
    )


def split_heads(matrix):
    return matrix.reshape(matrix.shape[0], HEADS, HDIM)


def head_scores(q_heads, k_heads, allowed):
    scores = jnp.einsum(
        "qhd,khd->hqk", q_heads, k_heads, preferred_element_type=jnp.float32
    ) * HDIM ** (-0.5)
    return jnp.where(allowed[None], scores, masked_score)


def attend(queries, key_rows, value_rows, allowed):
    scores = head_scores(split_heads(queries), split_heads(key_rows), allowed)
    score_peak = jnp.max(scores, axis=-1, keepdims=True)
    expo = jnp.exp(scores - score_peak)
    total = jnp.sum(expo, axis=-1, keepdims=True)
    softmaxed = (expo / total).astype(jnp.bfloat16)
    attended = jnp.einsum(
        "hqk,khd->qhd", softmaxed, split_heads(value_rows), preferred_element_type=jnp.float32
    )
    return (
        attended.reshape(queries.shape[0], -1).astype(jnp.bfloat16),
        score_peak + jnp.log(total),
    )


def attend_back(queries, key_rows, value_rows, allowed, log_total, grad_out):
    q_heads = split_heads(queries)
    k_heads = split_heads(key_rows)
    v_heads = split_heads(value_rows)
    g_heads = split_heads(grad_out)
    softmaxed = jnp.exp(head_scores(q_heads, k_heads, allowed) - log_total)
    grad_soft = jnp.einsum("qhd,khd->hqk", g_heads, v_heads, preferred_element_type=jnp.float32)
    row_dot = jnp.sum(softmaxed * grad_soft, axis=-1, keepdims=True)
    grad_scores = (softmaxed * (grad_soft - row_dot)).astype(jnp.bfloat16)
    scale = HDIM ** (-0.5)
    grad_q = (
        jnp.einsum("hqk,khd->qhd", grad_scores, k_heads, preferred_element_type=jnp.float32) * scale
    )
    grad_k = (
        jnp.einsum("hqk,qhd->khd", grad_scores, q_heads, preferred_element_type=jnp.float32) * scale
    )
    grad_v = jnp.einsum(
        "hqk,qhd->khd", softmaxed.astype(jnp.bfloat16), g_heads, preferred_element_type=jnp.float32
    )
    return (
        grad_q.reshape(queries.shape[0], -1),
        grad_k.reshape(key_rows.shape[0], -1),
        grad_v.reshape(key_rows.shape[0], -1),
    )


def block_forward(hidden_all, part, wide_rows, narrow_rows, gain_rows, allowed):
    model_width = hidden_all.shape[1]
    own_rows = allowed.shape[0]
    normed_all = layer_norm(hidden_all, gain_rows[0], gain_rows[1]).astype(jnp.bfloat16)
    hidden = lax.dynamic_slice_in_dim(hidden_all, part * own_rows, own_rows, 0)
    normed = lax.dynamic_slice_in_dim(normed_all, part * own_rows, own_rows, 0)
    queries = matmul_trans(normed, wide_rows[:model_width]).astype(jnp.bfloat16)
    key_rows = matmul_trans(normed_all, wide_rows[model_width : 2 * model_width]).astype(jnp.bfloat16)
    value_rows = matmul_trans(normed_all, wide_rows[2 * model_width : 3 * model_width]).astype(jnp.bfloat16)
    attended, log_total = attend(queries, key_rows, value_rows, allowed)
    middle = hidden + matmul_plain(attended, narrow_rows[:model_width])
    second = layer_norm(middle, gain_rows[2], gain_rows[3]).astype(jnp.bfloat16)
    upper_in = matmul_trans(second, wide_rows[3 * model_width :])
    active = gelu_tanh(upper_in).astype(jnp.bfloat16)
    result = middle + matmul_plain(active, narrow_rows[model_width:])
    return (
        result,
        (hidden, normed, queries, key_rows, value_rows, attended, log_total, middle, second, upper_in, active),
    )


def block_backward(grad_out, wide_rows, narrow_rows, gain_rows, allowed, saved, groups):
    (hidden, normed, queries, key_rows, value_rows, attended, log_total, middle, second, upper_in, active) = saved
    model_width = hidden.shape[1]
    grad_y = grad_out.astype(jnp.bfloat16)
    grad_down = matmul_outer(active, grad_y)
    grad_active = matmul_trans(grad_y, narrow_rows[model_width:])
    grad_upper = jax.vjp(gelu_tanh, upper_in)[1](grad_active)[0].astype(jnp.bfloat16)
    grad_up = matmul_outer(grad_upper, second)
    _, second_back = jax.vjp(layer_norm, middle, gain_rows[2], gain_rows[3])
    grad_mid, gain_two, offset_two = second_back(
        matmul_plain(grad_upper, wide_rows[3 * model_width :])
    )
    grad_mid = grad_mid + grad_out
    grad_attn = grad_mid.astype(jnp.bfloat16)
    grad_outproj = matmul_outer(attended, grad_attn)
    grad_att = matmul_trans(grad_attn, narrow_rows[:model_width]).astype(jnp.bfloat16)
    grad_q, grad_keys, grad_values = attend_back(
        queries, key_rows, value_rows, allowed, log_total, grad_att
    )
    grad_k = lax.psum_scatter(grad_keys, "band", scatter_dimension=0, tiled=True, axis_index_groups=groups)
    grad_v = lax.psum_scatter(grad_values, "band", scatter_dimension=0, tiled=True, axis_index_groups=groups)
    grad_mixed = jnp.concatenate([grad_q, grad_k, grad_v], axis=1).astype(jnp.bfloat16)
    grad_qkv = matmul_outer(grad_mixed, normed)
    _, first_back = jax.vjp(layer_norm, hidden, gain_rows[0], gain_rows[1])
    grad_in, gain_one, offset_one = first_back(
        matmul_plain(grad_mixed, wide_rows[: 3 * model_width])
    )
    gain_grads = jnp.stack([gain_one, offset_one, gain_two, offset_two], axis=0)
    return (
        grad_in + grad_mid,
        jnp.concatenate([grad_qkv, grad_up], axis=0),
        jnp.concatenate([grad_outproj, grad_down], axis=0),
        gain_grads,
    )


def pick_codes(code_rows, book_wide, code_width):
    fold = book_wide.shape[1] // code_width
    one_hot = (
        (code_rows // fold)[:, None] == jnp.arange(book_wide.shape[0], dtype=jnp.int32)[None, :]
    ).astype(jnp.bfloat16)
    lane_fold = jnp.arange(book_wide.shape[1], dtype=jnp.int32)[None, :] // code_width
    lane_mask = (code_rows % fold)[:, None] == lane_fold
    spread = jnp.where(lane_mask, matmul_plain(one_hot, book_wide), 0.0)
    chosen = sum(spread[:, k * code_width : (k + 1) * code_width] for k in range(fold))
    return chosen, one_hot, lane_mask


def row_step(gathered, norms, pixel_all, valid_rows, code_all, part, allowed, count, latent_total, groups):
    wide_all, narrow_all, edge_all, book_wide = gathered
    patch_size = pixel_all.shape[1]
    code_width = edge_all.shape[1] // 2 - patch_size
    own_rows = allowed.shape[0]
    edge_in = edge_all[:, :patch_size]
    edge_pix = edge_all[:, patch_size : 2 * patch_size]
    edge_qin = edge_all[:, 2 * patch_size : 2 * patch_size + code_width]
    edge_qout = edge_all[:, 2 * patch_size + code_width :]
    pixel_rows = lax.dynamic_slice_in_dim(pixel_all, part * own_rows, own_rows, 0)
    chosen_all, one_hot_all, lane_mask_all = pick_codes(code_all, book_wide, code_width)
    chosen_low_all = chosen_all.astype(jnp.bfloat16)
    chosen = lax.dynamic_slice_in_dim(chosen_all, part * own_rows, own_rows, 0)
    one_hot = lax.dynamic_slice_in_dim(one_hot_all, part * own_rows, own_rows, 0)
    lane_mask = lax.dynamic_slice_in_dim(lane_mask_all, part * own_rows, own_rows, 0)
    chosen_low = chosen.astype(jnp.bfloat16)
    begin = matmul_trans(chosen_low_all, edge_qout)
    decoded, dec_saved = block_forward(begin, part, wide_all[1], narrow_all[1], norms[4:8], allowed)
    final = layer_norm(decoded, norms[8], norms[9]).astype(jnp.bfloat16)
    predict = matmul_plain(final, edge_pix)
    error = predict - pixel_rows.astype(jnp.float32)
    pixel_mask = valid_rows.astype(jnp.float32)
    loss_pix = jnp.sum(pixel_mask * (error * error + jnp.abs(error))) / count
    grad_pred = (pixel_mask * (2.0 * error + jnp.sign(error)) / count).astype(jnp.bfloat16)
    grad_pixw = matmul_outer(final, grad_pred)
    _, final_back = jax.vjp(layer_norm, decoded, norms[8], norms[9])
    grad_dec, gain_last, offset_last = final_back(matmul_trans(grad_pred, edge_pix))
    grad_begin, dec_wide, dec_narrow, dec_gains = block_backward(
        grad_dec, wide_all[1], narrow_all[1], norms[4:8], allowed, dec_saved, groups
    )
    grad_begin_low = grad_begin.astype(jnp.bfloat16)
    grad_qout = matmul_outer(grad_begin_low, chosen_low)
    start = matmul_trans(pixel_all, edge_in)
    encoded, enc_saved = block_forward(start, part, wide_all[0], narrow_all[0], norms[0:4], allowed)
    encoded_low = encoded.astype(jnp.bfloat16)
    latent = matmul_plain(encoded_low, edge_qin)
    gap = chosen - latent
    loss_part = loss_pix + (1.0 + commitment) * jnp.sum(gap * gap) / latent_total
    grad_latent = (
        matmul_plain(grad_begin_low, edge_qout) - 2.0 * commitment * gap / latent_total
    ).astype(jnp.bfloat16)
    fold = lane_mask.shape[1] // code_width
    gap_wide = jnp.where(lane_mask, jnp.tile(2.0 * gap / latent_total, (1, fold)), 0.0)
    gap_high = gap_wide.astype(jnp.bfloat16)
    gap_rest = gap_wide - gap_high.astype(jnp.float32)
    gap_middle = gap_rest.astype(jnp.bfloat16)
    gap_low = (gap_rest - gap_middle.astype(jnp.float32)).astype(jnp.bfloat16)
    grad_book = (
        matmul_outer(one_hot, gap_high) + matmul_outer(one_hot, gap_middle)
    ) + matmul_outer(one_hot, gap_low)
    grad_qin = matmul_outer(encoded_low, grad_latent)
    grad_start, enc_wide, enc_narrow, enc_gains = block_backward(
        matmul_trans(grad_latent, edge_qin), wide_all[0], narrow_all[0], norms[0:4], allowed, enc_saved, groups
    )
    grad_inw = matmul_outer(grad_start.astype(jnp.bfloat16), pixel_rows)
    grads = (
        enc_wide, dec_wide, enc_narrow, dec_narrow,
        jnp.concatenate([grad_inw, grad_pixw, grad_qin, grad_qout], axis=1),
        grad_book,
    )
    norm_grad = jnp.concatenate([enc_gains, dec_gains, gain_last[None], offset_last[None]], axis=0)
    return (grads, norm_grad, loss_part)


def place():
    img_at = lax.axis_index("img")
    band_at = lax.axis_index("band")
    return img_at, band_at, band_at // 4, (band_at // 2) % 2, band_at % 2


def neighbours():
    img_at, band_at, y_at, x_at, c_at = place()
    return (
        (img_at, band_at + 1 - 2 * c_at),
        (img_at, band_at + 2 - 4 * x_at),
        (img_at, band_at + 4 - 8 * y_at),
    )


def peers():
    img_at, band_at = place()[:2]
    found = [((img_at + step) % 4, band_at) for step in range(1, 4)]
    return found + [(img_at, (band_at + step) % 8) for step in range(1, 8)]


def meet(others):
    barrier = pltpu.get_barrier_semaphore()
    for other in others:
        pl.semaphore_signal(barrier, inc=1, device_id=other, device_id_type=MESH)
    pl.semaphore_wait(barrier, len(others))


def far_copy(src, dst, send, recv, target):
    return pltpu.make_async_remote_copy(
        src_ref=src, dst_ref=dst, send_sem=send, recv_sem=recv, device_id=target, device_id_type=MESH
    )


def sum_everywhere(own_ref, img_buf, band_buf, send, recv, result_ref):
    img_at, band_at = place()[:2]
    img_buf[img_at] = own_ref[...]
    first = [
        far_copy(own_ref, img_buf.at[img_at], send.at[step], recv.at[step], ((img_at + step) % 4, band_at))
        for step in range(1, 4)
    ]
    for copy in first:
        copy.start()
    for copy in first:
        copy.wait()
    result_ref[...] = (img_buf[0] + img_buf[1]) + (img_buf[2] + img_buf[3])
    band_buf[band_at] = result_ref[...]
    second = [
        far_copy(
            result_ref, band_buf.at[band_at], send.at[3 + step], recv.at[3 + step], (img_at, (band_at + step) % 8)
        )
        for step in range(1, 8)
    ]
    for copy in second:
        copy.start()
    for copy in second:
        copy.wait()
    total = band_buf[0]
    for k in range(1, 8):
        total = total + band_buf[k]
    result_ref[...] = total


class Gather:
    def __init__(self, shards, wholes, cuts, near, z_send, z_recv, p_send, p_recv):
        self.shards, self.wholes, self.cuts = shards, wholes, cuts
        self.near, self.z_send, self.z_recv, self.p_send, self.p_recv = near, z_send, z_recv, p_send, p_recv
        self.flying = {}
        self.steps = [
            (beat - k, k) for beat in range(len(shards) + 3) for k in (3, 2, 1, 0) if 0 <= beat - k < len(shards)
        ]

    def copies(self, p, k):
        img_at, band_at, y_at, x_at, c_at = place()
        over_c, over_x, over_y = neighbours()
        whole, cut, rows = self.wholes[p], self.cuts[p], self.shards[p].shape[0]
        if k == 0:
            here = whole.at[img_at, y_at, x_at, c_at]
            found = [
                far_copy(
                    self.shards[p], here, self.z_send.at[p, step], self.z_recv.at[p, step],
                    ((img_at + step) % 4, band_at),
                )
                for step in range(1, 4)
            ]
            return found + [pltpu.make_async_copy(self.shards[p], here, self.near.at[p])]
        if k == 3:
            part = whole.at[:, :, :, c_at]
            return [far_copy(part, part, self.p_send.at[p, 4], self.p_recv.at[p, 4], over_c)]
        found = []
        for half, (first, count) in enumerate(((0, cut), (cut, rows - cut))):
            if count == 0:
                continue
            span = pl.ds(first, count)
            if k == 1:
                part = whole.at[:, y_at, x_at, c_at, span]
            elif half == 0:
                part = whole.at[:, :, x_at, c_at, span]
            else:
                part = whole.at[:, y_at, :, c_at, span]
            slot = 2 * (k - 1) + half
            target = over_y if (k == 1) == (half == 0) else over_x
            found.append(far_copy(part, part, self.p_send.at[p, slot], self.p_recv.at[p, slot], target))
        return found

    def launch(self, p, k):
        self.flying[p, k] = self.copies(p, k)
        for copy in self.flying[p, k]:
            copy.start()

    def begin(self):
        for p in range(len(self.shards)):
            self.launch(p, 0)

    def tick(self, count=1):
        for _ in range(count):
            if not self.steps:
                return
            p, k = self.steps.pop(0)
            for copy in self.flying.pop((p, k)):
                copy.wait()
            if k < 3:
                self.launch(p, k + 1)

    def until(self, p):
        while (p, 3) in self.steps:
            self.tick()


def gather_sems(count):
    dma = pltpu.SemaphoreType.DMA
    return [dma((count,)), dma((count, 4)), dma((count, 4)), dma((count, 5)), dma((count, 5))]


class Reduce:
    def __init__(
        self, slots, wait_z, full, pair, first_a, first_b, second_a, second_b, ours, last,
        near, p_send, p_recv, z_send, z_recv, free, free_z,
    ):
        self.slots, self.wait_z = slots, wait_z
        self.full, self.pair, self.ours, self.last = full, pair, ours, last
        self.first, self.second = (first_a, first_b), (second_a, second_b)
        self.near, self.p_send, self.p_recv, self.z_send, self.z_recv = near, p_send, p_recv, z_send, z_recv
        self.free, self.free_z = free, free_z
        self.pieces, self.flying, self.events, self.at_event = [], {}, [], 0
        self.queue, self.opened = [], 0

    def plan(self, pieces):
        self.pieces = pieces
        count = len(pieces)
        seen = [0] * 4
        for p, piece in enumerate(pieces):
            piece["slot"] = p % self.slots
            piece["place"] = p % (self.wait_z + 1)
            piece["order"] = seen[piece["z"]]
            seen[piece["z"]] += 1
        for piece in pieces:
            piece["again"] = piece["order"] + 2 < seen[piece["z"]]
        self.events += [("open", p) for p in range(min(self.slots, count))]
        for beat in range(count + 2 + self.wait_z):
            for k, p in enumerate((beat, beat - 1, beat - 2, beat - 2 - self.wait_z)):
                if 0 <= p < count:
                    self.events.append((k, p))
                    if k == 2 and p + self.slots < count:
                        self.events.append(("open", p + self.slots))

    def rows(self, p):
        return pl.ds(0, self.pieces[p]["rows"])

    def open(self, p):
        piece = self.pieces[p]
        slot, rows = piece["slot"], self.rows(p)
        c_at = place()[4]
        over_c = neighbours()[0]
        if p >= self.slots:
            for k in range(3):
                pl.semaphore_wait(self.free.at[slot, k], 1)
        landing = self.pair.at[slot, :, :, rows]
        send, recv = self.p_send.at[slot, 0], self.p_recv.at[slot, 0]
        if "emit" in piece:
            piece["emit"](self.full, slot)
            copies = [far_copy(self.full.at[slot, :, :, 1 - c_at, rows], landing, send, recv, over_c)]
        else:
            src, z = piece["src"], piece["z"]
            copies = [
                far_copy(src.at[z, :, :, 1 - c_at], landing, send, recv, over_c),
                pltpu.make_async_copy(src.at[z, :, :, c_at], self.full.at[slot, :, :, c_at, rows], self.near.at[slot]),
            ]
        self.flying[p] = copies
        for copy in copies:
            copy.start()

    def step(self, k, p):
        piece = self.pieces[p]
        slot, rows, z = piece["slot"], self.rows(p), piece["z"]
        img_at, band_at, y_at, x_at, c_at = place()
        over_c, over_x, over_y = neighbours()
        full, half = self.full, self.full.shape[5] // 2
        low, high = pl.ds(0, half), pl.ds(half, half)
        if k < 3:
            for copy in self.flying.pop(p):
                copy.wait()
        if k == 0:
            def add(n, carry):
                full[slot, n // 2, n % 2, c_at, rows] += self.pair[slot, n // 2, n % 2, rows]
                return carry
            lax.fori_loop(0, 4, add, 0)
            parts = (full.at[slot, :, 1 - x_at, c_at, rows, low], full.at[slot, 1 - y_at, :, c_at, rows, high])
            landings = [self.first[n].at[slot, :, rows] for n in range(2)]
            targets = (over_x, over_y)
        elif k == 1:
            def add(n, carry):
                full[slot, n, x_at, c_at, rows, low] += self.first[0][slot, n, rows]
                full[slot, y_at, n, c_at, rows, high] += self.first[1][slot, n, rows]
                return carry
            lax.fori_loop(0, 2, add, 0)
            parts = (full.at[slot, 1 - y_at, x_at, c_at, rows, low], full.at[slot, y_at, 1 - x_at, c_at, rows, high])
            landings = [self.second[n].at[slot, rows] for n in range(2)]
            targets = (over_y, over_x)
        if k < 2:
            self.flying[p] = [
                far_copy(
                    parts[n], landings[n], self.p_send.at[slot, 1 + 2 * k + n], self.p_recv.at[slot, 1 + 2 * k + n],
                    targets[n],
                )
                for n in range(2)
            ]
            for copy in self.flying[p]:
                copy.start()
            return
        spot, order = piece["place"], piece["order"] % 2
        mine = self.ours.at[spot, rows]
        owner = (z, band_at)

        def hop(n):
            return far_copy(mine, self.last.at[order, n, rows], self.z_send.at[spot], self.z_recv.at[order, n], owner)

        if k == 2:
            self.ours[spot, rows, low] = full[slot, y_at, x_at, c_at, rows, low] + self.second[0][slot, rows]
            self.ours[spot, rows, high] = full[slot, y_at, x_at, c_at, rows, high] + self.second[1][slot, rows]

            @pl.when(img_at != z)
            def _():
                if piece["order"] >= 2:
                    pl.semaphore_wait(self.free_z.at[z, order], 1)
                hop((img_at + 3 - z) % 4).start()

            if p + self.slots < len(self.pieces):
                for n, other in enumerate((over_c, over_x, over_y)):
                    pl.semaphore_signal(self.free.at[slot, n], inc=1, device_id=other, device_id_type=MESH)
            return

        @pl.when(img_at != z)
        def _():
            hop((img_at + 3 - z) % 4).wait_send()

        @pl.when(img_at == z)
        def _():
            for n in range(3):
                hop(n).wait_recv()
            piece["out"][...] = (self.ours[spot, rows] + self.last[order, 0, rows]) + (
                self.last[order, 1, rows] + self.last[order, 2, rows]
            )
            if piece["again"]:
                for n in range(1, 4):
                    pl.semaphore_signal(
                        self.free_z.at[z, order], inc=1, device_id=((img_at + n) % 4, band_at), device_id_type=MESH
                    )

    def open_ready(self, ready):
        while self.queue and self.pieces[self.queue[0]]["needs"] in ready:
            self.open(self.queue.pop(0))
            self.opened += 1

    def tick(self, count, ready=()):
        self.open_ready(ready)
        while count > 0 and self.at_event < len(self.events):
            what, p = self.events[self.at_event]
            if what == "open":
                self.queue.append(p)
                self.open_ready(ready)
            elif p >= self.opened:
                return
            else:
                self.step(what, p)
                count -= 1
            self.at_event += 1


def reduce_scratch(slots, wait_z, rows, width):
    f32 = jnp.float32
    dma = pltpu.SemaphoreType.DMA
    half = width // 2
    return [
        pltpu.VMEM((slots, 2, 2, 2, rows, width), f32),
        pltpu.VMEM((slots, 2, 2, rows, width), f32),
        pltpu.VMEM((slots, 2, rows, half), f32),
        pltpu.VMEM((slots, 2, rows, half), f32),
        pltpu.VMEM((slots, rows, half), f32),
        pltpu.VMEM((slots, rows, half), f32),
        pltpu.VMEM((wait_z + 1, rows, width), f32),
        pltpu.VMEM((2, 3, rows, width), f32),
        dma((slots,)),
        dma((slots, 5)), dma((slots, 5)),
        dma((wait_z + 1,)), dma((2, 3)),
        pltpu.SemaphoreType.REGULAR((slots, 3)),
        pltpu.SemaphoreType.REGULAR((4, 2)),
    ]


class ReduceSmall:
    def __init__(self, grads, shares, own, pair, first_a, first_b, second_a, second_b, last, near, p_send, p_recv, z_send, z_recv):
        self.grads, self.shares, self.own, self.pair = grads, shares, own, pair
        self.first, self.second, self.last = (first_a, first_b), (second_a, second_b), last
        self.near, self.p_send, self.p_recv, self.z_send, self.z_recv = near, p_send, p_recv, z_send, z_recv
        self.flying = {}

    def start(self, p, copies):
        self.flying[p] = copies
        for copy in copies:
            copy.start()

    def open(self, p):
        c_at = place()[4]
        over_c = neighbours()[0]
        self.start(p, [
            far_copy(self.grads[p].at[:, :, :, 1 - c_at], self.pair[p], self.p_send.at[p, 0], self.p_recv.at[p, 0], over_c),
            pltpu.make_async_copy(self.grads[p].at[:, :, :, c_at], self.own[p], self.near.at[p]),
        ])

    def step(self, p, k):
        img_at, band_at, y_at, x_at, c_at = place()
        over_c, over_x, over_y = neighbours()
        own = self.own[p]
        rows = own.shape[3]
        span = (pl.ds(0, rows // 2), pl.ds(rows // 2, rows // 2))
        for copy in self.flying.pop(p):
            copy.wait()

        def send(parts, landings, targets, slot):
            self.start(p, [
                far_copy(parts[n], landings[n], self.p_send.at[p, slot + n], self.p_recv.at[p, slot + n], targets[n])
                for n in range(2)
            ])

        if k == 0:
            own[...] += self.pair[p][...]
            send(
                (own.at[:, :, 1 - x_at, span[0]], own.at[:, 1 - y_at, :, span[1]]),
                (self.first[0][p], self.first[1][p]), (over_x, over_y), 1,
            )
        elif k == 1:
            own[:, :, x_at, span[0]] += self.first[0][p][...]
            own[:, y_at, :, span[1]] += self.first[1][p][...]
            send(
                (own.at[:, 1 - y_at, x_at, span[0]], own.at[:, y_at, 1 - x_at, span[1]]),
                (self.second[0][p], self.second[1][p]), (over_y, over_x), 3,
            )
        elif k == 2:
            own[:, y_at, x_at, span[0]] += self.second[0][p][...]
            own[:, y_at, x_at, span[1]] += self.second[1][p][...]
            copies = []
            for n in range(1, 4):
                target = (img_at + n) % 4
                copies.append(
                    far_copy(
                        own.at[target, y_at, x_at], self.last[p].at[n - 1], self.z_send.at[p, n], self.z_recv.at[p, n],
                        (target, band_at),
                    )
                )
            self.start(p, copies)
        else:
            last = self.last[p]
            self.shares[p][...] = (own[img_at, y_at, x_at] + last[0]) + (last[1] + last[2])


def reduce_small_scratch(shapes):
    f32 = jnp.float32
    dma = pltpu.SemaphoreType.DMA
    count = len(shapes)
    groups = [
        [(4, 2, 2, r, w) for r, w in shapes],
        [(4, 2, 2, r, w) for r, w in shapes],
        [(4, 2, r // 2, w) for r, w in shapes],
        [(4, 2, r // 2, w) for r, w in shapes],
        [(4, r // 2, w) for r, w in shapes],
        [(4, r // 2, w) for r, w in shapes],
        [(3, r, w) for r, w in shapes],
    ]
    return [pltpu.VMEM(shape, f32) for group in groups for shape in group] + [
        dma((count,)), dma((count, 5)), dma((count, 5)), dma((count, 4)), dma((count, 4)),
    ]


def dot_nn(a, b):
    return lax.dot_general(a, b, (((1,), (0,)), ((), ())), preferred_element_type=jnp.float32)


def dot_nt(a, b):
    return lax.dot_general(a, b, (((1,), (1,)), ((), ())), preferred_element_type=jnp.float32)


def dot_tn(a, b):
    return lax.dot_general(a, b, (((0,), (0,)), ((), ())), preferred_element_type=jnp.float32)


def norm_parts(h):
    centred = h - jnp.mean(h, axis=-1, keepdims=True)
    rate = lax.rsqrt(jnp.mean(centred * centred, axis=-1, keepdims=True) + norm_eps)
    return centred * rate, rate


def norm_back(grad, h, gain):
    shape, rate = norm_parts(h)
    inner = grad * gain
    back = rate * (
        inner
        - jnp.mean(inner, axis=-1, keepdims=True)
        - shape * jnp.mean(inner * shape, axis=-1, keepdims=True)
    )
    return (
        back,
        jnp.sum(grad * shape, axis=0, keepdims=True),
        jnp.sum(grad, axis=0, keepdims=True),
    )


STEP = 256


def at(k, start=0):
    return pl.ds(pl.multiple_of(start + k * STEP, STEP), STEP)


def lanes_at(k, size, start=0):
    return pl.ds(pl.multiple_of(start + k * size, 128), size)


def loop(first, last, body):
    def step(k, carry):
        body(k)
        return carry

    lax.fori_loop(first, last, step, 0)


class Block:
    def __init__(self, base, source, first_w, small, refs):
        names = (
            "wide", "narrow", "norms", "q_extra", "k_extra", "hidden", "normed", "q_buf", "kv", "mixed_in", "wide_in",
            "middle", "second", "slope", "grad_out", "grad_low", "mid_low", "gatt", "dkv", "dkv_in", "soft", "x_send",
            "x_recv", "x_free",
        )
        for name, ref in zip(names, refs, strict=True):
            setattr(self, name, ref)
        self.base, self.source, self.first_w, self.small = base, source, first_w, small
        self.part = place()[4]
        self.total, self.own = self.kv.shape[0], self.q_buf.shape[0]
        self.width = self.q_buf.shape[1]
        self.offset = pl.multiple_of(self.part * self.own, self.own)
        self.chunks = self.own // STEP
        lane_head = lax.broadcasted_iota(jnp.int32, (1, 128), 1) // HDIM
        self.pick = [jnp.where(lane_head == k, 1.0, 0.0).astype(jnp.bfloat16) for k in range(2)]

    def gain(self, k):
        return self.norms[pl.ds(self.base + k, 1), :]

    def add_small(self, row, value):
        self.small[pl.ds(row, 1), :] += value

    def add_loss(self, value):
        first_lane = lax.broadcasted_iota(jnp.int32, (1, self.width), 1) == 0
        self.add_small(6, jnp.where(first_lane, value, 0.0))

    def enter(self, first, last):
        def body(n):
            k = (n + self.chunks * (1 + self.part)) % (self.total // STEP)
            h = dot_nt(self.source(k), self.first_w())
            self.hidden[at(n % self.chunks)] = h
            shape, _ = norm_parts(h)
            self.normed[at(k)] = (shape * self.gain(0) + self.gain(1)).astype(jnp.bfloat16)

        loop(first, last, body)

    def make_kv(self, first, last):
        def body(k):
            self.kv[at(k)] = dot_nt(self.normed[at(k)], self.wide[self.width : 3 * self.width]).astype(jnp.bfloat16)

        loop(first, last, body)

    def make_q(self):
        def body(k):
            q = dot_nt(self.normed[at(k, self.offset)], self.wide[: self.width]).astype(jnp.bfloat16)
            self.q_buf[at(k)] = (q.astype(jnp.float32) * HDIM**-0.5).astype(jnp.bfloat16)

        loop(0, self.chunks, body)

    def scores(self, p, k, rows, k_cat):
        q_cat = jnp.concatenate([self.q_buf[rows, lanes_at(p, 128)] * self.pick[k], self.q_extra[rows]], axis=1)
        return dot_nt(q_cat, k_cat)

    def key_columns(self, p):
        return jnp.concatenate([self.kv[:, lanes_at(p, 128)], self.k_extra[...]], axis=1)

    def attend(self, first, last):
        head_lane = lax.broadcasted_iota(jnp.int32, (STEP, 128), 1)

        def pair(p):
            k_cat = self.key_columns(p)
            v_pair = self.kv[:, lanes_at(p, 128, self.width)]

            def body(j):
                rows = at(j)
                mixed = None
                for k in range(2):
                    scores = self.scores(p, k, rows, k_cat)
                    peak = jnp.max(scores, axis=-1, keepdims=True)
                    expo = jnp.exp(scores - peak)
                    total = jnp.sum(expo, axis=-1, keepdims=True)
                    prob = expo * (1.0 / total)
                    level = peak + jnp.log(total)
                    self.soft[rows] = jnp.where(head_lane == 2 * p + k, level, self.soft[rows])
                    term = dot_nn(prob.astype(jnp.bfloat16), v_pair * self.pick[k])
                    mixed = term if mixed is None else mixed + term
                self.mixed_in[rows, lanes_at(p, 128)] = mixed.astype(jnp.bfloat16)

            loop(0, self.chunks, body)

        loop(first, last, pair)

    def after_attention(self):
        def body(k):
            rows = at(k)
            mid = self.hidden[at(k)] + dot_nn(self.mixed_in[rows, : self.width], self.narrow[: self.width])
            self.middle[rows] = mid
            shape, _ = norm_parts(mid)
            self.second[rows] = (shape * self.gain(2) + self.gain(3)).astype(jnp.bfloat16)
            self.grad_out[rows] = mid

        loop(0, self.chunks, body)

    def mlp(self, first, last):
        width = self.width

        def body(n):
            f = n // self.chunks
            rows = at(n % self.chunks)
            u = dot_nt(self.second[rows], self.wide[lanes_at(3 + f, width)])
            squared = u * u
            bend = jnp.tanh(0.7978845608028654 * (u + 0.044715 * squared * u))
            low = (0.5 * u * (1.0 + bend)).astype(jnp.bfloat16)
            self.mixed_in[rows, lanes_at(1 + f, width)] = low
            self.slope[rows, lanes_at(f, width)] = 0.5 * (1.0 + bend) + (0.5 * u) * (1.0 - bend * bend) * (
                0.7978845608028654 * (1.0 + (3.0 * 0.044715) * squared)
            )
            self.grad_out[rows] += dot_nn(low, self.narrow[lanes_at(1 + f, width)])

        loop(first * self.chunks, last * self.chunks, body)

    def mlp_back(self, first, last):
        width = self.width

        def body(k):
            rows = at(k)
            gy = self.grad_low[rows]

            def feature_step(f, acc):
                ga = dot_nt(gy, self.narrow[lanes_at(1 + f, width)])
                low = (ga * self.slope[rows, lanes_at(f, width)]).astype(jnp.bfloat16)
                self.wide_in[rows, lanes_at(3 + f, width)] = low
                return acc + dot_nn(low, self.wide[lanes_at(3 + f, width)])

            grad_second = lax.fori_loop(0, 4, feature_step, jnp.zeros((STEP, width), jnp.float32))
            back, g_gain, g_offset = norm_back(grad_second, self.middle[rows], self.gain(2))
            self.add_small(2, g_gain)
            self.add_small(3, g_offset)
            grad_mid = back + self.grad_out[rows]
            self.grad_out[rows] = grad_mid
            low = grad_mid.astype(jnp.bfloat16)
            self.mid_low[rows] = low
            self.gatt[rows] = dot_nt(low, self.narrow[:width]).astype(jnp.bfloat16)

        loop(first, last, body)

    def attend_back(self, first, last):
        head_lane = lax.broadcasted_iota(jnp.int32, (STEP, 128), 1)
        f32, bf16 = jnp.float32, jnp.bfloat16

        def pair(p):
            k_pair = self.kv[:, lanes_at(p, 128)]
            v_pair = self.kv[:, lanes_at(p, 128, self.width)]
            k_cat = self.key_columns(p)
            key_lanes, value_lanes = lanes_at(p, 128), lanes_at(p, 128, self.width)
            self.dkv[:, key_lanes] = jnp.zeros((self.total, 128), f32)
            self.dkv[:, value_lanes] = jnp.zeros((self.total, 128), f32)

            def body(j):
                rows = at(j)
                q_pair = self.q_buf[rows, lanes_at(p, 128)]
                g_pair = self.gatt[rows, lanes_at(p, 128)]
                dq = None
                for k in range(2):
                    g_rows = g_pair * self.pick[k]
                    level = jnp.sum(jnp.where(head_lane == 2 * p + k, self.soft[rows], 0.0), axis=-1, keepdims=True)
                    prob = jnp.exp(self.scores(p, k, rows, k_cat) - level)
                    d_prob = dot_nt(g_rows, v_pair)
                    dot_row = jnp.sum(prob * d_prob, axis=-1, keepdims=True)
                    d_score = (prob * (d_prob - dot_row)).astype(bf16)
                    term = dot_nn(d_score, k_pair * self.pick[k])
                    dq = term if dq is None else dq + term
                    self.dkv[:, key_lanes] += dot_tn(d_score, q_pair * self.pick[k])
                    self.dkv[:, value_lanes] += dot_tn(prob.astype(bf16), g_rows)
                self.wide_in[rows, lanes_at(p, 128)] = (dq * HDIM**-0.5).astype(bf16)

            loop(0, self.chunks, body)

        loop(first, last, pair)

    def swap_start(self, again):
        if again:
            pl.semaphore_wait(self.x_free, 1)
        theirs = pl.ds(pl.multiple_of((1 - self.part) * self.own, self.own), self.own)
        self.swap = far_copy(self.dkv.at[theirs], self.dkv_in, self.x_send, self.x_recv, neighbours()[0])
        self.swap.start()

    def swap_finish(self, again):
        self.swap.wait()
        width = self.width

        def body(k):
            rows = at(k)
            self.wide_in[rows, width : 3 * width] = (self.dkv[at(k, self.offset)] + self.dkv_in[rows]).astype(jnp.bfloat16)

        loop(0, self.chunks, body)
        if not again:
            pl.semaphore_signal(self.x_free, inc=1, device_id=neighbours()[0], device_id_type=MESH)

    def leave_rows(self, k):
        rows = at(k)
        grad_normed = dot_nn(self.wide_in[rows, : 3 * self.width], self.wide[: 3 * self.width])
        back, g_gain, g_offset = norm_back(grad_normed, self.hidden[at(k)], self.gain(0))
        self.add_small(0, g_gain)
        self.add_small(1, g_offset)
        return (back + self.grad_out[rows]).astype(jnp.bfloat16)

    def wide_product(self, first, count):
        if first < 3 * self.width:
            right = self.normed[pl.ds(self.offset, self.own)]
        else:
            right = self.second[...]
        return dot_tn(self.wide_in[:, first : first + count], right)

    def narrow_product(self, first, count):
        right = self.mid_low if first < self.width else self.grad_low
        return dot_tn(self.mixed_in[:, first : first + count], right[...])


def pieces_of(first, count, border):
    if first < border < first + count:
        return [(first, border - first), (border, first + count - border)]
    return [(first, count)]


def block_scratch(total_rows, own_rows):
    width = 512
    f32, bf16 = jnp.float32, jnp.bfloat16
    shapes = [
        ((own_rows, width), f32),
        ((total_rows, width), bf16),
        ((own_rows, width), bf16),
        ((total_rows, 2 * width), bf16),
        ((own_rows, 5 * width), bf16),
        ((own_rows, 7 * width), bf16),
        ((own_rows, width), f32),
        ((own_rows, width), bf16),
        ((own_rows, 4 * width), f32),
        ((own_rows, width), f32),
        ((own_rows, width), bf16),
        ((own_rows, width), bf16),
        ((own_rows, width), bf16),
        ((total_rows, 2 * width), f32),
        ((own_rows, 2 * width), f32),
        ((own_rows, 128), f32),
    ]
    return [pltpu.VMEM(shape, dtype) for shape, dtype in shapes] + [
        pltpu.SemaphoreType.DMA, pltpu.SemaphoreType.DMA, pltpu.SemaphoreType.REGULAR
    ]


def step_kernel(slots, latent_total, *refs):
    shards, slab, code, tally, kind, norms = refs[:6], refs[6], refs[7], refs[8], refs[9], refs[10]
    refs = refs[11:]
    share_wide_dec, share_narrow_dec, share_wide, share_narrow, share_edge, share_book, small_all = refs[:7]
    land_wide_dec, land_narrow_dec, land_wide, land_narrow = refs[7:11]
    refs = refs[11:]
    sems_dec, sems_enc, red, red_small, refs = refs[:5], refs[5:10], refs[10:25], refs[25:44], refs[44:]
    (book, edge, slab_all, code_all, tally_all, t_img, t_band, e_near, e_send, e_recv, t_send, t_recv) = refs[:12]
    (code_col, code_row, spread, cross, split, g_pixw, g_qout, g_qin, g_inw, g_edge, g_book) = refs[12:23]
    (small_dec, small_enc, small_own, s_img, s_band, s_send, s_recv, load_sem, wide, narrow) = refs[23:33]
    q_extra, k_extra = refs[33:35]
    scratch = refs[35:]
    f32, bf16 = jnp.float32, jnp.bfloat16
    img_at, band_at, y_at, x_at, c_at = place()
    chip_at = band_at // 2
    over_c = neighbours()[0]
    width = wide.shape[1]
    common = (wide, narrow, norms, q_extra, k_extra) + tuple(scratch)

    def edge_columns(first, count):
        return edge[:, :, :, :, :, first : first + count].reshape(width, count)

    def e_in():
        return edge_columns(0, 256)

    def e_pix():
        return edge_columns(256, 256)

    def e_qin():
        return edge_columns(512, 128)

    def e_qout():
        return edge_columns(640, 128)

    def pixel_rows(k, first=0, start=0):
        return slab_all[pl.ds(start + 2 * k, 2), :, first : first + 256].reshape(STEP, 256)

    own_band = 4 * c_at
    dec = Block(4, lambda k: spread[at(k)], e_qout, small_dec, common)
    enc = Block(0, pixel_rows, e_in, small_enc, common)
    gather = Gather(shards[:4], (book, edge, land_wide_dec, land_narrow_dec), (0, 16, 64, 32), *sems_dec)
    gather_enc = Gather(shards[4:], (land_wide, land_narrow), (64, 32), *sems_enc)
    meet(peers())
    gather.begin()
    exchange = []
    for step in range(1, 4):
        chip = (chip_at + step) % 4
        target = (img_at, 2 * chip + c_at)
        here = band_at
        exchange.append(far_copy(slab.at[chip], slab_all.at[here], e_send.at[0, step], e_recv.at[0, step], target))
        exchange.append(far_copy(code.at[chip], code_all.at[here], e_send.at[1, step], e_recv.at[1, step], target))
    exchange.append(pltpu.make_async_copy(slab.at[chip_at], slab_all.at[band_at], e_near.at[0]))
    exchange.append(pltpu.make_async_copy(code.at[chip_at], code_all.at[band_at], e_near.at[1]))
    for copy in exchange:
        copy.start()
    segment_lane = lax.broadcasted_iota(jnp.int32, (enc.total, 128), 1)
    segment = jnp.where(kind[0:1, 0:1] == 0, 0, lax.broadcasted_iota(jnp.int32, (enc.total, 128), 0) // (enc.total // 4))
    k_extra[...] = jnp.where(segment_lane == segment, 1.0, 0.0).astype(bf16)
    segment_lane = lax.broadcasted_iota(jnp.int32, (enc.own, 128), 1)
    segment = lax.broadcasted_iota(jnp.int32, (enc.own, 128), 0) + enc.offset
    segment = jnp.where(kind[0:1, 0:1] == 0, 0, segment // (enc.total // 4))
    q_extra[...] = jnp.where((segment_lane < 4) & (segment_lane != segment), -(2.0**30), 0.0).astype(bf16)
    for ref in (small_dec, small_enc, g_pixw, g_qout, g_qin, g_inw):
        ref[...] = jnp.zeros(ref.shape, f32)
    for copy in exchange:
        copy.wait()
    late = []
    for k, dst in enumerate((slab_all, code_all)):
        for chip in range(4):
            part = dst.at[2 * chip + c_at]
            late.append(far_copy(part, part, e_send.at[k, 4 + chip], e_recv.at[k, 4 + chip], over_c))
    for copy in late:
        copy.start()
    gather.until(0)
    gather_enc.begin()
    for copy in late:
        copy.wait()
    for n in range(8):
        code_col[pl.ds(128 * n, 128)] = jnp.transpose(code_all[n])[:, 0:1]
    for n in range(4):
        code_row[:, pl.ds(128 * n, 128)] = code_all[own_band + n, 0:1]

    def pick_codes(k):
        rows = at(k)
        code_here = code_col[rows]
        picks = lax.broadcasted_iota(jnp.int32, (STEP, 512), 1)
        found = jnp.zeros((STEP, 128), f32)
        for z in range(4):
            hot = jnp.where(picks + 512 * z == code_here // 4, 1.0, 0.0).astype(bf16)
            found += dot_nn(hot, book[z].reshape(512, 128))
        lanes = lax.broadcasted_iota(jnp.int32, (STEP, 128), 1) // 32
        spread[rows] = jnp.where(lanes == code_here % 4, found, 0.0).astype(bf16)

    loop(0, dec.total // STEP, pick_codes)
    gather.until(1)
    dec.enter(0, dec.total // STEP)
    sum_everywhere(tally, t_img, t_band, t_send, t_recv, tally_all)

    def fetch(landed, ref, sem):
        rows = landed.shape[4]

        def body(n):
            src = landed.at[n // 8, (n // 4) % 2, (n // 2) % 2, n % 2]
            pltpu.make_async_copy(src, ref.at[pl.ds(pl.multiple_of(n * rows, 16), rows)], sem).start()

        loop(0, 32, body)
        return pltpu.make_async_copy(ref, ref, sem)

    reduce = Reduce(*slots, *red)
    tail = ReduceSmall(
        (g_edge, g_book), (share_edge, share_book),
        *[red_small[2 * n : 2 * n + 2] for n in range(7)], *red_small[14:],
    )

    def emit_wide(blk, z, full, slot):
        values = [blk.wide_product(*span) for span in pieces_of(896 * z, 896, 3 * width)]
        value = values[0] if len(values) == 1 else jnp.concatenate(values, axis=0)
        full[slot] = value.reshape(2, 2, 2, 112, width)

    def emit_narrow(blk, z, full, slot):
        values = [blk.narrow_product(*span) for span in pieces_of(640 * z, 640, width)]
        value = values[0] if len(values) == 1 else jnp.concatenate(values, axis=0)
        full[slot, :, :, :, :80] = value.reshape(2, 2, 2, 80, width)

    pieces = []
    for name, blk, out_wide, out_narrow in (
        ("dec", dec, share_wide_dec, share_narrow_dec), ("enc", enc, share_wide, share_narrow)
    ):
        for z in (3, 0, 2, 1):
            pieces.append(
                dict(emit=functools.partial(emit_narrow, blk, z), z=z, rows=80, out=out_narrow, needs=name + "1")
            )
        for z in (3, 2, 0, 1):
            pieces.append(
                dict(emit=functools.partial(emit_wide, blk, z), z=z, rows=112, out=out_wide, needs=name + str(1 + (z < 2)))
            )
    reduce.plan(pieces)
    ready = []

    def tick(count):
        reduce.tick(count, ready)

    def decoder_head(k):
        rows = at(k)
        out = dec.grad_out[rows]
        shape, _ = norm_parts(out)
        final = (shape * norms[pl.ds(8, 1), :] + norms[pl.ds(9, 1), :]).astype(bf16)
        error = dot_nn(final, e_pix()) - pixel_rows(k, 0, own_band).astype(f32)
        lane = lax.broadcasted_iota(jnp.int32, (STEP, 256), 1)
        counted = jnp.where(lane < 192, pltpu.roll(pixel_rows(k, 128, own_band).astype(f32), 192, 1), 0.0)
        number = tally_all[0:1, 0:1]
        dec.add_loss(jnp.sum(counted * (error * error + jnp.abs(error))) / number)
        sign = jnp.where(error > 0.0, 1.0, jnp.where(error < 0.0, -1.0, 0.0))
        grad_pred = (counted * (2.0 * error + sign) / number).astype(bf16)
        g_pixw[...] += dot_tn(final, grad_pred)
        back, g_gain, g_offset = norm_back(dot_nt(grad_pred, e_pix()), out, norms[pl.ds(8, 1), :])
        dec.add_small(4, g_gain)
        dec.add_small(5, g_offset)
        dec.grad_out[rows] = back
        dec.grad_low[rows] = back.astype(bf16)

    def encoder_head(k):
        rows = at(k)
        low = enc.grad_out[rows].astype(bf16)
        lanes = lax.broadcasted_iota(jnp.int32, (STEP, 128), 1) // 32
        mine = lanes == code_col[at(k, enc.offset)] % 4
        gap = jnp.where(mine, spread[at(k, enc.offset)].astype(f32) - dot_nn(low, e_qin()), 0.0)
        enc.add_loss((1.0 + commitment) * jnp.sum(gap * gap) / latent_total)
        grad_latent = jnp.where(mine, cross[rows] - 2.0 * commitment * gap / latent_total, 0.0).astype(bf16)
        g_qin[...] += dot_tn(low, grad_latent)
        back = dot_nt(grad_latent, e_qin())
        enc.grad_out[rows] = back
        enc.grad_low[rows] = back.astype(bf16)
        gap = 2.0 * gap / latent_total
        high = gap.astype(bf16)
        left = gap - high.astype(f32)
        between = left.astype(bf16)
        split[rows] = jnp.concatenate([high, between, (left - between.astype(f32)).astype(bf16)], axis=1)

    def book_rows(k):
        picks = lax.broadcasted_iota(jnp.int32, (STEP, enc.own), 0) + k * STEP
        hot = jnp.where(picks == code_row[...] // 4, 1.0, 0.0).astype(bf16)
        summed = dot_nn(hot, split[...])
        value = (summed[:, :128] + summed[:, 128:256]) + summed[:, 256:]
        g_book[k // 2, k % 2] = value.reshape(2, 2, 64, 128)

    def decoder_leave(k):
        low = dec.leave_rows(k)
        cross[at(k)] = dot_nn(low, e_qout())
        g_qout[...] += dot_tn(low, spread[at(k, dec.offset)])

    def encoder_leave(k):
        g_inw[...] += dot_tn(enc.leave_rows(k), pixel_rows(k, 0, own_band))

    gather.until(2)
    fetch(land_wide_dec, wide, load_sem.at[0]).wait()
    dec.make_kv(0, dec.total // STEP)
    dec.make_q()
    gather.until(3)
    fetched = fetch(land_narrow_dec, narrow, load_sem.at[1])
    dec.attend(0, 2)
    gather_enc.tick(2)
    dec.attend(2, 4)
    gather_enc.tick(1)
    fetched.wait()
    dec.after_attention()
    dec.mlp(0, 2)
    gather_enc.tick(1)
    dec.mlp(2, 4)
    gather_enc.tick(1)
    loop(0, dec.chunks, decoder_head)
    dec.mlp_back(0, dec.chunks)
    gather_enc.tick(1)
    ready.append("dec1")
    tick(1)
    for p in range(4):
        dec.attend_back(p, p + 1)
        tick(4)
        if p == 1:
            gather_enc.until(1)
    fetched = fetch(land_narrow, narrow, load_sem.at[1])
    dec.swap_start(False)
    tick(3)
    dec.swap_finish(False)
    ready.append("dec2")
    loop(0, dec.chunks, decoder_leave)
    fetched_wide = fetch(land_wide, wide, load_sem.at[0])
    while reduce.opened < 8:
        tick(1)
    fetched.wait()
    enc.enter(0, enc.total // STEP)
    tick(2)
    fetched_wide.wait()
    enc.make_kv(0, enc.total // STEP)
    enc.make_q()
    tick(3)
    for p in range(2):
        enc.attend(2 * p, 2 * p + 2)
        tick(4)
    enc.after_attention()
    tick(1)
    enc.mlp(0, 2)
    tick(3)
    enc.mlp(2, 4)
    tick(3)
    loop(0, enc.chunks, encoder_head)
    tick(2)
    loop(0, 8, book_rows)
    tick(2)
    tail.open(1)
    enc.mlp_back(0, 1)
    tick(2)
    tail.step(1, 0)
    enc.mlp_back(1, enc.chunks)
    ready.append("enc1")
    tick(2)
    tail.step(1, 1)
    for p in range(4):
        enc.attend_back(p, p + 1)
        tick(4)
        if p < 2:
            tail.step(1, 2 + p)
    enc.swap_start(True)
    tick(2)
    enc.swap_finish(True)
    ready.append("enc2")
    loop(0, enc.chunks, encoder_leave)

    def all_groups(value):
        value = value + pltpu.roll(value, 64, 1)
        return value + pltpu.roll(value, 32, 1)

    lane = lax.broadcasted_iota(jnp.int32, (width, 128), 1)
    mixed = jnp.where(lane < 64, g_inw[:, 128:], jnp.where(lane < 96, all_groups(g_qin[...]), all_groups(g_qout[...])))
    for first, value in ((0, g_inw[:, :128]), (128, mixed), (256, g_pixw[:, :128]), (384, g_pixw[:, 128:])):
        g_edge[:, :, :, :, :, pl.ds(first, 128)] = value.reshape(4, 2, 2, 2, 16, 128)
    tail.open(0)
    tick(4)
    for k in range(3):
        tail.step(0, k)
        tick(4)
    tick(1000)
    tail.step(0, 3)
    shares = (share_wide_dec, share_narrow_dec, share_wide, share_narrow, share_edge, share_book)
    squares = sum(jnp.sum(share[...] * share[...]) for share in shares)
    lane = lax.broadcasted_iota(jnp.int32, (8, width), 1)
    row = lax.broadcasted_iota(jnp.int32, (8, width), 0)
    small_own[0] = small_enc[...]
    small_own[1] = jnp.where((row == 7) & (lane == 0), squares, small_dec[...])
    sum_everywhere(small_own, s_img, s_band, s_send, s_recv, small_all)


def train_step(shards, slab, code, tally, kind, norms, latent_total, total_rows, own_rows):
    width = 512
    slots = (4, 4)
    f32, bf16, int32 = jnp.float32, jnp.bfloat16, jnp.int32
    any_space = pl.BlockSpec(memory_space=pl.ANY)
    vmem = pl.BlockSpec(memory_space=pltpu.VMEM)
    shape = jax.ShapeDtypeStruct
    out_shape = [
        shape((112, width), f32), shape((80, width), f32), shape((112, width), f32), shape((80, width), f32),
        shape((16, width), f32), shape((64, 128), f32), shape((2, 8, width), f32),
    ]
    out_shape += [shape((4, 2, 2, 2) + s.shape, s.dtype) for s in shards[2:]]
    dma = pltpu.SemaphoreType.DMA
    mem = pltpu.VMEM
    scratch = gather_sems(4) + gather_sems(2)
    scratch += reduce_scratch(*slots, 112, width) + reduce_small_scratch([(16, width), (64, 128)])
    scratch += [
        mem((4, 2, 2, 2, 64, 128), bf16), mem((4, 2, 2, 2, 16, 768), bf16),
        mem((8, 128, 384), bf16), mem((8, 8, 128), int32), mem((8, 128), f32),
        mem((4, 8, 128), f32), mem((8, 8, 128), f32),
        dma((2,)), dma((2, 8)), dma((2, 8)), dma((11,)), dma((11,)),
        mem((total_rows, 1), int32), mem((1, own_rows), int32), mem((total_rows, 128), bf16),
        mem((own_rows, 128), f32), mem((own_rows, 384), bf16),
        mem((width, 256), f32), mem((width, 128), f32), mem((width, 128), f32), mem((width, 256), f32),
        mem((4, 2, 2, 2, 16, width), f32), mem((4, 2, 2, 2, 64, 128), f32),
        mem((8, width), f32), mem((8, width), f32), mem((2, 8, width), f32),
        mem((4, 2, 8, width), f32), mem((8, 2, 8, width), f32), dma((11,)), dma((11,)),
        dma((2,)), mem((7 * width, width), bf16), mem((5 * width, width), bf16),
        mem((own_rows, 128), bf16), mem((total_rows, 128), bf16),
    ]
    scratch += block_scratch(total_rows, own_rows)
    return pl.pallas_call(
        functools.partial(step_kernel, slots, latent_total),
        out_shape=out_shape,
        in_specs=[any_space] * 8 + [vmem] * 3,
        out_specs=[vmem] * 7 + [any_space] * 4,
        scratch_shapes=scratch,
        compiler_params=pltpu.CompilerParams(collective_id=0, has_side_effects=True, vmem_limit_bytes=63 << 20),
        name="train_step",
    )(*shards, slab, code, tally, kind, norms)


def moments(gradient, first_old, second_old):
    first_new = beta_first * first_old + (1.0 - beta_first) * gradient
    second_new = beta_second * second_old + (1.0 - beta_second) * gradient * gradient
    return (first_new, second_new, first_new / (jnp.sqrt(second_new) + adam_eps))


def rotated_update(weight, gradient, first_old, second_old, basis_stack):
    turned = jnp.einsum("rld,lde->rle", gradient, basis_stack, precision=highest)
    first_new, second_new, direction = moments(turned, first_old, second_old)
    turned_back = jnp.einsum("rle,lde->rld", direction, basis_stack, precision=highest)
    return (weight - rate_matrix * (turned_back + weight_decay * weight), first_new, second_new)


def plain_update(weight, gradient, first_old, second_old):
    first_new, second_new, direction = moments(gradient, first_old, second_old)
    return (weight - rate_vector * (direction + weight_decay * weight), first_new, second_new)


def body(
    pixels,
    valid,
    codes,
    image_kind,
    w_wide,
    w_narrow,
    w_edge,
    codebook,
    norms,
    bases,
    basis_edge,
    m_wide,
    v_wide,
    m_narrow,
    v_narrow,
    m_edge,
    v_edge,
    m_code,
    v_code,
    m_norm,
    v_norm,
):
    band_count = lax.axis_size("band")
    band_index = lax.axis_index("band")
    row_count = pixels.shape[2]
    length = row_count * band_count
    batch_count = pixels.shape[0]
    group = band_count // batch_count
    row = band_index // group
    part = band_index % group
    own_rows = length // group
    groups = [[k * group + j for j in range(group)] for k in range(batch_count)]
    layer_count = w_wide.shape[1]
    code_width = codebook.shape[1]
    latent_total = batch_count * lax.axis_size("img") * length * code_width
    both = ("img", "band")

    direct = band_count == 8 and lax.axis_size("img") == 4 and batch_count == 4
    shards = [w_wide[:, l].astype(jnp.bfloat16) for l in range(layer_count)]
    shards += [w_narrow[:, l].astype(jnp.bfloat16) for l in range(layer_count)]
    shards += [w_edge.astype(jnp.bfloat16), codebook.astype(jnp.bfloat16).reshape(-1, 4 * code_width)]
    slab = jnp.concatenate([pixels[:, 0], valid[:, 0].astype(jnp.bfloat16)], axis=2)
    local_count = jnp.sum(valid.astype(jnp.float32))
    patch_size = pixels.shape[3]
    kind = lax.dynamic_index_in_dim(image_kind[:, 0], row, 0, keepdims=False)
    if direct:
        edge = shards[4]
        gap = jnp.zeros((edge.shape[0], 64), edge.dtype)
        qin = edge[:, 2 * patch_size : 2 * patch_size + code_width]
        qout = edge[:, 2 * patch_size + code_width :]
        shards[4] = jnp.concatenate(
            [edge[:, :patch_size], gap, edge[:, patch_size : 2 * patch_size], gap] + [qin] * 4 + [qout] * 4, axis=1
        )
        code_tile = jnp.broadcast_to(codes, (batch_count, 8, row_count))
        out = train_step(
            [shards[k] for k in (5, 4, 1, 3, 0, 2)], slab, code_tile, jnp.full((8, 128), local_count),
            jnp.full((8, 128), kind), norms, latent_total, length, own_rows,
        )
        small = out[6]
        norm_total = jnp.concatenate([small[0, :4], small[1, :6]], axis=0)
        loss_total = small[0, 6, 0] + small[1, 6, 0]
        square_total = small[1, 7, 0]
        edge_share = jnp.concatenate([out[4][:, :192], out[4][:, 256:448], out[4][:, 192:256]], axis=1)
        shares = [out[2], out[0], out[3], out[1], edge_share, out[5]]
    else:
        wholes = [lax.all_gather(shard, both, axis=0, tiled=True) for shard in shards]
        count = lax.psum(local_count, both)

        def whole_row(local):
            everywhere = lax.all_gather(local, "band", axis=0)
            chosen_row = lax.dynamic_index_in_dim(everywhere, row, axis=1, keepdims=False)
            return chosen_row.reshape((length,) + local.shape[2:])

        slab_all = whole_row(slab)
        code_all = whole_row(codes[:, 0])
        span = jnp.where(kind == 0, length, length // 4)
        positions = jnp.arange(length, dtype=jnp.int32)
        gathered = (wholes[:2], wholes[2:4], wholes[4], wholes[5])
        pixel_all = slab_all[:, :patch_size]
        valid_rows = lax.dynamic_slice_in_dim(slab_all, part * own_rows, own_rows, 0)[:, patch_size:]
        own_positions = part * own_rows + jnp.arange(own_rows, dtype=jnp.int32)
        allowed = (own_positions // span)[:, None] == (positions // span)[None, :]
        local_grads, norm_sum, loss_sum = row_step(
            gathered, norms, pixel_all, valid_rows, code_all, part, allowed, count, latent_total, groups
        )
        shares = [lax.psum_scatter(g, both, scatter_dimension=0, tiled=True) for g in local_grads]
        squares = sum(jnp.sum(share * share) for share in shares)
        norm_total, square_total, loss_total = lax.psum((norm_sum, squares, loss_sum), both)
    grad_sum = (
        jnp.stack([shares[0], shares[1]], axis=1),
        jnp.stack([shares[2], shares[3]], axis=1),
        shares[4],
        shares[5].reshape(-1, code_width),
    )
    grad_norm = jnp.sqrt(square_total + jnp.sum(norm_total * norm_total))
    factor = jnp.minimum(1.0, clip_level / grad_norm)
    grad_wide, grad_narrow, grad_edge, grad_book = grad_sum
    new_wide, new_m_wide, new_v_wide = rotated_update(
        w_wide, factor * grad_wide, m_wide, v_wide, bases[:layer_count]
    )
    new_narrow, new_m_narrow, new_v_narrow = rotated_update(
        w_narrow, factor * grad_narrow, m_narrow, v_narrow, bases[layer_count:]
    )
    new_edge, new_m_edge, new_v_edge = rotated_update(
        w_edge[:, None],
        factor * grad_edge[:, None],
        m_edge[:, None],
        v_edge[:, None],
        basis_edge[None],
    )
    new_book, new_m_code, new_v_code = plain_update(codebook, factor * grad_book, m_code, v_code)
    new_norms, new_m_norm, new_v_norm = plain_update(norms, factor * norm_total, m_norm, v_norm)
    return (
        new_wide,
        new_m_wide,
        new_v_wide,
        new_narrow,
        new_m_narrow,
        new_v_narrow,
        new_edge[:, 0],
        new_m_edge[:, 0],
        new_v_edge[:, 0],
        new_book,
        new_m_code,
        new_v_code,
        new_norms,
        new_m_norm,
        new_v_norm,
        grad_norm,
        loss_total,
    )


def solution(mesh):
    in_specs = (
        P(None, "img", "band", None),
        P(None, "img", "band", None),
        P(None, "img", "band"),
        P(None, "img"),
        P(("img", "band"), None, None),
        P(("img", "band"), None, None),
        P(("img", "band"), None),
        P(("img", "band"), None),
        P(),
        P(),
        P(),
        P(("img", "band"), None, None),
        P(("img", "band"), None, None),
        P(("img", "band"), None, None),
        P(("img", "band"), None, None),
        P(("img", "band"), None),
        P(("img", "band"), None),
        P(("img", "band"), None),
        P(("img", "band"), None),
        P(),
        P(),
    )
    out_specs = (
        P(("img", "band"), None, None),
        P(("img", "band"), None, None),
        P(("img", "band"), None, None),
        P(("img", "band"), None, None),
        P(("img", "band"), None, None),
        P(("img", "band"), None, None),
        P(("img", "band"), None),
        P(("img", "band"), None),
        P(("img", "band"), None),
        P(("img", "band"), None),
        P(("img", "band"), None),
        P(("img", "band"), None),
        P(),
        P(),
        P(),
        P(),
        P(),
    )
    return jax.shard_map(body, mesh=mesh, in_specs=in_specs, out_specs=out_specs, check_vma=False)
```

```python
import functools

import jax
import jax.numpy as jnp
from jax import lax
from jax.experimental import pallas as pl
from jax.experimental.pallas import tpu as pltpu
from jax.sharding import PartitionSpec as P

HEADS = 8
HDIM = 64
MESH = pl.DeviceIdType.MESH


norm_eps = 1e-05
adam_eps = 1e-08
clip_level = 0.001
beta_first = 0.5
beta_second = 0.6
rate_matrix = 0.02
rate_vector = 0.3
weight_decay = 0.01
commitment = 0.25
masked_score = -1000000000.0
highest = lax.Precision.HIGHEST


def matmul_plain(first_op, second_op):
    return jnp.dot(first_op, second_op, preferred_element_type=jnp.float32)


def matmul_trans(first_op, second_op):
    return lax.dot_general(
        first_op, second_op, (((1,), (1,)), ((), ())), preferred_element_type=jnp.float32
    )


def matmul_outer(first_op, second_op):
    return lax.dot_general(
        first_op, second_op, (((0,), (0,)), ((), ())), preferred_element_type=jnp.float32
    )


def layer_norm(hidden, scale_gain, offset):
    centred = hidden - jnp.mean(hidden, axis=-1, keepdims=True)
    spread = jnp.mean(centred * centred, axis=-1, keepdims=True)
    return centred * lax.rsqrt(spread + norm_eps) * scale_gain + offset


def gelu_tanh(inputs):
    return (
        0.5
        * inputs
        * (1.0 + jnp.tanh(0.7978845608028654 * (inputs + 0.044715 * inputs * inputs * inputs)))
    )


def split_heads(matrix):
    return matrix.reshape(matrix.shape[0], HEADS, HDIM)


def head_scores(q_heads, k_heads, allowed):
    scores = jnp.einsum(
        "qhd,khd->hqk", q_heads, k_heads, preferred_element_type=jnp.float32
    ) * HDIM ** (-0.5)
    return jnp.where(allowed[None], scores, masked_score)


def attend(queries, key_rows, value_rows, allowed):
    scores = head_scores(split_heads(queries), split_heads(key_rows), allowed)
    score_peak = jnp.max(scores, axis=-1, keepdims=True)
    expo = jnp.exp(scores - score_peak)
    total = jnp.sum(expo, axis=-1, keepdims=True)
    softmaxed = (expo / total).astype(jnp.bfloat16)
    attended = jnp.einsum(
        "hqk,khd->qhd", softmaxed, split_heads(value_rows), preferred_element_type=jnp.float32
    )
    return (
        attended.reshape(queries.shape[0], -1).astype(jnp.bfloat16),
        score_peak + jnp.log(total),
    )


def attend_back(queries, key_rows, value_rows, allowed, log_total, grad_out):
    q_heads = split_heads(queries)
    k_heads = split_heads(key_rows)
    v_heads = split_heads(value_rows)
    g_heads = split_heads(grad_out)
    softmaxed = jnp.exp(head_scores(q_heads, k_heads, allowed) - log_total)
    grad_soft = jnp.einsum("qhd,khd->hqk", g_heads, v_heads, preferred_element_type=jnp.float32)
    row_dot = jnp.sum(softmaxed * grad_soft, axis=-1, keepdims=True)
    grad_scores = (softmaxed * (grad_soft - row_dot)).astype(jnp.bfloat16)
    scale = HDIM ** (-0.5)
    grad_q = (
        jnp.einsum("hqk,khd->qhd", grad_scores, k_heads, preferred_element_type=jnp.float32) * scale
    )
    grad_k = (
        jnp.einsum("hqk,qhd->khd", grad_scores, q_heads, preferred_element_type=jnp.float32) * scale
    )
    grad_v = jnp.einsum(
        "hqk,qhd->khd", softmaxed.astype(jnp.bfloat16), g_heads, preferred_element_type=jnp.float32
    )
    return (
        grad_q.reshape(queries.shape[0], -1),
        grad_k.reshape(key_rows.shape[0], -1),
        grad_v.reshape(key_rows.shape[0], -1),
    )


def block_forward(hidden_all, part, wide_rows, narrow_rows, gain_rows, allowed):
    model_width = hidden_all.shape[1]
    own_rows = allowed.shape[0]
    normed_all = layer_norm(hidden_all, gain_rows[0], gain_rows[1]).astype(jnp.bfloat16)
    hidden = lax.dynamic_slice_in_dim(hidden_all, part * own_rows, own_rows, 0)
    normed = lax.dynamic_slice_in_dim(normed_all, part * own_rows, own_rows, 0)
    queries = matmul_trans(normed, wide_rows[:model_width]).astype(jnp.bfloat16)
    key_rows = matmul_trans(normed_all, wide_rows[model_width : 2 * model_width]).astype(jnp.bfloat16)
    value_rows = matmul_trans(normed_all, wide_rows[2 * model_width : 3 * model_width]).astype(jnp.bfloat16)
    attended, log_total = attend(queries, key_rows, value_rows, allowed)
    middle = hidden + matmul_plain(attended, narrow_rows[:model_width])
    second = layer_norm(middle, gain_rows[2], gain_rows[3]).astype(jnp.bfloat16)
    upper_in = matmul_trans(second, wide_rows[3 * model_width :])
    active = gelu_tanh(upper_in).astype(jnp.bfloat16)
    result = middle + matmul_plain(active, narrow_rows[model_width:])
    return (
        result,
        (hidden, normed, queries, key_rows, value_rows, attended, log_total, middle, second, upper_in, active),
    )


def block_backward(grad_out, wide_rows, narrow_rows, gain_rows, allowed, saved, groups):
    (hidden, normed, queries, key_rows, value_rows, attended, log_total, middle, second, upper_in, active) = saved
    model_width = hidden.shape[1]
    grad_y = grad_out.astype(jnp.bfloat16)
    grad_down = matmul_outer(active, grad_y)
    grad_active = matmul_trans(grad_y, narrow_rows[model_width:])
    grad_upper = jax.vjp(gelu_tanh, upper_in)[1](grad_active)[0].astype(jnp.bfloat16)
    grad_up = matmul_outer(grad_upper, second)
    _, second_back = jax.vjp(layer_norm, middle, gain_rows[2], gain_rows[3])
    grad_mid, gain_two, offset_two = second_back(
        matmul_plain(grad_upper, wide_rows[3 * model_width :])
    )
    grad_mid = grad_mid + grad_out
    grad_attn = grad_mid.astype(jnp.bfloat16)
    grad_outproj = matmul_outer(attended, grad_attn)
    grad_att = matmul_trans(grad_attn, narrow_rows[:model_width]).astype(jnp.bfloat16)
    grad_q, grad_keys, grad_values = attend_back(
        queries, key_rows, value_rows, allowed, log_total, grad_att
    )
    grad_k = lax.psum_scatter(grad_keys, "band", scatter_dimension=0, tiled=True, axis_index_groups=groups)
    grad_v = lax.psum_scatter(grad_values, "band", scatter_dimension=0, tiled=True, axis_index_groups=groups)
    grad_mixed = jnp.concatenate([grad_q, grad_k, grad_v], axis=1).astype(jnp.bfloat16)
    grad_qkv = matmul_outer(grad_mixed, normed)
    _, first_back = jax.vjp(layer_norm, hidden, gain_rows[0], gain_rows[1])
    grad_in, gain_one, offset_one = first_back(
        matmul_plain(grad_mixed, wide_rows[: 3 * model_width])
    )
    gain_grads = jnp.stack([gain_one, offset_one, gain_two, offset_two], axis=0)
    return (
        grad_in + grad_mid,
        jnp.concatenate([grad_qkv, grad_up], axis=0),
        jnp.concatenate([grad_outproj, grad_down], axis=0),
        gain_grads,
    )


def pick_codes(code_rows, book_wide, code_width):
    fold = book_wide.shape[1] // code_width
    one_hot = (
        (code_rows // fold)[:, None] == jnp.arange(book_wide.shape[0], dtype=jnp.int32)[None, :]
    ).astype(jnp.bfloat16)
    lane_fold = jnp.arange(book_wide.shape[1], dtype=jnp.int32)[None, :] // code_width
    lane_mask = (code_rows % fold)[:, None] == lane_fold
    spread = jnp.where(lane_mask, matmul_plain(one_hot, book_wide), 0.0)
    chosen = sum(spread[:, k * code_width : (k + 1) * code_width] for k in range(fold))
    return chosen, one_hot, lane_mask


def row_step(gathered, norms, pixel_all, valid_rows, code_all, part, allowed, count, latent_total, groups):
    wide_all, narrow_all, edge_all, book_wide = gathered
    patch_size = pixel_all.shape[1]
    code_width = edge_all.shape[1] // 2 - patch_size
    own_rows = allowed.shape[0]
    edge_in = edge_all[:, :patch_size]
    edge_pix = edge_all[:, patch_size : 2 * patch_size]
    edge_qin = edge_all[:, 2 * patch_size : 2 * patch_size + code_width]
    edge_qout = edge_all[:, 2 * patch_size + code_width :]
    pixel_rows = lax.dynamic_slice_in_dim(pixel_all, part * own_rows, own_rows, 0)
    chosen_all, one_hot_all, lane_mask_all = pick_codes(code_all, book_wide, code_width)
    chosen_low_all = chosen_all.astype(jnp.bfloat16)
    chosen = lax.dynamic_slice_in_dim(chosen_all, part * own_rows, own_rows, 0)
    one_hot = lax.dynamic_slice_in_dim(one_hot_all, part * own_rows, own_rows, 0)
    lane_mask = lax.dynamic_slice_in_dim(lane_mask_all, part * own_rows, own_rows, 0)
    chosen_low = chosen.astype(jnp.bfloat16)
    begin = matmul_trans(chosen_low_all, edge_qout)
    decoded, dec_saved = block_forward(begin, part, wide_all[1], narrow_all[1], norms[4:8], allowed)
    final = layer_norm(decoded, norms[8], norms[9]).astype(jnp.bfloat16)
    predict = matmul_plain(final, edge_pix)
    error = predict - pixel_rows.astype(jnp.float32)
    pixel_mask = valid_rows.astype(jnp.float32)
    loss_pix = jnp.sum(pixel_mask * (error * error + jnp.abs(error))) / count
    grad_pred = (pixel_mask * (2.0 * error + jnp.sign(error)) / count).astype(jnp.bfloat16)
    grad_pixw = matmul_outer(final, grad_pred)
    _, final_back = jax.vjp(layer_norm, decoded, norms[8], norms[9])
    grad_dec, gain_last, offset_last = final_back(matmul_trans(grad_pred, edge_pix))
    grad_begin, dec_wide, dec_narrow, dec_gains = block_backward(
        grad_dec, wide_all[1], narrow_all[1], norms[4:8], allowed, dec_saved, groups
    )
    grad_begin_low = grad_begin.astype(jnp.bfloat16)
    grad_qout = matmul_outer(grad_begin_low, chosen_low)
    start = matmul_trans(pixel_all, edge_in)
    encoded, enc_saved = block_forward(start, part, wide_all[0], narrow_all[0], norms[0:4], allowed)
    encoded_low = encoded.astype(jnp.bfloat16)
    latent = matmul_plain(encoded_low, edge_qin)
    gap = chosen - latent
    loss_part = loss_pix + (1.0 + commitment) * jnp.sum(gap * gap) / latent_total
    grad_latent = (
        matmul_plain(grad_begin_low, edge_qout) - 2.0 * commitment * gap / latent_total
    ).astype(jnp.bfloat16)
    fold = lane_mask.shape[1] // code_width
    gap_wide = jnp.where(lane_mask, jnp.tile(2.0 * gap / latent_total, (1, fold)), 0.0)
    gap_high = gap_wide.astype(jnp.bfloat16)
    gap_rest = gap_wide - gap_high.astype(jnp.float32)
    gap_middle = gap_rest.astype(jnp.bfloat16)
    gap_low = (gap_rest - gap_middle.astype(jnp.float32)).astype(jnp.bfloat16)
    grad_book = (
        matmul_outer(one_hot, gap_high) + matmul_outer(one_hot, gap_middle)
    ) + matmul_outer(one_hot, gap_low)
    grad_qin = matmul_outer(encoded_low, grad_latent)
    grad_start, enc_wide, enc_narrow, enc_gains = block_backward(
        matmul_trans(grad_latent, edge_qin), wide_all[0], narrow_all[0], norms[0:4], allowed, enc_saved, groups
    )
    grad_inw = matmul_outer(grad_start.astype(jnp.bfloat16), pixel_rows)
    grads = (
        enc_wide, dec_wide, enc_narrow, dec_narrow,
        jnp.concatenate([grad_inw, grad_pixw, grad_qin, grad_qout], axis=1),
        grad_book,
    )
    norm_grad = jnp.concatenate([enc_gains, dec_gains, gain_last[None], offset_last[None]], axis=0)
    return (grads, norm_grad, loss_part)


def place():
    img_at = lax.axis_index("img")
    band_at = lax.axis_index("band")
    return img_at, band_at, band_at // 4, (band_at // 2) % 2, band_at % 2


def neighbours():
    img_at, band_at, y_at, x_at, c_at = place()
    return (
        (img_at, band_at + 1 - 2 * c_at),
        (img_at, band_at + 2 - 4 * x_at),
        (img_at, band_at + 4 - 8 * y_at),
    )


def peers():
    img_at, band_at = place()[:2]
    found = [((img_at + step) % 4, band_at) for step in range(1, 4)]
    return found + [(img_at, (band_at + step) % 8) for step in range(1, 8)]


def meet(others):
    barrier = pltpu.get_barrier_semaphore()
    for other in others:
        pl.semaphore_signal(barrier, inc=1, device_id=other, device_id_type=MESH)
    pl.semaphore_wait(barrier, len(others))


def far_copy(src, dst, send, recv, target):
    return pltpu.make_async_remote_copy(
        src_ref=src, dst_ref=dst, send_sem=send, recv_sem=recv, device_id=target, device_id_type=MESH
    )


class Everywhere:
    def __init__(self, name, agenda, own_ref, img_buf, band_buf, send, recv, result_ref):
        self.name, self.agenda, self.done = name, agenda, False
        self.own, self.img_buf, self.band_buf, self.result = own_ref, img_buf, band_buf, result_ref
        self.send, self.recv = send, recv

    def begin(self):
        img_at, band_at = place()[:2]
        self.img_buf[img_at] = self.own[...]
        copies = [
            far_copy(
                self.own, self.img_buf.at[img_at], self.send.at[step], self.recv.at[step], ((img_at + step) % 4, band_at)
            )
            for step in range(1, 4)
        ]
        self.agenda.launch((self.name, 0), copies, [], self.middle)
        self.agenda.spend(0.5)

    def middle(self):
        img_at, band_at = place()[:2]
        buf = self.img_buf
        self.result[...] = (buf[0] + buf[1]) + (buf[2] + buf[3])
        self.band_buf[band_at] = self.result[...]
        copies = [
            far_copy(
                self.result, self.band_buf.at[band_at], self.send.at[3 + step], self.recv.at[3 + step],
                (img_at, (band_at + step) % 8),
            )
            for step in range(1, 8)
        ]
        self.agenda.launch((self.name, 1), copies, [], self.end)
        self.agenda.spend(1.0)

    def end(self):
        total = self.band_buf[0]
        for k in range(1, 8):
            total = total + self.band_buf[k]
        self.result[...] = total
        self.done = True

    def until(self):
        self.agenda.until(lambda: self.done)


LINK, CORE, LAG = 90e3, 500e3, 0.8


class Agenda:
    def __init__(self):
        self.now, self.free, self.flying = 0.0, {}, {}

    def launch(self, key, copies, loads, then):
        done = self.now
        for link, size in loads:
            begin = max(self.now, self.free.get(link, 0.0))
            self.free[link] = begin + size / (CORE if link == "c" else LINK) + 0.4
            done = max(done, self.free[link])
        for copy in copies:
            copy.start()
        self.flying[key] = (done + LAG, copies, then)

    def land(self, key):
        done, copies, then = self.flying.pop(key)
        self.now = max(self.now, done) + 0.5
        for copy in copies:
            copy.wait()
        then()

    def spend(self, time):
        self.now += time

    def tick(self):
        while self.flying:
            key = min(self.flying, key=lambda name: self.flying[name][0])
            if self.flying[key][0] > self.now:
                return
            self.land(key)

    def until(self, test):
        while not test():
            self.land(min(self.flying, key=lambda name: self.flying[name][0]))


class Gather:
    def __init__(self, name, agenda, pieces, near, z_send, z_recv, p_send, p_recv):
        self.name, self.agenda, self.pieces = name, agenda, pieces
        self.near, self.z_send, self.z_recv, self.p_send, self.p_recv = near, z_send, z_recv, p_send, p_recv
        self.done = set()

    def launch(self, p, k):
        img_at, band_at, y_at, x_at, c_at = place()
        over_c, over_x, over_y = neighbours()
        shard, whole, first, count = self.pieces[p]
        rows = pl.ds(first, count)
        width = shard.shape[1]
        size = count * max(width, 128) * 2
        lanes = width // 256 * 128
        found, loads = [], []
        if k == 0:
            here, own = whole.at[img_at, y_at, x_at, c_at, rows], shard.at[rows]
            found = [
                far_copy(own, here, self.z_send.at[p, step], self.z_recv.at[p, step], ((img_at + step) % 4, band_at))
                for step in range(1, 4)
            ]
            found.append(pltpu.make_async_copy(own, here, self.near.at[p]))
            loads = [("zf", 8 * size), ("zb", 8 * size)]
        elif k == 3:
            part = whole.at[:, :, :, c_at, rows]
            found = [far_copy(part, part, self.p_send.at[p, 4], self.p_recv.at[p, 4], over_c)]
            loads = [("c", 16 * size)]
        else:
            for half in range(2):
                span = pl.ds(lanes, width - lanes) if half else pl.ds(0, lanes)
                if lanes == 0 and half == 0:
                    continue
                if k == 1:
                    part = whole.at[:, y_at, x_at, c_at, rows, span]
                elif half == 0:
                    part = whole.at[:, :, x_at, c_at, rows, span]
                else:
                    part = whole.at[:, y_at, :, c_at, rows, span]
                slot = 2 * (k - 1) + half
                along_y = (k == 1) == (half == 0)
                target = over_y if along_y else over_x
                found.append(far_copy(part, part, self.p_send.at[p, slot], self.p_recv.at[p, slot], target))
                loads.append(("y" if along_y else "x", 4 * k * size))

        def then():
            if k < 3:
                self.launch(p, k + 1)
            else:
                self.done.add(p)

        self.agenda.launch((self.name, p), found, loads, then)

    def begin(self, first, last):
        for p in range(first, last):
            self.launch(p, 0)

    def until(self, *wanted):
        self.agenda.until(lambda: all(p in self.done for p in wanted))


def gather_sems(count):
    dma = pltpu.SemaphoreType.DMA
    return [dma((count,)), dma((count, 4)), dma((count, 4)), dma((count, 5)), dma((count, 5))]


class Reduce:
    def __init__(
        self, agenda, slots, wait_z, full, pair, first_a, first_b, second_a, second_b, ours, last,
        near, p_send, p_recv, z_send, z_recv, free, free_z,
    ):
        self.agenda, self.slots, self.wait_z = agenda, slots, wait_z
        self.full, self.pair, self.ours, self.last = full, pair, ours, last
        self.first, self.second = (first_a, first_b), (second_a, second_b)
        self.near, self.p_send, self.p_recv, self.z_send, self.z_recv = near, p_send, p_recv, z_send, z_recv
        self.free, self.free_z = free, free_z
        self.pieces, self.flying, self.events, self.at_event = [], {}, [], 0
        self.queue, self.opened = [], 0

    def plan(self, pieces):
        self.pieces = pieces
        seen = [0] * 4
        for p, piece in enumerate(pieces):
            piece["slot"] = p % self.slots
            piece["place"] = p % (self.wait_z + 1)
            piece["order"] = seen[piece["z"]]
            seen[piece["z"]] += 1
        for piece in pieces:
            piece["again"] = piece["order"] + 2 < seen[piece["z"]]
        self.opened, self.passed, self.ended = 0, set(), set()
        self.ready = {""}

    def feed(self):
        while self.opened < len(self.pieces):
            p = self.opened
            if self.pieces[p]["needs"] not in self.ready or (p >= self.slots and p - self.slots not in self.passed):
                return
            self.opened += 1
            self.open(p)

    def allow(self, name):
        self.ready.add(name)
        self.feed()

    def rows(self, p):
        return pl.ds(0, self.pieces[p]["rows"])

    def open(self, p):
        piece = self.pieces[p]
        slot, rows = piece["slot"], self.rows(p)
        c_at = place()[4]
        over_c = neighbours()[0]
        if p >= self.slots:
            for k in range(3):
                pl.semaphore_wait(self.free.at[slot, k], 1)
        landing = self.pair.at[slot, :, :, rows]
        send, recv = self.p_send.at[slot, 0], self.p_recv.at[slot, 0]
        if "stage" in piece:
            stage, first, count = piece["stage"], piece["first"], piece["rows"]
            copies = []
            for n in range(4):
                theirs = pl.ds(pl.multiple_of(first + (2 * n + 1 - c_at) * count, 8), count)
                ours = pl.ds(pl.multiple_of(first + (2 * n + c_at) * count, 8), count)
                spot = 0 if n == 0 else 4 + n
                copies.append(
                    far_copy(
                        stage.at[theirs], self.pair.at[slot, n // 2, n % 2, rows], self.p_send.at[slot, spot],
                        self.p_recv.at[slot, spot], over_c,
                    )
                )
                copies.append(
                    pltpu.make_async_copy(
                        stage.at[ours], self.full.at[slot, n // 2, n % 2, c_at, rows], self.near.at[slot, n]
                    )
                )
        else:
            piece["emit"](self.full, slot)
            copies = [far_copy(self.full.at[slot, :, :, 1 - c_at, rows], landing, send, recv, over_c)]
        size = piece["rows"] * self.full.shape[5] * 4
        self.agenda.launch(("r", p, 0), copies, [("c", 4 * size)], lambda: self.step(0, p))

    def step(self, k, p):
        piece = self.pieces[p]
        slot, rows, z = piece["slot"], self.rows(p), piece["z"]
        size = piece["rows"] * self.full.shape[5] * 4
        img_at, band_at, y_at, x_at, c_at = place()
        over_c, over_x, over_y = neighbours()
        full, half = self.full, self.full.shape[5] // 2
        low, high = pl.ds(0, half), pl.ds(half, half)
        tiles = piece["rows"] // 16

        def tile(n):
            return pl.ds(pl.multiple_of(n % tiles * 16, 16), 16)

        if k == 0:
            def add(n, carry):
                y, x = n // (2 * tiles), n // tiles % 2
                full[slot, y, x, c_at, tile(n)] += self.pair[slot, y, x, tile(n)]
                return carry
            lax.fori_loop(0, 4 * tiles, add, 0)
            parts = (full.at[slot, :, 1 - x_at, c_at, rows, low], full.at[slot, 1 - y_at, :, c_at, rows, high])
            landings = [self.first[n].at[slot, :, rows] for n in range(2)]
            targets = (over_x, over_y)
        elif k == 1:
            def add(n, carry):
                w = n // tiles
                full[slot, w, x_at, c_at, tile(n), low] += self.first[0][slot, w, tile(n)]
                full[slot, y_at, w, c_at, tile(n), high] += self.first[1][slot, w, tile(n)]
                return carry
            lax.fori_loop(0, 2 * tiles, add, 0)
            parts = (full.at[slot, 1 - y_at, x_at, c_at, rows, low], full.at[slot, y_at, 1 - x_at, c_at, rows, high])
            landings = [self.second[n].at[slot, rows] for n in range(2)]
            targets = (over_y, over_x)
        if k < 2:
            copies = [
                far_copy(
                    parts[n], landings[n], self.p_send.at[slot, 1 + 2 * k + n], self.p_recv.at[slot, 1 + 2 * k + n],
                    targets[n],
                )
                for n in range(2)
            ]
            load = 2 * size if k == 0 else size
            self.agenda.launch(("r", p, 1 + k), copies, [("x", load), ("y", load)], lambda: self.step(k + 1, p))
            return
        spot, order = piece["place"], piece["order"] % 2
        mine = self.ours.at[spot, rows]
        owner = (z, band_at)

        def hop(n):
            return far_copy(mine, self.last.at[order, n, rows], self.z_send.at[spot], self.z_recv.at[order, n], owner)

        if k == 2:
            self.agenda.until(lambda: p < self.wait_z + 1 or p - self.wait_z - 1 in self.ended)

            def add(n, carry):
                self.ours[spot, tile(n), low] = full[slot, y_at, x_at, c_at, tile(n), low] + self.second[0][slot, tile(n)]
                self.ours[spot, tile(n), high] = full[slot, y_at, x_at, c_at, tile(n), high] + self.second[1][slot, tile(n)]
                return carry
            lax.fori_loop(0, tiles, add, 0)

            assert p < self.wait_z + 1 or p - self.wait_z - 1 in self.ended

            @pl.when(img_at != z)
            def _():
                if piece["order"] >= 2:
                    pl.semaphore_wait(self.free_z.at[z, order], 1)
                hop((img_at + 3 - z) % 4).start()

            if p + self.slots < len(self.pieces):
                for n, other in enumerate((over_c, over_x, over_y)):
                    pl.semaphore_signal(self.free.at[slot, n], inc=1, device_id=other, device_id_type=MESH)
            self.passed.add(p)
            loads = {0: (0, 3), 1: (1, 2), 2: (2, 1), 3: (3, 0)}[z]
            self.agenda.launch(
                ("r", p, 3), [], [(link, 2 * n * size) for link, n in zip(("zf", "zb"), loads) if n], lambda: self.step(3, p)
            )
            self.feed()
            return

        @pl.when(img_at != z)
        def _():
            hop((img_at + 3 - z) % 4).wait_send()

        @pl.when(img_at == z)
        def _():
            for n in range(3):
                hop(n).wait_recv()

            def add(n, carry):
                piece["out"][tile(n)] = (self.ours[spot, tile(n)] + self.last[order, 0, tile(n)]) + (
                    self.last[order, 1, tile(n)] + self.last[order, 2, tile(n)]
                )
                return carry
            lax.fori_loop(0, tiles, add, 0)
            if piece["again"]:
                for n in range(1, 4):
                    pl.semaphore_signal(
                        self.free_z.at[z, order], inc=1, device_id=((img_at + n) % 4, band_at), device_id_type=MESH
                    )

        self.ended.add(p)


def reduce_scratch(slots, wait_z, rows, width):
    f32 = jnp.float32
    dma = pltpu.SemaphoreType.DMA
    half = width // 2
    return [
        pltpu.VMEM((slots, 2, 2, 2, rows, width), f32),
        pltpu.VMEM((slots, 2, 2, rows, width), f32),
        pltpu.VMEM((slots, 2, rows, half), f32),
        pltpu.VMEM((slots, 2, rows, half), f32),
        pltpu.VMEM((slots, rows, half), f32),
        pltpu.VMEM((slots, rows, half), f32),
        pltpu.VMEM((wait_z + 1, rows, width), f32),
        pltpu.VMEM((2, 3, rows, width), f32),
        dma((slots, 4)),
        dma((slots, 8)), dma((slots, 8)),
        dma((wait_z + 1,)), dma((2, 3)),
        pltpu.SemaphoreType.REGULAR((slots, 3)),
        pltpu.SemaphoreType.REGULAR((4, 2)),
    ]


class ReduceSmall:
    def __init__(self, agenda, grads, shares, own, pair, first_a, first_b, second_a, second_b, last, near, p_send, p_recv, z_send, z_recv):
        self.agenda, self.done = agenda, set()
        self.grads, self.shares, self.own, self.pair = grads, shares, own, pair
        self.first, self.second, self.last = (first_a, first_b), (second_a, second_b), last
        self.near, self.p_send, self.p_recv, self.z_send, self.z_recv = near, p_send, p_recv, z_send, z_recv
        self.flying = {}

    def start(self, p, copies, loads, k):
        size = self.own[p].shape[3] * self.own[p].shape[4] * 4
        self.agenda.launch(("s", p), copies, [(link, n * size) for link, n in loads], lambda: self.step(p, k))

    def open(self, p):
        c_at = place()[4]
        over_c = neighbours()[0]
        self.start(p, [
            far_copy(self.grads[p].at[:, :, :, 1 - c_at], self.pair[p], self.p_send.at[p, 0], self.p_recv.at[p, 0], over_c),
            pltpu.make_async_copy(self.grads[p].at[:, :, :, c_at], self.own[p], self.near.at[p]),
        ], [("c", 16)], 0)

    def step(self, p, k):
        img_at, band_at, y_at, x_at, c_at = place()
        over_c, over_x, over_y = neighbours()
        own = self.own[p]
        rows = own.shape[3]
        span = (pl.ds(0, rows // 2), pl.ds(rows // 2, rows // 2))

        def send(parts, landings, targets, slot):
            copies = [
                far_copy(parts[n], landings[n], self.p_send.at[p, slot + n], self.p_recv.at[p, slot + n], targets[n])
                for n in range(2)
            ]
            self.start(p, copies, [("x", 8 >> k), ("y", 8 >> k)], k + 1)

        if k == 0:
            own[...] += self.pair[p][...]
            send(
                (own.at[:, :, 1 - x_at, span[0]], own.at[:, 1 - y_at, :, span[1]]),
                (self.first[0][p], self.first[1][p]), (over_x, over_y), 1,
            )
        elif k == 1:
            own[:, :, x_at, span[0]] += self.first[0][p][...]
            own[:, y_at, :, span[1]] += self.first[1][p][...]
            send(
                (own.at[:, 1 - y_at, x_at, span[0]], own.at[:, y_at, 1 - x_at, span[1]]),
                (self.second[0][p], self.second[1][p]), (over_y, over_x), 3,
            )
        elif k == 2:
            own[:, y_at, x_at, span[0]] += self.second[0][p][...]
            own[:, y_at, x_at, span[1]] += self.second[1][p][...]
            copies = []
            for n in range(1, 4):
                target = (img_at + n) % 4
                copies.append(
                    far_copy(
                        own.at[target, y_at, x_at], self.last[p].at[n - 1], self.z_send.at[p, n], self.z_recv.at[p, n],
                        (target, band_at),
                    )
                )
            self.start(p, copies, [("zf", 8), ("zb", 8)], 3)
        else:
            last = self.last[p]
            self.done.add(p)
            self.shares[p][...] = (own[img_at, y_at, x_at] + last[0]) + (last[1] + last[2])


def reduce_small_scratch(shapes):
    f32 = jnp.float32
    dma = pltpu.SemaphoreType.DMA
    count = len(shapes)
    groups = [
        [(4, 2, 2, r, w) for r, w in shapes],
        [(4, 2, 2, r, w) for r, w in shapes],
        [(4, 2, r // 2, w) for r, w in shapes],
        [(4, 2, r // 2, w) for r, w in shapes],
        [(4, r // 2, w) for r, w in shapes],
        [(4, r // 2, w) for r, w in shapes],
        [(3, r, w) for r, w in shapes],
    ]
    return [pltpu.VMEM(shape, f32) for group in groups for shape in group] + [
        dma((count,)), dma((count, 5)), dma((count, 5)), dma((count, 4)), dma((count, 4)),
    ]


def dot_nn(a, b):
    return lax.dot_general(a, b, (((1,), (0,)), ((), ())), preferred_element_type=jnp.float32)


def dot_nt(a, b):
    return lax.dot_general(a, b, (((1,), (1,)), ((), ())), preferred_element_type=jnp.float32)


def dot_tn(a, b):
    return lax.dot_general(a, b, (((0,), (0,)), ((), ())), preferred_element_type=jnp.float32)


def norm_parts(h):
    centred = h - jnp.mean(h, axis=-1, keepdims=True)
    rate = lax.rsqrt(jnp.mean(centred * centred, axis=-1, keepdims=True) + norm_eps)
    return centred * rate, rate


def norm_back(grad, h, gain):
    shape, rate = norm_parts(h)
    inner = grad * gain
    back = rate * (
        inner
        - jnp.mean(inner, axis=-1, keepdims=True)
        - shape * jnp.mean(inner * shape, axis=-1, keepdims=True)
    )
    return (
        back,
        jnp.sum(grad * shape, axis=0, keepdims=True),
        jnp.sum(grad, axis=0, keepdims=True),
    )


STEP = 256


def at(k, start=0):
    return pl.ds(pl.multiple_of(start + k * STEP, STEP), STEP)


def lanes_at(k, size, start=0):
    return pl.ds(pl.multiple_of(start + k * size, 128), size)


def loop(first, last, body):
    def step(k, carry):
        body(k)
        return carry

    lax.fori_loop(first, last, step, 0)


class Block:
    def __init__(self, base, source, first_w, small, refs):
        names = (
            "wide", "narrow", "norms", "q_extra", "k_extra", "hidden", "normed", "q_buf", "kv", "mixed_in", "wide_in",
            "middle", "second", "slope", "grad_out", "grad_low", "mid_low", "gatt", "dkv", "dkv_in", "soft", "x_send",
            "x_recv", "x_free",
        )
        for name, ref in zip(names, refs, strict=True):
            setattr(self, name, ref)
        self.base, self.source, self.first_w, self.small = base, source, first_w, small
        self.part = place()[4]
        self.total, self.own = self.kv.shape[0], self.q_buf.shape[0]
        self.width = self.q_buf.shape[1]
        self.offset = pl.multiple_of(self.part * self.own, self.own)
        self.chunks = self.own // STEP
        lane_head = lax.broadcasted_iota(jnp.int32, (1, 128), 1) // HDIM
        self.pick = [jnp.where(lane_head == k, 1.0, 0.0).astype(jnp.bfloat16) for k in range(2)]

    def slope_rows(self, f, k):
        return pl.ds(pl.multiple_of(f * self.own + k * STEP, STEP), STEP)

    def gain(self, k):
        return self.norms[pl.ds(self.base + k, 1), :]

    def add_small(self, row, value):
        self.small[pl.ds(row, 1), :] += value

    def add_loss(self, value):
        first_lane = lax.broadcasted_iota(jnp.int32, (1, self.width), 1) == 0
        self.add_small(6, jnp.where(first_lane, value, 0.0))

    def enter(self, first, last):
        def body(n):
            k = (n + self.chunks * (1 + self.part)) % (self.total // STEP)
            h = dot_nt(self.source(k), self.first_w())
            self.hidden[at(n % self.chunks)] = h
            shape, _ = norm_parts(h)
            self.normed[at(k)] = (shape * self.gain(0) + self.gain(1)).astype(jnp.bfloat16)

        loop(first, last, body)

    def make_kv(self, first, last):
        def body(k):
            self.kv[at(k)] = dot_nt(self.normed[at(k)], self.wide[self.width : 3 * self.width]).astype(jnp.bfloat16)

        loop(first, last, body)

    def make_q(self):
        def body(k):
            q = dot_nt(self.normed[at(k, self.offset)], self.wide[: self.width]).astype(jnp.bfloat16)
            self.q_buf[at(k)] = (q.astype(jnp.float32) * HDIM**-0.5).astype(jnp.bfloat16)

        loop(0, self.chunks, body)

    def scores(self, p, k, rows, k_cat):
        q_cat = jnp.concatenate([self.q_buf[rows, lanes_at(p, 128)] * self.pick[k], self.q_extra[rows]], axis=1)
        return dot_nt(q_cat, k_cat)

    def key_columns(self, p):
        return jnp.concatenate([self.kv[:, lanes_at(p, 128)], self.k_extra[...]], axis=1)

    def attend(self, first, last):
        head_lane = lax.broadcasted_iota(jnp.int32, (STEP, 128), 1)

        def pair(p):
            k_cat = self.key_columns(p)
            v_pair = self.kv[:, lanes_at(p, 128, self.width)]

            def body(j):
                rows = at(j)
                mixed = None
                for k in range(2):
                    scores = self.scores(p, k, rows, k_cat)
                    peak = jnp.max(scores, axis=-1, keepdims=True)
                    expo = jnp.exp(scores - peak)
                    total = jnp.sum(expo, axis=-1, keepdims=True)
                    prob = expo * (1.0 / total)
                    level = peak + jnp.log(total)
                    self.soft[rows] = jnp.where(head_lane == 2 * p + k, level, self.soft[rows])
                    term = dot_nn(prob.astype(jnp.bfloat16), v_pair * self.pick[k])
                    mixed = term if mixed is None else mixed + term
                self.mixed_in[rows, lanes_at(p, 128)] = mixed.astype(jnp.bfloat16)

            loop(0, self.chunks, body)

        loop(first, last, pair)

    def after_attention(self):
        def body(k):
            rows = at(k)
            mid = self.hidden[at(k)] + dot_nn(self.mixed_in[rows, : self.width], self.narrow[: self.width])
            self.middle[rows] = mid
            shape, _ = norm_parts(mid)
            self.second[rows] = (shape * self.gain(2) + self.gain(3)).astype(jnp.bfloat16)
            self.grad_out[rows] = mid

        loop(0, self.chunks, body)

    def mlp(self, first, last):
        width = self.width

        def body(n):
            f, k = n // self.chunks, n % self.chunks
            rows = at(k)
            u = dot_nt(self.second[rows], self.wide[lanes_at(3 + f, width)])
            squared = u * u
            bend = jnp.tanh(0.7978845608028654 * (u + 0.044715 * squared * u))
            low = (0.5 * u * (1.0 + bend)).astype(jnp.bfloat16)
            self.mixed_in[rows, lanes_at(1 + f, width)] = low
            self.slope[self.slope_rows(f, k)] = 0.5 * (1.0 + bend) + (0.5 * u) * (1.0 - bend * bend) * (
                0.7978845608028654 * (1.0 + (3.0 * 0.044715) * squared)
            )
            self.grad_out[rows] += dot_nn(low, self.narrow[lanes_at(1 + f, width)])

        loop(first * self.chunks, last * self.chunks, body)

    def mlp_back(self, first, last):
        width = self.width

        def body(k):
            rows = at(k)
            gy = self.grad_low[rows]

            def feature_step(f, acc):
                ga = dot_nt(gy, self.narrow[lanes_at(1 + f, width)])
                low = (ga * self.slope[self.slope_rows(f, k)]).astype(jnp.bfloat16)
                self.wide_in[rows, lanes_at(3 + f, width)] = low
                return acc + dot_nn(low, self.wide[lanes_at(3 + f, width)])

            grad_second = lax.fori_loop(0, 4, feature_step, jnp.zeros((STEP, width), jnp.float32))
            back, g_gain, g_offset = norm_back(grad_second, self.middle[rows], self.gain(2))
            self.add_small(2, g_gain)
            self.add_small(3, g_offset)
            grad_mid = back + self.grad_out[rows]
            self.grad_out[rows] = grad_mid
            low = grad_mid.astype(jnp.bfloat16)
            self.mid_low[rows] = low
            self.gatt[rows] = dot_nt(low, self.narrow[:width]).astype(jnp.bfloat16)

        loop(first, last, body)

    def attend_back(self, first, last):
        head_lane = lax.broadcasted_iota(jnp.int32, (self.own, 128), 1)
        rows, bf16 = slice(None), jnp.bfloat16

        def pair(p):
            k_pair = self.kv[:, lanes_at(p, 128)]
            v_pair = self.kv[:, lanes_at(p, 128, self.width)]
            k_cat = self.key_columns(p)
            q_pair = self.q_buf[rows, lanes_at(p, 128)]
            g_pair = self.gatt[rows, lanes_at(p, 128)]
            dq, dk, dv = None, None, None
            for k in range(2):
                g_rows = g_pair * self.pick[k]
                level = jnp.sum(jnp.where(head_lane == 2 * p + k, self.soft[...], 0.0), axis=-1, keepdims=True)
                prob = jnp.exp(self.scores(p, k, rows, k_cat) - level)
                d_prob = dot_nt(g_rows, v_pair)
                dot_row = jnp.sum(prob * d_prob, axis=-1, keepdims=True)
                d_score = (prob * (d_prob - dot_row)).astype(bf16)
                terms = (
                    dot_nn(d_score, k_pair * self.pick[k]),
                    dot_tn(d_score, q_pair * self.pick[k]),
                    dot_tn(prob.astype(bf16), g_rows),
                )
                dq, dk, dv = terms if dq is None else (dq + terms[0], dk + terms[1], dv + terms[2])
            self.dkv[p - first, 0], self.dkv[p - first, 1] = dk, dv
            self.wide_in[rows, lanes_at(p, 128)] = (dq * HDIM**-0.5).astype(bf16)

        loop(first, last, pair)

    def swap(self, p):
        theirs = pl.ds(pl.multiple_of((1 - self.part) * self.own, self.own), self.own)
        return far_copy(
            self.dkv.at[p, :, theirs], self.dkv_in.at[p], self.x_send.at[p], self.x_recv.at[p], neighbours()[0]
        )

    def swap_start(self, opening):
        if not opening:
            pl.semaphore_wait(self.x_free, 1)
        for p in range(2):
            self.swap(p).start()

    def swap_finish(self, first, closing):
        for p in range(2):
            self.swap(p).wait()

        def body(n):
            p, k = n // self.chunks, n % self.chunks
            for side in range(2):
                total = self.dkv[p, side, at(k, self.offset)] + self.dkv_in[p, side, at(k)]
                self.wide_in[at(k), lanes_at(first + p, 128, (1 + side) * self.width)] = total.astype(jnp.bfloat16)

        loop(0, 2 * self.chunks, body)
        if not closing:
            pl.semaphore_signal(self.x_free, inc=1, device_id=neighbours()[0], device_id_type=MESH)

    def leave_rows(self, k):
        rows = at(k)
        grad_normed = dot_nn(self.wide_in[rows, : 3 * self.width], self.wide[: 3 * self.width])
        back, g_gain, g_offset = norm_back(grad_normed, self.hidden[at(k)], self.gain(0))
        self.add_small(0, g_gain)
        self.add_small(1, g_offset)
        return (back + self.grad_out[rows]).astype(jnp.bfloat16)

    def wide_product(self, first, count):
        if first < 3 * self.width:
            right = self.normed[pl.ds(self.offset, self.own)]
        else:
            right = self.second[...]
        return dot_tn(self.wide_in[:, first : first + count], right)

    def narrow_product(self, first, count):
        right = self.mid_low if first < self.width else self.grad_low
        return dot_tn(self.mixed_in[:, first : first + count], right[...])


def pieces_of(first, count, border):
    if first < border < first + count:
        return [(first, border - first), (border, first + count - border)]
    return [(first, count)]


def block_scratch(total_rows, own_rows):
    width = 512
    f32, bf16 = jnp.float32, jnp.bfloat16
    shapes = [
        ((own_rows, width), f32),
        ((total_rows, width), bf16),
        ((own_rows, width), bf16),
        ((total_rows, 2 * width), bf16),
        ((own_rows, 5 * width), bf16),
        ((own_rows, 7 * width), bf16),
        ((own_rows, width), f32),
        ((own_rows, width), bf16),
        ((4 * own_rows, width), f32),
        ((own_rows, width), f32),
        ((own_rows, width), bf16),
        ((own_rows, width), bf16),
        ((own_rows, width), bf16),
        ((2, 2, total_rows, 128), f32),
        ((2, 2, own_rows, 128), f32),
        ((own_rows, 128), f32),
    ]
    return [pltpu.VMEM(shape, dtype) for shape, dtype in shapes] + [
        pltpu.SemaphoreType.DMA((2,)), pltpu.SemaphoreType.DMA((2,)), pltpu.SemaphoreType.REGULAR
    ]


def step_kernel(slots, latent_total, *refs):
    shards, slab, code, kinds, norms = refs[:6], refs[6], refs[7], refs[8], refs[9]
    refs = refs[10:]
    share_wide_dec, share_narrow_dec, share_wide, share_narrow, share_edge, share_book, small_all = refs[:7]
    land_wide_dec, land_narrow_dec, land_wide, land_narrow = refs[7:11]
    refs = refs[11:]
    sems_dec, sems_enc, red, red_small, refs = refs[:5], refs[5:10], refs[10:25], refs[25:44], refs[44:]
    (book, edge, slab_all, code_all, tally, tally_all, t_img, t_band, e_near, e_send, e_recv, t_send, t_recv) = refs[:13]
    refs = refs[1:]
    (code_row, spread, cross, g_pixw, g_qout, g_qin, g_inw, g_edge, g_book) = refs[12:21]
    (small_dec, small_enc, small_own, s_img, s_band, s_send, s_recv, load_sem, wide, narrow) = refs[21:31]
    q_extra, k_extra = refs[31:33]
    scratch = refs[33:]
    f32, bf16 = jnp.float32, jnp.bfloat16
    img_at, band_at, y_at, x_at, c_at = place()
    chip_at = band_at // 2
    over_c = neighbours()[0]
    width = wide.shape[1]
    common = (wide, narrow, norms, q_extra, k_extra) + tuple(scratch)

    def edge_columns(first, count):
        return edge[:, :, :, :, :, first : first + count].reshape(width, count)

    def e_in():
        return edge_columns(0, 256)

    def e_pix():
        return edge_columns(256, 256)

    def e_qin():
        return edge_columns(512, 128)

    def e_qout():
        return edge_columns(640, 128)

    def pixel_rows(k, first=0, start=0):
        return slab_all[pl.ds(start + 2 * k, 2), :, first : first + 256].reshape(STEP, 256)

    own_band = 4 * c_at
    dec = Block(4, lambda k: spread[at(k)], e_qout, small_dec, common)
    enc = Block(0, pixel_rows, e_in, small_enc, common)
    agenda = Agenda()
    dec_pieces = [(shards[0], book, 0, 64), (shards[1], edge, 0, 16)]
    dec_pieces += [(shards[2], land_wide_dec, 0, 48), (shards[2], land_wide_dec, 48, 64), (shards[3], land_narrow_dec, 0, 80)]
    gather = Gather("d", agenda, dec_pieces, *sems_dec)
    enc_pieces = [(shards[4], land_wide, 0, 112), (shards[5], land_narrow, 0, 80)]
    gather_enc = Gather("e", agenda, enc_pieces, *sems_enc)
    count_all = Everywhere("n", agenda, tally, t_img, t_band, t_send, t_recv, tally_all)
    kind = kinds[pl.ds(chip_at, 1), :]
    meet(peers())
    agenda.spend(3.0)
    gather.begin(0, 3)
    exchange = []
    for step in range(1, 4):
        chip = (chip_at + step) % 4
        target = (img_at, 2 * chip + c_at)
        here = band_at
        exchange.append(far_copy(slab.at[chip], slab_all.at[here], e_send.at[0, step], e_recv.at[0, step], target))
        exchange.append(far_copy(code.at[chip], code_all.at[here], e_send.at[1, step], e_recv.at[1, step], target))
    exchange.append(pltpu.make_async_copy(slab.at[chip_at], slab_all.at[band_at], e_near.at[0]))
    exchange.append(pltpu.make_async_copy(code.at[chip_at], code_all.at[band_at], e_near.at[1]))

    def exchange_landed():
        late = []
        for k, dst in enumerate((slab_all, code_all)):
            for chip in range(4):
                part = dst.at[2 * chip + c_at]
                late.append(far_copy(part, part, e_send.at[k, 4 + chip], e_recv.at[k, 4 + chip], over_c))
        agenda.launch("x2", late, [("c", 4e5)], lambda: arrived.append(1))

    arrived = []
    agenda.launch("x1", exchange, [("x", 4e5), ("y", 4e5)], exchange_landed)
    gather.begin(3, 5)
    agenda.spend(1.0)
    segment_lane = lax.broadcasted_iota(jnp.int32, (enc.total, 128), 1)
    segment = jnp.where(kind == 0, 0, lax.broadcasted_iota(jnp.int32, (enc.total, 128), 0) // (enc.total // 4))
    k_extra[...] = jnp.where(segment_lane == segment, 1.0, 0.0).astype(bf16)
    segment_lane = lax.broadcasted_iota(jnp.int32, (enc.own, 128), 1)
    segment = lax.broadcasted_iota(jnp.int32, (enc.own, 128), 0) + enc.offset
    segment = jnp.where(kind == 0, 0, segment // (enc.total // 4))
    q_extra[...] = jnp.where((segment_lane < 4) & (segment_lane != segment), -(2.0**30), 0.0).astype(bf16)
    for ref in (small_dec, small_enc, g_pixw, g_qout, g_qin, g_inw):
        ref[...] = jnp.zeros(ref.shape, f32)
    agenda.spend(2.0)
    agenda.tick()
    agenda.until(lambda: arrived)
    def code_column(k, start=0):
        return jnp.concatenate(
            [jnp.transpose(jnp.broadcast_to(code_all[start + 2 * k + n], (8, 128)))[:, 0:1] for n in range(2)], axis=0
        )

    for n in range(4):
        code_row[:, pl.ds(128 * n, 128)] = code_all[own_band + n]

    def pick_codes(k):
        rows = at(k)
        code_here = code_column(k)
        picks = lax.broadcasted_iota(jnp.int32, (STEP, 512), 1)
        found = jnp.zeros((STEP, 128), f32)
        for z in range(4):
            hot = jnp.where(picks + 512 * z == code_here // 4, 1.0, 0.0).astype(bf16)
            found += dot_nn(hot, book[z].reshape(512, 128))
        lanes = lax.broadcasted_iota(jnp.int32, (STEP, 128), 1) // 32
        spread[rows] = jnp.where(lanes == code_here % 4, found, 0.0).astype(bf16)

    lane = lax.broadcasted_iota(jnp.int32, (4, 128, 256), 2)
    flags = slab_all[pl.ds(own_band, 4), :, 128:384].astype(f32)
    tally[...] = jnp.full(tally.shape, jnp.sum(jnp.where(lane < 64, 0.0, flags)))
    agenda.spend(1.0)
    agenda.tick()
    count_all.begin()
    gather.until(0)
    agenda.tick()
    for k in range(2):
        loop(2 * k, 2 * k + 2, pick_codes)
        agenda.spend(2.5)
        agenda.tick()
    gather.until(1)
    dec.enter(0, dec.total // STEP)
    agenda.spend(1.9)
    agenda.tick()

    def fetch(landed, ref, sem):
        rows = landed.shape[4]

        def body(n):
            src = landed.at[n // 8, (n // 4) % 2, (n // 2) % 2, n % 2]
            pltpu.make_async_copy(src, ref.at[pl.ds(pl.multiple_of(n * rows, 16), rows)], sem).start()

        loop(0, 32, body)
        return pltpu.make_async_copy(ref, ref, sem)

    reduce = Reduce(agenda, *slots, *red)
    tail = ReduceSmall(
        agenda, (g_edge, g_book), (share_edge, share_book),
        *[red_small[2 * n : 2 * n + 2] for n in range(7)], *red_small[14:],
    )

    def emit_wide(blk, z, full, slot):
        values = [blk.wide_product(*span) for span in pieces_of(896 * z, 896, 3 * width)]
        value = values[0] if len(values) == 1 else jnp.concatenate(values, axis=0)
        full[slot] = value.reshape(2, 2, 2, 112, width)
        agenda.spend(0.6)

    def emit_narrow(blk, z, full, slot):
        values = [blk.narrow_product(*span) for span in pieces_of(640 * z, 640, width)]
        value = values[0] if len(values) == 1 else jnp.concatenate(values, axis=0)
        full[slot, :, :, :, :80] = value.reshape(2, 2, 2, 80, width)
        agenda.spend(0.5)

    pieces = []
    for name, blk, out_wide, out_narrow in (
        ("dec", dec, share_wide_dec, share_narrow_dec), ("enc", enc, share_wide, share_narrow)
    ):
        for z in (3, 0, 2, 1):
            pieces.append(
                dict(emit=functools.partial(emit_narrow, blk, z), z=z, rows=80, out=out_narrow, needs=name + "1")
            )
        for z in (3, 2, 0, 1):
            piece = dict(z=z, rows=112, out=out_wide, needs=name + str(1 + (z < 2)))
            if name == "dec" and z < 2:
                piece.update(stage=dec.slope, first=896 * z)
            else:
                piece.update(emit=functools.partial(emit_wide, blk, z))
            pieces.append(piece)
    reduce.plan(pieces)

    def spend(time):
        agenda.spend(time)
        agenda.tick()

    def decoder_head(k):
        rows = at(k)
        out = dec.grad_out[rows]
        shape, _ = norm_parts(out)
        final = (shape * norms[pl.ds(8, 1), :] + norms[pl.ds(9, 1), :]).astype(bf16)
        error = dot_nn(final, e_pix()) - pixel_rows(k, 0, own_band).astype(f32)
        lane = lax.broadcasted_iota(jnp.int32, (STEP, 256), 1)
        counted = jnp.where(lane < 192, pltpu.roll(pixel_rows(k, 128, own_band).astype(f32), 192, 1), 0.0)
        number = tally_all[0:1, 0:1]
        dec.add_loss(jnp.sum(counted * (error * error + jnp.abs(error))) / number)
        sign = jnp.where(error > 0.0, 1.0, jnp.where(error < 0.0, -1.0, 0.0))
        grad_pred = (counted * (2.0 * error + sign) / number).astype(bf16)
        g_pixw[...] += dot_tn(final, grad_pred)
        back, g_gain, g_offset = norm_back(dot_nt(grad_pred, e_pix()), out, norms[pl.ds(8, 1), :])
        dec.add_small(4, g_gain)
        dec.add_small(5, g_offset)
        dec.grad_out[rows] = back
        dec.grad_low[rows] = back.astype(bf16)

    def encoder_head(k):
        rows = at(k)
        low = enc.grad_out[rows].astype(bf16)
        lanes = lax.broadcasted_iota(jnp.int32, (STEP, 128), 1) // 32
        mine = lanes == code_column(k, own_band) % 4
        gap = jnp.where(mine, spread[at(k, enc.offset)].astype(f32) - dot_nn(low, e_qin()), 0.0)
        enc.add_loss((1.0 + commitment) * jnp.sum(gap * gap) / latent_total)
        grad_latent = jnp.where(mine, cross[rows] - 2.0 * commitment * gap / latent_total, 0.0).astype(bf16)
        g_qin[...] += dot_tn(low, grad_latent)
        back = dot_nt(grad_latent, e_qin())
        enc.grad_out[rows] = back
        enc.grad_low[rows] = back.astype(bf16)
        gap = 2.0 * gap / latent_total
        high = gap.astype(bf16)
        left = gap - high.astype(f32)
        between = left.astype(bf16)
        enc.gatt[rows, :384] = jnp.concatenate([high, between, (left - between.astype(f32)).astype(bf16)], axis=1)

    def book_rows(k):
        picks = lax.broadcasted_iota(jnp.int32, (STEP, enc.own), 0) + k * STEP
        hot = jnp.where(picks == code_row[...] // 4, 1.0, 0.0).astype(bf16)
        summed = dot_nn(hot, enc.gatt[:, :384])
        value = (summed[:, :128] + summed[:, 128:256]) + summed[:, 256:]
        g_book[k // 2, k % 2] = value.reshape(2, 2, 64, 128)

    def decoder_leave(k):
        low = dec.leave_rows(k)
        cross[at(k)] = dot_nn(low, e_qout())
        g_qout[...] += dot_tn(low, spread[at(k, dec.offset)])

    def encoder_leave(k):
        g_inw[...] += dot_tn(enc.leave_rows(k), pixel_rows(k, 0, own_band))

    gather.until(2, 3)
    gather_enc.begin(0, 1)
    fetch(land_wide_dec, wide, load_sem.at[0]).wait()
    spend(2.0)
    dec.make_kv(0, dec.total // STEP)
    dec.make_q()
    spend(2.9)
    dec.attend(0, 2)
    spend(5.6)
    gather.until(4)
    gather_enc.begin(1, 2)
    fetched = fetch(land_narrow_dec, narrow, load_sem.at[1])
    dec.attend(2, 4)
    spend(5.6)
    fetched.wait()
    dec.after_attention()
    spend(1.1)
    dec.mlp(0, 4)
    spend(5.6)
    count_all.until()
    loop(0, dec.chunks, decoder_head)
    spend(2.0)
    dec.mlp_back(0, dec.chunks)
    agenda.spend(6.1)
    reduce.allow("dec1")
    agenda.tick()
    dec.attend_back(0, 2)
    dec.swap_start(True)
    spend(7.6)
    dec.swap_finish(0, False)
    dec.attend_back(2, 4)
    dec.swap_start(False)
    spend(7.6)
    gather_enc.until(0, 1)
    fetched = fetch(land_narrow, narrow, load_sem.at[1])
    dec.swap_finish(2, False)
    agenda.spend(2.0)
    for z in range(2):
        values = [dec.wide_product(*span) for span in pieces_of(896 * z, 896, 3 * width)]
        dec.slope[pl.ds(896 * z, 896)] = values[0] if len(values) == 1 else jnp.concatenate(values, axis=0)
    agenda.spend(1.2)
    reduce.allow("dec2")
    agenda.tick()
    loop(0, dec.chunks, decoder_leave)
    fetched_wide = fetch(land_wide, wide, load_sem.at[0])
    spend(2.0)
    agenda.until(lambda: reduce.opened >= 6)
    enc.enter(0, enc.total // STEP)
    spend(1.9)
    fetched_wide.wait()
    enc.make_kv(0, enc.total // STEP)
    enc.make_q()
    fetched.wait()
    spend(2.9)
    for p in range(2):
        enc.attend(2 * p, 2 * p + 2)
        spend(5.6)
    enc.after_attention()
    spend(1.1)
    agenda.until(lambda: reduce.opened >= 8 and not any(("r", p, 0) in agenda.flying for p in (6, 7)))
    enc.mlp(0, 4)
    spend(5.6)
    loop(0, enc.chunks, encoder_head)
    spend(2.0)
    loop(0, 8, book_rows)
    tail.open(1)
    spend(2.0)
    enc.mlp_back(0, enc.chunks)
    agenda.spend(6.1)
    reduce.allow("enc1")
    agenda.tick()
    enc.attend_back(0, 2)
    enc.swap_start(False)
    spend(7.6)
    enc.swap_finish(0, False)
    enc.attend_back(2, 4)
    enc.swap_start(False)
    spend(7.6)
    enc.swap_finish(2, True)
    agenda.spend(2.0)
    reduce.allow("enc2")
    agenda.tick()
    loop(0, enc.chunks, encoder_leave)
    agenda.spend(2.0)

    def all_groups(value):
        value = value + pltpu.roll(value, 64, 1)
        return value + pltpu.roll(value, 32, 1)

    lane = lax.broadcasted_iota(jnp.int32, (width, 128), 1)
    mixed = jnp.where(lane < 64, g_inw[:, 128:], jnp.where(lane < 96, all_groups(g_qin[...]), all_groups(g_qout[...])))
    for first, value in ((0, g_inw[:, :128]), (128, mixed), (256, g_pixw[:, :128]), (384, g_pixw[:, 128:])):
        g_edge[:, :, :, :, :, pl.ds(first, 128)] = value.reshape(4, 2, 2, 2, 16, 128)
    tail.open(0)
    agenda.until(lambda: len(reduce.ended) == len(pieces) and len(tail.done) == 2)
    shares = (share_wide_dec, share_narrow_dec, share_wide, share_narrow, share_edge, share_book)
    squares = sum(jnp.sum(share[...] * share[...]) for share in shares)
    lane = lax.broadcasted_iota(jnp.int32, (8, width), 1)
    row = lax.broadcasted_iota(jnp.int32, (8, width), 0)
    small_own[0] = small_enc[...]
    small_own[1] = jnp.where((row == 7) & (lane == 0), squares, small_dec[...])
    sum_all = Everywhere("a", agenda, small_own, s_img, s_band, s_send, s_recv, small_all)
    sum_all.begin()
    sum_all.until()


def train_step(shards, slab, code, kinds, norms, latent_total, total_rows, own_rows):
    width = 512
    slots = (4, 4)
    f32, bf16, int32 = jnp.float32, jnp.bfloat16, jnp.int32
    any_space = pl.BlockSpec(memory_space=pl.ANY)
    vmem = pl.BlockSpec(memory_space=pltpu.VMEM)
    shape = jax.ShapeDtypeStruct
    out_shape = [
        shape((112, width), f32), shape((80, width), f32), shape((112, width), f32), shape((80, width), f32),
        shape((16, width), f32), shape((64, 128), f32), shape((2, 8, width), f32),
    ]
    out_shape += [shape((4, 2, 2, 2) + s.shape, s.dtype) for s in shards[2:]]
    dma = pltpu.SemaphoreType.DMA
    mem = pltpu.VMEM
    scratch = gather_sems(5) + gather_sems(2)
    scratch += reduce_scratch(*slots, 112, width) + reduce_small_scratch([(16, width), (64, 128)])
    scratch += [
        mem((4, 2, 2, 2, 64, 128), bf16), mem((4, 2, 2, 2, 16, 768), bf16),
        mem((8, 128, 384), bf16), mem((8, 1, 128), int32), mem((8, 128), f32), mem((8, 128), f32),
        mem((4, 8, 128), f32), mem((8, 8, 128), f32),
        dma((2,)), dma((2, 8)), dma((2, 8)), dma((11,)), dma((11,)),
        mem((1, own_rows), int32), mem((total_rows, 128), bf16),
        mem((own_rows, 128), f32),
        mem((width, 256), f32), mem((width, 128), f32), mem((width, 128), f32), mem((width, 256), f32),
        mem((4, 2, 2, 2, 16, width), f32), mem((4, 2, 2, 2, 64, 128), f32),
        mem((8, width), f32), mem((8, width), f32), mem((2, 8, width), f32),
        mem((4, 2, 8, width), f32), mem((8, 2, 8, width), f32), dma((11,)), dma((11,)),
        dma((2,)), mem((7 * width, width), bf16), mem((5 * width, width), bf16),
        mem((own_rows, 128), bf16), mem((total_rows, 128), bf16),
    ]
    scratch += block_scratch(total_rows, own_rows)
    return pl.pallas_call(
        functools.partial(step_kernel, slots, latent_total),
        out_shape=out_shape,
        in_specs=[any_space] * 8 + [vmem] * 2,
        out_specs=[vmem] * 7 + [any_space] * 4,
        scratch_shapes=scratch,
        compiler_params=pltpu.CompilerParams(collective_id=0, has_side_effects=True, vmem_limit_bytes=(639 << 20) // 10),
        name="train_step",
    )(*shards, slab, code, kinds, norms)


def moments(gradient, first_old, second_old):
    first_new = beta_first * first_old + (1.0 - beta_first) * gradient
    second_new = beta_second * second_old + (1.0 - beta_second) * gradient * gradient
    return (first_new, second_new, first_new / (jnp.sqrt(second_new) + adam_eps))


def rotated_update(weight, gradient, first_old, second_old, basis_stack):
    turned = jnp.einsum("rld,lde->rle", gradient, basis_stack, precision=highest)
    first_new, second_new, direction = moments(turned, first_old, second_old)
    turned_back = jnp.einsum("rle,lde->rld", direction, basis_stack, precision=highest)
    return (weight - rate_matrix * (turned_back + weight_decay * weight), first_new, second_new)


def plain_update(weight, gradient, first_old, second_old):
    first_new, second_new, direction = moments(gradient, first_old, second_old)
    return (weight - rate_vector * (direction + weight_decay * weight), first_new, second_new)


def update_kernel(*refs):
    count = 20
    ins, refs = refs[:count], refs[count:]
    outs, held, sem = refs[:13], refs[13 : 13 + count], refs[13 + count]
    loads = [pltpu.make_async_copy(src, dst, sem.at[k]) for k, (src, dst) in enumerate(zip(ins, held))]
    for load in loads:
        load.start()
    for load in loads:
        load.wait()
    refs = held + outs
    wide_0, wide_1, narrow_0, narrow_1, edge, small = refs[:6]
    wide, narrow, edge_set, norm_set = refs[6:9], refs[9:12], refs[12:15], refs[15:18]
    bases, basis_edge = refs[18:20]
    new_wide, new_narrow, new_edge, new_norms, scalars = refs[20:23], refs[23:26], refs[26:29], refs[29:32], refs[32]
    norm_grad = jnp.concatenate([small[0, 0:4], small[1, 0:6]], axis=0)
    squares = small[1, 7:8, 0:1] + jnp.sum(norm_grad * norm_grad)
    grad_norm = jnp.sqrt(squares)
    factor = jnp.minimum(1.0, clip_level / grad_norm)
    scalars[0:1] = jnp.broadcast_to(grad_norm, (1, 128))
    scalars[1:2] = jnp.broadcast_to(factor, (1, 128))
    scalars[2:3] = jnp.broadcast_to(small[0, 6:7, 0:1] + small[1, 6:7, 0:1], (1, 128))
    scalars[3:8] = jnp.zeros((5, 128), jnp.float32)

    def turn(weight, gradient, first_old, second_old, basis):
        turned = jnp.dot(gradient, basis, precision=highest, preferred_element_type=jnp.float32)
        first_new, second_new, direction = moments(turned, first_old, second_old)
        back = lax.dot_general(
            direction, basis, (((1,), (1,)), ((), ())), precision=highest, preferred_element_type=jnp.float32
        )
        return weight - rate_matrix * (back + weight_decay * weight), first_new, second_new

    for k, (olds, news, grads) in enumerate(
        ((wide, new_wide, (wide_0, wide_1)), (narrow, new_narrow, (narrow_0, narrow_1)))
    ):
        for layer in range(2):
            found = turn(
                olds[0][:, layer], factor * grads[layer][...], olds[1][:, layer], olds[2][:, layer], bases[2 * k + layer]
            )
            for ref, value in zip(news, found):
                ref[:, layer] = value
    packed = edge[...]
    grad_edge = jnp.concatenate([packed[:, :192], packed[:, 256:448], packed[:, 192:256]], axis=1)
    found = turn(edge_set[0][...], factor * grad_edge, edge_set[1][...], edge_set[2][...], basis_edge[...])
    for ref, value in zip(new_edge, found):
        ref[...] = value
    found = plain_update(norm_set[0][...], factor * norm_grad, norm_set[1][...], norm_set[2][...])
    for ref, value in zip(new_norms, found):
        ref[...] = value


def update_all(grads, wide, narrow, edge, norms, bases, basis_edge):
    vmem = pl.BlockSpec(memory_space=pltpu.VMEM)
    shape = jax.ShapeDtypeStruct
    sets = wide + narrow + edge + norms
    return pl.pallas_call(
        update_kernel,
        out_shape=[shape(a.shape, a.dtype) for a in sets] + [shape((8, 128), jnp.float32)],
        in_specs=[pl.BlockSpec(memory_space=pl.ANY)] * (len(grads) + len(sets) + 2),
        out_specs=[vmem] * (len(sets) + 1),
        scratch_shapes=[pltpu.VMEM(a.shape, a.dtype) for a in (*grads, *sets, bases, basis_edge)]
        + [pltpu.SemaphoreType.DMA((len(grads) + len(sets) + 2,))],
        compiler_params=pltpu.CompilerParams(vmem_limit_bytes=63 << 20),
        name="update_all",
    )(*grads, *sets, bases, basis_edge)


def body(
    pixels,
    valid,
    codes,
    image_kind,
    w_wide,
    w_narrow,
    w_edge,
    codebook,
    norms,
    bases,
    basis_edge,
    m_wide,
    v_wide,
    m_narrow,
    v_narrow,
    m_edge,
    v_edge,
    m_code,
    v_code,
    m_norm,
    v_norm,
):
    band_count = lax.axis_size("band")
    band_index = lax.axis_index("band")
    row_count = pixels.shape[2]
    length = row_count * band_count
    batch_count = pixels.shape[0]
    group = band_count // batch_count
    row = band_index // group
    part = band_index % group
    own_rows = length // group
    groups = [[k * group + j for j in range(group)] for k in range(batch_count)]
    layer_count = w_wide.shape[1]
    code_width = codebook.shape[1]
    latent_total = batch_count * lax.axis_size("img") * length * code_width
    both = ("img", "band")

    direct = band_count == 8 and lax.axis_size("img") == 4 and batch_count == 4
    shards = [w_wide[:, l].astype(jnp.bfloat16) for l in range(layer_count)]
    shards += [w_narrow[:, l].astype(jnp.bfloat16) for l in range(layer_count)]
    shards += [w_edge.astype(jnp.bfloat16), codebook.astype(jnp.bfloat16).reshape(-1, 4 * code_width)]
    slab = jnp.concatenate([pixels[:, 0], valid[:, 0].astype(jnp.bfloat16)], axis=2)
    patch_size = pixels.shape[3]
    if direct:
        edge = shards[4]
        gap = jnp.zeros((edge.shape[0], 64), edge.dtype)
        qin = edge[:, 2 * patch_size : 2 * patch_size + code_width]
        qout = edge[:, 2 * patch_size + code_width :]
        shards[4] = jnp.concatenate(
            [edge[:, :patch_size], gap, edge[:, patch_size : 2 * patch_size], gap] + [qin] * 4 + [qout] * 4, axis=1
        )
        out = train_step(
            [shards[k] for k in (5, 4, 1, 3, 0, 2)], slab, codes, image_kind, norms, latent_total, length, own_rows
        )
        new = update_all(
            (out[2], out[0], out[3], out[1], out[4], out[6]), (w_wide, m_wide, v_wide), (w_narrow, m_narrow, v_narrow),
            (w_edge, m_edge, v_edge), (norms, m_norm, v_norm), bases, basis_edge,
        )
        scalars = new[12]
        grad_norm, factor, loss_total = scalars[0, 0], scalars[1, 0], scalars[2, 0]
        new_code = plain_update(codebook, factor * out[5].reshape(-1, code_width), m_code, v_code)
        return tuple(new[:9]) + new_code + tuple(new[9:12]) + (grad_norm, loss_total)
    wholes = [lax.all_gather(shard, both, axis=0, tiled=True) for shard in shards]
    count = lax.psum(jnp.sum(valid.astype(jnp.float32)), both)

    def whole_row(local):
        everywhere = lax.all_gather(local, "band", axis=0)
        chosen_row = lax.dynamic_index_in_dim(everywhere, row, axis=1, keepdims=False)
        return chosen_row.reshape((length,) + local.shape[2:])

    slab_all = whole_row(slab)
    code_all = whole_row(codes[:, 0])
    kind = lax.dynamic_index_in_dim(image_kind[:, 0], row, 0, keepdims=False)
    span = jnp.where(kind == 0, length, length // 4)
    positions = jnp.arange(length, dtype=jnp.int32)
    gathered = (wholes[:2], wholes[2:4], wholes[4], wholes[5])
    pixel_all = slab_all[:, :patch_size]
    valid_rows = lax.dynamic_slice_in_dim(slab_all, part * own_rows, own_rows, 0)[:, patch_size:]
    own_positions = part * own_rows + jnp.arange(own_rows, dtype=jnp.int32)
    allowed = (own_positions // span)[:, None] == (positions // span)[None, :]
    local_grads, norm_sum, loss_sum = row_step(
        gathered, norms, pixel_all, valid_rows, code_all, part, allowed, count, latent_total, groups
    )
    shares = [lax.psum_scatter(g, both, scatter_dimension=0, tiled=True) for g in local_grads]
    squares = sum(jnp.sum(share * share) for share in shares)
    norm_total, square_total, loss_total = lax.psum((norm_sum, squares, loss_sum), both)
    grad_sum = (
        jnp.stack([shares[0], shares[1]], axis=1),
        jnp.stack([shares[2], shares[3]], axis=1),
        shares[4],
        shares[5].reshape(-1, code_width),
    )
    grad_norm = jnp.sqrt(square_total + jnp.sum(norm_total * norm_total))
    factor = jnp.minimum(1.0, clip_level / grad_norm)
    grad_wide, grad_narrow, grad_edge, grad_book = grad_sum
    new_wide, new_m_wide, new_v_wide = rotated_update(
        w_wide, factor * grad_wide, m_wide, v_wide, bases[:layer_count]
    )
    new_narrow, new_m_narrow, new_v_narrow = rotated_update(
        w_narrow, factor * grad_narrow, m_narrow, v_narrow, bases[layer_count:]
    )
    new_edge, new_m_edge, new_v_edge = rotated_update(
        w_edge[:, None],
        factor * grad_edge[:, None],
        m_edge[:, None],
        v_edge[:, None],
        basis_edge[None],
    )
    new_book, new_m_code, new_v_code = plain_update(codebook, factor * grad_book, m_code, v_code)
    new_norms, new_m_norm, new_v_norm = plain_update(norms, factor * norm_total, m_norm, v_norm)
    return (
        new_wide,
        new_m_wide,
        new_v_wide,
        new_narrow,
        new_m_narrow,
        new_v_narrow,
        new_edge[:, 0],
        new_m_edge[:, 0],
        new_v_edge[:, 0],
        new_book,
        new_m_code,
        new_v_code,
        new_norms,
        new_m_norm,
        new_v_norm,
        grad_norm,
        loss_total,
    )


def solution(mesh):
    in_specs = (
        P(None, "img", "band", None),
        P(None, "img", "band", None),
        P(None, "img", "band"),
        P(None, "img"),
        P(("img", "band"), None, None),
        P(("img", "band"), None, None),
        P(("img", "band"), None),
        P(("img", "band"), None),
        P(),
        P(),
        P(),
        P(("img", "band"), None, None),
        P(("img", "band"), None, None),
        P(("img", "band"), None, None),
        P(("img", "band"), None, None),
        P(("img", "band"), None),
        P(("img", "band"), None),
        P(("img", "band"), None),
        P(("img", "band"), None),
        P(),
        P(),
    )
    out_specs = (
        P(("img", "band"), None, None),
        P(("img", "band"), None, None),
        P(("img", "band"), None, None),
        P(("img", "band"), None, None),
        P(("img", "band"), None, None),
        P(("img", "band"), None, None),
        P(("img", "band"), None),
        P(("img", "band"), None),
        P(("img", "band"), None),
        P(("img", "band"), None),
        P(("img", "band"), None),
        P(("img", "band"), None),
        P(),
        P(),
        P(),
        P(),
        P(),
    )
    return jax.shard_map(body, mesh=mesh, in_specs=in_specs, out_specs=out_specs, check_vma=False)
```

```python
import functools

import jax
import jax.numpy as jnp
from jax import lax
from jax.experimental import pallas as pl
from jax.experimental.pallas import tpu as pltpu
from jax.sharding import PartitionSpec as P

HEADS = 8
HDIM = 64
MESH = pl.DeviceIdType.MESH


norm_eps = 1e-05
adam_eps = 1e-08
clip_level = 0.001
beta_first = 0.5
beta_second = 0.6
rate_matrix = 0.02
rate_vector = 0.3
weight_decay = 0.01
commitment = 0.25
masked_score = -1000000000.0
highest = lax.Precision.HIGHEST


def matmul_plain(first_op, second_op):
    return jnp.dot(first_op, second_op, preferred_element_type=jnp.float32)


def matmul_trans(first_op, second_op):
    return lax.dot_general(
        first_op, second_op, (((1,), (1,)), ((), ())), preferred_element_type=jnp.float32
    )


def matmul_outer(first_op, second_op):
    return lax.dot_general(
        first_op, second_op, (((0,), (0,)), ((), ())), preferred_element_type=jnp.float32
    )


def layer_norm(hidden, scale_gain, offset):
    centred = hidden - jnp.mean(hidden, axis=-1, keepdims=True)
    spread = jnp.mean(centred * centred, axis=-1, keepdims=True)
    return centred * lax.rsqrt(spread + norm_eps) * scale_gain + offset


def gelu_tanh(inputs):
    return (
        0.5
        * inputs
        * (1.0 + jnp.tanh(0.7978845608028654 * (inputs + 0.044715 * inputs * inputs * inputs)))
    )


def split_heads(matrix):
    return matrix.reshape(matrix.shape[0], HEADS, HDIM)


def head_scores(q_heads, k_heads, allowed):
    scores = jnp.einsum(
        "qhd,khd->hqk", q_heads, k_heads, preferred_element_type=jnp.float32
    ) * HDIM ** (-0.5)
    return jnp.where(allowed[None], scores, masked_score)


def attend(queries, key_rows, value_rows, allowed):
    scores = head_scores(split_heads(queries), split_heads(key_rows), allowed)
    score_peak = jnp.max(scores, axis=-1, keepdims=True)
    expo = jnp.exp(scores - score_peak)
    total = jnp.sum(expo, axis=-1, keepdims=True)
    softmaxed = (expo / total).astype(jnp.bfloat16)
    attended = jnp.einsum(
        "hqk,khd->qhd", softmaxed, split_heads(value_rows), preferred_element_type=jnp.float32
    )
    return (
        attended.reshape(queries.shape[0], -1).astype(jnp.bfloat16),
        score_peak + jnp.log(total),
    )


def attend_back(queries, key_rows, value_rows, allowed, log_total, grad_out):
    q_heads = split_heads(queries)
    k_heads = split_heads(key_rows)
    v_heads = split_heads(value_rows)
    g_heads = split_heads(grad_out)
    softmaxed = jnp.exp(head_scores(q_heads, k_heads, allowed) - log_total)
    grad_soft = jnp.einsum("qhd,khd->hqk", g_heads, v_heads, preferred_element_type=jnp.float32)
    row_dot = jnp.sum(softmaxed * grad_soft, axis=-1, keepdims=True)
    grad_scores = (softmaxed * (grad_soft - row_dot)).astype(jnp.bfloat16)
    scale = HDIM ** (-0.5)
    grad_q = (
        jnp.einsum("hqk,khd->qhd", grad_scores, k_heads, preferred_element_type=jnp.float32) * scale
    )
    grad_k = (
        jnp.einsum("hqk,qhd->khd", grad_scores, q_heads, preferred_element_type=jnp.float32) * scale
    )
    grad_v = jnp.einsum(
        "hqk,qhd->khd", softmaxed.astype(jnp.bfloat16), g_heads, preferred_element_type=jnp.float32
    )
    return (
        grad_q.reshape(queries.shape[0], -1),
        grad_k.reshape(key_rows.shape[0], -1),
        grad_v.reshape(key_rows.shape[0], -1),
    )


def block_forward(hidden_all, part, wide_rows, narrow_rows, gain_rows, allowed):
    model_width = hidden_all.shape[1]
    own_rows = allowed.shape[0]
    normed_all = layer_norm(hidden_all, gain_rows[0], gain_rows[1]).astype(jnp.bfloat16)
    hidden = lax.dynamic_slice_in_dim(hidden_all, part * own_rows, own_rows, 0)
    normed = lax.dynamic_slice_in_dim(normed_all, part * own_rows, own_rows, 0)
    queries = matmul_trans(normed, wide_rows[:model_width]).astype(jnp.bfloat16)
    key_rows = matmul_trans(normed_all, wide_rows[model_width : 2 * model_width]).astype(jnp.bfloat16)
    value_rows = matmul_trans(normed_all, wide_rows[2 * model_width : 3 * model_width]).astype(jnp.bfloat16)
    attended, log_total = attend(queries, key_rows, value_rows, allowed)
    middle = hidden + matmul_plain(attended, narrow_rows[:model_width])
    second = layer_norm(middle, gain_rows[2], gain_rows[3]).astype(jnp.bfloat16)
    upper_in = matmul_trans(second, wide_rows[3 * model_width :])
    active = gelu_tanh(upper_in).astype(jnp.bfloat16)
    result = middle + matmul_plain(active, narrow_rows[model_width:])
    return (
        result,
        (hidden, normed, queries, key_rows, value_rows, attended, log_total, middle, second, upper_in, active),
    )


def block_backward(grad_out, wide_rows, narrow_rows, gain_rows, allowed, saved, groups):
    (hidden, normed, queries, key_rows, value_rows, attended, log_total, middle, second, upper_in, active) = saved
    model_width = hidden.shape[1]
    grad_y = grad_out.astype(jnp.bfloat16)
    grad_down = matmul_outer(active, grad_y)
    grad_active = matmul_trans(grad_y, narrow_rows[model_width:])
    grad_upper = jax.vjp(gelu_tanh, upper_in)[1](grad_active)[0].astype(jnp.bfloat16)
    grad_up = matmul_outer(grad_upper, second)
    _, second_back = jax.vjp(layer_norm, middle, gain_rows[2], gain_rows[3])
    grad_mid, gain_two, offset_two = second_back(
        matmul_plain(grad_upper, wide_rows[3 * model_width :])
    )
    grad_mid = grad_mid + grad_out
    grad_attn = grad_mid.astype(jnp.bfloat16)
    grad_outproj = matmul_outer(attended, grad_attn)
    grad_att = matmul_trans(grad_attn, narrow_rows[:model_width]).astype(jnp.bfloat16)
    grad_q, grad_keys, grad_values = attend_back(
        queries, key_rows, value_rows, allowed, log_total, grad_att
    )
    grad_k = lax.psum_scatter(grad_keys, "band", scatter_dimension=0, tiled=True, axis_index_groups=groups)
    grad_v = lax.psum_scatter(grad_values, "band", scatter_dimension=0, tiled=True, axis_index_groups=groups)
    grad_mixed = jnp.concatenate([grad_q, grad_k, grad_v], axis=1).astype(jnp.bfloat16)
    grad_qkv = matmul_outer(grad_mixed, normed)
    _, first_back = jax.vjp(layer_norm, hidden, gain_rows[0], gain_rows[1])
    grad_in, gain_one, offset_one = first_back(
        matmul_plain(grad_mixed, wide_rows[: 3 * model_width])
    )
    gain_grads = jnp.stack([gain_one, offset_one, gain_two, offset_two], axis=0)
    return (
        grad_in + grad_mid,
        jnp.concatenate([grad_qkv, grad_up], axis=0),
        jnp.concatenate([grad_outproj, grad_down], axis=0),
        gain_grads,
    )


def pick_codes(code_rows, book_wide, code_width):
    fold = book_wide.shape[1] // code_width
    one_hot = (
        (code_rows // fold)[:, None] == jnp.arange(book_wide.shape[0], dtype=jnp.int32)[None, :]
    ).astype(jnp.bfloat16)
    lane_fold = jnp.arange(book_wide.shape[1], dtype=jnp.int32)[None, :] // code_width
    lane_mask = (code_rows % fold)[:, None] == lane_fold
    spread = jnp.where(lane_mask, matmul_plain(one_hot, book_wide), 0.0)
    chosen = sum(spread[:, k * code_width : (k + 1) * code_width] for k in range(fold))
    return chosen, one_hot, lane_mask


def row_step(gathered, norms, pixel_all, valid_rows, code_all, part, allowed, count, latent_total, groups):
    wide_all, narrow_all, edge_all, book_wide = gathered
    patch_size = pixel_all.shape[1]
    code_width = edge_all.shape[1] // 2 - patch_size
    own_rows = allowed.shape[0]
    edge_in = edge_all[:, :patch_size]
    edge_pix = edge_all[:, patch_size : 2 * patch_size]
    edge_qin = edge_all[:, 2 * patch_size : 2 * patch_size + code_width]
    edge_qout = edge_all[:, 2 * patch_size + code_width :]
    pixel_rows = lax.dynamic_slice_in_dim(pixel_all, part * own_rows, own_rows, 0)
    chosen_all, one_hot_all, lane_mask_all = pick_codes(code_all, book_wide, code_width)
    chosen_low_all = chosen_all.astype(jnp.bfloat16)
    chosen = lax.dynamic_slice_in_dim(chosen_all, part * own_rows, own_rows, 0)
    one_hot = lax.dynamic_slice_in_dim(one_hot_all, part * own_rows, own_rows, 0)
    lane_mask = lax.dynamic_slice_in_dim(lane_mask_all, part * own_rows, own_rows, 0)
    chosen_low = chosen.astype(jnp.bfloat16)
    begin = matmul_trans(chosen_low_all, edge_qout)
    decoded, dec_saved = block_forward(begin, part, wide_all[1], narrow_all[1], norms[4:8], allowed)
    final = layer_norm(decoded, norms[8], norms[9]).astype(jnp.bfloat16)
    predict = matmul_plain(final, edge_pix)
    error = predict - pixel_rows.astype(jnp.float32)
    pixel_mask = valid_rows.astype(jnp.float32)
    loss_pix = jnp.sum(pixel_mask * (error * error + jnp.abs(error))) / count
    grad_pred = (pixel_mask * (2.0 * error + jnp.sign(error)) / count).astype(jnp.bfloat16)
    grad_pixw = matmul_outer(final, grad_pred)
    _, final_back = jax.vjp(layer_norm, decoded, norms[8], norms[9])
    grad_dec, gain_last, offset_last = final_back(matmul_trans(grad_pred, edge_pix))
    grad_begin, dec_wide, dec_narrow, dec_gains = block_backward(
        grad_dec, wide_all[1], narrow_all[1], norms[4:8], allowed, dec_saved, groups
    )
    grad_begin_low = grad_begin.astype(jnp.bfloat16)
    grad_qout = matmul_outer(grad_begin_low, chosen_low)
    start = matmul_trans(pixel_all, edge_in)
    encoded, enc_saved = block_forward(start, part, wide_all[0], narrow_all[0], norms[0:4], allowed)
    encoded_low = encoded.astype(jnp.bfloat16)
    latent = matmul_plain(encoded_low, edge_qin)
    gap = chosen - latent
    loss_part = loss_pix + (1.0 + commitment) * jnp.sum(gap * gap) / latent_total
    grad_latent = (
        matmul_plain(grad_begin_low, edge_qout) - 2.0 * commitment * gap / latent_total
    ).astype(jnp.bfloat16)
    fold = lane_mask.shape[1] // code_width
    gap_wide = jnp.where(lane_mask, jnp.tile(2.0 * gap / latent_total, (1, fold)), 0.0)
    gap_high = gap_wide.astype(jnp.bfloat16)
    gap_rest = gap_wide - gap_high.astype(jnp.float32)
    gap_middle = gap_rest.astype(jnp.bfloat16)
    gap_low = (gap_rest - gap_middle.astype(jnp.float32)).astype(jnp.bfloat16)
    grad_book = (
        matmul_outer(one_hot, gap_high) + matmul_outer(one_hot, gap_middle)
    ) + matmul_outer(one_hot, gap_low)
    grad_qin = matmul_outer(encoded_low, grad_latent)
    grad_start, enc_wide, enc_narrow, enc_gains = block_backward(
        matmul_trans(grad_latent, edge_qin), wide_all[0], narrow_all[0], norms[0:4], allowed, enc_saved, groups
    )
    grad_inw = matmul_outer(grad_start.astype(jnp.bfloat16), pixel_rows)
    grads = (
        enc_wide, dec_wide, enc_narrow, dec_narrow,
        jnp.concatenate([grad_inw, grad_pixw, grad_qin, grad_qout], axis=1),
        grad_book,
    )
    norm_grad = jnp.concatenate([enc_gains, dec_gains, gain_last[None], offset_last[None]], axis=0)
    return (grads, norm_grad, loss_part)


def place():
    img_at = lax.axis_index("img")
    band_at = lax.axis_index("band")
    return img_at, band_at, band_at // 4, (band_at // 2) % 2, band_at % 2


def neighbours():
    img_at, band_at, y_at, x_at, c_at = place()
    return (
        (img_at, band_at + 1 - 2 * c_at),
        (img_at, band_at + 2 - 4 * x_at),
        (img_at, band_at + 4 - 8 * y_at),
    )


def peers():
    img_at, band_at = place()[:2]
    found = [((img_at + step) % 4, band_at) for step in range(1, 4)]
    return found + [(img_at, (band_at + step) % 8) for step in range(1, 8)]


def meet(others):
    barrier = pltpu.get_barrier_semaphore()
    for other in others:
        pl.semaphore_signal(barrier, inc=1, device_id=other, device_id_type=MESH)
    pl.semaphore_wait(barrier, len(others))


def far_copy(src, dst, send, recv, target):
    return pltpu.make_async_remote_copy(
        src_ref=src, dst_ref=dst, send_sem=send, recv_sem=recv, device_id=target, device_id_type=MESH
    )


class Everywhere:
    def __init__(self, name, agenda, own_ref, img_buf, band_buf, send, recv, result_ref):
        self.name, self.agenda, self.done = name, agenda, False
        self.own, self.img_buf, self.band_buf, self.result = own_ref, img_buf, band_buf, result_ref
        self.send, self.recv = send, recv

    def begin(self):
        img_at, band_at = place()[:2]
        self.img_buf[img_at] = self.own[...]
        copies = [
            far_copy(
                self.own, self.img_buf.at[img_at], self.send.at[step], self.recv.at[step], ((img_at + step) % 4, band_at)
            )
            for step in range(1, 4)
        ]
        self.agenda.launch((self.name, 0), copies, [], self.middle)
        self.agenda.spend(0.5)

    def middle(self):
        img_at, band_at = place()[:2]
        buf = self.img_buf
        self.result[...] = (buf[0] + buf[1]) + (buf[2] + buf[3])
        self.band_buf[band_at] = self.result[...]
        copies = [
            far_copy(
                self.result, self.band_buf.at[band_at], self.send.at[3 + step], self.recv.at[3 + step],
                (img_at, (band_at + step) % 8),
            )
            for step in range(1, 8)
        ]
        self.agenda.launch((self.name, 1), copies, [], self.end)
        self.agenda.spend(1.0)

    def end(self):
        total = self.band_buf[0]
        for k in range(1, 8):
            total = total + self.band_buf[k]
        self.result[...] = total
        self.done = True

    def until(self):
        self.agenda.until(lambda: self.done)


LINK, CORE, LAG = 90e3, 500e3, 0.8
SPREAD = {"f01": 3, "f12": 4, "f23": 3, "b10": 3, "b21": 4, "b32": 3}
TOWARDS = (
    {"b10": 3, "b21": 2, "b32": 1},
    {"f01": 1, "b21": 2, "b32": 1},
    {"f01": 1, "f12": 2, "b32": 1},
    {"f01": 1, "f12": 2, "f23": 3},
)


def z_loads(table, size):
    return [(link, count * size) for link, count in table.items()]


class Agenda:
    def __init__(self):
        self.now, self.free, self.flying = 0.0, {}, {}

    def launch(self, key, copies, loads, then):
        done = self.now
        for link, size in loads:
            begin = max(self.now, self.free.get(link, 0.0))
            self.free[link] = begin + size / (CORE if link == "c" else LINK) + 0.4
            done = max(done, self.free[link])
        for copy in copies:
            copy.start()
        self.flying[key] = (done + LAG, copies, then)

    def land(self, key):
        done, copies, then = self.flying.pop(key)
        self.now = max(self.now, done) + 0.5
        for copy in copies:
            copy.wait()
        then()

    def spend(self, time):
        self.now += time

    def tick(self):
        while self.flying:
            key = min(self.flying, key=lambda name: self.flying[name][0])
            if self.flying[key][0] > self.now:
                return
            self.land(key)

    def until(self, test):
        while not test():
            self.land(min(self.flying, key=lambda name: self.flying[name][0]))


class Gather:
    def __init__(self, name, agenda, pieces, near, z_send, z_recv, p_send, p_recv):
        self.name, self.agenda, self.pieces = name, agenda, pieces
        self.near, self.z_send, self.z_recv, self.p_send, self.p_recv = near, z_send, z_recv, p_send, p_recv
        self.done = set()

    def launch(self, p, k):
        img_at, band_at, y_at, x_at, c_at = place()
        over_c, over_x, over_y = neighbours()
        shard, whole, first, count, z_last = self.pieces[p]
        rows = pl.ds(first, count)
        width = shard.shape[1]
        size = count * max(width, 128) * 2
        lanes = width // 256 * 128
        found, loads = [], []
        here, own = whole.at[img_at, y_at, x_at, c_at, rows], shard.at[rows]
        if z_last and k < 2:
            for half in range(2):
                span = pl.ds(lanes, width - lanes) if half else pl.ds(0, lanes)
                along_y = (k == 0) == (half == 0)
                if k == 0:
                    src, dst = shard.at[rows, span], whole.at[img_at, y_at, x_at, c_at, rows, span]
                elif half == 0:
                    src = dst = whole.at[img_at, :, x_at, c_at, rows, span]
                else:
                    src = dst = whole.at[img_at, y_at, :, c_at, rows, span]
                slot = 2 * k + half
                target = over_y if along_y else over_x
                found.append(far_copy(src, dst, self.p_send.at[p, slot], self.p_recv.at[p, slot], target))
                loads.append(("y" if along_y else "x", (1 + k) * size))
            if k == 0:
                found.append(pltpu.make_async_copy(own, here, self.near.at[p]))
        elif z_last and k == 2:
            part = whole.at[img_at, :, :, c_at, rows]
            found = [
                far_copy(part, part, self.z_send.at[p, step], self.z_recv.at[p, step], ((img_at + step) % 4, band_at))
                for step in range(1, 4)
            ]
            loads = z_loads(SPREAD, 8 * size)
        elif k == 0:
            found = [
                far_copy(own, here, self.z_send.at[p, step], self.z_recv.at[p, step], ((img_at + step) % 4, band_at))
                for step in range(1, 4)
            ]
            found.append(pltpu.make_async_copy(own, here, self.near.at[p]))
            loads = z_loads(SPREAD, 2 * size)
        elif k == 3:
            part = whole.at[:, :, :, c_at, rows]
            found = [far_copy(part, part, self.p_send.at[p, 4], self.p_recv.at[p, 4], over_c)]
            loads = [("c", 16 * size)]
        else:
            for half in range(2):
                span = pl.ds(lanes, width - lanes) if half else pl.ds(0, lanes)
                if lanes == 0 and half == 0:
                    continue
                if k == 1:
                    part = whole.at[:, y_at, x_at, c_at, rows, span]
                elif half == 0:
                    part = whole.at[:, :, x_at, c_at, rows, span]
                else:
                    part = whole.at[:, y_at, :, c_at, rows, span]
                slot = 2 * (k - 1) + half
                along_y = (k == 1) == (half == 0)
                target = over_y if along_y else over_x
                found.append(far_copy(part, part, self.p_send.at[p, slot], self.p_recv.at[p, slot], target))
                loads.append(("y" if along_y else "x", 4 * k * size))

        def then():
            if k < 3:
                self.launch(p, k + 1)
            else:
                self.done.add(p)

        self.agenda.launch((self.name, p), found, loads, then)

    def begin(self, first, last):
        for p in range(first, last):
            self.launch(p, 0)

    def until(self, *wanted):
        self.agenda.until(lambda: all(p in self.done for p in wanted))


def gather_sems(count):
    dma = pltpu.SemaphoreType.DMA
    return [dma((count,)), dma((count, 4)), dma((count, 4)), dma((count, 5)), dma((count, 5))]


class Reduce:
    def __init__(
        self, agenda, slots, wait_z, full, pair, first_a, first_b, second_a, second_b, ours, last,
        near, p_send, p_recv, z_send, z_recv, free, free_z,
    ):
        self.agenda, self.slots, self.wait_z = agenda, slots, wait_z
        self.full, self.pair, self.ours, self.last = full, pair, ours, last
        self.first, self.second = (first_a, first_b), (second_a, second_b)
        self.near, self.p_send, self.p_recv, self.z_send, self.z_recv = near, p_send, p_recv, z_send, z_recv
        self.free, self.free_z = free, free_z
        self.pieces, self.flying, self.events, self.at_event = [], {}, [], 0
        self.queue, self.opened = [], 0

    def plan(self, pieces):
        self.pieces = pieces
        seen = [0] * 4
        for p, piece in enumerate(pieces):
            piece["slot"] = p % self.slots
            piece["place"] = p % (self.wait_z + 1)
            piece["order"] = seen[piece["z"]]
            seen[piece["z"]] += 1
        for piece in pieces:
            piece["again"] = piece["order"] + 2 < seen[piece["z"]]
        self.opened, self.passed, self.ended = 0, set(), set()
        self.ready = {""}

    def feed(self):
        while self.opened < len(self.pieces):
            p = self.opened
            if self.pieces[p]["needs"] not in self.ready or (p >= self.slots and p - self.slots not in self.passed):
                return
            self.opened += 1
            self.open(p)

    def allow(self, name):
        self.ready.add(name)
        self.feed()

    def rows(self, p):
        return pl.ds(0, self.pieces[p]["rows"])

    def open(self, p):
        piece = self.pieces[p]
        slot, rows = piece["slot"], self.rows(p)
        c_at = place()[4]
        over_c = neighbours()[0]
        if p >= self.slots:
            for k in range(3):
                pl.semaphore_wait(self.free.at[slot, k], 1)
        landing = self.pair.at[slot, :, :, rows]
        send, recv = self.p_send.at[slot, 0], self.p_recv.at[slot, 0]
        if "stage" in piece:
            stage, first, count = piece["stage"], piece["first"], piece["rows"]
            copies = []
            for n in range(4):
                theirs = pl.ds(pl.multiple_of(first + (2 * n + 1 - c_at) * count, 8), count)
                ours = pl.ds(pl.multiple_of(first + (2 * n + c_at) * count, 8), count)
                spot = 0 if n == 0 else 4 + n
                copies.append(
                    far_copy(
                        stage.at[theirs], self.pair.at[slot, n // 2, n % 2, rows], self.p_send.at[slot, spot],
                        self.p_recv.at[slot, spot], over_c,
                    )
                )
                copies.append(
                    pltpu.make_async_copy(
                        stage.at[ours], self.full.at[slot, n // 2, n % 2, c_at, rows], self.near.at[slot, n]
                    )
                )
        else:
            piece["emit"](self.full, slot)
            copies = [far_copy(self.full.at[slot, :, :, 1 - c_at, rows], landing, send, recv, over_c)]
        size = piece["rows"] * self.full.shape[5] * 4
        self.agenda.launch(("r", p, 0), copies, [("c", 4 * size)], lambda: self.step(0, p))

    def step(self, k, p):
        piece = self.pieces[p]
        slot, rows, z = piece["slot"], self.rows(p), piece["z"]
        size = piece["rows"] * self.full.shape[5] * 4
        img_at, band_at, y_at, x_at, c_at = place()
        over_c, over_x, over_y = neighbours()
        full, half = self.full, self.full.shape[5] // 2
        low, high = pl.ds(0, half), pl.ds(half, half)
        tiles = piece["rows"] // 16

        def tile(n):
            return pl.ds(pl.multiple_of(n % tiles * 16, 16), 16)

        if k == 0:
            def add(n, carry):
                y, x = n // (2 * tiles), n // tiles % 2
                full[slot, y, x, c_at, tile(n)] += self.pair[slot, y, x, tile(n)]
                return carry
            lax.fori_loop(0, 4 * tiles, add, 0)
            parts = (full.at[slot, :, 1 - x_at, c_at, rows, low], full.at[slot, 1 - y_at, :, c_at, rows, high])
            landings = [self.first[n].at[slot, :, rows] for n in range(2)]
            targets = (over_x, over_y)
        elif k == 1:
            def add(n, carry):
                w = n // tiles
                full[slot, w, x_at, c_at, tile(n), low] += self.first[0][slot, w, tile(n)]
                full[slot, y_at, w, c_at, tile(n), high] += self.first[1][slot, w, tile(n)]
                return carry
            lax.fori_loop(0, 2 * tiles, add, 0)
            parts = (full.at[slot, 1 - y_at, x_at, c_at, rows, low], full.at[slot, y_at, 1 - x_at, c_at, rows, high])
            landings = [self.second[n].at[slot, rows] for n in range(2)]
            targets = (over_y, over_x)
        if k < 2:
            copies = [
                far_copy(
                    parts[n], landings[n], self.p_send.at[slot, 1 + 2 * k + n], self.p_recv.at[slot, 1 + 2 * k + n],
                    targets[n],
                )
                for n in range(2)
            ]
            load = 2 * size if k == 0 else size
            self.agenda.launch(("r", p, 1 + k), copies, [("x", load), ("y", load)], lambda: self.step(k + 1, p))
            return
        spot, order = piece["place"], piece["order"] % 2
        mine = self.ours.at[spot, rows]
        owner = (z, band_at)

        def hop(n):
            return far_copy(mine, self.last.at[order, n, rows], self.z_send.at[spot], self.z_recv.at[order, n], owner)

        if k == 2:
            self.agenda.until(lambda: p < self.wait_z + 1 or p - self.wait_z - 1 in self.ended)

            def add(n, carry):
                self.ours[spot, tile(n), low] = full[slot, y_at, x_at, c_at, tile(n), low] + self.second[0][slot, tile(n)]
                self.ours[spot, tile(n), high] = full[slot, y_at, x_at, c_at, tile(n), high] + self.second[1][slot, tile(n)]
                return carry
            lax.fori_loop(0, tiles, add, 0)

            assert p < self.wait_z + 1 or p - self.wait_z - 1 in self.ended

            @pl.when(img_at != z)
            def _():
                if piece["order"] >= 2:
                    pl.semaphore_wait(self.free_z.at[z, order], 1)
                hop((img_at + 3 - z) % 4).start()

            if p + self.slots < len(self.pieces):
                for n, other in enumerate((over_c, over_x, over_y)):
                    pl.semaphore_signal(self.free.at[slot, n], inc=1, device_id=other, device_id_type=MESH)
            self.passed.add(p)
            self.agenda.launch(("r", p, 3), [], z_loads(TOWARDS[z], 2 * size), lambda: self.step(3, p))
            self.feed()
            return

        @pl.when(img_at != z)
        def _():
            hop((img_at + 3 - z) % 4).wait_send()

        @pl.when(img_at == z)
        def _():
            for n in range(3):
                hop(n).wait_recv()

            def add(n, carry):
                piece["out"][tile(n)] = (self.ours[spot, tile(n)] + self.last[order, 0, tile(n)]) + (
                    self.last[order, 1, tile(n)] + self.last[order, 2, tile(n)]
                )
                return carry
            lax.fori_loop(0, tiles, add, 0)
            if piece["again"]:
                for n in range(1, 4):
                    pl.semaphore_signal(
                        self.free_z.at[z, order], inc=1, device_id=((img_at + n) % 4, band_at), device_id_type=MESH
                    )

        self.ended.add(p)


def reduce_scratch(slots, wait_z, rows, width):
    f32 = jnp.float32
    dma = pltpu.SemaphoreType.DMA
    half = width // 2
    return [
        pltpu.VMEM((slots, 2, 2, 2, rows, width), f32),
        pltpu.VMEM((slots, 2, 2, rows, width), f32),
        pltpu.VMEM((slots, 2, rows, half), f32),
        pltpu.VMEM((slots, 2, rows, half), f32),
        pltpu.VMEM((slots, rows, half), f32),
        pltpu.VMEM((slots, rows, half), f32),
        pltpu.VMEM((wait_z + 1, rows, width), f32),
        pltpu.VMEM((2, 3, rows, width), f32),
        dma((slots, 4)),
        dma((slots, 8)), dma((slots, 8)),
        dma((wait_z + 1,)), dma((2, 3)),
        pltpu.SemaphoreType.REGULAR((slots, 3)),
        pltpu.SemaphoreType.REGULAR((4, 2)),
    ]


class ReduceSmall:
    def __init__(self, agenda, grads, shares, own, pair, first_a, first_b, second_a, second_b, last, near, p_send, p_recv, z_send, z_recv):
        self.agenda, self.done = agenda, set()
        self.grads, self.shares, self.own, self.pair = grads, shares, own, pair
        self.first, self.second, self.last = (first_a, first_b), (second_a, second_b), last
        self.near, self.p_send, self.p_recv, self.z_send, self.z_recv = near, p_send, p_recv, z_send, z_recv
        self.flying = {}

    def start(self, p, copies, loads, k):
        size = self.own[p].shape[3] * self.own[p].shape[4] * 4
        self.agenda.launch(("s", p), copies, [(link, n * size) for link, n in loads], lambda: self.step(p, k))

    def open(self, p):
        c_at = place()[4]
        over_c = neighbours()[0]
        self.start(p, [
            far_copy(self.grads[p].at[:, :, :, 1 - c_at], self.pair[p], self.p_send.at[p, 0], self.p_recv.at[p, 0], over_c),
            pltpu.make_async_copy(self.grads[p].at[:, :, :, c_at], self.own[p], self.near.at[p]),
        ], [("c", 16)], 0)

    def step(self, p, k):
        img_at, band_at, y_at, x_at, c_at = place()
        over_c, over_x, over_y = neighbours()
        own = self.own[p]
        rows = own.shape[3]
        span = (pl.ds(0, rows // 2), pl.ds(rows // 2, rows // 2))

        def send(parts, landings, targets, slot):
            copies = [
                far_copy(parts[n], landings[n], self.p_send.at[p, slot + n], self.p_recv.at[p, slot + n], targets[n])
                for n in range(2)
            ]
            self.start(p, copies, [("x", 8 >> k), ("y", 8 >> k)], k + 1)

        if k == 0:
            own[...] += self.pair[p][...]
            send(
                (own.at[:, :, 1 - x_at, span[0]], own.at[:, 1 - y_at, :, span[1]]),
                (self.first[0][p], self.first[1][p]), (over_x, over_y), 1,
            )
        elif k == 1:
            own[:, :, x_at, span[0]] += self.first[0][p][...]
            own[:, y_at, :, span[1]] += self.first[1][p][...]
            send(
                (own.at[:, 1 - y_at, x_at, span[0]], own.at[:, y_at, 1 - x_at, span[1]]),
                (self.second[0][p], self.second[1][p]), (over_y, over_x), 3,
            )
        elif k == 2:
            own[:, y_at, x_at, span[0]] += self.second[0][p][...]
            own[:, y_at, x_at, span[1]] += self.second[1][p][...]
            copies = []
            for n in range(1, 4):
                target = (img_at + n) % 4
                copies.append(
                    far_copy(
                        own.at[target, y_at, x_at], self.last[p].at[n - 1], self.z_send.at[p, n], self.z_recv.at[p, n],
                        (target, band_at),
                    )
                )
            self.start(p, copies, z_loads(SPREAD, 2), 3)
        else:
            last = self.last[p]
            self.done.add(p)
            self.shares[p][...] = (own[img_at, y_at, x_at] + last[0]) + (last[1] + last[2])


def reduce_small_scratch(shapes):
    f32 = jnp.float32
    dma = pltpu.SemaphoreType.DMA
    count = len(shapes)
    groups = [
        [(4, 2, 2, r, w) for r, w in shapes],
        [(4, 2, 2, r, w) for r, w in shapes],
        [(4, 2, r // 2, w) for r, w in shapes],
        [(4, 2, r // 2, w) for r, w in shapes],
        [(4, r // 2, w) for r, w in shapes],
        [(4, r // 2, w) for r, w in shapes],
        [(3, r, w) for r, w in shapes],
    ]
    return [pltpu.VMEM(shape, f32) for group in groups for shape in group] + [
        dma((count,)), dma((count, 5)), dma((count, 5)), dma((count, 4)), dma((count, 4)),
    ]


def dot_nn(a, b):
    return lax.dot_general(a, b, (((1,), (0,)), ((), ())), preferred_element_type=jnp.float32)


def dot_nt(a, b):
    return lax.dot_general(a, b, (((1,), (1,)), ((), ())), preferred_element_type=jnp.float32)


def dot_tn(a, b):
    return lax.dot_general(a, b, (((0,), (0,)), ((), ())), preferred_element_type=jnp.float32)


def norm_parts(h):
    centred = h - jnp.mean(h, axis=-1, keepdims=True)
    rate = lax.rsqrt(jnp.mean(centred * centred, axis=-1, keepdims=True) + norm_eps)
    return centred * rate, rate


def norm_back(grad, h, gain):
    shape, rate = norm_parts(h)
    inner = grad * gain
    back = rate * (
        inner
        - jnp.mean(inner, axis=-1, keepdims=True)
        - shape * jnp.mean(inner * shape, axis=-1, keepdims=True)
    )
    return (
        back,
        jnp.sum(grad * shape, axis=0, keepdims=True),
        jnp.sum(grad, axis=0, keepdims=True),
    )


STEP = 256


def at(k, start=0):
    return pl.ds(pl.multiple_of(start + k * STEP, STEP), STEP)


def lanes_at(k, size, start=0):
    return pl.ds(pl.multiple_of(start + k * size, 128), size)


def loop(first, last, body):
    def step(k, carry):
        body(k)
        return carry

    lax.fori_loop(first, last, step, 0)


class Block:
    def __init__(self, base, source, first_w, small, refs):
        names = (
            "wide", "narrow", "norms", "q_extra", "k_extra", "hidden", "normed", "q_buf", "kv", "mixed_in", "wide_in",
            "middle", "second", "slope", "grad_out", "grad_low", "mid_low", "gatt", "dkv", "dkv_in", "soft", "x_send",
            "x_recv", "x_free",
        )
        for name, ref in zip(names, refs, strict=True):
            setattr(self, name, ref)
        self.base, self.source, self.first_w, self.small = base, source, first_w, small
        self.part = place()[4]
        self.total, self.own = self.kv.shape[0], self.q_buf.shape[0]
        self.width = self.q_buf.shape[1]
        self.offset = pl.multiple_of(self.part * self.own, self.own)
        self.chunks = self.own // STEP
        lane_head = lax.broadcasted_iota(jnp.int32, (1, 128), 1) // HDIM
        self.pick = [jnp.where(lane_head == k, 1.0, 0.0).astype(jnp.bfloat16) for k in range(2)]

    def slope_rows(self, f, k):
        return pl.ds(pl.multiple_of(f * self.own + k * STEP, STEP), STEP)

    def gain(self, k):
        return self.norms[pl.ds(self.base + k, 1), :]

    def add_small(self, row, value):
        self.small[pl.ds(row, 1), :] += value

    def add_loss(self, value):
        first_lane = lax.broadcasted_iota(jnp.int32, (1, self.width), 1) == 0
        self.add_small(6, jnp.where(first_lane, value, 0.0))

    def enter(self, first, last):
        def body(n):
            k = (n + self.chunks * (1 + self.part)) % (self.total // STEP)
            h = dot_nt(self.source(k), self.first_w())
            self.hidden[at(n % self.chunks)] = h
            shape, _ = norm_parts(h)
            self.normed[at(k)] = (shape * self.gain(0) + self.gain(1)).astype(jnp.bfloat16)

        loop(first, last, body)

    def make_kv(self, first, last):
        def body(k):
            self.kv[at(k)] = dot_nt(self.normed[at(k)], self.wide[self.width : 3 * self.width]).astype(jnp.bfloat16)

        loop(first, last, body)

    def make_q(self):
        def body(k):
            q = dot_nt(self.normed[at(k, self.offset)], self.wide[: self.width]).astype(jnp.bfloat16)
            self.q_buf[at(k)] = (q.astype(jnp.float32) * HDIM**-0.5).astype(jnp.bfloat16)

        loop(0, self.chunks, body)

    def scores(self, p, k, rows, k_cat):
        q_cat = jnp.concatenate([self.q_buf[rows, lanes_at(p, 128)] * self.pick[k], self.q_extra[rows]], axis=1)
        return dot_nt(q_cat, k_cat)

    def key_columns(self, p):
        return jnp.concatenate([self.kv[:, lanes_at(p, 128)], self.k_extra[...]], axis=1)

    def attend(self, first, last):
        head_lane = lax.broadcasted_iota(jnp.int32, (STEP, 128), 1)

        def pair(p):
            k_cat = self.key_columns(p)
            v_pair = self.kv[:, lanes_at(p, 128, self.width)]

            def body(j):
                rows = at(j)
                mixed = None
                for k in range(2):
                    scores = self.scores(p, k, rows, k_cat)
                    peak = jnp.max(scores, axis=-1, keepdims=True)
                    expo = jnp.exp(scores - peak)
                    total = jnp.sum(expo, axis=-1, keepdims=True)
                    prob = expo * (1.0 / total)
                    level = peak + jnp.log(total)
                    self.soft[rows] = jnp.where(head_lane == 2 * p + k, level, self.soft[rows])
                    term = dot_nn(prob.astype(jnp.bfloat16), v_pair * self.pick[k])
                    mixed = term if mixed is None else mixed + term
                self.mixed_in[rows, lanes_at(p, 128)] = mixed.astype(jnp.bfloat16)

            loop(0, self.chunks, body)

        loop(first, last, pair)

    def after_attention(self):
        def body(k):
            rows = at(k)
            mid = self.hidden[at(k)] + dot_nn(self.mixed_in[rows, : self.width], self.narrow[: self.width])
            self.middle[rows] = mid
            shape, _ = norm_parts(mid)
            self.second[rows] = (shape * self.gain(2) + self.gain(3)).astype(jnp.bfloat16)
            self.grad_out[rows] = mid

        loop(0, self.chunks, body)

    def mlp(self, first, last):
        width = self.width

        def body(n):
            f, k = n // self.chunks, n % self.chunks
            rows = at(k)
            u = dot_nt(self.second[rows], self.wide[lanes_at(3 + f, width)])
            squared = u * u
            bend = jnp.tanh(0.7978845608028654 * (u + 0.044715 * squared * u))
            low = (0.5 * u * (1.0 + bend)).astype(jnp.bfloat16)
            self.mixed_in[rows, lanes_at(1 + f, width)] = low
            self.slope[self.slope_rows(f, k)] = 0.5 * (1.0 + bend) + (0.5 * u) * (1.0 - bend * bend) * (
                0.7978845608028654 * (1.0 + (3.0 * 0.044715) * squared)
            )
            self.grad_out[rows] += dot_nn(low, self.narrow[lanes_at(1 + f, width)])

        loop(first * self.chunks, last * self.chunks, body)

    def mlp_back(self, first, last):
        width = self.width

        def body(k):
            rows = at(k)
            gy = self.grad_low[rows]

            def feature_step(f, acc):
                ga = dot_nt(gy, self.narrow[lanes_at(1 + f, width)])
                low = (ga * self.slope[self.slope_rows(f, k)]).astype(jnp.bfloat16)
                self.wide_in[rows, lanes_at(3 + f, width)] = low
                return acc + dot_nn(low, self.wide[lanes_at(3 + f, width)])

            grad_second = lax.fori_loop(0, 4, feature_step, jnp.zeros((STEP, width), jnp.float32))
            back, g_gain, g_offset = norm_back(grad_second, self.middle[rows], self.gain(2))
            self.add_small(2, g_gain)
            self.add_small(3, g_offset)
            grad_mid = back + self.grad_out[rows]
            self.grad_out[rows] = grad_mid
            low = grad_mid.astype(jnp.bfloat16)
            self.mid_low[rows] = low
            self.gatt[rows] = dot_nt(low, self.narrow[:width]).astype(jnp.bfloat16)

        loop(first, last, body)

    def attend_back(self, first, last):
        head_lane = lax.broadcasted_iota(jnp.int32, (self.own, 128), 1)
        lane_head = lax.broadcasted_iota(jnp.int32, (1, 128), 1) // HDIM
        rows, bf16 = slice(None), jnp.bfloat16

        def head(h):
            p = h // 2
            pick = jnp.where(lane_head == h % 2, 1.0, 0.0).astype(bf16)
            k_pair = self.kv[:, lanes_at(p, 128)]
            g_rows = self.gatt[rows, lanes_at(p, 128)] * pick
            q_rows = self.q_buf[rows, lanes_at(p, 128)] * pick
            level = jnp.sum(jnp.where(head_lane == h, self.soft[...], 0.0), axis=-1, keepdims=True)
            scores = dot_nt(
                jnp.concatenate([q_rows, self.q_extra[...]], axis=1), jnp.concatenate([k_pair, self.k_extra[...]], axis=1)
            )
            prob = jnp.exp(scores - level)
            d_prob = dot_nt(g_rows, self.kv[:, lanes_at(p, 128, self.width)])
            dot_row = jnp.sum(prob * d_prob, axis=-1, keepdims=True)
            d_score = (prob * (d_prob - dot_row)).astype(bf16)
            dq = (dot_nn(d_score, k_pair * pick) * HDIM**-0.5).astype(bf16)
            self.dkv[p, 0] += dot_tn(d_score, q_rows)
            self.dkv[p, 1] += dot_tn(prob.astype(bf16), g_rows)
            self.wide_in[rows, lanes_at(p, 128)] = self.wide_in[rows, lanes_at(p, 128)] + dq

        self.dkv[first:last] = jnp.zeros((last - first,) + self.dkv.shape[1:], jnp.float32)
        self.wide_in[:, 128 * first : 128 * last] = jnp.zeros((self.own, 128 * (last - first)), bf16)
        loop(2 * first, 2 * last, head)

    def swap(self, p):
        theirs = pl.ds(pl.multiple_of((1 - self.part) * self.own, self.own), self.own)
        return far_copy(
            self.dkv.at[p, :, theirs], self.dkv_in.at[p], self.x_send.at[p], self.x_recv.at[p], neighbours()[0]
        )

    def swap_start(self, first, opening):
        if not opening and first == 0:
            pl.semaphore_wait(self.x_free, 1)
        for p in range(first, first + 2):
            self.swap(p).start()

    def swap_finish(self, closing):
        for p in range(4):
            self.swap(p).wait()

        def body(n):
            p, k = n // self.chunks, n % self.chunks
            for side in range(2):
                total = self.dkv[p, side, at(k, self.offset)] + self.dkv_in[p, side, at(k)]
                self.wide_in[at(k), lanes_at(p, 128, (1 + side) * self.width)] = total.astype(jnp.bfloat16)

        loop(0, 4 * self.chunks, body)
        if not closing:
            pl.semaphore_signal(self.x_free, inc=1, device_id=neighbours()[0], device_id_type=MESH)

    def leave_rows(self, k):
        rows = at(k)
        grad_normed = dot_nn(self.wide_in[rows, : 3 * self.width], self.wide[: 3 * self.width])
        back, g_gain, g_offset = norm_back(grad_normed, self.hidden[at(k)], self.gain(0))
        self.add_small(0, g_gain)
        self.add_small(1, g_offset)
        return (back + self.grad_out[rows]).astype(jnp.bfloat16)

    def wide_product(self, first, count):
        if first < 3 * self.width:
            right = self.normed[pl.ds(self.offset, self.own)]
        else:
            right = self.second[...]
        return dot_tn(self.wide_in[:, first : first + count], right)

    def narrow_product(self, first, count):
        right = self.mid_low if first < self.width else self.grad_low
        return dot_tn(self.mixed_in[:, first : first + count], right[...])


def pieces_of(first, count, border):
    if first < border < first + count:
        return [(first, border - first), (border, first + count - border)]
    return [(first, count)]


def block_scratch(total_rows, own_rows):
    width = 512
    f32, bf16 = jnp.float32, jnp.bfloat16
    shapes = [
        ((own_rows, width), f32),
        ((total_rows, width), bf16),
        ((own_rows, width), bf16),
        ((total_rows, 2 * width), bf16),
        ((own_rows, 5 * width), bf16),
        ((own_rows, 7 * width), bf16),
        ((own_rows, width), f32),
        ((own_rows, width), bf16),
        ((4 * own_rows, width), f32),
        ((own_rows, width), f32),
        ((own_rows, width), bf16),
        ((own_rows, width), bf16),
        ((own_rows, width), bf16),
        ((4, 2, total_rows, 128), f32),
        ((4, 2, own_rows, 128), f32),
        ((own_rows, 128), f32),
    ]
    return [pltpu.VMEM(shape, dtype) for shape, dtype in shapes] + [
        pltpu.SemaphoreType.DMA((4,)), pltpu.SemaphoreType.DMA((4,)), pltpu.SemaphoreType.REGULAR
    ]


DEC_NARROW = ((0, 80, False),)
ENC_WIDE = ((0, 112, False),)
ENC_NARROW = ((0, 80, False),)
DEC_ORDER = (("n", 3), ("n", 1), ("n", 2), ("n", 0), ("w", 3), ("w", 2), ("w", 0), ("w", 1))
ENC_ORDER = (("n", 3), ("n", 1), ("n", 0), ("w", 3), ("w", 2), ("w", 0), ("w", 1), ("n", 2))


def step_kernel(slots, latent_total, *refs):
    shards, slab, code, kinds, norms = refs[:6], refs[6], refs[7], refs[8], refs[9]
    refs = refs[10:]
    share_wide_dec, share_narrow_dec, share_wide, share_narrow, share_edge, share_book, small_all = refs[:7]
    land_wide_dec, land_narrow_dec, land_wide, land_narrow = refs[7:11]
    refs = refs[11:]
    sems_dec, sems_enc, red, red_small, refs = refs[:5], refs[5:10], refs[10:25], refs[25:44], refs[44:]
    (book, edge, slab_all, code_all, tally, tally_all, t_img, t_band, e_near, e_send, e_recv, t_send, t_recv) = refs[:13]
    refs = refs[1:]
    (code_row, spread, cross, g_pixw, g_qout, g_qin, g_inw, g_edge, g_book) = refs[12:21]
    (small_dec, small_enc, small_own, s_img, s_band, s_send, s_recv, load_sem, wide, narrow) = refs[21:31]
    q_extra, k_extra = refs[31:33]
    scratch = refs[33:]
    f32, bf16 = jnp.float32, jnp.bfloat16
    img_at, band_at, y_at, x_at, c_at = place()
    chip_at = band_at // 2
    over_c = neighbours()[0]
    width = wide.shape[1]
    common = (wide, narrow, norms, q_extra, k_extra) + tuple(scratch)

    def edge_columns(first, count):
        return edge[:, :, :, :, :, first : first + count].reshape(width, count)

    def e_in():
        return edge_columns(0, 256)

    def e_pix():
        return edge_columns(256, 256)

    def e_qin():
        return edge_columns(512, 128)

    def e_qout():
        return edge_columns(640, 128)

    def pixel_rows(k, first=0, start=0):
        return slab_all[pl.ds(start + 2 * k, 2), :, first : first + 256].reshape(STEP, 256)

    own_band = 4 * c_at
    dec = Block(4, lambda k: spread[at(k)], e_qout, small_dec, common)
    enc = Block(0, pixel_rows, e_in, small_enc, common)
    agenda = Agenda()
    dec_pieces = [(shards[0], book, 0, 64, False), (shards[1], edge, 0, 16, False)]
    dec_pieces += [(shards[2], land_wide_dec, 96, 16, True)]
    dec_pieces += [(shards[2], land_wide_dec, 0, 48, False), (shards[2], land_wide_dec, 48, 48, False)]
    dec_pieces += [(shards[3], land_narrow_dec, first, count, last) for first, count, last in DEC_NARROW]
    gather = Gather("d", agenda, dec_pieces, *sems_dec)
    enc_pieces = [(shards[4], land_wide, first, count, last) for first, count, last in ENC_WIDE]
    enc_pieces += [(shards[5], land_narrow, first, count, last) for first, count, last in ENC_NARROW]
    gather_enc = Gather("e", agenda, enc_pieces, *sems_enc)
    count_all = Everywhere("n", agenda, tally, t_img, t_band, t_send, t_recv, tally_all)
    spots = lax.broadcasted_iota(jnp.int32, (1, 4), 1)
    kind = jnp.sum(jnp.where(spots == chip_at, kinds[...], 0).astype(f32), axis=1, keepdims=True)
    meet(peers())
    agenda.spend(3.0)
    gather.begin(0, 5)
    exchange = []
    for step in range(1, 4):
        chip = (chip_at + step) % 4
        target = (img_at, 2 * chip + c_at)
        here = band_at
        exchange.append(far_copy(slab.at[chip], slab_all.at[here], e_send.at[0, step], e_recv.at[0, step], target))
        exchange.append(far_copy(code.at[chip], code_all.at[here], e_send.at[1, step], e_recv.at[1, step], target))
    exchange.append(pltpu.make_async_copy(slab.at[chip_at], slab_all.at[band_at], e_near.at[0]))
    exchange.append(pltpu.make_async_copy(code.at[chip_at], code_all.at[band_at], e_near.at[1]))

    def exchange_landed():
        late = []
        for k, dst in enumerate((slab_all, code_all)):
            for chip in range(4):
                part = dst.at[2 * chip + c_at]
                late.append(far_copy(part, part, e_send.at[k, 4 + chip], e_recv.at[k, 4 + chip], over_c))
        agenda.launch("x2", late, [("c", 4e5)], lambda: arrived.append(1))

    arrived = []
    agenda.launch("x1", exchange, [("x", 4e5), ("y", 4e5)], exchange_landed)
    agenda.spend(1.0)
    segment_lane = lax.broadcasted_iota(jnp.int32, (enc.total, 128), 1)
    segment = jnp.where(kind < 0.5, 0, lax.broadcasted_iota(jnp.int32, (enc.total, 128), 0) // (enc.total // 4))
    k_extra[...] = jnp.where(segment_lane == segment, 1.0, 0.0).astype(bf16)
    segment_lane = lax.broadcasted_iota(jnp.int32, (enc.own, 128), 1)
    segment = lax.broadcasted_iota(jnp.int32, (enc.own, 128), 0) + enc.offset
    segment = jnp.where(kind < 0.5, 0, segment // (enc.total // 4))
    q_extra[...] = jnp.where((segment_lane < 4) & (segment_lane != segment), -(2.0**30), 0.0).astype(bf16)
    for ref in (small_dec, small_enc, g_pixw, g_qout, g_qin, g_inw):
        ref[...] = jnp.zeros(ref.shape, f32)
    agenda.spend(2.0)
    agenda.tick()
    agenda.until(lambda: arrived)
    def code_column(k, start=0):
        return jnp.concatenate(
            [jnp.transpose(jnp.broadcast_to(code_all[start + 2 * k + n], (8, 128)))[:, 0:1] for n in range(2)], axis=0
        )

    for n in range(4):
        code_row[:, pl.ds(128 * n, 128)] = code_all[own_band + n]

    def pick_codes(k):
        rows = at(k)
        code_here = code_column(k)
        picks = lax.broadcasted_iota(jnp.int32, (STEP, 512), 1)
        found = jnp.zeros((STEP, 128), f32)
        for z in range(4):
            hot = jnp.where(picks + 512 * z == code_here // 4, 1.0, 0.0).astype(bf16)
            found += dot_nn(hot, book[z].reshape(512, 128))
        lanes = lax.broadcasted_iota(jnp.int32, (STEP, 128), 1) // 32
        spread[rows] = jnp.where(lanes == code_here % 4, found, 0.0).astype(bf16)

    lane = lax.broadcasted_iota(jnp.int32, (4, 128, 256), 2)
    flags = slab_all[pl.ds(own_band, 4), :, 128:384].astype(f32)
    tally[...] = jnp.full(tally.shape, jnp.sum(jnp.where(lane < 64, 0.0, flags)))
    agenda.spend(1.0)
    agenda.tick()
    count_all.begin()
    gather.begin(5, len(dec_pieces))
    gather.until(0)
    agenda.tick()
    loop(0, dec.total // STEP, pick_codes)
    agenda.spend(4.0)
    agenda.tick()
    gather.until(1)
    dec.enter(0, dec.total // STEP)
    agenda.spend(1.9)
    agenda.tick()

    def fetch(landed, ref, sem):
        rows = landed.shape[4]

        def body(n):
            src = landed.at[n // 8, (n // 4) % 2, (n // 2) % 2, n % 2]
            pltpu.make_async_copy(src, ref.at[pl.ds(pl.multiple_of(n * rows, 16), rows)], sem).start()

        loop(0, 32, body)
        return pltpu.make_async_copy(ref, ref, sem)

    reduce = Reduce(agenda, *slots, *red)
    tail = ReduceSmall(
        agenda, (g_edge, g_book), (share_edge, share_book),
        *[red_small[2 * n : 2 * n + 2] for n in range(7)], *red_small[14:],
    )

    def emit_wide(blk, z, full, slot):
        values = [blk.wide_product(*span) for span in pieces_of(896 * z, 896, 3 * width)]
        value = values[0] if len(values) == 1 else jnp.concatenate(values, axis=0)
        full[slot] = value.reshape(2, 2, 2, 112, width)
        agenda.spend(0.6)

    def emit_narrow(blk, z, full, slot):
        values = [blk.narrow_product(*span) for span in pieces_of(640 * z, 640, width)]
        value = values[0] if len(values) == 1 else jnp.concatenate(values, axis=0)
        full[slot, :, :, :, :80] = value.reshape(2, 2, 2, 80, width)
        agenda.spend(0.5)

    pieces = []
    for name, blk, out_wide, out_narrow, order in (
        ("dec", dec, share_wide_dec, share_narrow_dec, DEC_ORDER), ("enc", enc, share_wide, share_narrow, ENC_ORDER)
    ):
        for kind_of, z in order:
            if kind_of == "n":
                needs = name + str(int(z == 0))
                pieces.append(dict(emit=functools.partial(emit_narrow, blk, z), z=z, rows=80, out=out_narrow, needs=needs))
                continue
            piece = dict(z=z, rows=112, out=out_wide, needs=name + str(1 + (z < 2)))
            if name == "dec" and z < 2:
                piece.update(stage=dec.slope, first=896 * z)
            else:
                piece.update(emit=functools.partial(emit_wide, blk, z))
            pieces.append(piece)
    reduce.plan(pieces)

    def spend(time):
        agenda.spend(time)
        agenda.tick()

    def decoder_head(k):
        rows = at(k)
        out = dec.grad_out[rows]
        shape, _ = norm_parts(out)
        final = (shape * norms[pl.ds(8, 1), :] + norms[pl.ds(9, 1), :]).astype(bf16)
        error = dot_nn(final, e_pix()) - pixel_rows(k, 0, own_band).astype(f32)
        lane = lax.broadcasted_iota(jnp.int32, (STEP, 256), 1)
        counted = jnp.where(lane < 192, pltpu.roll(pixel_rows(k, 128, own_band).astype(f32), 192, 1), 0.0)
        number = tally_all[0:1, 0:1]
        dec.add_loss(jnp.sum(counted * (error * error + jnp.abs(error))) / number)
        sign = jnp.where(error > 0.0, 1.0, jnp.where(error < 0.0, -1.0, 0.0))
        grad_pred = (counted * (2.0 * error + sign) / number).astype(bf16)
        g_pixw[...] += dot_tn(final, grad_pred)
        back, g_gain, g_offset = norm_back(dot_nt(grad_pred, e_pix()), out, norms[pl.ds(8, 1), :])
        dec.add_small(4, g_gain)
        dec.add_small(5, g_offset)
        dec.grad_out[rows] = back
        dec.grad_low[rows] = back.astype(bf16)

    def encoder_head(k):
        rows = at(k)
        low = enc.grad_out[rows].astype(bf16)
        lanes = lax.broadcasted_iota(jnp.int32, (STEP, 128), 1) // 32
        mine = lanes == code_column(k, own_band) % 4
        gap = jnp.where(mine, spread[at(k, enc.offset)].astype(f32) - dot_nn(low, e_qin()), 0.0)
        enc.add_loss((1.0 + commitment) * jnp.sum(gap * gap) / latent_total)
        grad_latent = jnp.where(mine, cross[rows] - 2.0 * commitment * gap / latent_total, 0.0).astype(bf16)
        g_qin[...] += dot_tn(low, grad_latent)
        back = dot_nt(grad_latent, e_qin())
        enc.grad_out[rows] = back
        enc.grad_low[rows] = back.astype(bf16)
        gap = 2.0 * gap / latent_total
        high = gap.astype(bf16)
        left = gap - high.astype(f32)
        between = left.astype(bf16)
        enc.gatt[rows, :384] = jnp.concatenate([high, between, (left - between.astype(f32)).astype(bf16)], axis=1)

    def book_rows(k):
        picks = lax.broadcasted_iota(jnp.int32, (STEP, enc.own), 0) + k * STEP
        hot = jnp.where(picks == code_row[...] // 4, 1.0, 0.0).astype(bf16)
        summed = dot_nn(hot, enc.gatt[:, :384])
        value = (summed[:, :128] + summed[:, 128:256]) + summed[:, 256:]
        g_book[k // 2, k % 2] = value.reshape(2, 2, 64, 128)

    def decoder_leave(k):
        low = dec.leave_rows(k)
        cross[at(k)] = dot_nn(low, e_qout())
        g_qout[...] += dot_tn(low, spread[at(k, dec.offset)])

    def encoder_leave(k):
        g_inw[...] += dot_tn(enc.leave_rows(k), pixel_rows(k, 0, own_band))

    gather_enc.begin(0, len(enc_pieces))
    gather.until(2, 3, 4)
    fetch(land_wide_dec, wide, load_sem.at[0]).wait()
    spend(2.0)
    dec.make_kv(0, dec.total // STEP)
    dec.make_q()
    spend(2.9)
    dec.attend(0, 4)
    spend(11.1)
    gather.until(*range(5, len(dec_pieces)))
    fetched = fetch(land_narrow_dec, narrow, load_sem.at[1])
    agenda.spend(1.0)
    fetched.wait()
    dec.after_attention()
    spend(1.1)
    dec.mlp(0, 4)
    spend(5.6)
    count_all.until()
    loop(0, dec.chunks, decoder_head)
    agenda.spend(2.0)
    reduce.allow("dec0")
    agenda.tick()
    dec.mlp_back(0, dec.chunks)
    agenda.spend(6.1)
    reduce.allow("dec1")
    agenda.tick()
    dec.attend_back(0, 2)
    dec.swap_start(0, True)
    spend(7.9)
    dec.attend_back(2, 4)
    dec.swap_start(2, True)
    spend(7.9)
    gather_enc.until(*range(len(enc_pieces)))
    fetched = fetch(land_narrow, narrow, load_sem.at[1])
    dec.swap_finish(False)
    agenda.spend(2.0)
    for z in range(2):
        values = [dec.wide_product(*span) for span in pieces_of(896 * z, 896, 3 * width)]
        dec.slope[pl.ds(896 * z, 896)] = values[0] if len(values) == 1 else jnp.concatenate(values, axis=0)
    agenda.spend(1.2)
    reduce.allow("dec2")
    agenda.tick()
    loop(0, dec.chunks, decoder_leave)
    fetched_wide = fetch(land_wide, wide, load_sem.at[0])
    spend(2.0)
    emitted = 1 + max(p for p in range(8) if "emit" in pieces[p])
    staged = [p for p in range(8) if "stage" in pieces[p]]
    agenda.until(lambda: reduce.opened >= emitted)
    enc.enter(0, enc.total // STEP)
    spend(1.9)
    fetched_wide.wait()
    enc.make_kv(0, enc.total // STEP)
    enc.make_q()
    fetched.wait()
    spend(2.9)
    for p in range(2):
        enc.attend(2 * p, 2 * p + 2)
        spend(5.6)
    enc.after_attention()
    spend(1.1)
    agenda.until(lambda: reduce.opened > max(staged) and not any(("r", p, 0) in agenda.flying for p in staged))
    enc.mlp(0, 4)
    spend(5.6)
    loop(0, enc.chunks, encoder_head)
    agenda.spend(2.0)
    reduce.allow("enc0")
    agenda.tick()
    loop(0, 8, book_rows)
    tail.open(1)
    spend(2.0)
    enc.mlp_back(0, enc.chunks)
    agenda.spend(6.1)
    reduce.allow("enc1")
    agenda.tick()
    enc.attend_back(0, 2)
    enc.swap_start(0, False)
    spend(7.9)
    enc.attend_back(2, 4)
    enc.swap_start(2, False)
    spend(7.9)
    enc.swap_finish(True)
    agenda.spend(2.0)
    reduce.allow("enc2")
    agenda.tick()
    loop(0, enc.chunks, encoder_leave)
    agenda.spend(2.0)

    def all_groups(value):
        value = value + pltpu.roll(value, 64, 1)
        return value + pltpu.roll(value, 32, 1)

    lane = lax.broadcasted_iota(jnp.int32, (width, 128), 1)
    mixed = jnp.where(lane < 64, g_inw[:, 128:], jnp.where(lane < 96, all_groups(g_qin[...]), all_groups(g_qout[...])))
    for first, value in ((0, g_inw[:, :128]), (128, mixed), (256, g_pixw[:, :128]), (384, g_pixw[:, 128:])):
        g_edge[:, :, :, :, :, pl.ds(first, 128)] = value.reshape(4, 2, 2, 2, 16, 128)
    tail.open(0)
    agenda.until(lambda: len(reduce.ended) == len(pieces) and len(tail.done) == 2)
    shares = (share_wide_dec, share_narrow_dec, share_wide, share_narrow, share_edge, share_book)
    squares = sum(jnp.sum(share[...] * share[...]) for share in shares)
    lane = lax.broadcasted_iota(jnp.int32, (8, width), 1)
    row = lax.broadcasted_iota(jnp.int32, (8, width), 0)
    small_own[0] = small_enc[...]
    small_own[1] = jnp.where((row == 7) & (lane == 0), squares, small_dec[...])
    sum_all = Everywhere("a", agenda, small_own, s_img, s_band, s_send, s_recv, small_all)
    sum_all.begin()
    sum_all.until()


def train_step(shards, slab, code, kinds, norms, latent_total, total_rows, own_rows):
    width = 512
    slots = (4, 4)
    f32, bf16, int32 = jnp.float32, jnp.bfloat16, jnp.int32
    any_space = pl.BlockSpec(memory_space=pl.ANY)
    vmem = pl.BlockSpec(memory_space=pltpu.VMEM)
    shape = jax.ShapeDtypeStruct
    out_shape = [
        shape((112, width), f32), shape((80, width), f32), shape((112, width), f32), shape((80, width), f32),
        shape((16, width), f32), shape((64, 128), f32), shape((2, 8, width), f32),
    ]
    out_shape += [shape((4, 2, 2, 2) + s.shape, s.dtype) for s in shards[2:]]
    dma = pltpu.SemaphoreType.DMA
    mem = pltpu.VMEM
    scratch = gather_sems(5 + len(DEC_NARROW)) + gather_sems(len(ENC_WIDE) + len(ENC_NARROW))
    scratch += reduce_scratch(*slots, 112, width) + reduce_small_scratch([(16, width), (64, 128)])
    scratch += [
        mem((4, 2, 2, 2, 64, 128), bf16), mem((4, 2, 2, 2, 16, 768), bf16),
        mem((8, 128, 384), bf16), mem((8, 1, 128), int32), mem((8, 128), f32), mem((8, 128), f32),
        mem((4, 8, 128), f32), mem((8, 8, 128), f32),
        dma((2,)), dma((2, 8)), dma((2, 8)), dma((11,)), dma((11,)),
        mem((1, own_rows), int32), mem((total_rows, 128), bf16),
        mem((own_rows, 128), f32),
        mem((width, 256), f32), mem((width, 128), f32), mem((width, 128), f32), mem((width, 256), f32),
        mem((4, 2, 2, 2, 16, width), f32), mem((4, 2, 2, 2, 64, 128), f32),
        mem((8, width), f32), mem((8, width), f32), mem((2, 8, width), f32),
        mem((4, 2, 8, width), f32), mem((8, 2, 8, width), f32), dma((11,)), dma((11,)),
        dma((2,)), mem((7 * width, width), bf16), mem((5 * width, width), bf16),
        mem((own_rows, 128), bf16), mem((total_rows, 128), bf16),
    ]
    scratch += block_scratch(total_rows, own_rows)
    return pl.pallas_call(
        functools.partial(step_kernel, slots, latent_total),
        out_shape=out_shape,
        in_specs=[any_space] * 8 + [vmem] * 2,
        out_specs=[vmem] * 7 + [any_space] * 4,
        scratch_shapes=scratch,
        compiler_params=pltpu.CompilerParams(collective_id=0, has_side_effects=True, vmem_limit_bytes=(639 << 20) // 10),
        name="train_step",
    )(*shards, slab, code, kinds, norms)


def moments(gradient, first_old, second_old):
    first_new = beta_first * first_old + (1.0 - beta_first) * gradient
    second_new = beta_second * second_old + (1.0 - beta_second) * gradient * gradient
    return (first_new, second_new, first_new / (jnp.sqrt(second_new) + adam_eps))


def rotated_update(weight, gradient, first_old, second_old, basis_stack):
    turned = jnp.einsum("rld,lde->rle", gradient, basis_stack, precision=highest)
    first_new, second_new, direction = moments(turned, first_old, second_old)
    turned_back = jnp.einsum("rle,lde->rld", direction, basis_stack, precision=highest)
    return (weight - rate_matrix * (turned_back + weight_decay * weight), first_new, second_new)


def plain_update(weight, gradient, first_old, second_old):
    first_new, second_new, direction = moments(gradient, first_old, second_old)
    return (weight - rate_vector * (direction + weight_decay * weight), first_new, second_new)


def update_kernel(*refs):
    count = 20
    ins, refs = refs[:count], refs[count:]
    outs, held, sem = refs[:13], refs[13 : 13 + count], refs[13 + count]
    loads = [pltpu.make_async_copy(src, dst, sem.at[k]) for k, (src, dst) in enumerate(zip(ins, held))]
    for load in loads:
        load.start()
    for load in loads:
        load.wait()
    refs = held + outs
    wide_0, wide_1, narrow_0, narrow_1, edge, small = refs[:6]
    wide, narrow, edge_set, norm_set = refs[6:9], refs[9:12], refs[12:15], refs[15:18]
    bases, basis_edge = refs[18:20]
    new_wide, new_narrow, new_edge, new_norms, scalars = refs[20:23], refs[23:26], refs[26:29], refs[29:32], refs[32]
    norm_grad = jnp.concatenate([small[0, 0:4], small[1, 0:6]], axis=0)
    squares = small[1, 7:8, 0:1] + jnp.sum(norm_grad * norm_grad)
    grad_norm = jnp.sqrt(squares)
    factor = jnp.minimum(1.0, clip_level / grad_norm)
    scalars[0:1] = jnp.broadcast_to(grad_norm, (1, 128))
    scalars[1:2] = jnp.broadcast_to(factor, (1, 128))
    scalars[2:3] = jnp.broadcast_to(small[0, 6:7, 0:1] + small[1, 6:7, 0:1], (1, 128))
    scalars[3:8] = jnp.zeros((5, 128), jnp.float32)

    def halves(value):
        high = value.astype(jnp.bfloat16)
        return high, (value - high.astype(jnp.float32)).astype(jnp.bfloat16)

    def product(left, right, dot):
        (high, low), (right_high, right_low) = halves(left), right
        return dot(high, right_high) + (dot(high, right_low) + dot(low, right_high))

    def turn(weight, gradient, first_old, second_old, basis):
        right = halves(basis)
        turned = product(gradient, right, dot_nn)
        first_new, second_new, direction = moments(turned, first_old, second_old)
        back = product(direction, right, dot_nt)
        return weight - rate_matrix * (back + weight_decay * weight), first_new, second_new

    for k, (olds, news, grads) in enumerate(
        ((wide, new_wide, (wide_0, wide_1)), (narrow, new_narrow, (narrow_0, narrow_1)))
    ):
        for layer in range(2):
            found = turn(
                olds[0][:, layer], factor * grads[layer][...], olds[1][:, layer], olds[2][:, layer], bases[2 * k + layer]
            )
            for ref, value in zip(news, found):
                ref[:, layer] = value
    packed = edge[...]
    grad_edge = jnp.concatenate([packed[:, :192], packed[:, 256:448], packed[:, 192:256]], axis=1)
    found = turn(edge_set[0][...], factor * grad_edge, edge_set[1][...], edge_set[2][...], basis_edge[...])
    for ref, value in zip(new_edge, found):
        ref[...] = value
    found = plain_update(norm_set[0][...], factor * norm_grad, norm_set[1][...], norm_set[2][...])
    for ref, value in zip(new_norms, found):
        ref[...] = value


def update_all(grads, wide, narrow, edge, norms, bases, basis_edge):
    vmem = pl.BlockSpec(memory_space=pltpu.VMEM)
    shape = jax.ShapeDtypeStruct
    sets = wide + narrow + edge + norms
    return pl.pallas_call(
        update_kernel,
        out_shape=[shape(a.shape, a.dtype) for a in sets] + [shape((8, 128), jnp.float32)],
        in_specs=[pl.BlockSpec(memory_space=pl.ANY)] * (len(grads) + len(sets) + 2),
        out_specs=[vmem] * (len(sets) + 1),
        scratch_shapes=[pltpu.VMEM(a.shape, a.dtype) for a in (*grads, *sets, bases, basis_edge)]
        + [pltpu.SemaphoreType.DMA((len(grads) + len(sets) + 2,))],
        compiler_params=pltpu.CompilerParams(vmem_limit_bytes=63 << 20),
        name="update_all",
    )(*grads, *sets, bases, basis_edge)


def body(
    pixels,
    valid,
    codes,
    image_kind,
    w_wide,
    w_narrow,
    w_edge,
    codebook,
    norms,
    bases,
    basis_edge,
    m_wide,
    v_wide,
    m_narrow,
    v_narrow,
    m_edge,
    v_edge,
    m_code,
    v_code,
    m_norm,
    v_norm,
):
    band_count = lax.axis_size("band")
    band_index = lax.axis_index("band")
    row_count = pixels.shape[2]
    length = row_count * band_count
    batch_count = pixels.shape[0]
    group = band_count // batch_count
    row = band_index // group
    part = band_index % group
    own_rows = length // group
    groups = [[k * group + j for j in range(group)] for k in range(batch_count)]
    layer_count = w_wide.shape[1]
    code_width = codebook.shape[1]
    latent_total = batch_count * lax.axis_size("img") * length * code_width
    both = ("img", "band")

    direct = band_count == 8 and lax.axis_size("img") == 4 and batch_count == 4
    shards = [w_wide[:, l].astype(jnp.bfloat16) for l in range(layer_count)]
    shards += [w_narrow[:, l].astype(jnp.bfloat16) for l in range(layer_count)]
    shards += [w_edge.astype(jnp.bfloat16), codebook.astype(jnp.bfloat16).reshape(-1, 4 * code_width)]
    slab = jnp.concatenate([pixels[:, 0], valid[:, 0].astype(jnp.bfloat16)], axis=2)
    patch_size = pixels.shape[3]
    if direct:
        edge = shards[4]
        gap = jnp.zeros((edge.shape[0], 64), edge.dtype)
        qin = edge[:, 2 * patch_size : 2 * patch_size + code_width]
        qout = edge[:, 2 * patch_size + code_width :]
        shards[4] = jnp.concatenate(
            [edge[:, :patch_size], gap, edge[:, patch_size : 2 * patch_size], gap] + [qin] * 4 + [qout] * 4, axis=1
        )
        out = train_step(
            [shards[k] for k in (5, 4, 1, 3, 0, 2)], slab, codes, image_kind.reshape(1, -1), norms, latent_total, length, own_rows
        )
        new = update_all(
            (out[2], out[0], out[3], out[1], out[4], out[6]), (w_wide, m_wide, v_wide), (w_narrow, m_narrow, v_narrow),
            (w_edge, m_edge, v_edge), (norms, m_norm, v_norm), bases, basis_edge,
        )
        scalars = new[12]
        grad_norm, factor, loss_total = scalars[0, 0], scalars[1, 0], scalars[2, 0]
        new_code = plain_update(codebook, factor * out[5].reshape(-1, code_width), m_code, v_code)
        return tuple(new[:9]) + new_code + tuple(new[9:12]) + (grad_norm, loss_total)
    wholes = [lax.all_gather(shard, both, axis=0, tiled=True) for shard in shards]
    count = lax.psum(jnp.sum(valid.astype(jnp.float32)), both)

    def whole_row(local):
        everywhere = lax.all_gather(local, "band", axis=0)
        chosen_row = lax.dynamic_index_in_dim(everywhere, row, axis=1, keepdims=False)
        return chosen_row.reshape((length,) + local.shape[2:])

    slab_all = whole_row(slab)
    code_all = whole_row(codes[:, 0])
    kind = lax.dynamic_index_in_dim(image_kind[:, 0], row, 0, keepdims=False)
    span = jnp.where(kind == 0, length, length // 4)
    positions = jnp.arange(length, dtype=jnp.int32)
    gathered = (wholes[:2], wholes[2:4], wholes[4], wholes[5])
    pixel_all = slab_all[:, :patch_size]
    valid_rows = lax.dynamic_slice_in_dim(slab_all, part * own_rows, own_rows, 0)[:, patch_size:]
    own_positions = part * own_rows + jnp.arange(own_rows, dtype=jnp.int32)
    allowed = (own_positions // span)[:, None] == (positions // span)[None, :]
    local_grads, norm_sum, loss_sum = row_step(
        gathered, norms, pixel_all, valid_rows, code_all, part, allowed, count, latent_total, groups
    )
    shares = [lax.psum_scatter(g, both, scatter_dimension=0, tiled=True) for g in local_grads]
    squares = sum(jnp.sum(share * share) for share in shares)
    norm_total, square_total, loss_total = lax.psum((norm_sum, squares, loss_sum), both)
    grad_sum = (
        jnp.stack([shares[0], shares[1]], axis=1),
        jnp.stack([shares[2], shares[3]], axis=1),
        shares[4],
        shares[5].reshape(-1, code_width),
    )
    grad_norm = jnp.sqrt(square_total + jnp.sum(norm_total * norm_total))
    factor = jnp.minimum(1.0, clip_level / grad_norm)
    grad_wide, grad_narrow, grad_edge, grad_book = grad_sum
    new_wide, new_m_wide, new_v_wide = rotated_update(
        w_wide, factor * grad_wide, m_wide, v_wide, bases[:layer_count]
    )
    new_narrow, new_m_narrow, new_v_narrow = rotated_update(
        w_narrow, factor * grad_narrow, m_narrow, v_narrow, bases[layer_count:]
    )
    new_edge, new_m_edge, new_v_edge = rotated_update(
        w_edge[:, None],
        factor * grad_edge[:, None],
        m_edge[:, None],
        v_edge[:, None],
        basis_edge[None],
    )
    new_book, new_m_code, new_v_code = plain_update(codebook, factor * grad_book, m_code, v_code)
    new_norms, new_m_norm, new_v_norm = plain_update(norms, factor * norm_total, m_norm, v_norm)
    return (
        new_wide,
        new_m_wide,
        new_v_wide,
        new_narrow,
        new_m_narrow,
        new_v_narrow,
        new_edge[:, 0],
        new_m_edge[:, 0],
        new_v_edge[:, 0],
        new_book,
        new_m_code,
        new_v_code,
        new_norms,
        new_m_norm,
        new_v_norm,
        grad_norm,
        loss_total,
    )


def solution(mesh):
    in_specs = (
        P(None, "img", "band", None),
        P(None, "img", "band", None),
        P(None, "img", "band"),
        P(None, "img"),
        P(("img", "band"), None, None),
        P(("img", "band"), None, None),
        P(("img", "band"), None),
        P(("img", "band"), None),
        P(),
        P(),
        P(),
        P(("img", "band"), None, None),
        P(("img", "band"), None, None),
        P(("img", "band"), None, None),
        P(("img", "band"), None, None),
        P(("img", "band"), None),
        P(("img", "band"), None),
        P(("img", "band"), None),
        P(("img", "band"), None),
        P(),
        P(),
    )
    out_specs = (
        P(("img", "band"), None, None),
        P(("img", "band"), None, None),
        P(("img", "band"), None, None),
        P(("img", "band"), None, None),
        P(("img", "band"), None, None),
        P(("img", "band"), None, None),
        P(("img", "band"), None),
        P(("img", "band"), None),
        P(("img", "band"), None),
        P(("img", "band"), None),
        P(("img", "band"), None),
        P(("img", "band"), None),
        P(),
        P(),
        P(),
        P(),
        P(),
    )
    return jax.shard_map(body, mesh=mesh, in_specs=in_specs, out_specs=out_specs, check_vma=False)
```

```python
import functools

import jax
import jax.numpy as jnp
from jax import lax
from jax.experimental import pallas as pl
from jax.experimental.pallas import tpu as pltpu
from jax.sharding import PartitionSpec as P

HEADS = 8
HDIM = 64
MESH = pl.DeviceIdType.MESH


norm_eps = 1e-05
adam_eps = 1e-08
clip_level = 0.001
beta_first = 0.5
beta_second = 0.6
rate_matrix = 0.02
rate_vector = 0.3
weight_decay = 0.01
commitment = 0.25
masked_score = -1000000000.0
highest = lax.Precision.HIGHEST


def matmul_plain(first_op, second_op):
    return jnp.dot(first_op, second_op, preferred_element_type=jnp.float32)


def matmul_trans(first_op, second_op):
    return lax.dot_general(
        first_op, second_op, (((1,), (1,)), ((), ())), preferred_element_type=jnp.float32
    )


def matmul_outer(first_op, second_op):
    return lax.dot_general(
        first_op, second_op, (((0,), (0,)), ((), ())), preferred_element_type=jnp.float32
    )


def layer_norm(hidden, scale_gain, offset):
    centred = hidden - jnp.mean(hidden, axis=-1, keepdims=True)
    spread = jnp.mean(centred * centred, axis=-1, keepdims=True)
    return centred * lax.rsqrt(spread + norm_eps) * scale_gain + offset


def gelu_tanh(inputs):
    return (
        0.5
        * inputs
        * (1.0 + jnp.tanh(0.7978845608028654 * (inputs + 0.044715 * inputs * inputs * inputs)))
    )


def split_heads(matrix):
    return matrix.reshape(matrix.shape[0], HEADS, HDIM)


def head_scores(q_heads, k_heads, allowed):
    scores = jnp.einsum(
        "qhd,khd->hqk", q_heads, k_heads, preferred_element_type=jnp.float32
    ) * HDIM ** (-0.5)
    return jnp.where(allowed[None], scores, masked_score)


def attend(queries, key_rows, value_rows, allowed):
    scores = head_scores(split_heads(queries), split_heads(key_rows), allowed)
    score_peak = jnp.max(scores, axis=-1, keepdims=True)
    expo = jnp.exp(scores - score_peak)
    total = jnp.sum(expo, axis=-1, keepdims=True)
    softmaxed = (expo / total).astype(jnp.bfloat16)
    attended = jnp.einsum(
        "hqk,khd->qhd", softmaxed, split_heads(value_rows), preferred_element_type=jnp.float32
    )
    return (
        attended.reshape(queries.shape[0], -1).astype(jnp.bfloat16),
        score_peak + jnp.log(total),
    )


def attend_back(queries, key_rows, value_rows, allowed, log_total, grad_out):
    q_heads = split_heads(queries)
    k_heads = split_heads(key_rows)
    v_heads = split_heads(value_rows)
    g_heads = split_heads(grad_out)
    softmaxed = jnp.exp(head_scores(q_heads, k_heads, allowed) - log_total)
    grad_soft = jnp.einsum("qhd,khd->hqk", g_heads, v_heads, preferred_element_type=jnp.float32)
    row_dot = jnp.sum(softmaxed * grad_soft, axis=-1, keepdims=True)
    grad_scores = (softmaxed * (grad_soft - row_dot)).astype(jnp.bfloat16)
    scale = HDIM ** (-0.5)
    grad_q = (
        jnp.einsum("hqk,khd->qhd", grad_scores, k_heads, preferred_element_type=jnp.float32) * scale
    )
    grad_k = (
        jnp.einsum("hqk,qhd->khd", grad_scores, q_heads, preferred_element_type=jnp.float32) * scale
    )
    grad_v = jnp.einsum(
        "hqk,qhd->khd", softmaxed.astype(jnp.bfloat16), g_heads, preferred_element_type=jnp.float32
    )
    return (
        grad_q.reshape(queries.shape[0], -1),
        grad_k.reshape(key_rows.shape[0], -1),
        grad_v.reshape(key_rows.shape[0], -1),
    )


def block_forward(hidden_all, part, wide_rows, narrow_rows, gain_rows, allowed):
    model_width = hidden_all.shape[1]
    own_rows = allowed.shape[0]
    normed_all = layer_norm(hidden_all, gain_rows[0], gain_rows[1]).astype(jnp.bfloat16)
    hidden = lax.dynamic_slice_in_dim(hidden_all, part * own_rows, own_rows, 0)
    normed = lax.dynamic_slice_in_dim(normed_all, part * own_rows, own_rows, 0)
    queries = matmul_trans(normed, wide_rows[:model_width]).astype(jnp.bfloat16)
    key_rows = matmul_trans(normed_all, wide_rows[model_width : 2 * model_width]).astype(jnp.bfloat16)
    value_rows = matmul_trans(normed_all, wide_rows[2 * model_width : 3 * model_width]).astype(jnp.bfloat16)
    attended, log_total = attend(queries, key_rows, value_rows, allowed)
    middle = hidden + matmul_plain(attended, narrow_rows[:model_width])
    second = layer_norm(middle, gain_rows[2], gain_rows[3]).astype(jnp.bfloat16)
    upper_in = matmul_trans(second, wide_rows[3 * model_width :])
    active = gelu_tanh(upper_in).astype(jnp.bfloat16)
    result = middle + matmul_plain(active, narrow_rows[model_width:])
    return (
        result,
        (hidden, normed, queries, key_rows, value_rows, attended, log_total, middle, second, upper_in, active),
    )


def block_backward(grad_out, wide_rows, narrow_rows, gain_rows, allowed, saved, groups):
    (hidden, normed, queries, key_rows, value_rows, attended, log_total, middle, second, upper_in, active) = saved
    model_width = hidden.shape[1]
    grad_y = grad_out.astype(jnp.bfloat16)
    grad_down = matmul_outer(active, grad_y)
    grad_active = matmul_trans(grad_y, narrow_rows[model_width:])
    grad_upper = jax.vjp(gelu_tanh, upper_in)[1](grad_active)[0].astype(jnp.bfloat16)
    grad_up = matmul_outer(grad_upper, second)
    _, second_back = jax.vjp(layer_norm, middle, gain_rows[2], gain_rows[3])
    grad_mid, gain_two, offset_two = second_back(
        matmul_plain(grad_upper, wide_rows[3 * model_width :])
    )
    grad_mid = grad_mid + grad_out
    grad_attn = grad_mid.astype(jnp.bfloat16)
    grad_outproj = matmul_outer(attended, grad_attn)
    grad_att = matmul_trans(grad_attn, narrow_rows[:model_width]).astype(jnp.bfloat16)
    grad_q, grad_keys, grad_values = attend_back(
        queries, key_rows, value_rows, allowed, log_total, grad_att
    )
    grad_k = lax.psum_scatter(grad_keys, "band", scatter_dimension=0, tiled=True, axis_index_groups=groups)
    grad_v = lax.psum_scatter(grad_values, "band", scatter_dimension=0, tiled=True, axis_index_groups=groups)
    grad_mixed = jnp.concatenate([grad_q, grad_k, grad_v], axis=1).astype(jnp.bfloat16)
    grad_qkv = matmul_outer(grad_mixed, normed)
    _, first_back = jax.vjp(layer_norm, hidden, gain_rows[0], gain_rows[1])
    grad_in, gain_one, offset_one = first_back(
        matmul_plain(grad_mixed, wide_rows[: 3 * model_width])
    )
    gain_grads = jnp.stack([gain_one, offset_one, gain_two, offset_two], axis=0)
    return (
        grad_in + grad_mid,
        jnp.concatenate([grad_qkv, grad_up], axis=0),
        jnp.concatenate([grad_outproj, grad_down], axis=0),
        gain_grads,
    )


def pick_codes(code_rows, book_wide, code_width):
    fold = book_wide.shape[1] // code_width
    one_hot = (
        (code_rows // fold)[:, None] == jnp.arange(book_wide.shape[0], dtype=jnp.int32)[None, :]
    ).astype(jnp.bfloat16)
    lane_fold = jnp.arange(book_wide.shape[1], dtype=jnp.int32)[None, :] // code_width
    lane_mask = (code_rows % fold)[:, None] == lane_fold
    spread = jnp.where(lane_mask, matmul_plain(one_hot, book_wide), 0.0)
    chosen = sum(spread[:, k * code_width : (k + 1) * code_width] for k in range(fold))
    return chosen, one_hot, lane_mask


def row_step(gathered, norms, pixel_all, valid_rows, code_all, part, allowed, count, latent_total, groups):
    wide_all, narrow_all, edge_all, book_wide = gathered
    patch_size = pixel_all.shape[1]
    code_width = edge_all.shape[1] // 2 - patch_size
    own_rows = allowed.shape[0]
    edge_in = edge_all[:, :patch_size]
    edge_pix = edge_all[:, patch_size : 2 * patch_size]
    edge_qin = edge_all[:, 2 * patch_size : 2 * patch_size + code_width]
    edge_qout = edge_all[:, 2 * patch_size + code_width :]
    pixel_rows = lax.dynamic_slice_in_dim(pixel_all, part * own_rows, own_rows, 0)
    chosen_all, one_hot_all, lane_mask_all = pick_codes(code_all, book_wide, code_width)
    chosen_low_all = chosen_all.astype(jnp.bfloat16)
    chosen = lax.dynamic_slice_in_dim(chosen_all, part * own_rows, own_rows, 0)
    one_hot = lax.dynamic_slice_in_dim(one_hot_all, part * own_rows, own_rows, 0)
    lane_mask = lax.dynamic_slice_in_dim(lane_mask_all, part * own_rows, own_rows, 0)
    chosen_low = chosen.astype(jnp.bfloat16)
    begin = matmul_trans(chosen_low_all, edge_qout)
    decoded, dec_saved = block_forward(begin, part, wide_all[1], narrow_all[1], norms[4:8], allowed)
    final = layer_norm(decoded, norms[8], norms[9]).astype(jnp.bfloat16)
    predict = matmul_plain(final, edge_pix)
    error = predict - pixel_rows.astype(jnp.float32)
    pixel_mask = valid_rows.astype(jnp.float32)
    loss_pix = jnp.sum(pixel_mask * (error * error + jnp.abs(error))) / count
    grad_pred = (pixel_mask * (2.0 * error + jnp.sign(error)) / count).astype(jnp.bfloat16)
    grad_pixw = matmul_outer(final, grad_pred)
    _, final_back = jax.vjp(layer_norm, decoded, norms[8], norms[9])
    grad_dec, gain_last, offset_last = final_back(matmul_trans(grad_pred, edge_pix))
    grad_begin, dec_wide, dec_narrow, dec_gains = block_backward(
        grad_dec, wide_all[1], narrow_all[1], norms[4:8], allowed, dec_saved, groups
    )
    grad_begin_low = grad_begin.astype(jnp.bfloat16)
    grad_qout = matmul_outer(grad_begin_low, chosen_low)
    start = matmul_trans(pixel_all, edge_in)
    encoded, enc_saved = block_forward(start, part, wide_all[0], narrow_all[0], norms[0:4], allowed)
    encoded_low = encoded.astype(jnp.bfloat16)
    latent = matmul_plain(encoded_low, edge_qin)
    gap = chosen - latent
    loss_part = loss_pix + (1.0 + commitment) * jnp.sum(gap * gap) / latent_total
    grad_latent = (
        matmul_plain(grad_begin_low, edge_qout) - 2.0 * commitment * gap / latent_total
    ).astype(jnp.bfloat16)
    fold = lane_mask.shape[1] // code_width
    gap_wide = jnp.where(lane_mask, jnp.tile(2.0 * gap / latent_total, (1, fold)), 0.0)
    gap_high = gap_wide.astype(jnp.bfloat16)
    gap_rest = gap_wide - gap_high.astype(jnp.float32)
    gap_middle = gap_rest.astype(jnp.bfloat16)
    gap_low = (gap_rest - gap_middle.astype(jnp.float32)).astype(jnp.bfloat16)
    grad_book = (
        matmul_outer(one_hot, gap_high) + matmul_outer(one_hot, gap_middle)
    ) + matmul_outer(one_hot, gap_low)
    grad_qin = matmul_outer(encoded_low, grad_latent)
    grad_start, enc_wide, enc_narrow, enc_gains = block_backward(
        matmul_trans(grad_latent, edge_qin), wide_all[0], narrow_all[0], norms[0:4], allowed, enc_saved, groups
    )
    grad_inw = matmul_outer(grad_start.astype(jnp.bfloat16), pixel_rows)
    grads = (
        enc_wide, dec_wide, enc_narrow, dec_narrow,
        jnp.concatenate([grad_inw, grad_pixw, grad_qin, grad_qout], axis=1),
        grad_book,
    )
    norm_grad = jnp.concatenate([enc_gains, dec_gains, gain_last[None], offset_last[None]], axis=0)
    return (grads, norm_grad, loss_part)


def place():
    img_at = lax.axis_index("img")
    band_at = lax.axis_index("band")
    return img_at, band_at, band_at // 4, (band_at // 2) % 2, band_at % 2


def neighbours():
    img_at, band_at, y_at, x_at, c_at = place()
    return (
        (img_at, band_at + 1 - 2 * c_at),
        (img_at, band_at + 2 - 4 * x_at),
        (img_at, band_at + 4 - 8 * y_at),
    )


def peers():
    img_at, band_at = place()[:2]
    found = [((img_at + step) % 4, band_at) for step in range(1, 4)]
    return found + [(img_at, (band_at + step) % 8) for step in range(1, 8)]


def meet(others):
    barrier = pltpu.get_barrier_semaphore()
    for other in others:
        pl.semaphore_signal(barrier, inc=1, device_id=other, device_id_type=MESH)
    pl.semaphore_wait(barrier, len(others))


def far_copy(src, dst, send, recv, target):
    return pltpu.make_async_remote_copy(
        src_ref=src, dst_ref=dst, send_sem=send, recv_sem=recv, device_id=target, device_id_type=MESH
    )


class Everywhere:
    def __init__(self, name, agenda, own_ref, img_buf, band_buf, send, recv, result_ref):
        self.name, self.agenda, self.done = name, agenda, False
        self.own, self.img_buf, self.band_buf, self.result = own_ref, img_buf, band_buf, result_ref
        self.send, self.recv = send, recv

    def begin(self):
        img_at, band_at = place()[:2]
        self.img_buf[img_at] = self.own[...]
        copies = [
            far_copy(
                self.own, self.img_buf.at[img_at], self.send.at[step], self.recv.at[step], ((img_at + step) % 4, band_at)
            )
            for step in range(1, 4)
        ]
        self.agenda.launch((self.name, 0), copies, [], self.middle)
        self.agenda.spend(0.5)

    def middle(self):
        img_at, band_at = place()[:2]
        buf = self.img_buf
        self.result[...] = (buf[0] + buf[1]) + (buf[2] + buf[3])
        self.band_buf[band_at] = self.result[...]
        copies = [
            far_copy(
                self.result, self.band_buf.at[band_at], self.send.at[3 + step], self.recv.at[3 + step],
                (img_at, (band_at + step) % 8),
            )
            for step in range(1, 8)
        ]
        self.agenda.launch((self.name, 1), copies, [], self.end)
        self.agenda.spend(1.0)

    def end(self):
        total = self.band_buf[0]
        for k in range(1, 8):
            total = total + self.band_buf[k]
        self.result[...] = total
        self.done = True

    def until(self):
        self.agenda.until(lambda: self.done)


LINK, CORE, LAG = 90e3, 500e3, 0.8
SPREAD = {"f01": 3, "f12": 4, "f23": 3, "b10": 3, "b21": 4, "b32": 3}
TOWARDS = (
    {"b10": 3, "b21": 2, "b32": 1},
    {"f01": 1, "b21": 2, "b32": 1},
    {"f01": 1, "f12": 2, "b32": 1},
    {"f01": 1, "f12": 2, "f23": 3},
)


def z_loads(table, size):
    return [(link, count * size) for link, count in table.items()]


class Agenda:
    def __init__(self):
        self.now, self.free, self.flying = 0.0, {}, {}

    def launch(self, key, copies, loads, then):
        done = self.now
        for link, size in loads:
            begin = max(self.now, self.free.get(link, 0.0))
            self.free[link] = begin + size / (CORE if link == "c" else LINK) + 0.4
            done = max(done, self.free[link])
        for copy in copies:
            copy.start()
        self.flying[key] = (done + LAG, copies, then)

    def land(self, key):
        done, copies, then = self.flying.pop(key)
        self.now = max(self.now, done) + 0.5
        for copy in copies:
            copy.wait()
        then()

    def spend(self, time):
        self.now += time

    def tick(self):
        while self.flying:
            key = min(self.flying, key=lambda name: self.flying[name][0])
            if self.flying[key][0] > self.now:
                return
            self.land(key)

    def until(self, test):
        while not test():
            self.land(min(self.flying, key=lambda name: self.flying[name][0]))


class Gather:
    def __init__(self, name, agenda, pieces, near, z_send, z_recv, p_send, p_recv):
        self.name, self.agenda, self.pieces = name, agenda, pieces
        self.near, self.z_send, self.z_recv, self.p_send, self.p_recv = near, z_send, z_recv, p_send, p_recv
        self.done = set()

    def launch(self, p, k):
        img_at, band_at, y_at, x_at, c_at = place()
        over_c, over_x, over_y = neighbours()
        shard, whole, first, count, z_last = self.pieces[p]
        rows = pl.ds(first, count)
        width = shard.shape[1]
        size = count * max(width, 128) * 2
        lanes = width // 256 * 128
        found, loads = [], []
        here, own = whole.at[img_at, y_at, x_at, c_at, rows], shard.at[rows]
        if z_last and k < 2:
            for half in range(2):
                span = pl.ds(lanes, width - lanes) if half else pl.ds(0, lanes)
                along_y = (k == 0) == (half == 0)
                if k == 0:
                    src, dst = shard.at[rows, span], whole.at[img_at, y_at, x_at, c_at, rows, span]
                elif half == 0:
                    src = dst = whole.at[img_at, :, x_at, c_at, rows, span]
                else:
                    src = dst = whole.at[img_at, y_at, :, c_at, rows, span]
                slot = 2 * k + half
                target = over_y if along_y else over_x
                found.append(far_copy(src, dst, self.p_send.at[p, slot], self.p_recv.at[p, slot], target))
                loads.append(("y" if along_y else "x", (1 + k) * size))
            if k == 0:
                found.append(pltpu.make_async_copy(own, here, self.near.at[p]))
        elif z_last and k == 2:
            part = whole.at[img_at, :, :, c_at, rows]
            found = [
                far_copy(part, part, self.z_send.at[p, step], self.z_recv.at[p, step], ((img_at + step) % 4, band_at))
                for step in range(1, 4)
            ]
            loads = z_loads(SPREAD, 8 * size)
        elif k == 0:
            found = [
                far_copy(own, here, self.z_send.at[p, step], self.z_recv.at[p, step], ((img_at + step) % 4, band_at))
                for step in range(1, 4)
            ]
            found.append(pltpu.make_async_copy(own, here, self.near.at[p]))
            loads = z_loads(SPREAD, 2 * size)
        elif k == 3:
            part = whole.at[:, :, :, c_at, rows]
            found = [far_copy(part, part, self.p_send.at[p, 4], self.p_recv.at[p, 4], over_c)]
            loads = [("c", 16 * size)]
        else:
            for half in range(2):
                span = pl.ds(lanes, width - lanes) if half else pl.ds(0, lanes)
                if lanes == 0 and half == 0:
                    continue
                if k == 1:
                    part = whole.at[:, y_at, x_at, c_at, rows, span]
                elif half == 0:
                    part = whole.at[:, :, x_at, c_at, rows, span]
                else:
                    part = whole.at[:, y_at, :, c_at, rows, span]
                slot = 2 * (k - 1) + half
                along_y = (k == 1) == (half == 0)
                target = over_y if along_y else over_x
                found.append(far_copy(part, part, self.p_send.at[p, slot], self.p_recv.at[p, slot], target))
                loads.append(("y" if along_y else "x", 4 * k * size))

        def then():
            if k < 3:
                self.launch(p, k + 1)
            else:
                self.done.add(p)

        self.agenda.launch((self.name, p), found, loads, then)

    def begin(self, first, last):
        for p in range(first, last):
            self.launch(p, 0)

    def until(self, *wanted):
        self.agenda.until(lambda: all(p in self.done for p in wanted))


def gather_sems(count):
    dma = pltpu.SemaphoreType.DMA
    return [dma((count,)), dma((count, 4)), dma((count, 4)), dma((count, 5)), dma((count, 5))]


class Reduce:
    def __init__(
        self, agenda, slots, wait_z, full, pair, first_a, first_b, second_a, second_b, ours, last,
        near, p_send, p_recv, z_send, z_recv, free, free_z,
    ):
        self.agenda, self.slots, self.wait_z = agenda, slots, wait_z
        self.full, self.pair, self.ours, self.last = full, pair, ours, last
        self.first, self.second = (first_a, first_b), (second_a, second_b)
        self.near, self.p_send, self.p_recv, self.z_send, self.z_recv = near, p_send, p_recv, z_send, z_recv
        self.free, self.free_z = free, free_z
        self.pieces, self.flying, self.events, self.at_event = [], {}, [], 0
        self.queue, self.opened = [], 0

    def plan(self, pieces):
        self.pieces = pieces
        seen = [0] * 4
        for p, piece in enumerate(pieces):
            piece["slot"] = p % self.slots
            piece["place"] = p % (self.wait_z + 1)
            piece["order"] = seen[piece["z"]]
            seen[piece["z"]] += 1
        for piece in pieces:
            piece["again"] = piece["order"] + 2 < seen[piece["z"]]
        self.opened, self.passed, self.ended = 0, set(), set()
        self.ready = {""}

    def feed(self):
        while self.opened < len(self.pieces):
            p = self.opened
            if self.pieces[p]["needs"] not in self.ready or (p >= self.slots and p - self.slots not in self.passed):
                return
            self.opened += 1
            self.open(p)

    def allow(self, name):
        self.ready.add(name)
        self.feed()

    def rows(self, p):
        return pl.ds(0, self.pieces[p]["rows"])

    def open(self, p):
        piece = self.pieces[p]
        slot, rows = piece["slot"], self.rows(p)
        c_at = place()[4]
        over_c = neighbours()[0]
        if p >= self.slots:
            for k in range(3):
                pl.semaphore_wait(self.free.at[slot, k], 1)
        landing = self.pair.at[slot, :, :, rows]
        send, recv = self.p_send.at[slot, 0], self.p_recv.at[slot, 0]
        if "stage" in piece:
            stage, first, count = piece["stage"], piece["first"], piece["rows"]
            copies = []
            for n in range(4):
                theirs = pl.ds(pl.multiple_of(first + (2 * n + 1 - c_at) * count, 8), count)
                ours = pl.ds(pl.multiple_of(first + (2 * n + c_at) * count, 8), count)
                spot = 0 if n == 0 else 4 + n
                copies.append(
                    far_copy(
                        stage.at[theirs], self.pair.at[slot, n // 2, n % 2, rows], self.p_send.at[slot, spot],
                        self.p_recv.at[slot, spot], over_c,
                    )
                )
                copies.append(
                    pltpu.make_async_copy(
                        stage.at[ours], self.full.at[slot, n // 2, n % 2, c_at, rows], self.near.at[slot, n]
                    )
                )
        else:
            piece["emit"](self.full, slot)
            copies = [far_copy(self.full.at[slot, :, :, 1 - c_at, rows], landing, send, recv, over_c)]
        size = piece["rows"] * self.full.shape[5] * 4
        self.agenda.launch(("r", p, 0), copies, [("c", 4 * size)], lambda: self.step(0, p))

    def step(self, k, p):
        piece = self.pieces[p]
        slot, rows, z = piece["slot"], self.rows(p), piece["z"]
        size = piece["rows"] * self.full.shape[5] * 4
        img_at, band_at, y_at, x_at, c_at = place()
        over_c, over_x, over_y = neighbours()
        full, half = self.full, self.full.shape[5] // 2
        low, high = pl.ds(0, half), pl.ds(half, half)
        tiles = piece["rows"] // 16

        def tile(n):
            return pl.ds(pl.multiple_of(n % tiles * 16, 16), 16)

        if k == 0:
            def add(n, carry):
                y, x = n // (2 * tiles), n // tiles % 2
                full[slot, y, x, c_at, tile(n)] += self.pair[slot, y, x, tile(n)]
                return carry
            lax.fori_loop(0, 4 * tiles, add, 0)
            parts = (full.at[slot, :, 1 - x_at, c_at, rows, low], full.at[slot, 1 - y_at, :, c_at, rows, high])
            landings = [self.first[n].at[slot, :, rows] for n in range(2)]
            targets = (over_x, over_y)
        elif k == 1:
            def add(n, carry):
                w = n // tiles
                full[slot, w, x_at, c_at, tile(n), low] += self.first[0][slot, w, tile(n)]
                full[slot, y_at, w, c_at, tile(n), high] += self.first[1][slot, w, tile(n)]
                return carry
            lax.fori_loop(0, 2 * tiles, add, 0)
            parts = (full.at[slot, 1 - y_at, x_at, c_at, rows, low], full.at[slot, y_at, 1 - x_at, c_at, rows, high])
            landings = [self.second[n].at[slot, rows] for n in range(2)]
            targets = (over_y, over_x)
        if k < 2:
            copies = [
                far_copy(
                    parts[n], landings[n], self.p_send.at[slot, 1 + 2 * k + n], self.p_recv.at[slot, 1 + 2 * k + n],
                    targets[n],
                )
                for n in range(2)
            ]
            load = 2 * size if k == 0 else size
            self.agenda.launch(("r", p, 1 + k), copies, [("x", load), ("y", load)], lambda: self.step(k + 1, p))
            return
        spot, order = piece["place"], piece["order"] % 2
        mine = self.ours.at[spot, rows]
        owner = (z, band_at)

        def hop(n):
            return far_copy(mine, self.last.at[order, n, rows], self.z_send.at[spot], self.z_recv.at[order, n], owner)

        if k == 2:
            self.agenda.until(lambda: p < self.wait_z + 1 or p - self.wait_z - 1 in self.ended)

            def add(n, carry):
                self.ours[spot, tile(n), low] = full[slot, y_at, x_at, c_at, tile(n), low] + self.second[0][slot, tile(n)]
                self.ours[spot, tile(n), high] = full[slot, y_at, x_at, c_at, tile(n), high] + self.second[1][slot, tile(n)]
                return carry
            lax.fori_loop(0, tiles, add, 0)

            assert p < self.wait_z + 1 or p - self.wait_z - 1 in self.ended

            @pl.when(img_at != z)
            def _():
                if piece["order"] >= 2:
                    pl.semaphore_wait(self.free_z.at[z, order], 1)
                hop((img_at + 3 - z) % 4).start()

            if p + self.slots < len(self.pieces):
                for n, other in enumerate((over_c, over_x, over_y)):
                    pl.semaphore_signal(self.free.at[slot, n], inc=1, device_id=other, device_id_type=MESH)
            self.passed.add(p)
            self.agenda.launch(("r", p, 3), [], z_loads(TOWARDS[z], 2 * size), lambda: self.step(3, p))
            self.feed()
            return

        @pl.when(img_at != z)
        def _():
            hop((img_at + 3 - z) % 4).wait_send()

        @pl.when(img_at == z)
        def _():
            for n in range(3):
                hop(n).wait_recv()

            def add(n, carry):
                piece["out"][tile(n)] = (self.ours[spot, tile(n)] + self.last[order, 0, tile(n)]) + (
                    self.last[order, 1, tile(n)] + self.last[order, 2, tile(n)]
                )
                return carry
            lax.fori_loop(0, tiles, add, 0)
            if piece["again"]:
                for n in range(1, 4):
                    pl.semaphore_signal(
                        self.free_z.at[z, order], inc=1, device_id=((img_at + n) % 4, band_at), device_id_type=MESH
                    )

        self.ended.add(p)


def reduce_scratch(slots, wait_z, rows, width):
    f32 = jnp.float32
    dma = pltpu.SemaphoreType.DMA
    half = width // 2
    return [
        pltpu.VMEM((slots, 2, 2, 2, rows, width), f32),
        pltpu.VMEM((slots, 2, 2, rows, width), f32),
        pltpu.VMEM((slots, 2, rows, half), f32),
        pltpu.VMEM((slots, 2, rows, half), f32),
        pltpu.VMEM((slots, rows, half), f32),
        pltpu.VMEM((slots, rows, half), f32),
        pltpu.VMEM((wait_z + 1, rows, width), f32),
        pltpu.VMEM((2, 3, rows, width), f32),
        dma((slots, 4)),
        dma((slots, 8)), dma((slots, 8)),
        dma((wait_z + 1,)), dma((2, 3)),
        pltpu.SemaphoreType.REGULAR((slots, 3)),
        pltpu.SemaphoreType.REGULAR((4, 2)),
    ]


class ReduceSmall:
    def __init__(self, agenda, grads, shares, own, pair, first_a, first_b, second_a, second_b, last, near, p_send, p_recv, z_send, z_recv):
        self.agenda, self.done = agenda, set()
        self.grads, self.shares, self.own, self.pair = grads, shares, own, pair
        self.first, self.second, self.last = (first_a, first_b), (second_a, second_b), last
        self.near, self.p_send, self.p_recv, self.z_send, self.z_recv = near, p_send, p_recv, z_send, z_recv
        self.flying = {}

    def start(self, p, copies, loads, k):
        size = self.own[p].shape[3] * self.own[p].shape[4] * 4
        self.agenda.launch(("s", p), copies, [(link, n * size) for link, n in loads], lambda: self.step(p, k))

    def open(self, p):
        c_at = place()[4]
        over_c = neighbours()[0]
        self.start(p, [
            far_copy(self.grads[p].at[:, :, :, 1 - c_at], self.pair[p], self.p_send.at[p, 0], self.p_recv.at[p, 0], over_c),
            pltpu.make_async_copy(self.grads[p].at[:, :, :, c_at], self.own[p], self.near.at[p]),
        ], [("c", 16)], 0)

    def step(self, p, k):
        img_at, band_at, y_at, x_at, c_at = place()
        over_c, over_x, over_y = neighbours()
        own = self.own[p]
        rows = own.shape[3]
        span = (pl.ds(0, rows // 2), pl.ds(rows // 2, rows // 2))

        def send(parts, landings, targets, slot):
            copies = [
                far_copy(parts[n], landings[n], self.p_send.at[p, slot + n], self.p_recv.at[p, slot + n], targets[n])
                for n in range(2)
            ]
            self.start(p, copies, [("x", 8 >> k), ("y", 8 >> k)], k + 1)

        if k == 0:
            own[...] += self.pair[p][...]
            send(
                (own.at[:, :, 1 - x_at, span[0]], own.at[:, 1 - y_at, :, span[1]]),
                (self.first[0][p], self.first[1][p]), (over_x, over_y), 1,
            )
        elif k == 1:
            own[:, :, x_at, span[0]] += self.first[0][p][...]
            own[:, y_at, :, span[1]] += self.first[1][p][...]
            send(
                (own.at[:, 1 - y_at, x_at, span[0]], own.at[:, y_at, 1 - x_at, span[1]]),
                (self.second[0][p], self.second[1][p]), (over_y, over_x), 3,
            )
        elif k == 2:
            own[:, y_at, x_at, span[0]] += self.second[0][p][...]
            own[:, y_at, x_at, span[1]] += self.second[1][p][...]
            copies = []
            for n in range(1, 4):
                target = (img_at + n) % 4
                copies.append(
                    far_copy(
                        own.at[target, y_at, x_at], self.last[p].at[n - 1], self.z_send.at[p, n], self.z_recv.at[p, n],
                        (target, band_at),
                    )
                )
            self.start(p, copies, z_loads(SPREAD, 2), 3)
        else:
            last = self.last[p]
            self.done.add(p)
            self.shares[p][...] = (own[img_at, y_at, x_at] + last[0]) + (last[1] + last[2])


def reduce_small_scratch(shapes):
    f32 = jnp.float32
    dma = pltpu.SemaphoreType.DMA
    count = len(shapes)
    groups = [
        [(4, 2, 2, r, w) for r, w in shapes],
        [(4, 2, 2, r, w) for r, w in shapes],
        [(4, 2, r // 2, w) for r, w in shapes],
        [(4, 2, r // 2, w) for r, w in shapes],
        [(4, r // 2, w) for r, w in shapes],
        [(4, r // 2, w) for r, w in shapes],
        [(3, r, w) for r, w in shapes],
    ]
    return [pltpu.VMEM(shape, f32) for group in groups for shape in group] + [
        dma((count,)), dma((count, 5)), dma((count, 5)), dma((count, 4)), dma((count, 4)),
    ]


def dot_nn(a, b):
    return lax.dot_general(a, b, (((1,), (0,)), ((), ())), preferred_element_type=jnp.float32)


def dot_nt(a, b):
    return lax.dot_general(a, b, (((1,), (1,)), ((), ())), preferred_element_type=jnp.float32)


def dot_tn(a, b):
    return lax.dot_general(a, b, (((0,), (0,)), ((), ())), preferred_element_type=jnp.float32)


def norm_parts(h):
    centred = h - jnp.mean(h, axis=-1, keepdims=True)
    rate = lax.rsqrt(jnp.mean(centred * centred, axis=-1, keepdims=True) + norm_eps)
    return centred * rate, rate


def norm_back(grad, h, gain):
    shape, rate = norm_parts(h)
    inner = grad * gain
    back = rate * (
        inner
        - jnp.mean(inner, axis=-1, keepdims=True)
        - shape * jnp.mean(inner * shape, axis=-1, keepdims=True)
    )
    return (
        back,
        jnp.sum(grad * shape, axis=0, keepdims=True),
        jnp.sum(grad, axis=0, keepdims=True),
    )


STEP = 256


def at(k, start=0):
    return pl.ds(pl.multiple_of(start + k * STEP, STEP), STEP)


def lanes_at(k, size, start=0):
    return pl.ds(pl.multiple_of(start + k * size, 128), size)


def loop(first, last, body):
    def step(k, carry):
        body(k)
        return carry

    lax.fori_loop(first, last, step, 0)


class Block:
    def __init__(self, base, source, first_w, small, refs):
        names = (
            "wide", "narrow", "norms", "q_extra", "k_extra", "hidden", "normed", "q_buf", "kv", "mixed_in", "wide_in",
            "middle", "second", "slope", "grad_out", "grad_low", "mid_low", "gatt", "dkv", "dkv_in", "soft", "x_send",
            "x_recv", "x_free",
        )
        for name, ref in zip(names, refs, strict=True):
            setattr(self, name, ref)
        self.base, self.source, self.first_w, self.small = base, source, first_w, small
        self.part = place()[4]
        self.total, self.own = self.kv.shape[0], self.q_buf.shape[0]
        self.width = self.q_buf.shape[1]
        self.offset = pl.multiple_of(self.part * self.own, self.own)
        self.chunks = self.own // STEP
        lane_head = lax.broadcasted_iota(jnp.int32, (1, 128), 1) // HDIM
        self.pick = [jnp.where(lane_head == k, 1.0, 0.0).astype(jnp.bfloat16) for k in range(2)]

    def slope_rows(self, f, k):
        return pl.ds(pl.multiple_of(f * self.own + k * STEP, STEP), STEP)

    def gain(self, k):
        return self.norms[pl.ds(self.base + k, 1), :]

    def add_small(self, row, value):
        self.small[pl.ds(row, 1), :] += value

    def add_loss(self, value):
        first_lane = lax.broadcasted_iota(jnp.int32, (1, self.width), 1) == 0
        self.add_small(6, jnp.where(first_lane, value, 0.0))

    def enter(self, first, last):
        def body(n):
            k = (n + self.chunks * (1 + self.part)) % (self.total // STEP)
            h = dot_nt(self.source(k), self.first_w())
            self.hidden[at(n % self.chunks)] = h
            shape, _ = norm_parts(h)
            self.normed[at(k)] = (shape * self.gain(0) + self.gain(1)).astype(jnp.bfloat16)

        loop(first, last, body)

    def make_kv(self, first, last):
        def body(k):
            self.kv[at(k)] = dot_nt(self.normed[at(k)], self.wide[self.width : 3 * self.width]).astype(jnp.bfloat16)

        loop(first, last, body)

    def make_q(self):
        def body(k):
            q = dot_nt(self.normed[at(k, self.offset)], self.wide[: self.width]).astype(jnp.bfloat16)
            self.q_buf[at(k)] = (q.astype(jnp.float32) * HDIM**-0.5).astype(jnp.bfloat16)

        loop(0, self.chunks, body)

    def scores(self, p, k, rows, k_cat):
        q_cat = jnp.concatenate([self.q_buf[rows, lanes_at(p, 128)] * self.pick[k], self.q_extra[rows]], axis=1)
        return dot_nt(q_cat, k_cat)

    def key_columns(self, p):
        return jnp.concatenate([self.kv[:, lanes_at(p, 128)], self.k_extra[...]], axis=1)

    def attend(self, first, last):
        head_lane = lax.broadcasted_iota(jnp.int32, (STEP, 128), 1)

        def pair(p):
            k_cat = self.key_columns(p)
            v_pair = self.kv[:, lanes_at(p, 128, self.width)]

            def body(j):
                rows = at(j)
                mixed = None
                for k in range(2):
                    scores = self.scores(p, k, rows, k_cat)
                    peak = jnp.max(scores, axis=-1, keepdims=True)
                    expo = jnp.exp(scores - peak)
                    total = jnp.sum(expo, axis=-1, keepdims=True)
                    prob = expo * (1.0 / total)
                    level = peak + jnp.log(total)
                    self.soft[rows] = jnp.where(head_lane == 2 * p + k, level, self.soft[rows])
                    term = dot_nn(prob.astype(jnp.bfloat16), v_pair * self.pick[k])
                    mixed = term if mixed is None else mixed + term
                self.mixed_in[rows, lanes_at(p, 128)] = mixed.astype(jnp.bfloat16)

            loop(0, self.chunks, body)

        loop(first, last, pair)

    def after_attention(self):
        def body(k):
            rows = at(k)
            mid = self.hidden[at(k)] + dot_nn(self.mixed_in[rows, : self.width], self.narrow[: self.width])
            self.middle[rows] = mid
            shape, _ = norm_parts(mid)
            self.second[rows] = (shape * self.gain(2) + self.gain(3)).astype(jnp.bfloat16)
            self.grad_out[rows] = mid

        loop(0, self.chunks, body)

    def mlp(self, first, last):
        width = self.width

        def body(n):
            f, k = n // self.chunks, n % self.chunks
            rows = at(k)
            u = dot_nt(self.second[rows], self.wide[lanes_at(3 + f, width)])
            squared = u * u
            bend = jnp.tanh(0.7978845608028654 * (u + 0.044715 * squared * u))
            low = (0.5 * u * (1.0 + bend)).astype(jnp.bfloat16)
            self.mixed_in[rows, lanes_at(1 + f, width)] = low
            self.slope[self.slope_rows(f, k)] = 0.5 * (1.0 + bend) + (0.5 * u) * (1.0 - bend * bend) * (
                0.7978845608028654 * (1.0 + (3.0 * 0.044715) * squared)
            )
            self.grad_out[rows] += dot_nn(low, self.narrow[lanes_at(1 + f, width)])

        loop(first * self.chunks, last * self.chunks, body)

    def mlp_back(self, first, last):
        width = self.width

        def body(k):
            rows = at(k)
            gy = self.grad_low[rows]

            def feature_step(f, acc):
                ga = dot_nt(gy, self.narrow[lanes_at(1 + f, width)])
                low = (ga * self.slope[self.slope_rows(f, k)]).astype(jnp.bfloat16)
                self.wide_in[rows, lanes_at(3 + f, width)] = low
                return acc + dot_nn(low, self.wide[lanes_at(3 + f, width)])

            grad_second = lax.fori_loop(0, 4, feature_step, jnp.zeros((STEP, width), jnp.float32))
            back, g_gain, g_offset = norm_back(grad_second, self.middle[rows], self.gain(2))
            self.add_small(2, g_gain)
            self.add_small(3, g_offset)
            grad_mid = back + self.grad_out[rows]
            self.grad_out[rows] = grad_mid
            low = grad_mid.astype(jnp.bfloat16)
            self.mid_low[rows] = low
            self.gatt[rows] = dot_nt(low, self.narrow[:width]).astype(jnp.bfloat16)

        loop(first, last, body)

    def attend_back(self, first, last):
        head_lane = lax.broadcasted_iota(jnp.int32, (self.own, 128), 1)
        lane_head = lax.broadcasted_iota(jnp.int32, (1, 128), 1) // HDIM
        rows, bf16 = slice(None), jnp.bfloat16

        def head(h):
            p = h // 2
            pick = jnp.where(lane_head == h % 2, 1.0, 0.0).astype(bf16)
            k_pair = self.kv[:, lanes_at(p, 128)]
            g_rows = self.gatt[rows, lanes_at(p, 128)] * pick
            q_rows = self.q_buf[rows, lanes_at(p, 128)] * pick
            level = jnp.sum(jnp.where(head_lane == h, self.soft[...], 0.0), axis=-1, keepdims=True)
            scores = dot_nt(
                jnp.concatenate([q_rows, self.q_extra[...]], axis=1), jnp.concatenate([k_pair, self.k_extra[...]], axis=1)
            )
            prob = jnp.exp(scores - level)
            d_prob = dot_nt(g_rows, self.kv[:, lanes_at(p, 128, self.width)])
            dot_row = jnp.sum(prob * d_prob, axis=-1, keepdims=True)
            d_score = (prob * (d_prob - dot_row)).astype(bf16)
            dq = (dot_nn(d_score, k_pair * pick) * HDIM**-0.5).astype(bf16)
            self.dkv[p, 0] += dot_tn(d_score, q_rows)
            self.dkv[p, 1] += dot_tn(prob.astype(bf16), g_rows)
            self.wide_in[rows, lanes_at(p, 128)] = self.wide_in[rows, lanes_at(p, 128)] + dq

        self.dkv[pl.ds(first, 2)] = jnp.zeros((2,) + self.dkv.shape[1:], jnp.float32)
        self.wide_in[:, pl.ds(pl.multiple_of(128 * first, 128), 256)] = jnp.zeros((self.own, 256), bf16)
        loop(2 * first, 2 * last, head)

    def swap(self, p):
        theirs = pl.ds(pl.multiple_of((1 - self.part) * self.own, self.own), self.own)
        return far_copy(
            self.dkv.at[p, :, theirs], self.dkv_in.at[p], self.x_send.at[p], self.x_recv.at[p], neighbours()[0]
        )

    def attend_back_all(self, opening):
        if not opening:
            pl.semaphore_wait(self.x_free, 1)

        def half(n):
            self.attend_back(2 * n, 2 * n + 2)
            for p in range(2):
                self.swap(2 * n + p).start()

        loop(0, 2, half)

    def swap_start(self, first, opening):
        if not opening and first == 0:
            pl.semaphore_wait(self.x_free, 1)
        for p in range(first, first + 2):
            self.swap(p).start()

    def swap_finish(self, closing):
        for p in range(4):
            self.swap(p).wait()

        def body(n):
            p, k = n // self.chunks, n % self.chunks
            for side in range(2):
                total = self.dkv[p, side, at(k, self.offset)] + self.dkv_in[p, side, at(k)]
                self.wide_in[at(k), lanes_at(p, 128, (1 + side) * self.width)] = total.astype(jnp.bfloat16)

        loop(0, 4 * self.chunks, body)
        if not closing:
            pl.semaphore_signal(self.x_free, inc=1, device_id=neighbours()[0], device_id_type=MESH)

    def leave_rows(self, k):
        rows = at(k)
        grad_normed = dot_nn(self.wide_in[rows, : 3 * self.width], self.wide[: 3 * self.width])
        back, g_gain, g_offset = norm_back(grad_normed, self.hidden[at(k)], self.gain(0))
        self.add_small(0, g_gain)
        self.add_small(1, g_offset)
        return (back + self.grad_out[rows]).astype(jnp.bfloat16)

    def wide_product(self, first, count):
        if first < 3 * self.width:
            right = self.normed[pl.ds(self.offset, self.own)]
        else:
            right = self.second[...]
        return dot_tn(self.wide_in[:, first : first + count], right)

    def narrow_product(self, first, count):
        right = self.mid_low if first < self.width else self.grad_low
        return dot_tn(self.mixed_in[:, first : first + count], right[...])


def pieces_of(first, count, border):
    if first < border < first + count:
        return [(first, border - first), (border, first + count - border)]
    return [(first, count)]


def block_scratch(total_rows, own_rows):
    width = 512
    f32, bf16 = jnp.float32, jnp.bfloat16
    shapes = [
        ((own_rows, width), f32),
        ((total_rows, width), bf16),
        ((own_rows, width), bf16),
        ((total_rows, 2 * width), bf16),
        ((own_rows, 5 * width), bf16),
        ((own_rows, 7 * width), bf16),
        ((own_rows, width), f32),
        ((own_rows, width), bf16),
        ((4 * own_rows, width), f32),
        ((own_rows, width), f32),
        ((own_rows, width), bf16),
        ((own_rows, width), bf16),
        ((own_rows, width), bf16),
        ((4, 2, total_rows, 128), f32),
        ((4, 2, own_rows, 128), f32),
        ((own_rows, 128), f32),
    ]
    return [pltpu.VMEM(shape, dtype) for shape, dtype in shapes] + [
        pltpu.SemaphoreType.DMA((4,)), pltpu.SemaphoreType.DMA((4,)), pltpu.SemaphoreType.REGULAR
    ]


DEC_NARROW = ((0, 80, False),)
ENC_WIDE = ((0, 112, False),)
ENC_NARROW = ((0, 80, False),)
DEC_ORDER = (("n", 3), ("n", 1), ("n", 2), ("n", 0), ("w", 3), ("w", 2), ("w", 0), ("w", 1))
ENC_ORDER = (("n", 3), ("n", 1), ("n", 0), ("w", 3), ("w", 2), ("w", 0), ("w", 1), ("n", 2))


def step_kernel(slots, latent_total, *refs):
    shards, slab, code, kinds, norms = refs[:6], refs[6], refs[7], refs[8], refs[9]
    refs = refs[10:]
    share_wide_dec, share_narrow_dec, share_wide, share_narrow, share_edge, share_book, small_all = refs[:7]
    land_wide_dec, land_narrow_dec, land_wide, land_narrow = refs[7:11]
    refs = refs[11:]
    sems_dec, sems_enc, red, red_small, refs = refs[:5], refs[5:10], refs[10:25], refs[25:44], refs[44:]
    (book, edge, slab_all, code_all, tally, tally_all, t_img, t_band, e_near, e_send, e_recv, t_send, t_recv) = refs[:13]
    refs = refs[1:]
    (code_row, spread, cross, g_pixw, g_qout, g_qin, g_inw, g_edge, g_book) = refs[12:21]
    (small_dec, small_enc, small_own, s_img, s_band, s_send, s_recv, load_sem, wide, narrow) = refs[21:31]
    q_extra, k_extra = refs[31:33]
    scratch = refs[33:]
    f32, bf16 = jnp.float32, jnp.bfloat16
    img_at, band_at, y_at, x_at, c_at = place()
    chip_at = band_at // 2
    over_c = neighbours()[0]
    width = wide.shape[1]
    common = (wide, narrow, norms, q_extra, k_extra) + tuple(scratch)

    def edge_columns(first, count):
        return edge[:, :, :, :, :, first : first + count].reshape(width, count)

    def e_in():
        return edge_columns(0, 256)

    def e_pix():
        return edge_columns(256, 256)

    def e_qin():
        return edge_columns(512, 128)

    def e_qout():
        return edge_columns(640, 128)

    def pixel_rows(k, first=0, start=0):
        return slab_all[pl.ds(start + 2 * k, 2), :, first : first + 256].reshape(STEP, 256)

    own_band = 4 * c_at
    dec = Block(4, lambda k: spread[at(k)], e_qout, small_dec, common)
    enc = Block(0, pixel_rows, e_in, small_enc, common)
    agenda = Agenda()
    dec_pieces = [(shards[0], book, 0, 64, False), (shards[1], edge, 0, 16, False)]
    dec_pieces += [(shards[2], land_wide_dec, 96, 16, True)]
    dec_pieces += [(shards[2], land_wide_dec, 0, 48, False), (shards[2], land_wide_dec, 48, 48, False)]
    dec_pieces += [(shards[3], land_narrow_dec, first, count, last) for first, count, last in DEC_NARROW]
    gather = Gather("d", agenda, dec_pieces, *sems_dec)
    enc_pieces = [(shards[4], land_wide, first, count, last) for first, count, last in ENC_WIDE]
    enc_pieces += [(shards[5], land_narrow, first, count, last) for first, count, last in ENC_NARROW]
    gather_enc = Gather("e", agenda, enc_pieces, *sems_enc)
    count_all = Everywhere("n", agenda, tally, t_img, t_band, t_send, t_recv, tally_all)
    spots = lax.broadcasted_iota(jnp.int32, (1, 4), 1)
    kind = jnp.sum(jnp.where(spots == chip_at, kinds[...], 0).astype(f32), axis=1, keepdims=True)
    meet(peers())
    agenda.spend(3.0)
    gather.begin(0, 5)
    exchange = []
    for step in range(1, 4):
        chip = (chip_at + step) % 4
        target = (img_at, 2 * chip + c_at)
        here = band_at
        exchange.append(far_copy(slab.at[chip], slab_all.at[here], e_send.at[0, step], e_recv.at[0, step], target))
        exchange.append(far_copy(code.at[chip], code_all.at[here], e_send.at[1, step], e_recv.at[1, step], target))
    exchange.append(pltpu.make_async_copy(slab.at[chip_at], slab_all.at[band_at], e_near.at[0]))
    exchange.append(pltpu.make_async_copy(code.at[chip_at], code_all.at[band_at], e_near.at[1]))

    def exchange_landed():
        late = []
        for k, dst in enumerate((slab_all, code_all)):
            for chip in range(4):
                part = dst.at[2 * chip + c_at]
                late.append(far_copy(part, part, e_send.at[k, 4 + chip], e_recv.at[k, 4 + chip], over_c))
        agenda.launch("x2", late, [("c", 4e5)], lambda: arrived.append(1))

    arrived = []
    agenda.launch("x1", exchange, [("x", 4e5), ("y", 4e5)], exchange_landed)
    agenda.spend(1.0)
    segment_lane = lax.broadcasted_iota(jnp.int32, (enc.total, 128), 1)
    segment = jnp.where(kind < 0.5, 0, lax.broadcasted_iota(jnp.int32, (enc.total, 128), 0) // (enc.total // 4))
    k_extra[...] = jnp.where(segment_lane == segment, 1.0, 0.0).astype(bf16)
    segment_lane = lax.broadcasted_iota(jnp.int32, (enc.own, 128), 1)
    segment = lax.broadcasted_iota(jnp.int32, (enc.own, 128), 0) + enc.offset
    segment = jnp.where(kind < 0.5, 0, segment // (enc.total // 4))
    q_extra[...] = jnp.where((segment_lane < 4) & (segment_lane != segment), -(2.0**30), 0.0).astype(bf16)
    for ref in (small_dec, small_enc, g_pixw, g_qout, g_qin, g_inw):
        ref[...] = jnp.zeros(ref.shape, f32)
    agenda.spend(2.0)
    agenda.tick()
    agenda.until(lambda: arrived)
    def code_column(k, start=0):
        return jnp.concatenate(
            [jnp.transpose(jnp.broadcast_to(code_all[start + 2 * k + n], (8, 128)))[:, 0:1] for n in range(2)], axis=0
        )

    for n in range(4):
        code_row[:, pl.ds(128 * n, 128)] = code_all[own_band + n]

    def pick_codes(k):
        rows = at(k)
        code_here = code_column(k)
        picks = lax.broadcasted_iota(jnp.int32, (STEP, 512), 1)
        found = jnp.zeros((STEP, 128), f32)
        for z in range(4):
            hot = jnp.where(picks + 512 * z == code_here // 4, 1.0, 0.0).astype(bf16)
            found += dot_nn(hot, book[z].reshape(512, 128))
        lanes = lax.broadcasted_iota(jnp.int32, (STEP, 128), 1) // 32
        spread[rows] = jnp.where(lanes == code_here % 4, found, 0.0).astype(bf16)

    lane = lax.broadcasted_iota(jnp.int32, (4, 128, 256), 2)
    flags = slab_all[pl.ds(own_band, 4), :, 128:384].astype(f32)
    tally[...] = jnp.full(tally.shape, jnp.sum(jnp.where(lane < 64, 0.0, flags)))
    agenda.spend(1.0)
    agenda.tick()
    count_all.begin()
    gather.begin(5, len(dec_pieces))
    gather.until(0)
    agenda.tick()
    loop(0, dec.total // STEP, pick_codes)
    agenda.spend(4.0)
    agenda.tick()
    gather.until(1)
    dec.enter(0, dec.total // STEP)
    agenda.spend(1.9)
    agenda.tick()

    def fetch(landed, ref, sem):
        rows = landed.shape[4]

        def body(n):
            src = landed.at[n // 8, (n // 4) % 2, (n // 2) % 2, n % 2]
            pltpu.make_async_copy(src, ref.at[pl.ds(pl.multiple_of(n * rows, 16), rows)], sem).start()

        loop(0, 32, body)
        return pltpu.make_async_copy(ref, ref, sem)

    reduce = Reduce(agenda, *slots, *red)
    tail = ReduceSmall(
        agenda, (g_edge, g_book), (share_edge, share_book),
        *[red_small[2 * n : 2 * n + 2] for n in range(7)], *red_small[14:],
    )

    def emit_wide(blk, z, full, slot):
        values = [blk.wide_product(*span) for span in pieces_of(896 * z, 896, 3 * width)]
        value = values[0] if len(values) == 1 else jnp.concatenate(values, axis=0)
        full[slot] = value.reshape(2, 2, 2, 112, width)
        agenda.spend(0.6)

    def emit_narrow(blk, z, full, slot):
        values = [blk.narrow_product(*span) for span in pieces_of(640 * z, 640, width)]
        value = values[0] if len(values) == 1 else jnp.concatenate(values, axis=0)
        full[slot, :, :, :, :80] = value.reshape(2, 2, 2, 80, width)
        agenda.spend(0.5)

    pieces = []
    for name, blk, out_wide, out_narrow, order in (
        ("dec", dec, share_wide_dec, share_narrow_dec, DEC_ORDER), ("enc", enc, share_wide, share_narrow, ENC_ORDER)
    ):
        for kind_of, z in order:
            if kind_of == "n":
                needs = name + str(int(z == 0))
                pieces.append(dict(emit=functools.partial(emit_narrow, blk, z), z=z, rows=80, out=out_narrow, needs=needs))
                continue
            piece = dict(z=z, rows=112, out=out_wide, needs=name + str(1 + (z < 2)))
            if name == "dec" and z < 2:
                piece.update(stage=dec.slope, first=896 * z)
            else:
                piece.update(emit=functools.partial(emit_wide, blk, z))
            pieces.append(piece)
    reduce.plan(pieces)

    def spend(time):
        agenda.spend(time)
        agenda.tick()

    def decoder_head(k):
        rows = at(k)
        out = dec.grad_out[rows]
        shape, _ = norm_parts(out)
        final = (shape * norms[pl.ds(8, 1), :] + norms[pl.ds(9, 1), :]).astype(bf16)
        error = dot_nn(final, e_pix()) - pixel_rows(k, 0, own_band).astype(f32)
        lane = lax.broadcasted_iota(jnp.int32, (STEP, 256), 1)
        counted = jnp.where(lane < 192, pltpu.roll(pixel_rows(k, 128, own_band).astype(f32), 192, 1), 0.0)
        number = tally_all[0:1, 0:1]
        dec.add_loss(jnp.sum(counted * (error * error + jnp.abs(error))) / number)
        sign = jnp.where(error > 0.0, 1.0, jnp.where(error < 0.0, -1.0, 0.0))
        grad_pred = (counted * (2.0 * error + sign) / number).astype(bf16)
        g_pixw[...] += dot_tn(final, grad_pred)
        back, g_gain, g_offset = norm_back(dot_nt(grad_pred, e_pix()), out, norms[pl.ds(8, 1), :])
        dec.add_small(4, g_gain)
        dec.add_small(5, g_offset)
        dec.grad_out[rows] = back
        dec.grad_low[rows] = back.astype(bf16)

    def encoder_head(k):
        rows = at(k)
        low = enc.grad_out[rows].astype(bf16)
        lanes = lax.broadcasted_iota(jnp.int32, (STEP, 128), 1) // 32
        mine = lanes == code_column(k, own_band) % 4
        gap = jnp.where(mine, spread[at(k, enc.offset)].astype(f32) - dot_nn(low, e_qin()), 0.0)
        enc.add_loss((1.0 + commitment) * jnp.sum(gap * gap) / latent_total)
        grad_latent = jnp.where(mine, cross[rows] - 2.0 * commitment * gap / latent_total, 0.0).astype(bf16)
        g_qin[...] += dot_tn(low, grad_latent)
        back = dot_nt(grad_latent, e_qin())
        enc.grad_out[rows] = back
        enc.grad_low[rows] = back.astype(bf16)
        gap = 2.0 * gap / latent_total
        high = gap.astype(bf16)
        left = gap - high.astype(f32)
        between = left.astype(bf16)
        enc.gatt[rows, :384] = jnp.concatenate([high, between, (left - between.astype(f32)).astype(bf16)], axis=1)

    def book_rows(k):
        picks = lax.broadcasted_iota(jnp.int32, (STEP, enc.own), 0) + k * STEP
        hot = jnp.where(picks == code_row[...] // 4, 1.0, 0.0).astype(bf16)
        summed = dot_nn(hot, enc.gatt[:, :384])
        value = (summed[:, :128] + summed[:, 128:256]) + summed[:, 256:]
        g_book[k // 2, k % 2] = value.reshape(2, 2, 64, 128)

    def decoder_leave(k):
        low = dec.leave_rows(k)
        cross[at(k)] = dot_nn(low, e_qout())
        g_qout[...] += dot_tn(low, spread[at(k, dec.offset)])

    def encoder_leave(k):
        g_inw[...] += dot_tn(enc.leave_rows(k), pixel_rows(k, 0, own_band))

    gather_enc.begin(0, len(enc_pieces))
    gather.until(2, 3, 4)
    fetch(land_wide_dec, wide, load_sem.at[0]).wait()
    spend(2.0)
    dec.make_kv(0, dec.total // STEP)
    dec.make_q()
    spend(2.9)
    dec.attend(0, 4)
    spend(11.1)
    gather.until(*range(5, len(dec_pieces)))
    fetched = fetch(land_narrow_dec, narrow, load_sem.at[1])
    agenda.spend(1.0)
    fetched.wait()
    dec.after_attention()
    spend(1.1)
    dec.mlp(0, 4)
    spend(5.6)
    count_all.until()
    loop(0, dec.chunks, decoder_head)
    agenda.spend(2.0)
    reduce.allow("dec0")
    agenda.tick()
    dec.mlp_back(0, dec.chunks)
    agenda.spend(6.1)
    reduce.allow("dec1")
    agenda.tick()
    dec.attend_back_all(True)
    spend(15.8)
    gather_enc.until(*range(len(enc_pieces)))
    fetched = fetch(land_narrow, narrow, load_sem.at[1])
    dec.swap_finish(False)
    agenda.spend(2.0)
    for z in range(2):
        values = [dec.wide_product(*span) for span in pieces_of(896 * z, 896, 3 * width)]
        dec.slope[pl.ds(896 * z, 896)] = values[0] if len(values) == 1 else jnp.concatenate(values, axis=0)
    agenda.spend(1.2)
    reduce.allow("dec2")
    agenda.tick()
    loop(0, dec.chunks, decoder_leave)
    fetched_wide = fetch(land_wide, wide, load_sem.at[0])
    spend(2.0)
    emitted = 1 + max(p for p in range(8) if "emit" in pieces[p])
    staged = [p for p in range(8) if "stage" in pieces[p]]
    agenda.until(lambda: reduce.opened >= emitted)
    enc.enter(0, enc.total // STEP)
    spend(1.9)
    fetched_wide.wait()
    enc.make_kv(0, enc.total // STEP)
    enc.make_q()
    fetched.wait()
    spend(2.9)
    enc.attend(0, 4)
    spend(11.1)
    enc.after_attention()
    spend(1.1)
    agenda.until(lambda: reduce.opened > max(staged) and not any(("r", p, 0) in agenda.flying for p in staged))
    enc.mlp(0, 4)
    spend(5.6)
    loop(0, enc.chunks, encoder_head)
    agenda.spend(2.0)
    reduce.allow("enc0")
    agenda.tick()
    loop(0, 8, book_rows)
    tail.open(1)
    spend(2.0)
    enc.mlp_back(0, enc.chunks)
    agenda.spend(6.1)
    reduce.allow("enc1")
    agenda.tick()
    enc.attend_back(0, 2)
    enc.swap_start(0, False)
    spend(7.9)
    enc.attend_back(2, 4)
    enc.swap_start(2, False)
    spend(7.9)
    enc.swap_finish(True)
    agenda.spend(2.0)
    reduce.allow("enc2")
    agenda.tick()
    loop(0, enc.chunks, encoder_leave)
    agenda.spend(2.0)

    def all_groups(value):
        value = value + pltpu.roll(value, 64, 1)
        return value + pltpu.roll(value, 32, 1)

    lane = lax.broadcasted_iota(jnp.int32, (width, 128), 1)
    mixed = jnp.where(lane < 64, g_inw[:, 128:], jnp.where(lane < 96, all_groups(g_qin[...]), all_groups(g_qout[...])))
    for first, value in ((0, g_inw[:, :128]), (128, mixed), (256, g_pixw[:, :128]), (384, g_pixw[:, 128:])):
        g_edge[:, :, :, :, :, pl.ds(first, 128)] = value.reshape(4, 2, 2, 2, 16, 128)
    tail.open(0)
    agenda.until(lambda: len(reduce.ended) == len(pieces) and len(tail.done) == 2)
    shares = (share_wide_dec, share_narrow_dec, share_wide, share_narrow, share_edge, share_book)
    squares = sum(jnp.sum(share[...] * share[...]) for share in shares)
    lane = lax.broadcasted_iota(jnp.int32, (8, width), 1)
    row = lax.broadcasted_iota(jnp.int32, (8, width), 0)
    small_own[0] = small_enc[...]
    small_own[1] = jnp.where((row == 7) & (lane == 0), squares, small_dec[...])
    sum_all = Everywhere("a", agenda, small_own, s_img, s_band, s_send, s_recv, small_all)
    sum_all.begin()
    sum_all.until()


def train_step(shards, slab, code, kinds, norms, latent_total, total_rows, own_rows):
    width = 512
    slots = (4, 4)
    f32, bf16, int32 = jnp.float32, jnp.bfloat16, jnp.int32
    any_space = pl.BlockSpec(memory_space=pl.ANY)
    vmem = pl.BlockSpec(memory_space=pltpu.VMEM)
    shape = jax.ShapeDtypeStruct
    out_shape = [
        shape((112, width), f32), shape((80, width), f32), shape((112, width), f32), shape((80, width), f32),
        shape((16, width), f32), shape((64, 128), f32), shape((2, 8, width), f32),
    ]
    out_shape += [shape((4, 2, 2, 2) + s.shape, s.dtype) for s in shards[2:]]
    dma = pltpu.SemaphoreType.DMA
    mem = pltpu.VMEM
    scratch = gather_sems(5 + len(DEC_NARROW)) + gather_sems(len(ENC_WIDE) + len(ENC_NARROW))
    scratch += reduce_scratch(*slots, 112, width) + reduce_small_scratch([(16, width), (64, 128)])
    scratch += [
        mem((4, 2, 2, 2, 64, 128), bf16), mem((4, 2, 2, 2, 16, 768), bf16),
        mem((8, 128, 384), bf16), mem((8, 1, 128), int32), mem((8, 128), f32), mem((8, 128), f32),
        mem((4, 8, 128), f32), mem((8, 8, 128), f32),
        dma((2,)), dma((2, 8)), dma((2, 8)), dma((11,)), dma((11,)),
        mem((1, own_rows), int32), mem((total_rows, 128), bf16),
        mem((own_rows, 128), f32),
        mem((width, 256), f32), mem((width, 128), f32), mem((width, 128), f32), mem((width, 256), f32),
        mem((4, 2, 2, 2, 16, width), f32), mem((4, 2, 2, 2, 64, 128), f32),
        mem((8, width), f32), mem((8, width), f32), mem((2, 8, width), f32),
        mem((4, 2, 8, width), f32), mem((8, 2, 8, width), f32), dma((11,)), dma((11,)),
        dma((2,)), mem((7 * width, width), bf16), mem((5 * width, width), bf16),
        mem((own_rows, 128), bf16), mem((total_rows, 128), bf16),
    ]
    scratch += block_scratch(total_rows, own_rows)
    return pl.pallas_call(
        functools.partial(step_kernel, slots, latent_total),
        out_shape=out_shape,
        in_specs=[any_space] * 8 + [vmem] * 2,
        out_specs=[vmem] * 7 + [any_space] * 4,
        scratch_shapes=scratch,
        compiler_params=pltpu.CompilerParams(collective_id=0, has_side_effects=True, vmem_limit_bytes=(639 << 20) // 10),
        name="train_step",
    )(*shards, slab, code, kinds, norms)


def moments(gradient, first_old, second_old):
    first_new = beta_first * first_old + (1.0 - beta_first) * gradient
    second_new = beta_second * second_old + (1.0 - beta_second) * gradient * gradient
    return (first_new, second_new, first_new / (jnp.sqrt(second_new) + adam_eps))


def rotated_update(weight, gradient, first_old, second_old, basis_stack):
    turned = jnp.einsum("rld,lde->rle", gradient, basis_stack, precision=highest)
    first_new, second_new, direction = moments(turned, first_old, second_old)
    turned_back = jnp.einsum("rle,lde->rld", direction, basis_stack, precision=highest)
    return (weight - rate_matrix * (turned_back + weight_decay * weight), first_new, second_new)


def plain_update(weight, gradient, first_old, second_old):
    first_new, second_new, direction = moments(gradient, first_old, second_old)
    return (weight - rate_vector * (direction + weight_decay * weight), first_new, second_new)


def update_kernel(*refs):
    count = 20
    ins, refs = refs[:count], refs[count:]
    outs, held, sem = refs[:13], refs[13 : 13 + count], refs[13 + count]
    loads = [pltpu.make_async_copy(src, dst, sem.at[k]) for k, (src, dst) in enumerate(zip(ins, held))]
    for load in loads:
        load.start()
    for load in loads:
        load.wait()
    refs = held + outs
    wide_0, wide_1, narrow_0, narrow_1, edge, small = refs[:6]
    wide, narrow, edge_set, norm_set = refs[6:9], refs[9:12], refs[12:15], refs[15:18]
    bases, basis_edge = refs[18:20]
    new_wide, new_narrow, new_edge, new_norms, scalars = refs[20:23], refs[23:26], refs[26:29], refs[29:32], refs[32]
    norm_grad = jnp.concatenate([small[0, 0:4], small[1, 0:6]], axis=0)
    squares = small[1, 7:8, 0:1] + jnp.sum(norm_grad * norm_grad)
    grad_norm = jnp.sqrt(squares)
    factor = jnp.minimum(1.0, clip_level / grad_norm)
    scalars[0:1] = jnp.broadcast_to(grad_norm, (1, 128))
    scalars[1:2] = jnp.broadcast_to(factor, (1, 128))
    scalars[2:3] = jnp.broadcast_to(small[0, 6:7, 0:1] + small[1, 6:7, 0:1], (1, 128))
    scalars[3:8] = jnp.zeros((5, 128), jnp.float32)

    def halves(value):
        high = value.astype(jnp.bfloat16)
        return high, (value - high.astype(jnp.float32)).astype(jnp.bfloat16)

    def product(left, right, dot):
        (high, low), (right_high, right_low) = halves(left), right
        return dot(high, right_high) + (dot(high, right_low) + dot(low, right_high))

    def turn(weight, gradient, first_old, second_old, basis):
        right = halves(basis)
        turned = product(gradient, right, dot_nn)
        first_new, second_new, direction = moments(turned, first_old, second_old)
        back = product(direction, right, dot_nt)
        return weight - rate_matrix * (back + weight_decay * weight), first_new, second_new

    for k, (olds, news, grads) in enumerate(
        ((wide, new_wide, (wide_0, wide_1)), (narrow, new_narrow, (narrow_0, narrow_1)))
    ):
        for layer in range(2):
            found = turn(
                olds[0][:, layer], factor * grads[layer][...], olds[1][:, layer], olds[2][:, layer], bases[2 * k + layer]
            )
            for ref, value in zip(news, found):
                ref[:, layer] = value
    packed = edge[...]
    grad_edge = jnp.concatenate([packed[:, :192], packed[:, 256:448], packed[:, 192:256]], axis=1)
    found = turn(edge_set[0][...], factor * grad_edge, edge_set[1][...], edge_set[2][...], basis_edge[...])
    for ref, value in zip(new_edge, found):
        ref[...] = value
    found = plain_update(norm_set[0][...], factor * norm_grad, norm_set[1][...], norm_set[2][...])
    for ref, value in zip(new_norms, found):
        ref[...] = value


def update_all(grads, wide, narrow, edge, norms, bases, basis_edge):
    vmem = pl.BlockSpec(memory_space=pltpu.VMEM)
    shape = jax.ShapeDtypeStruct
    sets = wide + narrow + edge + norms
    return pl.pallas_call(
        update_kernel,
        out_shape=[shape(a.shape, a.dtype) for a in sets] + [shape((8, 128), jnp.float32)],
        in_specs=[pl.BlockSpec(memory_space=pl.ANY)] * (len(grads) + len(sets) + 2),
        out_specs=[vmem] * (len(sets) + 1),
        scratch_shapes=[pltpu.VMEM(a.shape, a.dtype) for a in (*grads, *sets, bases, basis_edge)]
        + [pltpu.SemaphoreType.DMA((len(grads) + len(sets) + 2,))],
        compiler_params=pltpu.CompilerParams(vmem_limit_bytes=63 << 20),
        name="update_all",
    )(*grads, *sets, bases, basis_edge)


def body(
    pixels,
    valid,
    codes,
    image_kind,
    w_wide,
    w_narrow,
    w_edge,
    codebook,
    norms,
    bases,
    basis_edge,
    m_wide,
    v_wide,
    m_narrow,
    v_narrow,
    m_edge,
    v_edge,
    m_code,
    v_code,
    m_norm,
    v_norm,
):
    band_count = lax.axis_size("band")
    band_index = lax.axis_index("band")
    row_count = pixels.shape[2]
    length = row_count * band_count
    batch_count = pixels.shape[0]
    group = band_count // batch_count
    row = band_index // group
    part = band_index % group
    own_rows = length // group
    groups = [[k * group + j for j in range(group)] for k in range(batch_count)]
    layer_count = w_wide.shape[1]
    code_width = codebook.shape[1]
    latent_total = batch_count * lax.axis_size("img") * length * code_width
    both = ("img", "band")

    direct = band_count == 8 and lax.axis_size("img") == 4 and batch_count == 4
    shards = [w_wide[:, l].astype(jnp.bfloat16) for l in range(layer_count)]
    shards += [w_narrow[:, l].astype(jnp.bfloat16) for l in range(layer_count)]
    shards += [w_edge.astype(jnp.bfloat16), codebook.astype(jnp.bfloat16).reshape(-1, 4 * code_width)]
    slab = jnp.concatenate([pixels[:, 0], valid[:, 0].astype(jnp.bfloat16)], axis=2)
    patch_size = pixels.shape[3]
    if direct:
        edge = shards[4]
        gap = jnp.zeros((edge.shape[0], 64), edge.dtype)
        qin = edge[:, 2 * patch_size : 2 * patch_size + code_width]
        qout = edge[:, 2 * patch_size + code_width :]
        shards[4] = jnp.concatenate(
            [edge[:, :patch_size], gap, edge[:, patch_size : 2 * patch_size], gap] + [qin] * 4 + [qout] * 4, axis=1
        )
        out = train_step(
            [shards[k] for k in (5, 4, 1, 3, 0, 2)], slab, codes, image_kind.reshape(1, -1), norms, latent_total, length, own_rows
        )
        new = update_all(
            (out[2], out[0], out[3], out[1], out[4], out[6]), (w_wide, m_wide, v_wide), (w_narrow, m_narrow, v_narrow),
            (w_edge, m_edge, v_edge), (norms, m_norm, v_norm), bases, basis_edge,
        )
        scalars = new[12]
        grad_norm, factor, loss_total = scalars[0, 0], scalars[1, 0], scalars[2, 0]
        new_code = plain_update(codebook, factor * out[5].reshape(-1, code_width), m_code, v_code)
        return tuple(new[:9]) + new_code + tuple(new[9:12]) + (grad_norm, loss_total)
    wholes = [lax.all_gather(shard, both, axis=0, tiled=True) for shard in shards]
    count = lax.psum(jnp.sum(valid.astype(jnp.float32)), both)

    def whole_row(local):
        everywhere = lax.all_gather(local, "band", axis=0)
        chosen_row = lax.dynamic_index_in_dim(everywhere, row, axis=1, keepdims=False)
        return chosen_row.reshape((length,) + local.shape[2:])

    slab_all = whole_row(slab)
    code_all = whole_row(codes[:, 0])
    kind = lax.dynamic_index_in_dim(image_kind[:, 0], row, 0, keepdims=False)
    span = jnp.where(kind == 0, length, length // 4)
    positions = jnp.arange(length, dtype=jnp.int32)
    gathered = (wholes[:2], wholes[2:4], wholes[4], wholes[5])
    pixel_all = slab_all[:, :patch_size]
    valid_rows = lax.dynamic_slice_in_dim(slab_all, part * own_rows, own_rows, 0)[:, patch_size:]
    own_positions = part * own_rows + jnp.arange(own_rows, dtype=jnp.int32)
    allowed = (own_positions // span)[:, None] == (positions // span)[None, :]
    local_grads, norm_sum, loss_sum = row_step(
        gathered, norms, pixel_all, valid_rows, code_all, part, allowed, count, latent_total, groups
    )
    shares = [lax.psum_scatter(g, both, scatter_dimension=0, tiled=True) for g in local_grads]
    squares = sum(jnp.sum(share * share) for share in shares)
    norm_total, square_total, loss_total = lax.psum((norm_sum, squares, loss_sum), both)
    grad_sum = (
        jnp.stack([shares[0], shares[1]], axis=1),
        jnp.stack([shares[2], shares[3]], axis=1),
        shares[4],
        shares[5].reshape(-1, code_width),
    )
    grad_norm = jnp.sqrt(square_total + jnp.sum(norm_total * norm_total))
    factor = jnp.minimum(1.0, clip_level / grad_norm)
    grad_wide, grad_narrow, grad_edge, grad_book = grad_sum
    new_wide, new_m_wide, new_v_wide = rotated_update(
        w_wide, factor * grad_wide, m_wide, v_wide, bases[:layer_count]
    )
    new_narrow, new_m_narrow, new_v_narrow = rotated_update(
        w_narrow, factor * grad_narrow, m_narrow, v_narrow, bases[layer_count:]
    )
    new_edge, new_m_edge, new_v_edge = rotated_update(
        w_edge[:, None],
        factor * grad_edge[:, None],
        m_edge[:, None],
        v_edge[:, None],
        basis_edge[None],
    )
    new_book, new_m_code, new_v_code = plain_update(codebook, factor * grad_book, m_code, v_code)
    new_norms, new_m_norm, new_v_norm = plain_update(norms, factor * norm_total, m_norm, v_norm)
    return (
        new_wide,
        new_m_wide,
        new_v_wide,
        new_narrow,
        new_m_narrow,
        new_v_narrow,
        new_edge[:, 0],
        new_m_edge[:, 0],
        new_v_edge[:, 0],
        new_book,
        new_m_code,
        new_v_code,
        new_norms,
        new_m_norm,
        new_v_norm,
        grad_norm,
        loss_total,
    )


def solution(mesh):
    in_specs = (
        P(None, "img", "band", None),
        P(None, "img", "band", None),
        P(None, "img", "band"),
        P(None, "img"),
        P(("img", "band"), None, None),
        P(("img", "band"), None, None),
        P(("img", "band"), None),
        P(("img", "band"), None),
        P(),
        P(),
        P(),
        P(("img", "band"), None, None),
        P(("img", "band"), None, None),
        P(("img", "band"), None, None),
        P(("img", "band"), None, None),
        P(("img", "band"), None),
        P(("img", "band"), None),
        P(("img", "band"), None),
        P(("img", "band"), None),
        P(),
        P(),
    )
    out_specs = (
        P(("img", "band"), None, None),
        P(("img", "band"), None, None),
        P(("img", "band"), None, None),
        P(("img", "band"), None, None),
        P(("img", "band"), None, None),
        P(("img", "band"), None, None),
        P(("img", "band"), None),
        P(("img", "band"), None),
        P(("img", "band"), None),
        P(("img", "band"), None),
        P(("img", "band"), None),
        P(("img", "band"), None),
        P(),
        P(),
        P(),
        P(),
        P(),
    )
    return jax.shard_map(body, mesh=mesh, in_specs=in_specs, out_specs=out_specs, check_vma=False)
```

```python
import functools

import jax
import jax.numpy as jnp
from jax import lax
from jax.experimental import pallas as pl
from jax.experimental.pallas import tpu as pltpu
from jax.sharding import PartitionSpec as P

HEADS = 8
HDIM = 64
MESH = pl.DeviceIdType.MESH


norm_eps = 1e-05
adam_eps = 1e-08
clip_level = 0.001
beta_first = 0.5
beta_second = 0.6
rate_matrix = 0.02
rate_vector = 0.3
weight_decay = 0.01
commitment = 0.25
masked_score = -1000000000.0
highest = lax.Precision.HIGHEST


def matmul_plain(first_op, second_op):
    return jnp.dot(first_op, second_op, preferred_element_type=jnp.float32)


def matmul_trans(first_op, second_op):
    return lax.dot_general(
        first_op, second_op, (((1,), (1,)), ((), ())), preferred_element_type=jnp.float32
    )


def matmul_outer(first_op, second_op):
    return lax.dot_general(
        first_op, second_op, (((0,), (0,)), ((), ())), preferred_element_type=jnp.float32
    )


def layer_norm(hidden, scale_gain, offset):
    centred = hidden - jnp.mean(hidden, axis=-1, keepdims=True)
    spread = jnp.mean(centred * centred, axis=-1, keepdims=True)
    return centred * lax.rsqrt(spread + norm_eps) * scale_gain + offset


def gelu_tanh(inputs):
    return (
        0.5
        * inputs
        * (1.0 + jnp.tanh(0.7978845608028654 * (inputs + 0.044715 * inputs * inputs * inputs)))
    )


def split_heads(matrix):
    return matrix.reshape(matrix.shape[0], HEADS, HDIM)


def head_scores(q_heads, k_heads, allowed):
    scores = jnp.einsum(
        "qhd,khd->hqk", q_heads, k_heads, preferred_element_type=jnp.float32
    ) * HDIM ** (-0.5)
    return jnp.where(allowed[None], scores, masked_score)


def attend(queries, key_rows, value_rows, allowed):
    scores = head_scores(split_heads(queries), split_heads(key_rows), allowed)
    score_peak = jnp.max(scores, axis=-1, keepdims=True)
    expo = jnp.exp(scores - score_peak)
    total = jnp.sum(expo, axis=-1, keepdims=True)
    softmaxed = (expo / total).astype(jnp.bfloat16)
    attended = jnp.einsum(
        "hqk,khd->qhd", softmaxed, split_heads(value_rows), preferred_element_type=jnp.float32
    )
    return (
        attended.reshape(queries.shape[0], -1).astype(jnp.bfloat16),
        score_peak + jnp.log(total),
    )


def attend_back(queries, key_rows, value_rows, allowed, log_total, grad_out):
    q_heads = split_heads(queries)
    k_heads = split_heads(key_rows)
    v_heads = split_heads(value_rows)
    g_heads = split_heads(grad_out)
    softmaxed = jnp.exp(head_scores(q_heads, k_heads, allowed) - log_total)
    grad_soft = jnp.einsum("qhd,khd->hqk", g_heads, v_heads, preferred_element_type=jnp.float32)
    row_dot = jnp.sum(softmaxed * grad_soft, axis=-1, keepdims=True)
    grad_scores = (softmaxed * (grad_soft - row_dot)).astype(jnp.bfloat16)
    scale = HDIM ** (-0.5)
    grad_q = (
        jnp.einsum("hqk,khd->qhd", grad_scores, k_heads, preferred_element_type=jnp.float32) * scale
    )
    grad_k = (
        jnp.einsum("hqk,qhd->khd", grad_scores, q_heads, preferred_element_type=jnp.float32) * scale
    )
    grad_v = jnp.einsum(
        "hqk,qhd->khd", softmaxed.astype(jnp.bfloat16), g_heads, preferred_element_type=jnp.float32
    )
    return (
        grad_q.reshape(queries.shape[0], -1),
        grad_k.reshape(key_rows.shape[0], -1),
        grad_v.reshape(key_rows.shape[0], -1),
    )


def block_forward(hidden_all, part, wide_rows, narrow_rows, gain_rows, allowed):
    model_width = hidden_all.shape[1]
    own_rows = allowed.shape[0]
    normed_all = layer_norm(hidden_all, gain_rows[0], gain_rows[1]).astype(jnp.bfloat16)
    hidden = lax.dynamic_slice_in_dim(hidden_all, part * own_rows, own_rows, 0)
    normed = lax.dynamic_slice_in_dim(normed_all, part * own_rows, own_rows, 0)
    queries = matmul_trans(normed, wide_rows[:model_width]).astype(jnp.bfloat16)
    key_rows = matmul_trans(normed_all, wide_rows[model_width : 2 * model_width]).astype(jnp.bfloat16)
    value_rows = matmul_trans(normed_all, wide_rows[2 * model_width : 3 * model_width]).astype(jnp.bfloat16)
    attended, log_total = attend(queries, key_rows, value_rows, allowed)
    middle = hidden + matmul_plain(attended, narrow_rows[:model_width])
    second = layer_norm(middle, gain_rows[2], gain_rows[3]).astype(jnp.bfloat16)
    upper_in = matmul_trans(second, wide_rows[3 * model_width :])
    active = gelu_tanh(upper_in).astype(jnp.bfloat16)
    result = middle + matmul_plain(active, narrow_rows[model_width:])
    return (
        result,
        (hidden, normed, queries, key_rows, value_rows, attended, log_total, middle, second, upper_in, active),
    )


def block_backward(grad_out, wide_rows, narrow_rows, gain_rows, allowed, saved, groups):
    (hidden, normed, queries, key_rows, value_rows, attended, log_total, middle, second, upper_in, active) = saved
    model_width = hidden.shape[1]
    grad_y = grad_out.astype(jnp.bfloat16)
    grad_down = matmul_outer(active, grad_y)
    grad_active = matmul_trans(grad_y, narrow_rows[model_width:])
    grad_upper = jax.vjp(gelu_tanh, upper_in)[1](grad_active)[0].astype(jnp.bfloat16)
    grad_up = matmul_outer(grad_upper, second)
    _, second_back = jax.vjp(layer_norm, middle, gain_rows[2], gain_rows[3])
    grad_mid, gain_two, offset_two = second_back(
        matmul_plain(grad_upper, wide_rows[3 * model_width :])
    )
    grad_mid = grad_mid + grad_out
    grad_attn = grad_mid.astype(jnp.bfloat16)
    grad_outproj = matmul_outer(attended, grad_attn)
    grad_att = matmul_trans(grad_attn, narrow_rows[:model_width]).astype(jnp.bfloat16)
    grad_q, grad_keys, grad_values = attend_back(
        queries, key_rows, value_rows, allowed, log_total, grad_att
    )
    grad_k = lax.psum_scatter(grad_keys, "band", scatter_dimension=0, tiled=True, axis_index_groups=groups)
    grad_v = lax.psum_scatter(grad_values, "band", scatter_dimension=0, tiled=True, axis_index_groups=groups)
    grad_mixed = jnp.concatenate([grad_q, grad_k, grad_v], axis=1).astype(jnp.bfloat16)
    grad_qkv = matmul_outer(grad_mixed, normed)
    _, first_back = jax.vjp(layer_norm, hidden, gain_rows[0], gain_rows[1])
    grad_in, gain_one, offset_one = first_back(
        matmul_plain(grad_mixed, wide_rows[: 3 * model_width])
    )
    gain_grads = jnp.stack([gain_one, offset_one, gain_two, offset_two], axis=0)
    return (
        grad_in + grad_mid,
        jnp.concatenate([grad_qkv, grad_up], axis=0),
        jnp.concatenate([grad_outproj, grad_down], axis=0),
        gain_grads,
    )


def pick_codes(code_rows, book_wide, code_width):
    fold = book_wide.shape[1] // code_width
    one_hot = (
        (code_rows // fold)[:, None] == jnp.arange(book_wide.shape[0], dtype=jnp.int32)[None, :]
    ).astype(jnp.bfloat16)
    lane_fold = jnp.arange(book_wide.shape[1], dtype=jnp.int32)[None, :] // code_width
    lane_mask = (code_rows % fold)[:, None] == lane_fold
    spread = jnp.where(lane_mask, matmul_plain(one_hot, book_wide), 0.0)
    chosen = sum(spread[:, k * code_width : (k + 1) * code_width] for k in range(fold))
    return chosen, one_hot, lane_mask


def row_step(gathered, norms, pixel_all, valid_rows, code_all, part, allowed, count, latent_total, groups):
    wide_all, narrow_all, edge_all, book_wide = gathered
    patch_size = pixel_all.shape[1]
    code_width = edge_all.shape[1] // 2 - patch_size
    own_rows = allowed.shape[0]
    edge_in = edge_all[:, :patch_size]
    edge_pix = edge_all[:, patch_size : 2 * patch_size]
    edge_qin = edge_all[:, 2 * patch_size : 2 * patch_size + code_width]
    edge_qout = edge_all[:, 2 * patch_size + code_width :]
    pixel_rows = lax.dynamic_slice_in_dim(pixel_all, part * own_rows, own_rows, 0)
    chosen_all, one_hot_all, lane_mask_all = pick_codes(code_all, book_wide, code_width)
    chosen_low_all = chosen_all.astype(jnp.bfloat16)
    chosen = lax.dynamic_slice_in_dim(chosen_all, part * own_rows, own_rows, 0)
    one_hot = lax.dynamic_slice_in_dim(one_hot_all, part * own_rows, own_rows, 0)
    lane_mask = lax.dynamic_slice_in_dim(lane_mask_all, part * own_rows, own_rows, 0)
    chosen_low = chosen.astype(jnp.bfloat16)
    begin = matmul_trans(chosen_low_all, edge_qout)
    decoded, dec_saved = block_forward(begin, part, wide_all[1], narrow_all[1], norms[4:8], allowed)
    final = layer_norm(decoded, norms[8], norms[9]).astype(jnp.bfloat16)
    predict = matmul_plain(final, edge_pix)
    error = predict - pixel_rows.astype(jnp.float32)
    pixel_mask = valid_rows.astype(jnp.float32)
    loss_pix = jnp.sum(pixel_mask * (error * error + jnp.abs(error))) / count
    grad_pred = (pixel_mask * (2.0 * error + jnp.sign(error)) / count).astype(jnp.bfloat16)
    grad_pixw = matmul_outer(final, grad_pred)
    _, final_back = jax.vjp(layer_norm, decoded, norms[8], norms[9])
    grad_dec, gain_last, offset_last = final_back(matmul_trans(grad_pred, edge_pix))
    grad_begin, dec_wide, dec_narrow, dec_gains = block_backward(
        grad_dec, wide_all[1], narrow_all[1], norms[4:8], allowed, dec_saved, groups
    )
    grad_begin_low = grad_begin.astype(jnp.bfloat16)
    grad_qout = matmul_outer(grad_begin_low, chosen_low)
    start = matmul_trans(pixel_all, edge_in)
    encoded, enc_saved = block_forward(start, part, wide_all[0], narrow_all[0], norms[0:4], allowed)
    encoded_low = encoded.astype(jnp.bfloat16)
    latent = matmul_plain(encoded_low, edge_qin)
    gap = chosen - latent
    loss_part = loss_pix + (1.0 + commitment) * jnp.sum(gap * gap) / latent_total
    grad_latent = (
        matmul_plain(grad_begin_low, edge_qout) - 2.0 * commitment * gap / latent_total
    ).astype(jnp.bfloat16)
    fold = lane_mask.shape[1] // code_width
    gap_wide = jnp.where(lane_mask, jnp.tile(2.0 * gap / latent_total, (1, fold)), 0.0)
    gap_high = gap_wide.astype(jnp.bfloat16)
    gap_rest = gap_wide - gap_high.astype(jnp.float32)
    gap_middle = gap_rest.astype(jnp.bfloat16)
    gap_low = (gap_rest - gap_middle.astype(jnp.float32)).astype(jnp.bfloat16)
    grad_book = (
        matmul_outer(one_hot, gap_high) + matmul_outer(one_hot, gap_middle)
    ) + matmul_outer(one_hot, gap_low)
    grad_qin = matmul_outer(encoded_low, grad_latent)
    grad_start, enc_wide, enc_narrow, enc_gains = block_backward(
        matmul_trans(grad_latent, edge_qin), wide_all[0], narrow_all[0], norms[0:4], allowed, enc_saved, groups
    )
    grad_inw = matmul_outer(grad_start.astype(jnp.bfloat16), pixel_rows)
    grads = (
        enc_wide, dec_wide, enc_narrow, dec_narrow,
        jnp.concatenate([grad_inw, grad_pixw, grad_qin, grad_qout], axis=1),
        grad_book,
    )
    norm_grad = jnp.concatenate([enc_gains, dec_gains, gain_last[None], offset_last[None]], axis=0)
    return (grads, norm_grad, loss_part)


def place():
    img_at = lax.axis_index("img")
    band_at = lax.axis_index("band")
    return img_at, band_at, band_at // 4, (band_at // 2) % 2, band_at % 2


def neighbours():
    img_at, band_at, y_at, x_at, c_at = place()
    return (
        (img_at, band_at + 1 - 2 * c_at),
        (img_at, band_at + 2 - 4 * x_at),
        (img_at, band_at + 4 - 8 * y_at),
    )


def peers():
    img_at, band_at = place()[:2]
    found = [((img_at + step) % 4, band_at) for step in range(1, 4)]
    return found + [(img_at, (band_at + step) % 8) for step in range(1, 8)]


def meet(others):
    barrier = pltpu.get_barrier_semaphore()
    for other in others:
        pl.semaphore_signal(barrier, inc=1, device_id=other, device_id_type=MESH)
    pl.semaphore_wait(barrier, len(others))


def far_copy(src, dst, send, recv, target):
    return pltpu.make_async_remote_copy(
        src_ref=src, dst_ref=dst, send_sem=send, recv_sem=recv, device_id=target, device_id_type=MESH
    )


class Everywhere:
    def __init__(self, name, agenda, own_ref, img_buf, band_buf, send, recv, result_ref):
        self.name, self.agenda, self.done = name, agenda, False
        self.own, self.img_buf, self.band_buf, self.result = own_ref, img_buf, band_buf, result_ref
        self.send, self.recv = send, recv

    def begin(self):
        img_at, band_at = place()[:2]
        self.img_buf[img_at] = self.own[...]
        copies = [
            far_copy(
                self.own, self.img_buf.at[img_at], self.send.at[step], self.recv.at[step], ((img_at + step) % 4, band_at)
            )
            for step in range(1, 4)
        ]
        self.agenda.launch((self.name, 0), copies, [], self.middle)
        self.agenda.spend(0.5)

    def middle(self):
        img_at, band_at = place()[:2]
        buf = self.img_buf
        self.result[...] = (buf[0] + buf[1]) + (buf[2] + buf[3])
        self.band_buf[band_at] = self.result[...]
        copies = [
            far_copy(
                self.result, self.band_buf.at[band_at], self.send.at[3 + step], self.recv.at[3 + step],
                (img_at, (band_at + step) % 8),
            )
            for step in range(1, 8)
        ]
        self.agenda.launch((self.name, 1), copies, [], self.end)
        self.agenda.spend(1.0)

    def end(self):
        total = self.band_buf[0]
        for k in range(1, 8):
            total = total + self.band_buf[k]
        self.result[...] = total
        self.done = True

    def until(self):
        self.agenda.until(lambda: self.done)


LINK, CORE, LAG = 100e3, 500e3, 0.6
SPREAD = {"f01": 3, "f12": 4, "f23": 3, "b10": 3, "b21": 4, "b32": 3}
TOWARDS = (
    {"b10": 3, "b21": 2, "b32": 1},
    {"f01": 1, "b21": 2, "b32": 1},
    {"f01": 1, "f12": 2, "b32": 1},
    {"f01": 1, "f12": 2, "f23": 3},
)


def z_loads(table, size):
    return [(link, count * size) for link, count in table.items()]


class Agenda:
    def __init__(self):
        self.now, self.free, self.flying = 0.0, {}, {}

    def launch(self, key, copies, loads, then):
        done = self.now
        for link, size in loads:
            begin = max(self.now, self.free.get(link, 0.0))
            self.free[link] = begin + size / (CORE if link == "c" else LINK) + 0.4
            done = max(done, self.free[link])
        for copy in copies:
            copy.start()
        self.flying[key] = (done + LAG, copies, then)

    def land(self, key):
        done, copies, then = self.flying.pop(key)
        self.now = max(self.now, done) + 0.5
        for copy in copies:
            copy.wait()
        then()

    def spend(self, time):
        self.now += time

    def tick(self):
        while self.flying:
            key = min(self.flying, key=lambda name: self.flying[name][0])
            if self.flying[key][0] > self.now:
                return
            self.land(key)

    def until(self, test):
        while not test():
            self.land(min(self.flying, key=lambda name: self.flying[name][0]))


class Gather:
    def __init__(self, name, agenda, pieces, near, z_send, z_recv, p_send, p_recv):
        self.name, self.agenda, self.pieces = name, agenda, pieces
        self.near, self.z_send, self.z_recv, self.p_send, self.p_recv = near, z_send, z_recv, p_send, p_recv
        self.done = set()

    def launch(self, p, k):
        img_at, band_at, y_at, x_at, c_at = place()
        over_c, over_x, over_y = neighbours()
        shard, whole, first, count, z_last = self.pieces[p]
        rows = pl.ds(first, count)
        width = shard.shape[1]
        size = count * max(width, 128) * 2
        lanes = width // 256 * 128
        found, loads = [], []
        here, own = whole.at[img_at, y_at, x_at, c_at, rows], shard.at[rows]
        if z_last and k < 2:
            for half in range(2):
                span = pl.ds(lanes, width - lanes) if half else pl.ds(0, lanes)
                along_y = (k == 0) == (half == 0)
                if k == 0:
                    src, dst = shard.at[rows, span], whole.at[img_at, y_at, x_at, c_at, rows, span]
                elif half == 0:
                    src = dst = whole.at[img_at, :, x_at, c_at, rows, span]
                else:
                    src = dst = whole.at[img_at, y_at, :, c_at, rows, span]
                slot = 2 * k + half
                target = over_y if along_y else over_x
                found.append(far_copy(src, dst, self.p_send.at[p, slot], self.p_recv.at[p, slot], target))
                loads.append(("y" if along_y else "x", (1 + k) * size))
            if k == 0:
                found.append(pltpu.make_async_copy(own, here, self.near.at[p]))
        elif z_last and k == 2:
            part = whole.at[img_at, :, :, c_at, rows]
            found = [
                far_copy(part, part, self.z_send.at[p, step], self.z_recv.at[p, step], ((img_at + step) % 4, band_at))
                for step in range(1, 4)
            ]
            loads = z_loads(SPREAD, 8 * size)
        elif k == 0:
            found = [
                far_copy(own, here, self.z_send.at[p, step], self.z_recv.at[p, step], ((img_at + step) % 4, band_at))
                for step in range(1, 4)
            ]
            found.append(pltpu.make_async_copy(own, here, self.near.at[p]))
            loads = z_loads(SPREAD, 2 * size)
        elif k == 3:
            part = whole.at[:, :, :, c_at, rows]
            found = [far_copy(part, part, self.p_send.at[p, 4], self.p_recv.at[p, 4], over_c)]
            loads = [("c", 16 * size)]
        else:
            for half in range(2):
                span = pl.ds(lanes, width - lanes) if half else pl.ds(0, lanes)
                if lanes == 0 and half == 0:
                    continue
                if k == 1:
                    part = whole.at[:, y_at, x_at, c_at, rows, span]
                elif half == 0:
                    part = whole.at[:, :, x_at, c_at, rows, span]
                else:
                    part = whole.at[:, y_at, :, c_at, rows, span]
                slot = 2 * (k - 1) + half
                along_y = (k == 1) == (half == 0)
                target = over_y if along_y else over_x
                found.append(far_copy(part, part, self.p_send.at[p, slot], self.p_recv.at[p, slot], target))
                loads.append(("y" if along_y else "x", 4 * k * size))

        def then():
            if k < 3:
                self.launch(p, k + 1)
            else:
                self.done.add(p)

        self.agenda.launch((self.name, p), found, loads, then)

    def begin(self, first, last):
        for p in range(first, last):
            self.launch(p, 0)

    def until(self, *wanted):
        self.agenda.until(lambda: all(p in self.done for p in wanted))


def gather_sems(count):
    dma = pltpu.SemaphoreType.DMA
    return [dma((count,)), dma((count, 4)), dma((count, 4)), dma((count, 5)), dma((count, 5))]


class Reduce:
    def __init__(
        self, agenda, slots, wait_z, full, pair, first_a, first_b, second_a, second_b, ours, last,
        near, p_send, p_recv, z_send, z_recv, free, free_z,
    ):
        self.agenda, self.slots, self.wait_z = agenda, slots, wait_z
        self.full, self.pair, self.ours, self.last = full, pair, ours, last
        self.first, self.second = (first_a, first_b), (second_a, second_b)
        self.near, self.p_send, self.p_recv, self.z_send, self.z_recv = near, p_send, p_recv, z_send, z_recv
        self.free, self.free_z = free, free_z
        self.pieces, self.flying, self.events, self.at_event = [], {}, [], 0
        self.queue, self.opened = [], 0

    def plan(self, pieces):
        self.pieces = pieces
        seen = [0] * 4
        for p, piece in enumerate(pieces):
            piece["slot"] = p % self.slots
            piece["place"] = p % (self.wait_z + 1)
            piece["order"] = seen[piece["z"]]
            seen[piece["z"]] += 1
        for piece in pieces:
            piece["again"] = piece["order"] + 2 < seen[piece["z"]]
        self.opened, self.passed, self.ended = 0, set(), set()
        self.ready = {""}

    def feed(self):
        while self.opened < len(self.pieces):
            p = self.opened
            if self.pieces[p]["needs"] not in self.ready or (p >= self.slots and p - self.slots not in self.passed):
                return
            self.opened += 1
            self.open(p)

    def allow(self, name):
        self.ready.add(name)
        self.feed()

    def rows(self, p):
        return pl.ds(0, self.pieces[p]["rows"])

    def open(self, p):
        piece = self.pieces[p]
        slot, rows = piece["slot"], self.rows(p)
        c_at = place()[4]
        over_c = neighbours()[0]
        if p >= self.slots:
            for k in range(3):
                pl.semaphore_wait(self.free.at[slot, k], 1)
        landing = self.pair.at[slot, :, :, rows]
        send, recv = self.p_send.at[slot, 0], self.p_recv.at[slot, 0]
        if "stage" in piece:
            stage, first, count = piece["stage"], piece["first"], piece["rows"]
            copies = []
            for n in range(4):
                theirs = pl.ds(pl.multiple_of(first + (2 * n + 1 - c_at) * count, 8), count)
                ours = pl.ds(pl.multiple_of(first + (2 * n + c_at) * count, 8), count)
                spot = 0 if n == 0 else 4 + n
                copies.append(
                    far_copy(
                        stage.at[theirs], self.pair.at[slot, n // 2, n % 2, rows], self.p_send.at[slot, spot],
                        self.p_recv.at[slot, spot], over_c,
                    )
                )
                copies.append(
                    pltpu.make_async_copy(
                        stage.at[ours], self.full.at[slot, n // 2, n % 2, c_at, rows], self.near.at[slot, n]
                    )
                )
        else:
            piece["emit"](self.full, slot)
            copies = [far_copy(self.full.at[slot, :, :, 1 - c_at, rows], landing, send, recv, over_c)]
        size = piece["rows"] * self.full.shape[5] * 4
        self.agenda.launch(("r", p, 0), copies, [("c", 4 * size)], lambda: self.step(0, p))

    def step(self, k, p):
        piece = self.pieces[p]
        slot, rows, z = piece["slot"], self.rows(p), piece["z"]
        size = piece["rows"] * self.full.shape[5] * 4
        img_at, band_at, y_at, x_at, c_at = place()
        over_c, over_x, over_y = neighbours()
        full, half = self.full, self.full.shape[5] // 2
        low, high = pl.ds(0, half), pl.ds(half, half)
        tiles = piece["rows"] // 16

        def tile(n):
            return pl.ds(pl.multiple_of(n % tiles * 16, 16), 16)

        if k == 0:
            def add(n, carry):
                y, x = n // (2 * tiles), n // tiles % 2
                full[slot, y, x, c_at, tile(n)] += self.pair[slot, y, x, tile(n)]
                return carry
            lax.fori_loop(0, 4 * tiles, add, 0)
            parts = (full.at[slot, :, 1 - x_at, c_at, rows, low], full.at[slot, 1 - y_at, :, c_at, rows, high])
            landings = [self.first[n].at[slot, :, rows] for n in range(2)]
            targets = (over_x, over_y)
        elif k == 1:
            def add(n, carry):
                w = n // tiles
                full[slot, w, x_at, c_at, tile(n), low] += self.first[0][slot, w, tile(n)]
                full[slot, y_at, w, c_at, tile(n), high] += self.first[1][slot, w, tile(n)]
                return carry
            lax.fori_loop(0, 2 * tiles, add, 0)
            parts = (full.at[slot, 1 - y_at, x_at, c_at, rows, low], full.at[slot, y_at, 1 - x_at, c_at, rows, high])
            landings = [self.second[n].at[slot, rows] for n in range(2)]
            targets = (over_y, over_x)
        if k < 2:
            copies = [
                far_copy(
                    parts[n], landings[n], self.p_send.at[slot, 1 + 2 * k + n], self.p_recv.at[slot, 1 + 2 * k + n],
                    targets[n],
                )
                for n in range(2)
            ]
            load = 2 * size if k == 0 else size
            self.agenda.launch(("r", p, 1 + k), copies, [("x", load), ("y", load)], lambda: self.step(k + 1, p))
            return
        spot, order = piece["place"], piece["order"] % 2
        mine = self.ours.at[spot, rows]
        owner = (z, band_at)

        def hop(n):
            return far_copy(mine, self.last.at[order, n, rows], self.z_send.at[spot], self.z_recv.at[order, n], owner)

        if k == 2:
            self.agenda.until(lambda: p < self.wait_z + 1 or p - self.wait_z - 1 in self.ended)

            def add(n, carry):
                self.ours[spot, tile(n), low] = full[slot, y_at, x_at, c_at, tile(n), low] + self.second[0][slot, tile(n)]
                self.ours[spot, tile(n), high] = full[slot, y_at, x_at, c_at, tile(n), high] + self.second[1][slot, tile(n)]
                return carry
            lax.fori_loop(0, tiles, add, 0)

            assert p < self.wait_z + 1 or p - self.wait_z - 1 in self.ended

            @pl.when(img_at != z)
            def _():
                if piece["order"] >= 2:
                    pl.semaphore_wait(self.free_z.at[z, order], 1)
                hop((img_at + 3 - z) % 4).start()

            if p + self.slots < len(self.pieces):
                for n, other in enumerate((over_c, over_x, over_y)):
                    pl.semaphore_signal(self.free.at[slot, n], inc=1, device_id=other, device_id_type=MESH)
            self.passed.add(p)
            self.agenda.launch(("r", p, 3), [], z_loads(TOWARDS[z], 2 * size), lambda: self.step(3, p))
            self.feed()
            return

        @pl.when(img_at != z)
        def _():
            hop((img_at + 3 - z) % 4).wait_send()

        @pl.when(img_at == z)
        def _():
            for n in range(3):
                hop(n).wait_recv()

            def add(n, carry):
                piece["out"][tile(n)] = (self.ours[spot, tile(n)] + self.last[order, 0, tile(n)]) + (
                    self.last[order, 1, tile(n)] + self.last[order, 2, tile(n)]
                )
                return carry
            lax.fori_loop(0, tiles, add, 0)
            if piece["again"]:
                for n in range(1, 4):
                    pl.semaphore_signal(
                        self.free_z.at[z, order], inc=1, device_id=((img_at + n) % 4, band_at), device_id_type=MESH
                    )

        self.ended.add(p)


def reduce_scratch(slots, wait_z, rows, width):
    f32 = jnp.float32
    dma = pltpu.SemaphoreType.DMA
    half = width // 2
    return [
        pltpu.VMEM((slots, 2, 2, 2, rows, width), f32),
        pltpu.VMEM((slots, 2, 2, rows, width), f32),
        pltpu.VMEM((slots, 2, rows, half), f32),
        pltpu.VMEM((slots, 2, rows, half), f32),
        pltpu.VMEM((slots, rows, half), f32),
        pltpu.VMEM((slots, rows, half), f32),
        pltpu.VMEM((wait_z + 1, rows, width), f32),
        pltpu.VMEM((2, 3, rows, width), f32),
        dma((slots, 4)),
        dma((slots, 8)), dma((slots, 8)),
        dma((wait_z + 1,)), dma((2, 3)),
        pltpu.SemaphoreType.REGULAR((slots, 3)),
        pltpu.SemaphoreType.REGULAR((4, 2)),
    ]


class ReduceSmall:
    def __init__(self, agenda, grads, shares, own, pair, first_a, first_b, second_a, second_b, last, near, p_send, p_recv, z_send, z_recv):
        self.agenda, self.done = agenda, set()
        self.grads, self.shares, self.own, self.pair = grads, shares, own, pair
        self.first, self.second, self.last = (first_a, first_b), (second_a, second_b), last
        self.near, self.p_send, self.p_recv, self.z_send, self.z_recv = near, p_send, p_recv, z_send, z_recv
        self.flying = {}

    def start(self, p, copies, loads, k):
        size = self.own[p].shape[3] * self.own[p].shape[4] * 4
        self.agenda.launch(("s", p), copies, [(link, n * size) for link, n in loads], lambda: self.step(p, k))

    def open(self, p):
        c_at = place()[4]
        over_c = neighbours()[0]
        self.start(p, [
            far_copy(self.grads[p].at[:, :, :, 1 - c_at], self.pair[p], self.p_send.at[p, 0], self.p_recv.at[p, 0], over_c),
            pltpu.make_async_copy(self.grads[p].at[:, :, :, c_at], self.own[p], self.near.at[p]),
        ], [("c", 16)], 0)

    def step(self, p, k):
        img_at, band_at, y_at, x_at, c_at = place()
        over_c, over_x, over_y = neighbours()
        own = self.own[p]
        rows = own.shape[3]
        span = (pl.ds(0, rows // 2), pl.ds(rows // 2, rows // 2))

        def send(parts, landings, targets, slot):
            copies = [
                far_copy(parts[n], landings[n], self.p_send.at[p, slot + n], self.p_recv.at[p, slot + n], targets[n])
                for n in range(2)
            ]
            self.start(p, copies, [("x", 8 >> k), ("y", 8 >> k)], k + 1)

        if k == 0:
            own[...] += self.pair[p][...]
            send(
                (own.at[:, :, 1 - x_at, span[0]], own.at[:, 1 - y_at, :, span[1]]),
                (self.first[0][p], self.first[1][p]), (over_x, over_y), 1,
            )
        elif k == 1:
            own[:, :, x_at, span[0]] += self.first[0][p][...]
            own[:, y_at, :, span[1]] += self.first[1][p][...]
            send(
                (own.at[:, 1 - y_at, x_at, span[0]], own.at[:, y_at, 1 - x_at, span[1]]),
                (self.second[0][p], self.second[1][p]), (over_y, over_x), 3,
            )
        elif k == 2:
            own[:, y_at, x_at, span[0]] += self.second[0][p][...]
            own[:, y_at, x_at, span[1]] += self.second[1][p][...]
            copies = []
            for n in range(1, 4):
                target = (img_at + n) % 4
                copies.append(
                    far_copy(
                        own.at[target, y_at, x_at], self.last[p].at[n - 1], self.z_send.at[p, n], self.z_recv.at[p, n],
                        (target, band_at),
                    )
                )
            self.start(p, copies, z_loads(SPREAD, 2), 3)
        else:
            last = self.last[p]
            self.done.add(p)
            self.shares[p][...] = (own[img_at, y_at, x_at] + last[0]) + (last[1] + last[2])


def reduce_small_scratch(shapes):
    f32 = jnp.float32
    dma = pltpu.SemaphoreType.DMA
    count = len(shapes)
    groups = [
        [(4, 2, 2, r, w) for r, w in shapes],
        [(4, 2, 2, r, w) for r, w in shapes],
        [(4, 2, r // 2, w) for r, w in shapes],
        [(4, 2, r // 2, w) for r, w in shapes],
        [(4, r // 2, w) for r, w in shapes],
        [(4, r // 2, w) for r, w in shapes],
        [(3, r, w) for r, w in shapes],
    ]
    return [pltpu.VMEM(shape, f32) for group in groups for shape in group] + [
        dma((count,)), dma((count, 5)), dma((count, 5)), dma((count, 4)), dma((count, 4)),
    ]


def dot_nn(a, b):
    return lax.dot_general(a, b, (((1,), (0,)), ((), ())), preferred_element_type=jnp.float32)


def dot_nt(a, b):
    return lax.dot_general(a, b, (((1,), (1,)), ((), ())), preferred_element_type=jnp.float32)


def dot_tn(a, b):
    return lax.dot_general(a, b, (((0,), (0,)), ((), ())), preferred_element_type=jnp.float32)


def norm_parts(h):
    centred = h - jnp.mean(h, axis=-1, keepdims=True)
    rate = lax.rsqrt(jnp.mean(centred * centred, axis=-1, keepdims=True) + norm_eps)
    return centred * rate, rate


def norm_back(grad, h, gain):
    shape, rate = norm_parts(h)
    inner = grad * gain
    back = rate * (
        inner
        - jnp.mean(inner, axis=-1, keepdims=True)
        - shape * jnp.mean(inner * shape, axis=-1, keepdims=True)
    )
    return (
        back,
        jnp.sum(grad * shape, axis=0, keepdims=True),
        jnp.sum(grad, axis=0, keepdims=True),
    )


STEP = 256


def at(k, start=0):
    return pl.ds(pl.multiple_of(start + k * STEP, STEP), STEP)


def lanes_at(k, size, start=0):
    return pl.ds(pl.multiple_of(start + k * size, 128), size)


def loop(first, last, body):
    def step(k, carry):
        body(k)
        return carry

    lax.fori_loop(first, last, step, 0)


class Block:
    def __init__(self, base, source, first_w, small, refs):
        names = (
            "wide", "narrow", "norms", "q_extra", "k_extra", "hidden", "normed", "q_buf", "kv", "mixed_in", "wide_in",
            "middle", "second", "slope", "grad_out", "grad_low", "mid_low", "gatt", "dkv", "dkv_in", "soft", "x_send",
            "x_recv", "x_free",
        )
        for name, ref in zip(names, refs, strict=True):
            setattr(self, name, ref)
        self.base, self.source, self.first_w, self.small = base, source, first_w, small
        self.part = place()[4]
        self.total, self.own = self.kv.shape[0], self.q_buf.shape[0]
        self.width = self.q_buf.shape[1]
        self.offset = pl.multiple_of(self.part * self.own, self.own)
        self.chunks = self.own // STEP
        lane_head = lax.broadcasted_iota(jnp.int32, (1, 128), 1) // HDIM
        self.pick = [jnp.where(lane_head == k, 1.0, 0.0).astype(jnp.bfloat16) for k in range(2)]

    def slope_rows(self, f, k):
        return pl.ds(pl.multiple_of(f * self.own + k * STEP, STEP), STEP)

    def gain(self, k):
        return self.norms[pl.ds(self.base + k, 1), :]

    def add_small(self, row, value):
        self.small[pl.ds(row, 1), :] += value

    def add_loss(self, value):
        first_lane = lax.broadcasted_iota(jnp.int32, (1, self.width), 1) == 0
        self.add_small(6, jnp.where(first_lane, value, 0.0))

    def enter(self, first, last):
        def body(n):
            k = (n + self.chunks * (1 + self.part)) % (self.total // STEP)
            h = dot_nt(self.source(k), self.first_w())
            self.hidden[at(n % self.chunks)] = h
            shape, _ = norm_parts(h)
            self.normed[at(k)] = (shape * self.gain(0) + self.gain(1)).astype(jnp.bfloat16)

        loop(first, last, body)

    def make_kv(self, first, last):
        def body(k):
            self.kv[at(k)] = dot_nt(self.normed[at(k)], self.wide[self.width : 3 * self.width]).astype(jnp.bfloat16)

        loop(first, last, body)

    def make_q(self):
        def body(k):
            q = dot_nt(self.normed[at(k, self.offset)], self.wide[: self.width]).astype(jnp.bfloat16)
            self.q_buf[at(k)] = (q.astype(jnp.float32) * HDIM**-0.5).astype(jnp.bfloat16)

        loop(0, self.chunks, body)

    def scores(self, p, k, rows, k_cat):
        q_cat = jnp.concatenate([self.q_buf[rows, lanes_at(p, 128)] * self.pick[k], self.q_extra[rows]], axis=1)
        return dot_nt(q_cat, k_cat)

    def key_columns(self, p):
        return jnp.concatenate([self.kv[:, lanes_at(p, 128)], self.k_extra[...]], axis=1)

    def attend(self, first, last):
        head_lane = lax.broadcasted_iota(jnp.int32, (STEP, 128), 1)

        def pair(p):
            k_cat = self.key_columns(p)
            v_pair = self.kv[:, lanes_at(p, 128, self.width)]

            def body(j):
                rows = at(j)
                mixed = None
                for k in range(2):
                    scores = self.scores(p, k, rows, k_cat)
                    peak = jnp.max(scores, axis=-1, keepdims=True)
                    expo = jnp.exp(scores - peak)
                    total = jnp.sum(expo, axis=-1, keepdims=True)
                    prob = expo * (1.0 / total)
                    level = peak + jnp.log(total)
                    self.soft[rows] = jnp.where(head_lane == 2 * p + k, level, self.soft[rows])
                    term = dot_nn(prob.astype(jnp.bfloat16), v_pair * self.pick[k])
                    mixed = term if mixed is None else mixed + term
                self.mixed_in[rows, lanes_at(p, 128)] = mixed.astype(jnp.bfloat16)

            loop(0, self.chunks, body)

        loop(first, last, pair)

    def after_attention(self):
        def body(k):
            rows = at(k)
            mid = self.hidden[at(k)] + dot_nn(self.mixed_in[rows, : self.width], self.narrow[: self.width])
            self.middle[rows] = mid
            shape, _ = norm_parts(mid)
            self.second[rows] = (shape * self.gain(2) + self.gain(3)).astype(jnp.bfloat16)
            self.grad_out[rows] = mid

        loop(0, self.chunks, body)

    def mlp(self, first, last):
        width = self.width

        def body(n):
            f, k = n // self.chunks, n % self.chunks
            rows = at(k)
            u = dot_nt(self.second[rows], self.wide[lanes_at(3 + f, width)])
            squared = u * u
            bend = jnp.tanh(0.7978845608028654 * (u + 0.044715 * squared * u))
            low = (0.5 * u * (1.0 + bend)).astype(jnp.bfloat16)
            self.mixed_in[rows, lanes_at(1 + f, width)] = low
            self.slope[self.slope_rows(f, k)] = 0.5 * (1.0 + bend) + (0.5 * u) * (1.0 - bend * bend) * (
                0.7978845608028654 * (1.0 + (3.0 * 0.044715) * squared)
            )
            self.grad_out[rows] += dot_nn(low, self.narrow[lanes_at(1 + f, width)])

        loop(first * self.chunks, last * self.chunks, body)

    def mlp_back(self, first, last):
        width = self.width

        def body(k):
            rows = at(k)
            gy = self.grad_low[rows]

            def feature_step(f, acc):
                ga = dot_nt(gy, self.narrow[lanes_at(1 + f, width)])
                low = (ga * self.slope[self.slope_rows(f, k)]).astype(jnp.bfloat16)
                self.wide_in[rows, lanes_at(3 + f, width)] = low
                return acc + dot_nn(low, self.wide[lanes_at(3 + f, width)])

            grad_second = lax.fori_loop(0, 4, feature_step, jnp.zeros((STEP, width), jnp.float32))
            back, g_gain, g_offset = norm_back(grad_second, self.middle[rows], self.gain(2))
            self.add_small(2, g_gain)
            self.add_small(3, g_offset)
            grad_mid = back + self.grad_out[rows]
            self.grad_out[rows] = grad_mid
            low = grad_mid.astype(jnp.bfloat16)
            self.mid_low[rows] = low
            self.gatt[rows] = dot_nt(low, self.narrow[:width]).astype(jnp.bfloat16)

        loop(first, last, body)

    def attend_back(self, first, last):
        head_lane = lax.broadcasted_iota(jnp.int32, (self.own, 128), 1)
        lane_head = lax.broadcasted_iota(jnp.int32, (1, 128), 1) // HDIM
        rows, bf16 = slice(None), jnp.bfloat16

        def head(h):
            p = h // 2
            pick = jnp.where(lane_head == h % 2, 1.0, 0.0).astype(bf16)
            k_pair = self.kv[:, lanes_at(p, 128)]
            g_rows = self.gatt[rows, lanes_at(p, 128)] * pick
            q_rows = self.q_buf[rows, lanes_at(p, 128)] * pick
            level = jnp.sum(jnp.where(head_lane == h, self.soft[...], 0.0), axis=-1, keepdims=True)
            scores = dot_nt(
                jnp.concatenate([q_rows, self.q_extra[...]], axis=1), jnp.concatenate([k_pair, self.k_extra[...]], axis=1)
            )
            prob = jnp.exp(scores - level)
            d_prob = dot_nt(g_rows, self.kv[:, lanes_at(p, 128, self.width)])
            dot_row = jnp.sum(prob * d_prob, axis=-1, keepdims=True)
            d_score = (prob * (d_prob - dot_row)).astype(bf16)
            dq = (dot_nn(d_score, k_pair * pick) * HDIM**-0.5).astype(bf16)
            self.dkv[p, 0] += dot_tn(d_score, q_rows)
            self.dkv[p, 1] += dot_tn(prob.astype(bf16), g_rows)
            self.wide_in[rows, lanes_at(p, 128)] = self.wide_in[rows, lanes_at(p, 128)] + dq

        self.dkv[pl.ds(first, 2)] = jnp.zeros((2,) + self.dkv.shape[1:], jnp.float32)
        self.wide_in[:, pl.ds(pl.multiple_of(128 * first, 128), 256)] = jnp.zeros((self.own, 256), bf16)
        loop(2 * first, 2 * last, head)

    def swap(self, p):
        theirs = pl.ds(pl.multiple_of((1 - self.part) * self.own, self.own), self.own)
        return far_copy(
            self.dkv.at[p, :, theirs], self.dkv_in.at[p], self.x_send.at[p], self.x_recv.at[p], neighbours()[0]
        )

    def attend_back_all(self, opening):
        if not opening:
            pl.semaphore_wait(self.x_free, 1)

        def half(n):
            self.attend_back(2 * n, 2 * n + 2)
            for p in range(2):
                self.swap(2 * n + p).start()

        loop(0, 2, half)

    def swap_start(self, first, opening):
        if not opening and first == 0:
            pl.semaphore_wait(self.x_free, 1)
        for p in range(first, first + 2):
            self.swap(p).start()

    def swap_finish(self, closing):
        for p in range(4):
            self.swap(p).wait()

        def body(n):
            p, k = n // self.chunks, n % self.chunks
            for side in range(2):
                total = self.dkv[p, side, at(k, self.offset)] + self.dkv_in[p, side, at(k)]
                self.wide_in[at(k), lanes_at(p, 128, (1 + side) * self.width)] = total.astype(jnp.bfloat16)

        loop(0, 4 * self.chunks, body)
        if not closing:
            pl.semaphore_signal(self.x_free, inc=1, device_id=neighbours()[0], device_id_type=MESH)

    def leave_rows(self, k):
        rows = at(k)
        grad_normed = dot_nn(self.wide_in[rows, : 3 * self.width], self.wide[: 3 * self.width])
        back, g_gain, g_offset = norm_back(grad_normed, self.hidden[at(k)], self.gain(0))
        self.add_small(0, g_gain)
        self.add_small(1, g_offset)
        return (back + self.grad_out[rows]).astype(jnp.bfloat16)

    def wide_product(self, first, count):
        if first < 3 * self.width:
            right = self.normed[pl.ds(self.offset, self.own)]
        else:
            right = self.second[...]
        return dot_tn(self.wide_in[:, first : first + count], right)

    def narrow_product(self, first, count):
        right = self.mid_low if first < self.width else self.grad_low
        return dot_tn(self.mixed_in[:, first : first + count], right[...])


def pieces_of(first, count, border):
    if first < border < first + count:
        return [(first, border - first), (border, first + count - border)]
    return [(first, count)]


def block_scratch(total_rows, own_rows):
    width = 512
    f32, bf16 = jnp.float32, jnp.bfloat16
    shapes = [
        ((own_rows, width), f32),
        ((total_rows, width), bf16),
        ((own_rows, width), bf16),
        ((total_rows, 2 * width), bf16),
        ((own_rows, 5 * width), bf16),
        ((own_rows, 7 * width), bf16),
        ((own_rows, width), f32),
        ((own_rows, width), bf16),
        ((4 * own_rows, width), f32),
        ((own_rows, width), f32),
        ((own_rows, width), bf16),
        ((own_rows, width), bf16),
        ((own_rows, width), bf16),
        ((4, 2, total_rows, 128), f32),
        ((4, 2, own_rows, 128), f32),
        ((own_rows, 128), f32),
    ]
    return [pltpu.VMEM(shape, dtype) for shape, dtype in shapes] + [
        pltpu.SemaphoreType.DMA((4,)), pltpu.SemaphoreType.DMA((4,)), pltpu.SemaphoreType.REGULAR
    ]


DEC_NARROW = ((0, 80, False),)
ENC_WIDE = ((0, 112, False),)
ENC_NARROW = ((0, 80, False),)
DEC_ORDER = (("n", 3), ("n", 1), ("n", 2), ("n", 0), ("w", 3), ("w", 2), ("w", 0), ("w", 1))
ENC_ORDER = (("n", 3), ("n", 1), ("n", 0), ("w", 3), ("w", 2), ("w", 0), ("w", 1), ("n", 2))


def step_kernel(slots, latent_total, *refs):
    shards, slab, code, kinds, norms = refs[:6], refs[6], refs[7], refs[8], refs[9]
    refs = refs[10:]
    share_wide_dec, share_narrow_dec, share_wide, share_narrow, share_edge, share_book, small_all = refs[:7]
    land_wide_dec, land_narrow_dec, land_wide, land_narrow = refs[7:11]
    refs = refs[11:]
    sems_dec, sems_enc, red, red_small, refs = refs[:5], refs[5:10], refs[10:25], refs[25:44], refs[44:]
    (book, edge, slab_all, code_all, tally, tally_all, t_img, t_band, e_near, e_send, e_recv, t_send, t_recv) = refs[:13]
    refs = refs[1:]
    (code_row, spread, cross, g_pixw, g_qout, g_qin, g_inw, g_edge, g_book) = refs[12:21]
    (small_dec, small_enc, small_own, s_img, s_band, s_send, s_recv, load_sem, wide, narrow) = refs[21:31]
    q_extra, k_extra = refs[31:33]
    scratch = refs[33:]
    f32, bf16 = jnp.float32, jnp.bfloat16
    img_at, band_at, y_at, x_at, c_at = place()
    chip_at = band_at // 2
    over_c = neighbours()[0]
    width = wide.shape[1]
    common = (wide, narrow, norms, q_extra, k_extra) + tuple(scratch)

    def edge_columns(first, count):
        return edge[:, :, :, :, :, first : first + count].reshape(width, count)

    def e_in():
        return edge_columns(0, 256)

    def e_pix():
        return edge_columns(256, 256)

    def e_qin():
        return edge_columns(512, 128)

    def e_qout():
        return edge_columns(640, 128)

    def pixel_rows(k, first=0, start=0):
        return slab_all[pl.ds(start + 2 * k, 2), :, first : first + 256].reshape(STEP, 256)

    own_band = 4 * c_at
    dec = Block(4, lambda k: spread[at(k)], e_qout, small_dec, common)
    enc = Block(0, pixel_rows, e_in, small_enc, common)
    agenda = Agenda()
    dec_pieces = [(shards[0], book, 0, 64, False), (shards[1], edge, 0, 16, False)]
    dec_pieces += [(shards[2], land_wide_dec, 96, 16, True)]
    dec_pieces += [(shards[2], land_wide_dec, 0, 48, False), (shards[2], land_wide_dec, 48, 48, False)]
    dec_pieces += [(shards[3], land_narrow_dec, first, count, last) for first, count, last in DEC_NARROW]
    gather = Gather("d", agenda, dec_pieces, *sems_dec)
    enc_pieces = [(shards[4], land_wide, first, count, last) for first, count, last in ENC_WIDE]
    enc_pieces += [(shards[5], land_narrow, first, count, last) for first, count, last in ENC_NARROW]
    gather_enc = Gather("e", agenda, enc_pieces, *sems_enc)
    count_all = Everywhere("n", agenda, tally, t_img, t_band, t_send, t_recv, tally_all)
    spots = lax.broadcasted_iota(jnp.int32, (1, 4), 1)
    kind = jnp.sum(jnp.where(spots == chip_at, kinds[...], 0).astype(f32), axis=1, keepdims=True)
    meet(peers())
    agenda.spend(3.0)
    gather.begin(0, 5)
    exchange = []
    for step in range(1, 4):
        chip = (chip_at + step) % 4
        target = (img_at, 2 * chip + c_at)
        here = band_at
        exchange.append(far_copy(slab.at[chip], slab_all.at[here], e_send.at[0, step], e_recv.at[0, step], target))
        exchange.append(far_copy(code.at[chip], code_all.at[here], e_send.at[1, step], e_recv.at[1, step], target))
    exchange.append(pltpu.make_async_copy(slab.at[chip_at], slab_all.at[band_at], e_near.at[0]))
    exchange.append(pltpu.make_async_copy(code.at[chip_at], code_all.at[band_at], e_near.at[1]))

    def exchange_landed():
        late = []
        for k, dst in enumerate((slab_all, code_all)):
            for chip in range(4):
                part = dst.at[2 * chip + c_at]
                late.append(far_copy(part, part, e_send.at[k, 4 + chip], e_recv.at[k, 4 + chip], over_c))
        agenda.launch("x2", late, [("c", 4e5)], lambda: arrived.append(1))

    arrived = []
    agenda.launch("x1", exchange, [("x", 4e5), ("y", 4e5)], exchange_landed)
    agenda.spend(1.0)
    segment_lane = lax.broadcasted_iota(jnp.int32, (enc.total, 128), 1)
    segment = jnp.where(kind < 0.5, 0, lax.broadcasted_iota(jnp.int32, (enc.total, 128), 0) // (enc.total // 4))
    k_extra[...] = jnp.where(segment_lane == segment, 1.0, 0.0).astype(bf16)
    segment_lane = lax.broadcasted_iota(jnp.int32, (enc.own, 128), 1)
    segment = lax.broadcasted_iota(jnp.int32, (enc.own, 128), 0) + enc.offset
    segment = jnp.where(kind < 0.5, 0, segment // (enc.total // 4))
    q_extra[...] = jnp.where((segment_lane < 4) & (segment_lane != segment), -(2.0**30), 0.0).astype(bf16)
    for ref in (small_dec, small_enc, g_pixw, g_qout, g_qin, g_inw):
        ref[...] = jnp.zeros(ref.shape, f32)
    agenda.spend(2.0)
    agenda.tick()
    agenda.until(lambda: arrived)
    def code_column(k, start=0):
        return jnp.concatenate(
            [jnp.transpose(jnp.broadcast_to(code_all[start + 2 * k + n], (8, 128)))[:, 0:1] for n in range(2)], axis=0
        )

    for n in range(4):
        code_row[:, pl.ds(128 * n, 128)] = code_all[own_band + n]

    def pick_codes(k):
        rows = at(k)
        code_here = code_column(k)
        picks = lax.broadcasted_iota(jnp.int32, (STEP, 512), 1)
        found = jnp.zeros((STEP, 128), f32)
        for z in range(4):
            hot = jnp.where(picks + 512 * z == code_here // 4, 1.0, 0.0).astype(bf16)
            found += dot_nn(hot, book[z].reshape(512, 128))
        lanes = lax.broadcasted_iota(jnp.int32, (STEP, 128), 1) // 32
        spread[rows] = jnp.where(lanes == code_here % 4, found, 0.0).astype(bf16)

    lane = lax.broadcasted_iota(jnp.int32, (4, 128, 256), 2)
    flags = slab_all[pl.ds(own_band, 4), :, 128:384].astype(f32)
    tally[...] = jnp.full(tally.shape, jnp.sum(jnp.where(lane < 64, 0.0, flags)))
    agenda.spend(1.0)
    agenda.tick()
    count_all.begin()
    gather.begin(5, len(dec_pieces))
    gather.until(0)
    agenda.tick()
    loop(0, dec.total // STEP, pick_codes)
    agenda.spend(4.0)
    agenda.tick()
    gather.until(1)
    dec.enter(0, dec.total // STEP)
    agenda.spend(1.9)
    agenda.tick()

    def fetch(landed, ref, sem):
        rows = landed.shape[4]

        def body(n):
            src = landed.at[n // 8, (n // 4) % 2, (n // 2) % 2, n % 2]
            pltpu.make_async_copy(src, ref.at[pl.ds(pl.multiple_of(n * rows, 16), rows)], sem).start()

        loop(0, 32, body)
        return pltpu.make_async_copy(ref, ref, sem)

    reduce = Reduce(agenda, *slots, *red)
    tail = ReduceSmall(
        agenda, (g_edge, g_book), (share_edge, share_book),
        *[red_small[2 * n : 2 * n + 2] for n in range(7)], *red_small[14:],
    )

    def emit_wide(blk, z, full, slot):
        values = [blk.wide_product(*span) for span in pieces_of(896 * z, 896, 3 * width)]
        value = values[0] if len(values) == 1 else jnp.concatenate(values, axis=0)
        full[slot] = value.reshape(2, 2, 2, 112, width)
        agenda.spend(0.6)

    def emit_narrow(blk, z, full, slot):
        values = [blk.narrow_product(*span) for span in pieces_of(640 * z, 640, width)]
        value = values[0] if len(values) == 1 else jnp.concatenate(values, axis=0)
        full[slot, :, :, :, :80] = value.reshape(2, 2, 2, 80, width)
        agenda.spend(0.5)

    pieces = []
    for name, blk, out_wide, out_narrow, order in (
        ("dec", dec, share_wide_dec, share_narrow_dec, DEC_ORDER), ("enc", enc, share_wide, share_narrow, ENC_ORDER)
    ):
        for kind_of, z in order:
            if kind_of == "n":
                needs = name + str(int(z == 0))
                pieces.append(dict(emit=functools.partial(emit_narrow, blk, z), z=z, rows=80, out=out_narrow, needs=needs))
                continue
            piece = dict(z=z, rows=112, out=out_wide, needs=name + str(1 + (z < 2)))
            if name == "dec" and z < 2:
                piece.update(stage=dec.slope, first=896 * z)
            else:
                piece.update(emit=functools.partial(emit_wide, blk, z))
            pieces.append(piece)
    reduce.plan(pieces)

    def spend(time):
        agenda.spend(time)
        agenda.tick()

    def decoder_head(k):
        rows = at(k)
        out = dec.grad_out[rows]
        shape, _ = norm_parts(out)
        final = (shape * norms[pl.ds(8, 1), :] + norms[pl.ds(9, 1), :]).astype(bf16)
        error = dot_nn(final, e_pix()) - pixel_rows(k, 0, own_band).astype(f32)
        lane = lax.broadcasted_iota(jnp.int32, (STEP, 256), 1)
        counted = jnp.where(lane < 192, pltpu.roll(pixel_rows(k, 128, own_band).astype(f32), 192, 1), 0.0)
        number = tally_all[0:1, 0:1]
        dec.add_loss(jnp.sum(counted * (error * error + jnp.abs(error))) / number)
        sign = jnp.where(error > 0.0, 1.0, jnp.where(error < 0.0, -1.0, 0.0))
        grad_pred = (counted * (2.0 * error + sign) / number).astype(bf16)
        g_pixw[...] += dot_tn(final, grad_pred)
        back, g_gain, g_offset = norm_back(dot_nt(grad_pred, e_pix()), out, norms[pl.ds(8, 1), :])
        dec.add_small(4, g_gain)
        dec.add_small(5, g_offset)
        dec.grad_out[rows] = back
        dec.grad_low[rows] = back.astype(bf16)

    def encoder_head(k):
        rows = at(k)
        low = enc.grad_out[rows].astype(bf16)
        lanes = lax.broadcasted_iota(jnp.int32, (STEP, 128), 1) // 32
        mine = lanes == code_column(k, own_band) % 4
        gap = jnp.where(mine, spread[at(k, enc.offset)].astype(f32) - dot_nn(low, e_qin()), 0.0)
        enc.add_loss((1.0 + commitment) * jnp.sum(gap * gap) / latent_total)
        grad_latent = jnp.where(mine, cross[rows] - 2.0 * commitment * gap / latent_total, 0.0).astype(bf16)
        g_qin[...] += dot_tn(low, grad_latent)
        back = dot_nt(grad_latent, e_qin())
        enc.grad_out[rows] = back
        enc.grad_low[rows] = back.astype(bf16)
        gap = 2.0 * gap / latent_total
        high = gap.astype(bf16)
        left = gap - high.astype(f32)
        between = left.astype(bf16)
        enc.gatt[rows, :384] = jnp.concatenate([high, between, (left - between.astype(f32)).astype(bf16)], axis=1)

    def book_rows(k):
        picks = lax.broadcasted_iota(jnp.int32, (STEP, enc.own), 0) + k * STEP
        hot = jnp.where(picks == code_row[...] // 4, 1.0, 0.0).astype(bf16)
        summed = dot_nn(hot, enc.gatt[:, :384])
        value = (summed[:, :128] + summed[:, 128:256]) + summed[:, 256:]
        g_book[k // 2, k % 2] = value.reshape(2, 2, 64, 128)

    def decoder_leave(k):
        low = dec.leave_rows(k)
        cross[at(k)] = dot_nn(low, e_qout())
        g_qout[...] += dot_tn(low, spread[at(k, dec.offset)])

    def encoder_leave(k):
        g_inw[...] += dot_tn(enc.leave_rows(k), pixel_rows(k, 0, own_band))

    gather_enc.begin(0, len(enc_pieces))
    gather.until(2, 3, 4)
    fetch(land_wide_dec, wide, load_sem.at[0]).wait()
    spend(2.0)
    dec.make_kv(0, dec.total // STEP)
    dec.make_q()
    spend(2.9)
    dec.attend(0, 4)
    spend(11.1)
    gather.until(*range(5, len(dec_pieces)))
    fetched = fetch(land_narrow_dec, narrow, load_sem.at[1])
    agenda.spend(1.0)
    fetched.wait()
    dec.after_attention()
    spend(1.1)
    dec.mlp(0, 4)
    spend(5.6)
    count_all.until()
    loop(0, dec.chunks, decoder_head)
    agenda.spend(2.0)
    reduce.allow("dec0")
    agenda.tick()
    dec.mlp_back(0, dec.chunks)
    agenda.spend(6.1)
    reduce.allow("dec1")
    agenda.tick()
    dec.attend_back_all(True)
    spend(15.8)
    gather_enc.until(*range(len(enc_pieces)))
    fetched = fetch(land_narrow, narrow, load_sem.at[1])
    dec.swap_finish(False)
    agenda.spend(2.0)
    for z in range(2):
        values = [dec.wide_product(*span) for span in pieces_of(896 * z, 896, 3 * width)]
        dec.slope[pl.ds(896 * z, 896)] = values[0] if len(values) == 1 else jnp.concatenate(values, axis=0)
    agenda.spend(1.2)
    reduce.allow("dec2")
    agenda.tick()
    loop(0, dec.chunks, decoder_leave)
    fetched_wide = fetch(land_wide, wide, load_sem.at[0])
    spend(2.0)
    emitted = 1 + max(p for p in range(8) if "emit" in pieces[p])
    staged = [p for p in range(8) if "stage" in pieces[p]]
    agenda.until(lambda: reduce.opened >= emitted)
    enc.enter(0, enc.total // STEP)
    spend(1.9)
    fetched_wide.wait()
    enc.make_kv(0, enc.total // STEP)
    enc.make_q()
    fetched.wait()
    spend(2.9)
    enc.attend(0, 4)
    spend(11.1)
    enc.after_attention()
    spend(1.1)
    agenda.until(lambda: reduce.opened > max(staged) and not any(("r", p, 0) in agenda.flying for p in staged))
    enc.mlp(0, 4)
    spend(5.6)
    loop(0, enc.chunks, encoder_head)
    agenda.spend(2.0)
    reduce.allow("enc0")
    agenda.tick()
    loop(0, 8, book_rows)
    tail.open(1)
    spend(2.0)
    enc.mlp_back(0, enc.chunks)
    agenda.spend(6.1)
    reduce.allow("enc1")
    agenda.tick()
    enc.attend_back(0, 2)
    enc.swap_start(0, False)
    spend(7.9)
    enc.attend_back(2, 4)
    enc.swap_start(2, False)
    spend(7.9)
    enc.swap_finish(True)
    agenda.spend(2.0)
    reduce.allow("enc2")
    agenda.tick()
    loop(0, enc.chunks, encoder_leave)
    agenda.spend(2.0)

    def all_groups(value):
        value = value + pltpu.roll(value, 64, 1)
        return value + pltpu.roll(value, 32, 1)

    lane = lax.broadcasted_iota(jnp.int32, (width, 128), 1)
    mixed = jnp.where(lane < 64, g_inw[:, 128:], jnp.where(lane < 96, all_groups(g_qin[...]), all_groups(g_qout[...])))
    for first, value in ((0, g_inw[:, :128]), (128, mixed), (256, g_pixw[:, :128]), (384, g_pixw[:, 128:])):
        g_edge[:, :, :, :, :, pl.ds(first, 128)] = value.reshape(4, 2, 2, 2, 16, 128)
    tail.open(0)
    agenda.until(lambda: len(reduce.ended) == len(pieces) and len(tail.done) == 2)
    shares = (share_wide_dec, share_narrow_dec, share_wide, share_narrow, share_edge, share_book)
    squares = sum(jnp.sum(share[...] * share[...]) for share in shares)
    lane = lax.broadcasted_iota(jnp.int32, (8, width), 1)
    row = lax.broadcasted_iota(jnp.int32, (8, width), 0)
    small_own[0] = small_enc[...]
    small_own[1] = jnp.where((row == 7) & (lane == 0), squares, small_dec[...])
    sum_all = Everywhere("a", agenda, small_own, s_img, s_band, s_send, s_recv, small_all)
    sum_all.begin()
    sum_all.until()


def train_step(shards, slab, code, kinds, norms, latent_total, total_rows, own_rows):
    width = 512
    slots = (4, 4)
    f32, bf16, int32 = jnp.float32, jnp.bfloat16, jnp.int32
    any_space = pl.BlockSpec(memory_space=pl.ANY)
    vmem = pl.BlockSpec(memory_space=pltpu.VMEM)
    shape = jax.ShapeDtypeStruct
    out_shape = [
        shape((112, width), f32), shape((80, width), f32), shape((112, width), f32), shape((80, width), f32),
        shape((16, width), f32), shape((64, 128), f32), shape((2, 8, width), f32),
    ]
    out_shape += [shape((4, 2, 2, 2) + s.shape, s.dtype) for s in shards[2:]]
    dma = pltpu.SemaphoreType.DMA
    mem = pltpu.VMEM
    scratch = gather_sems(5 + len(DEC_NARROW)) + gather_sems(len(ENC_WIDE) + len(ENC_NARROW))
    scratch += reduce_scratch(*slots, 112, width) + reduce_small_scratch([(16, width), (64, 128)])
    scratch += [
        mem((4, 2, 2, 2, 64, 128), bf16), mem((4, 2, 2, 2, 16, 768), bf16),
        mem((8, 128, 384), bf16), mem((8, 1, 128), int32), mem((8, 128), f32), mem((8, 128), f32),
        mem((4, 8, 128), f32), mem((8, 8, 128), f32),
        dma((2,)), dma((2, 8)), dma((2, 8)), dma((11,)), dma((11,)),
        mem((1, own_rows), int32), mem((total_rows, 128), bf16),
        mem((own_rows, 128), f32),
        mem((width, 256), f32), mem((width, 128), f32), mem((width, 128), f32), mem((width, 256), f32),
        mem((4, 2, 2, 2, 16, width), f32), mem((4, 2, 2, 2, 64, 128), f32),
        mem((8, width), f32), mem((8, width), f32), mem((2, 8, width), f32),
        mem((4, 2, 8, width), f32), mem((8, 2, 8, width), f32), dma((11,)), dma((11,)),
        dma((2,)), mem((7 * width, width), bf16), mem((5 * width, width), bf16),
        mem((own_rows, 128), bf16), mem((total_rows, 128), bf16),
    ]
    scratch += block_scratch(total_rows, own_rows)
    return pl.pallas_call(
        functools.partial(step_kernel, slots, latent_total),
        out_shape=out_shape,
        in_specs=[any_space] * 8 + [vmem] * 2,
        out_specs=[vmem] * 7 + [any_space] * 4,
        scratch_shapes=scratch,
        compiler_params=pltpu.CompilerParams(collective_id=0, has_side_effects=True, vmem_limit_bytes=(639 << 20) // 10),
        name="train_step",
    )(*shards, slab, code, kinds, norms)


def moments(gradient, first_old, second_old):
    first_new = beta_first * first_old + (1.0 - beta_first) * gradient
    second_new = beta_second * second_old + (1.0 - beta_second) * gradient * gradient
    return (first_new, second_new, first_new / (jnp.sqrt(second_new) + adam_eps))


def rotated_update(weight, gradient, first_old, second_old, basis_stack):
    turned = jnp.einsum("rld,lde->rle", gradient, basis_stack, precision=highest)
    first_new, second_new, direction = moments(turned, first_old, second_old)
    turned_back = jnp.einsum("rle,lde->rld", direction, basis_stack, precision=highest)
    return (weight - rate_matrix * (turned_back + weight_decay * weight), first_new, second_new)


def plain_update(weight, gradient, first_old, second_old):
    first_new, second_new, direction = moments(gradient, first_old, second_old)
    return (weight - rate_vector * (direction + weight_decay * weight), first_new, second_new)


def update_kernel(*refs):
    count = 20
    ins, refs = refs[:count], refs[count:]
    outs, held, sem = refs[:13], refs[13 : 13 + count], refs[13 + count]
    loads = {k: [pltpu.make_async_copy(ins[k], held[k], sem.at[k])] for k in range(count) if k != 18}
    loads[18] = [pltpu.make_async_copy(ins[18].at[k], held[18].at[k], sem.at[18 if k == 0 else 19 + k]) for k in range(4)]
    order = (5, 15, 16, 17, 4, 12, 13, 14, 19, 0, 1, 6, 7, 8, 18, 2, 3, 9, 10, 11)
    for k in order:
        for load in loads[k]:
            load.start()

    def need(*wanted):
        for k in wanted:
            while loads[k]:
                loads[k].pop(0).wait()

    refs = held + outs
    wide_0, wide_1, narrow_0, narrow_1, edge, small = refs[:6]
    wide, narrow, edge_set, norm_set = refs[6:9], refs[9:12], refs[12:15], refs[15:18]
    bases, basis_edge = refs[18:20]
    new_wide, new_narrow, new_edge, new_norms, scalars = refs[20:23], refs[23:26], refs[26:29], refs[29:32], refs[32]
    need(5, 15, 16, 17)
    norm_grad = jnp.concatenate([small[0, 0:4], small[1, 0:6]], axis=0)
    squares = small[1, 7:8, 0:1] + jnp.sum(norm_grad * norm_grad)
    grad_norm = jnp.sqrt(squares)
    factor = jnp.minimum(1.0, clip_level / grad_norm)
    scalars[0:1] = jnp.broadcast_to(grad_norm, (1, 128))
    scalars[1:2] = jnp.broadcast_to(factor, (1, 128))
    scalars[2:3] = jnp.broadcast_to(small[0, 6:7, 0:1] + small[1, 6:7, 0:1], (1, 128))
    scalars[3:8] = jnp.zeros((5, 128), jnp.float32)

    def halves(value):
        high = value.astype(jnp.bfloat16)
        return high, (value - high.astype(jnp.float32)).astype(jnp.bfloat16)

    def product(left, right, dot):
        (high, low), (right_high, right_low) = halves(left), right
        both = dot(jnp.concatenate([high, low], axis=0), right_high)
        rows = left.shape[0]
        return both[:rows] + (dot(high, right_low) + both[rows:])

    def turn(weight, gradient, first_old, second_old, basis):
        right = halves(basis)
        turned = product(gradient, right, dot_nn)
        first_new, second_new, direction = moments(turned, first_old, second_old)
        back = product(direction, right, dot_nt)
        return weight - rate_matrix * (back + weight_decay * weight), first_new, second_new

    need(4, 12, 13, 14, 19)
    packed = edge[...]
    grad_edge = jnp.concatenate([packed[:, :192], packed[:, 256:448], packed[:, 192:256]], axis=1)
    found = turn(edge_set[0][...], factor * grad_edge, edge_set[1][...], edge_set[2][...], basis_edge[...])
    for ref, value in zip(new_edge, found):
        ref[...] = value
    found = plain_update(norm_set[0][...], factor * norm_grad, norm_set[1][...], norm_set[2][...])
    for ref, value in zip(new_norms, found):
        ref[...] = value
    for k, (olds, news, grads) in enumerate(
        ((wide, new_wide, (wide_0, wide_1)), (narrow, new_narrow, (narrow_0, narrow_1)))
    ):
        for layer in range(2):
            need(2 * k + layer, 6 + 3 * k, 7 + 3 * k, 8 + 3 * k)
            loads[18].pop(0).wait()
            found = turn(
                olds[0][:, layer], factor * grads[layer][...], olds[1][:, layer], olds[2][:, layer], bases[2 * k + layer]
            )
            for ref, value in zip(news, found):
                ref[:, layer] = value


def update_all(grads, wide, narrow, edge, norms, bases, basis_edge):
    vmem = pl.BlockSpec(memory_space=pltpu.VMEM)
    shape = jax.ShapeDtypeStruct
    sets = wide + narrow + edge + norms
    return pl.pallas_call(
        update_kernel,
        out_shape=[shape(a.shape, a.dtype) for a in sets] + [shape((8, 128), jnp.float32)],
        in_specs=[pl.BlockSpec(memory_space=pl.ANY)] * (len(grads) + len(sets) + 2),
        out_specs=[vmem] * (len(sets) + 1),
        scratch_shapes=[pltpu.VMEM(a.shape, a.dtype) for a in (*grads, *sets, bases, basis_edge)]
        + [pltpu.SemaphoreType.DMA((len(grads) + len(sets) + 5,))],
        compiler_params=pltpu.CompilerParams(vmem_limit_bytes=63 << 20),
        name="update_all",
    )(*grads, *sets, bases, basis_edge)


def body(
    pixels,
    valid,
    codes,
    image_kind,
    w_wide,
    w_narrow,
    w_edge,
    codebook,
    norms,
    bases,
    basis_edge,
    m_wide,
    v_wide,
    m_narrow,
    v_narrow,
    m_edge,
    v_edge,
    m_code,
    v_code,
    m_norm,
    v_norm,
):
    band_count = lax.axis_size("band")
    band_index = lax.axis_index("band")
    row_count = pixels.shape[2]
    length = row_count * band_count
    batch_count = pixels.shape[0]
    group = band_count // batch_count
    row = band_index // group
    part = band_index % group
    own_rows = length // group
    groups = [[k * group + j for j in range(group)] for k in range(batch_count)]
    layer_count = w_wide.shape[1]
    code_width = codebook.shape[1]
    latent_total = batch_count * lax.axis_size("img") * length * code_width
    both = ("img", "band")

    direct = band_count == 8 and lax.axis_size("img") == 4 and batch_count == 4
    shards = [w_wide[:, l].astype(jnp.bfloat16) for l in range(layer_count)]
    shards += [w_narrow[:, l].astype(jnp.bfloat16) for l in range(layer_count)]
    shards += [w_edge.astype(jnp.bfloat16), codebook.astype(jnp.bfloat16).reshape(-1, 4 * code_width)]
    slab = jnp.concatenate([pixels[:, 0], valid[:, 0].astype(jnp.bfloat16)], axis=2)
    patch_size = pixels.shape[3]
    if direct:
        edge = shards[4]
        gap = jnp.zeros((edge.shape[0], 64), edge.dtype)
        qin = edge[:, 2 * patch_size : 2 * patch_size + code_width]
        qout = edge[:, 2 * patch_size + code_width :]
        shards[4] = jnp.concatenate(
            [edge[:, :patch_size], gap, edge[:, patch_size : 2 * patch_size], gap] + [qin] * 4 + [qout] * 4, axis=1
        )
        out = train_step(
            [shards[k] for k in (5, 4, 1, 3, 0, 2)], slab, codes, image_kind.reshape(1, -1), norms, latent_total, length, own_rows
        )
        new = update_all(
            (out[2], out[0], out[3], out[1], out[4], out[6]), (w_wide, m_wide, v_wide), (w_narrow, m_narrow, v_narrow),
            (w_edge, m_edge, v_edge), (norms, m_norm, v_norm), bases, basis_edge,
        )
        scalars = new[12]
        grad_norm, factor, loss_total = scalars[0, 0], scalars[1, 0], scalars[2, 0]
        new_code = plain_update(codebook, factor * out[5].reshape(-1, code_width), m_code, v_code)
        return tuple(new[:9]) + new_code + tuple(new[9:12]) + (grad_norm, loss_total)
    wholes = [lax.all_gather(shard, both, axis=0, tiled=True) for shard in shards]
    count = lax.psum(jnp.sum(valid.astype(jnp.float32)), both)

    def whole_row(local):
        everywhere = lax.all_gather(local, "band", axis=0)
        chosen_row = lax.dynamic_index_in_dim(everywhere, row, axis=1, keepdims=False)
        return chosen_row.reshape((length,) + local.shape[2:])

    slab_all = whole_row(slab)
    code_all = whole_row(codes[:, 0])
    kind = lax.dynamic_index_in_dim(image_kind[:, 0], row, 0, keepdims=False)
    span = jnp.where(kind == 0, length, length // 4)
    positions = jnp.arange(length, dtype=jnp.int32)
    gathered = (wholes[:2], wholes[2:4], wholes[4], wholes[5])
    pixel_all = slab_all[:, :patch_size]
    valid_rows = lax.dynamic_slice_in_dim(slab_all, part * own_rows, own_rows, 0)[:, patch_size:]
    own_positions = part * own_rows + jnp.arange(own_rows, dtype=jnp.int32)
    allowed = (own_positions // span)[:, None] == (positions // span)[None, :]
    local_grads, norm_sum, loss_sum = row_step(
        gathered, norms, pixel_all, valid_rows, code_all, part, allowed, count, latent_total, groups
    )
    shares = [lax.psum_scatter(g, both, scatter_dimension=0, tiled=True) for g in local_grads]
    squares = sum(jnp.sum(share * share) for share in shares)
    norm_total, square_total, loss_total = lax.psum((norm_sum, squares, loss_sum), both)
    grad_sum = (
        jnp.stack([shares[0], shares[1]], axis=1),
        jnp.stack([shares[2], shares[3]], axis=1),
        shares[4],
        shares[5].reshape(-1, code_width),
    )
    grad_norm = jnp.sqrt(square_total + jnp.sum(norm_total * norm_total))
    factor = jnp.minimum(1.0, clip_level / grad_norm)
    grad_wide, grad_narrow, grad_edge, grad_book = grad_sum
    new_wide, new_m_wide, new_v_wide = rotated_update(
        w_wide, factor * grad_wide, m_wide, v_wide, bases[:layer_count]
    )
    new_narrow, new_m_narrow, new_v_narrow = rotated_update(
        w_narrow, factor * grad_narrow, m_narrow, v_narrow, bases[layer_count:]
    )
    new_edge, new_m_edge, new_v_edge = rotated_update(
        w_edge[:, None],
        factor * grad_edge[:, None],
        m_edge[:, None],
        v_edge[:, None],
        basis_edge[None],
    )
    new_book, new_m_code, new_v_code = plain_update(codebook, factor * grad_book, m_code, v_code)
    new_norms, new_m_norm, new_v_norm = plain_update(norms, factor * norm_total, m_norm, v_norm)
    return (
        new_wide,
        new_m_wide,
        new_v_wide,
        new_narrow,
        new_m_narrow,
        new_v_narrow,
        new_edge[:, 0],
        new_m_edge[:, 0],
        new_v_edge[:, 0],
        new_book,
        new_m_code,
        new_v_code,
        new_norms,
        new_m_norm,
        new_v_norm,
        grad_norm,
        loss_total,
    )


def solution(mesh):
    in_specs = (
        P(None, "img", "band", None),
        P(None, "img", "band", None),
        P(None, "img", "band"),
        P(None, "img"),
        P(("img", "band"), None, None),
        P(("img", "band"), None, None),
        P(("img", "band"), None),
        P(("img", "band"), None),
        P(),
        P(),
        P(),
        P(("img", "band"), None, None),
        P(("img", "band"), None, None),
        P(("img", "band"), None, None),
        P(("img", "band"), None, None),
        P(("img", "band"), None),
        P(("img", "band"), None),
        P(("img", "band"), None),
        P(("img", "band"), None),
        P(),
        P(),
    )
    out_specs = (
        P(("img", "band"), None, None),
        P(("img", "band"), None, None),
        P(("img", "band"), None, None),
        P(("img", "band"), None, None),
        P(("img", "band"), None, None),
        P(("img", "band"), None, None),
        P(("img", "band"), None),
        P(("img", "band"), None),
        P(("img", "band"), None),
        P(("img", "band"), None),
        P(("img", "band"), None),
        P(("img", "band"), None),
        P(),
        P(),
        P(),
        P(),
        P(),
    )
    return jax.shard_map(body, mesh=mesh, in_specs=in_specs, out_specs=out_specs, check_vma=False)
```

```python
import functools

import jax
import jax.numpy as jnp
from jax import lax
from jax.experimental import pallas as pl
from jax.experimental.pallas import tpu as pltpu
from jax.sharding import PartitionSpec as P

HEADS = 8
HDIM = 64
MESH = pl.DeviceIdType.MESH


norm_eps = 1e-05
adam_eps = 1e-08
clip_level = 0.001
beta_first = 0.5
beta_second = 0.6
rate_matrix = 0.02
rate_vector = 0.3
weight_decay = 0.01
commitment = 0.25
masked_score = -1000000000.0
highest = lax.Precision.HIGHEST


def matmul_plain(first_op, second_op):
    return jnp.dot(first_op, second_op, preferred_element_type=jnp.float32)


def matmul_trans(first_op, second_op):
    return lax.dot_general(
        first_op, second_op, (((1,), (1,)), ((), ())), preferred_element_type=jnp.float32
    )


def matmul_outer(first_op, second_op):
    return lax.dot_general(
        first_op, second_op, (((0,), (0,)), ((), ())), preferred_element_type=jnp.float32
    )


def layer_norm(hidden, scale_gain, offset):
    centred = hidden - jnp.mean(hidden, axis=-1, keepdims=True)
    spread = jnp.mean(centred * centred, axis=-1, keepdims=True)
    return centred * lax.rsqrt(spread + norm_eps) * scale_gain + offset


def gelu_tanh(inputs):
    return (
        0.5
        * inputs
        * (1.0 + jnp.tanh(0.7978845608028654 * (inputs + 0.044715 * inputs * inputs * inputs)))
    )


def split_heads(matrix):
    return matrix.reshape(matrix.shape[0], HEADS, HDIM)


def head_scores(q_heads, k_heads, allowed):
    scores = jnp.einsum(
        "qhd,khd->hqk", q_heads, k_heads, preferred_element_type=jnp.float32
    ) * HDIM ** (-0.5)
    return jnp.where(allowed[None], scores, masked_score)


def attend(queries, key_rows, value_rows, allowed):
    scores = head_scores(split_heads(queries), split_heads(key_rows), allowed)
    score_peak = jnp.max(scores, axis=-1, keepdims=True)
    expo = jnp.exp(scores - score_peak)
    total = jnp.sum(expo, axis=-1, keepdims=True)
    softmaxed = (expo / total).astype(jnp.bfloat16)
    attended = jnp.einsum(
        "hqk,khd->qhd", softmaxed, split_heads(value_rows), preferred_element_type=jnp.float32
    )
    return (
        attended.reshape(queries.shape[0], -1).astype(jnp.bfloat16),
        score_peak + jnp.log(total),
    )


def attend_back(queries, key_rows, value_rows, allowed, log_total, grad_out):
    q_heads = split_heads(queries)
    k_heads = split_heads(key_rows)
    v_heads = split_heads(value_rows)
    g_heads = split_heads(grad_out)
    softmaxed = jnp.exp(head_scores(q_heads, k_heads, allowed) - log_total)
    grad_soft = jnp.einsum("qhd,khd->hqk", g_heads, v_heads, preferred_element_type=jnp.float32)
    row_dot = jnp.sum(softmaxed * grad_soft, axis=-1, keepdims=True)
    grad_scores = (softmaxed * (grad_soft - row_dot)).astype(jnp.bfloat16)
    scale = HDIM ** (-0.5)
    grad_q = (
        jnp.einsum("hqk,khd->qhd", grad_scores, k_heads, preferred_element_type=jnp.float32) * scale
    )
    grad_k = (
        jnp.einsum("hqk,qhd->khd", grad_scores, q_heads, preferred_element_type=jnp.float32) * scale
    )
    grad_v = jnp.einsum(
        "hqk,qhd->khd", softmaxed.astype(jnp.bfloat16), g_heads, preferred_element_type=jnp.float32
    )
    return (
        grad_q.reshape(queries.shape[0], -1),
        grad_k.reshape(key_rows.shape[0], -1),
        grad_v.reshape(key_rows.shape[0], -1),
    )


def block_forward(hidden_all, part, wide_rows, narrow_rows, gain_rows, allowed):
    model_width = hidden_all.shape[1]
    own_rows = allowed.shape[0]
    normed_all = layer_norm(hidden_all, gain_rows[0], gain_rows[1]).astype(jnp.bfloat16)
    hidden = lax.dynamic_slice_in_dim(hidden_all, part * own_rows, own_rows, 0)
    normed = lax.dynamic_slice_in_dim(normed_all, part * own_rows, own_rows, 0)
    queries = matmul_trans(normed, wide_rows[:model_width]).astype(jnp.bfloat16)
    key_rows = matmul_trans(normed_all, wide_rows[model_width : 2 * model_width]).astype(jnp.bfloat16)
    value_rows = matmul_trans(normed_all, wide_rows[2 * model_width : 3 * model_width]).astype(jnp.bfloat16)
    attended, log_total = attend(queries, key_rows, value_rows, allowed)
    middle = hidden + matmul_plain(attended, narrow_rows[:model_width])
    second = layer_norm(middle, gain_rows[2], gain_rows[3]).astype(jnp.bfloat16)
    upper_in = matmul_trans(second, wide_rows[3 * model_width :])
    active = gelu_tanh(upper_in).astype(jnp.bfloat16)
    result = middle + matmul_plain(active, narrow_rows[model_width:])
    return (
        result,
        (hidden, normed, queries, key_rows, value_rows, attended, log_total, middle, second, upper_in, active),
    )


def block_backward(grad_out, wide_rows, narrow_rows, gain_rows, allowed, saved, groups):
    (hidden, normed, queries, key_rows, value_rows, attended, log_total, middle, second, upper_in, active) = saved
    model_width = hidden.shape[1]
    grad_y = grad_out.astype(jnp.bfloat16)
    grad_down = matmul_outer(active, grad_y)
    grad_active = matmul_trans(grad_y, narrow_rows[model_width:])
    grad_upper = jax.vjp(gelu_tanh, upper_in)[1](grad_active)[0].astype(jnp.bfloat16)
    grad_up = matmul_outer(grad_upper, second)
    _, second_back = jax.vjp(layer_norm, middle, gain_rows[2], gain_rows[3])
    grad_mid, gain_two, offset_two = second_back(
        matmul_plain(grad_upper, wide_rows[3 * model_width :])
    )
    grad_mid = grad_mid + grad_out
    grad_attn = grad_mid.astype(jnp.bfloat16)
    grad_outproj = matmul_outer(attended, grad_attn)
    grad_att = matmul_trans(grad_attn, narrow_rows[:model_width]).astype(jnp.bfloat16)
    grad_q, grad_keys, grad_values = attend_back(
        queries, key_rows, value_rows, allowed, log_total, grad_att
    )
    grad_k = lax.psum_scatter(grad_keys, "band", scatter_dimension=0, tiled=True, axis_index_groups=groups)
    grad_v = lax.psum_scatter(grad_values, "band", scatter_dimension=0, tiled=True, axis_index_groups=groups)
    grad_mixed = jnp.concatenate([grad_q, grad_k, grad_v], axis=1).astype(jnp.bfloat16)
    grad_qkv = matmul_outer(grad_mixed, normed)
    _, first_back = jax.vjp(layer_norm, hidden, gain_rows[0], gain_rows[1])
    grad_in, gain_one, offset_one = first_back(
        matmul_plain(grad_mixed, wide_rows[: 3 * model_width])
    )
    gain_grads = jnp.stack([gain_one, offset_one, gain_two, offset_two], axis=0)
    return (
        grad_in + grad_mid,
        jnp.concatenate([grad_qkv, grad_up], axis=0),
        jnp.concatenate([grad_outproj, grad_down], axis=0),
        gain_grads,
    )


def pick_codes(code_rows, book_wide, code_width):
    fold = book_wide.shape[1] // code_width
    one_hot = (
        (code_rows // fold)[:, None] == jnp.arange(book_wide.shape[0], dtype=jnp.int32)[None, :]
    ).astype(jnp.bfloat16)
    lane_fold = jnp.arange(book_wide.shape[1], dtype=jnp.int32)[None, :] // code_width
    lane_mask = (code_rows % fold)[:, None] == lane_fold
    spread = jnp.where(lane_mask, matmul_plain(one_hot, book_wide), 0.0)
    chosen = sum(spread[:, k * code_width : (k + 1) * code_width] for k in range(fold))
    return chosen, one_hot, lane_mask


def row_step(gathered, norms, pixel_all, valid_rows, code_all, part, allowed, count, latent_total, groups):
    wide_all, narrow_all, edge_all, book_wide = gathered
    patch_size = pixel_all.shape[1]
    code_width = edge_all.shape[1] // 2 - patch_size
    own_rows = allowed.shape[0]
    edge_in = edge_all[:, :patch_size]
    edge_pix = edge_all[:, patch_size : 2 * patch_size]
    edge_qin = edge_all[:, 2 * patch_size : 2 * patch_size + code_width]
    edge_qout = edge_all[:, 2 * patch_size + code_width :]
    pixel_rows = lax.dynamic_slice_in_dim(pixel_all, part * own_rows, own_rows, 0)
    chosen_all, one_hot_all, lane_mask_all = pick_codes(code_all, book_wide, code_width)
    chosen_low_all = chosen_all.astype(jnp.bfloat16)
    chosen = lax.dynamic_slice_in_dim(chosen_all, part * own_rows, own_rows, 0)
    one_hot = lax.dynamic_slice_in_dim(one_hot_all, part * own_rows, own_rows, 0)
    lane_mask = lax.dynamic_slice_in_dim(lane_mask_all, part * own_rows, own_rows, 0)
    chosen_low = chosen.astype(jnp.bfloat16)
    begin = matmul_trans(chosen_low_all, edge_qout)
    decoded, dec_saved = block_forward(begin, part, wide_all[1], narrow_all[1], norms[4:8], allowed)
    final = layer_norm(decoded, norms[8], norms[9]).astype(jnp.bfloat16)
    predict = matmul_plain(final, edge_pix)
    error = predict - pixel_rows.astype(jnp.float32)
    pixel_mask = valid_rows.astype(jnp.float32)
    loss_pix = jnp.sum(pixel_mask * (error * error + jnp.abs(error))) / count
    grad_pred = (pixel_mask * (2.0 * error + jnp.sign(error)) / count).astype(jnp.bfloat16)
    grad_pixw = matmul_outer(final, grad_pred)
    _, final_back = jax.vjp(layer_norm, decoded, norms[8], norms[9])
    grad_dec, gain_last, offset_last = final_back(matmul_trans(grad_pred, edge_pix))
    grad_begin, dec_wide, dec_narrow, dec_gains = block_backward(
        grad_dec, wide_all[1], narrow_all[1], norms[4:8], allowed, dec_saved, groups
    )
    grad_begin_low = grad_begin.astype(jnp.bfloat16)
    grad_qout = matmul_outer(grad_begin_low, chosen_low)
    start = matmul_trans(pixel_all, edge_in)
    encoded, enc_saved = block_forward(start, part, wide_all[0], narrow_all[0], norms[0:4], allowed)
    encoded_low = encoded.astype(jnp.bfloat16)
    latent = matmul_plain(encoded_low, edge_qin)
    gap = chosen - latent
    loss_part = loss_pix + (1.0 + commitment) * jnp.sum(gap * gap) / latent_total
    grad_latent = (
        matmul_plain(grad_begin_low, edge_qout) - 2.0 * commitment * gap / latent_total
    ).astype(jnp.bfloat16)
    fold = lane_mask.shape[1] // code_width
    gap_wide = jnp.where(lane_mask, jnp.tile(2.0 * gap / latent_total, (1, fold)), 0.0)
    gap_high = gap_wide.astype(jnp.bfloat16)
    gap_rest = gap_wide - gap_high.astype(jnp.float32)
    gap_middle = gap_rest.astype(jnp.bfloat16)
    gap_low = (gap_rest - gap_middle.astype(jnp.float32)).astype(jnp.bfloat16)
    grad_book = (
        matmul_outer(one_hot, gap_high) + matmul_outer(one_hot, gap_middle)
    ) + matmul_outer(one_hot, gap_low)
    grad_qin = matmul_outer(encoded_low, grad_latent)
    grad_start, enc_wide, enc_narrow, enc_gains = block_backward(
        matmul_trans(grad_latent, edge_qin), wide_all[0], narrow_all[0], norms[0:4], allowed, enc_saved, groups
    )
    grad_inw = matmul_outer(grad_start.astype(jnp.bfloat16), pixel_rows)
    grads = (
        enc_wide, dec_wide, enc_narrow, dec_narrow,
        jnp.concatenate([grad_inw, grad_pixw, grad_qin, grad_qout], axis=1),
        grad_book,
    )
    norm_grad = jnp.concatenate([enc_gains, dec_gains, gain_last[None], offset_last[None]], axis=0)
    return (grads, norm_grad, loss_part)


def place():
    img_at = lax.axis_index("img")
    band_at = lax.axis_index("band")
    return img_at, band_at, band_at // 4, (band_at // 2) % 2, band_at % 2


def neighbours():
    img_at, band_at, y_at, x_at, c_at = place()
    return (
        (img_at, band_at + 1 - 2 * c_at),
        (img_at, band_at + 2 - 4 * x_at),
        (img_at, band_at + 4 - 8 * y_at),
    )


def peers():
    img_at, band_at = place()[:2]
    found = [((img_at + step) % 4, band_at) for step in range(1, 4)]
    return found + [(img_at, (band_at + step) % 8) for step in range(1, 8)]


def meet(others):
    barrier = pltpu.get_barrier_semaphore()
    for other in others:
        pl.semaphore_signal(barrier, inc=1, device_id=other, device_id_type=MESH)
    pl.semaphore_wait(barrier, len(others))


def far_copy(src, dst, send, recv, target):
    return pltpu.make_async_remote_copy(
        src_ref=src, dst_ref=dst, send_sem=send, recv_sem=recv, device_id=target, device_id_type=MESH
    )


class Everywhere:
    def __init__(self, name, agenda, own_ref, img_buf, band_buf, send, recv, result_ref):
        self.name, self.agenda, self.done = name, agenda, False
        self.own, self.img_buf, self.band_buf, self.result = own_ref, img_buf, band_buf, result_ref
        self.send, self.recv = send, recv

    def begin(self):
        img_at, band_at = place()[:2]
        self.img_buf[img_at] = self.own[...]
        copies = [
            far_copy(
                self.own, self.img_buf.at[img_at], self.send.at[step], self.recv.at[step], ((img_at + step) % 4, band_at)
            )
            for step in range(1, 4)
        ]
        self.agenda.launch((self.name, 0), copies, [], self.middle)
        self.agenda.spend(0.5)

    def middle(self):
        img_at, band_at = place()[:2]
        buf = self.img_buf
        self.result[...] = (buf[0] + buf[1]) + (buf[2] + buf[3])
        self.band_buf[band_at] = self.result[...]
        copies = [
            far_copy(
                self.result, self.band_buf.at[band_at], self.send.at[3 + step], self.recv.at[3 + step],
                (img_at, (band_at + step) % 8),
            )
            for step in range(1, 8)
        ]
        self.agenda.launch((self.name, 1), copies, [], self.end)
        self.agenda.spend(1.0)

    def end(self):
        total = self.band_buf[0]
        for k in range(1, 8):
            total = total + self.band_buf[k]
        self.result[...] = total
        self.done = True

    def until(self):
        self.agenda.until(lambda: self.done)


LINK, CORE, LAG = 100e3, 500e3, 0.6
SPREAD = {"f01": 3, "f12": 4, "f23": 3, "b10": 3, "b21": 4, "b32": 3}
TOWARDS = (
    {"b10": 3, "b21": 2, "b32": 1},
    {"f01": 1, "b21": 2, "b32": 1},
    {"f01": 1, "f12": 2, "b32": 1},
    {"f01": 1, "f12": 2, "f23": 3},
)


def z_loads(table, size):
    return [(link, count * size) for link, count in table.items()]


class Agenda:
    def __init__(self):
        self.now, self.free, self.flying = 0.0, {}, {}

    def launch(self, key, copies, loads, then):
        done = self.now
        for link, size in loads:
            begin = max(self.now, self.free.get(link, 0.0))
            self.free[link] = begin + size / (CORE if link == "c" else LINK) + 0.4
            done = max(done, self.free[link])
        for copy in copies:
            copy.start()
        self.flying[key] = (done + LAG, copies, then)

    def land(self, key):
        done, copies, then = self.flying.pop(key)
        self.now = max(self.now, done) + 0.5
        for copy in copies:
            copy.wait()
        then()

    def spend(self, time):
        self.now += time

    def tick(self):
        while self.flying:
            key = min(self.flying, key=lambda name: self.flying[name][0])
            if self.flying[key][0] > self.now:
                return
            self.land(key)

    def until(self, test):
        while not test():
            self.land(min(self.flying, key=lambda name: self.flying[name][0]))


class Gather:
    def __init__(self, name, agenda, pieces, near, z_send, z_recv, p_send, p_recv):
        self.name, self.agenda, self.pieces = name, agenda, pieces
        self.near, self.z_send, self.z_recv, self.p_send, self.p_recv = near, z_send, z_recv, p_send, p_recv
        self.done = set()

    def launch(self, p, k):
        img_at, band_at, y_at, x_at, c_at = place()
        over_c, over_x, over_y = neighbours()
        shard, whole, first, count, z_last = self.pieces[p]
        rows = pl.ds(first, count)
        width = shard.shape[1]
        size = count * max(width, 128) * 2
        lanes = width // 256 * 128
        found, loads = [], []
        here, own = whole.at[img_at, y_at, x_at, c_at, rows], shard.at[rows]
        if z_last and k < 2:
            for half in range(2):
                span = pl.ds(lanes, width - lanes) if half else pl.ds(0, lanes)
                along_y = (k == 0) == (half == 0)
                if k == 0:
                    src, dst = shard.at[rows, span], whole.at[img_at, y_at, x_at, c_at, rows, span]
                elif half == 0:
                    src = dst = whole.at[img_at, :, x_at, c_at, rows, span]
                else:
                    src = dst = whole.at[img_at, y_at, :, c_at, rows, span]
                slot = 2 * k + half
                target = over_y if along_y else over_x
                found.append(far_copy(src, dst, self.p_send.at[p, slot], self.p_recv.at[p, slot], target))
                loads.append(("y" if along_y else "x", (1 + k) * size))
            if k == 0:
                found.append(pltpu.make_async_copy(own, here, self.near.at[p]))
        elif z_last and k == 2:
            part = whole.at[img_at, :, :, c_at, rows]
            found = [
                far_copy(part, part, self.z_send.at[p, step], self.z_recv.at[p, step], ((img_at + step) % 4, band_at))
                for step in range(1, 4)
            ]
            loads = z_loads(SPREAD, 8 * size)
        elif k == 0:
            found = [
                far_copy(own, here, self.z_send.at[p, step], self.z_recv.at[p, step], ((img_at + step) % 4, band_at))
                for step in range(1, 4)
            ]
            found.append(pltpu.make_async_copy(own, here, self.near.at[p]))
            loads = z_loads(SPREAD, 2 * size)
        elif k == 3:
            part = whole.at[:, :, :, c_at, rows]
            found = [far_copy(part, part, self.p_send.at[p, 4], self.p_recv.at[p, 4], over_c)]
            loads = [("c", 16 * size)]
        else:
            for half in range(2):
                span = pl.ds(lanes, width - lanes) if half else pl.ds(0, lanes)
                if lanes == 0 and half == 0:
                    continue
                if k == 1:
                    part = whole.at[:, y_at, x_at, c_at, rows, span]
                elif half == 0:
                    part = whole.at[:, :, x_at, c_at, rows, span]
                else:
                    part = whole.at[:, y_at, :, c_at, rows, span]
                slot = 2 * (k - 1) + half
                along_y = (k == 1) == (half == 0)
                target = over_y if along_y else over_x
                found.append(far_copy(part, part, self.p_send.at[p, slot], self.p_recv.at[p, slot], target))
                loads.append(("y" if along_y else "x", 4 * k * size))

        def then():
            if k < 3:
                self.launch(p, k + 1)
            else:
                self.done.add(p)

        self.agenda.launch((self.name, p), found, loads, then)

    def begin(self, first, last):
        for p in range(first, last):
            self.launch(p, 0)

    def until(self, *wanted):
        self.agenda.until(lambda: all(p in self.done for p in wanted))


def gather_sems(count):
    dma = pltpu.SemaphoreType.DMA
    return [dma((count,)), dma((count, 4)), dma((count, 4)), dma((count, 5)), dma((count, 5))]


class Reduce:
    def __init__(
        self, agenda, slots, wait_z, full, pair, first_a, first_b, second_a, second_b, ours, last,
        near, p_send, p_recv, z_send, z_recv, free, free_z,
    ):
        self.agenda, self.slots, self.wait_z = agenda, slots, wait_z
        self.full, self.pair, self.ours, self.last = full, pair, ours, last
        self.first, self.second = (first_a, first_b), (second_a, second_b)
        self.near, self.p_send, self.p_recv, self.z_send, self.z_recv = near, p_send, p_recv, z_send, z_recv
        self.free, self.free_z = free, free_z
        self.pieces, self.flying, self.events, self.at_event = [], {}, [], 0
        self.queue, self.opened = [], 0

    def plan(self, pieces):
        self.pieces = pieces
        seen = [0] * 4
        for p, piece in enumerate(pieces):
            piece["slot"] = p % self.slots
            piece["place"] = p % (self.wait_z + 1)
            piece["order"] = seen[piece["z"]]
            seen[piece["z"]] += 1
        for piece in pieces:
            piece["again"] = piece["order"] + 2 < seen[piece["z"]]
        self.opened, self.passed, self.ended = 0, set(), set()
        self.ready = {""}

    def feed(self):
        while self.opened < len(self.pieces):
            p = self.opened
            if self.pieces[p]["needs"] not in self.ready or (p >= self.slots and p - self.slots not in self.passed):
                return
            self.opened += 1
            self.open(p)

    def allow(self, name):
        self.ready.add(name)
        self.feed()

    def rows(self, p):
        return pl.ds(0, self.pieces[p]["rows"])

    def open(self, p):
        piece = self.pieces[p]
        slot, rows = piece["slot"], self.rows(p)
        c_at = place()[4]
        over_c = neighbours()[0]
        if p >= self.slots:
            for k in range(3):
                pl.semaphore_wait(self.free.at[slot, k], 1)
        landing = self.pair.at[slot, :, :, rows]
        send, recv = self.p_send.at[slot, 0], self.p_recv.at[slot, 0]
        if "stage" in piece:
            stage, first, count = piece["stage"], piece["first"], piece["rows"]
            copies = []
            for n in range(4):
                theirs = pl.ds(pl.multiple_of(first + (2 * n + 1 - c_at) * count, 8), count)
                ours = pl.ds(pl.multiple_of(first + (2 * n + c_at) * count, 8), count)
                spot = 0 if n == 0 else 4 + n
                copies.append(
                    far_copy(
                        stage.at[theirs], self.pair.at[slot, n // 2, n % 2, rows], self.p_send.at[slot, spot],
                        self.p_recv.at[slot, spot], over_c,
                    )
                )
                copies.append(
                    pltpu.make_async_copy(
                        stage.at[ours], self.full.at[slot, n // 2, n % 2, c_at, rows], self.near.at[slot, n]
                    )
                )
        else:
            piece["emit"](self.full, slot)
            copies = [far_copy(self.full.at[slot, :, :, 1 - c_at, rows], landing, send, recv, over_c)]
        size = piece["rows"] * self.full.shape[5] * 4
        self.agenda.launch(("r", p, 0), copies, [("c", 4 * size)], lambda: self.step(0, p))

    def step(self, k, p):
        piece = self.pieces[p]
        slot, rows, z = piece["slot"], self.rows(p), piece["z"]
        size = piece["rows"] * self.full.shape[5] * 4
        img_at, band_at, y_at, x_at, c_at = place()
        over_c, over_x, over_y = neighbours()
        full, half = self.full, self.full.shape[5] // 2
        low, high = pl.ds(0, half), pl.ds(half, half)
        tiles = piece["rows"] // 16

        def tile(n):
            return pl.ds(pl.multiple_of(n % tiles * 16, 16), 16)

        if k == 0:
            def add(n, carry):
                y, x = n // (2 * tiles), n // tiles % 2
                full[slot, y, x, c_at, tile(n)] += self.pair[slot, y, x, tile(n)]
                return carry
            lax.fori_loop(0, 4 * tiles, add, 0)
            parts = (full.at[slot, :, 1 - x_at, c_at, rows, low], full.at[slot, 1 - y_at, :, c_at, rows, high])
            landings = [self.first[n].at[slot, :, rows] for n in range(2)]
            targets = (over_x, over_y)
        elif k == 1:
            def add(n, carry):
                w = n // tiles
                full[slot, w, x_at, c_at, tile(n), low] += self.first[0][slot, w, tile(n)]
                full[slot, y_at, w, c_at, tile(n), high] += self.first[1][slot, w, tile(n)]
                return carry
            lax.fori_loop(0, 2 * tiles, add, 0)
            parts = (full.at[slot, 1 - y_at, x_at, c_at, rows, low], full.at[slot, y_at, 1 - x_at, c_at, rows, high])
            landings = [self.second[n].at[slot, rows] for n in range(2)]
            targets = (over_y, over_x)
        if k < 2:
            copies = [
                far_copy(
                    parts[n], landings[n], self.p_send.at[slot, 1 + 2 * k + n], self.p_recv.at[slot, 1 + 2 * k + n],
                    targets[n],
                )
                for n in range(2)
            ]
            load = 2 * size if k == 0 else size
            self.agenda.launch(("r", p, 1 + k), copies, [("x", load), ("y", load)], lambda: self.step(k + 1, p))
            return
        spot, order = piece["place"], piece["order"] % 2
        mine = self.ours.at[spot, rows]
        owner = (z, band_at)

        def hop(n):
            return far_copy(mine, self.last.at[order, n, rows], self.z_send.at[spot], self.z_recv.at[order, n], owner)

        if k == 2:
            self.agenda.until(lambda: p < self.wait_z + 1 or p - self.wait_z - 1 in self.ended)

            def add(n, carry):
                self.ours[spot, tile(n), low] = full[slot, y_at, x_at, c_at, tile(n), low] + self.second[0][slot, tile(n)]
                self.ours[spot, tile(n), high] = full[slot, y_at, x_at, c_at, tile(n), high] + self.second[1][slot, tile(n)]
                return carry
            lax.fori_loop(0, tiles, add, 0)

            assert p < self.wait_z + 1 or p - self.wait_z - 1 in self.ended

            @pl.when(img_at != z)
            def _():
                if piece["order"] >= 2:
                    pl.semaphore_wait(self.free_z.at[z, order], 1)
                hop((img_at + 3 - z) % 4).start()

            if p + self.slots < len(self.pieces):
                for n, other in enumerate((over_c, over_x, over_y)):
                    pl.semaphore_signal(self.free.at[slot, n], inc=1, device_id=other, device_id_type=MESH)
            self.passed.add(p)
            self.agenda.launch(("r", p, 3), [], z_loads(TOWARDS[z], 2 * size), lambda: self.step(3, p))
            self.feed()
            return

        @pl.when(img_at != z)
        def _():
            hop((img_at + 3 - z) % 4).wait_send()

        @pl.when(img_at == z)
        def _():
            for n in range(3):
                hop(n).wait_recv()

            def add(n, carry):
                piece["out"][tile(n)] = (self.ours[spot, tile(n)] + self.last[order, 0, tile(n)]) + (
                    self.last[order, 1, tile(n)] + self.last[order, 2, tile(n)]
                )
                return carry
            lax.fori_loop(0, tiles, add, 0)
            if piece["again"]:
                for n in range(1, 4):
                    pl.semaphore_signal(
                        self.free_z.at[z, order], inc=1, device_id=((img_at + n) % 4, band_at), device_id_type=MESH
                    )

        self.ended.add(p)


def reduce_scratch(slots, wait_z, rows, width):
    f32 = jnp.float32
    dma = pltpu.SemaphoreType.DMA
    half = width // 2
    return [
        pltpu.VMEM((slots, 2, 2, 2, rows, width), f32),
        pltpu.VMEM((slots, 2, 2, rows, width), f32),
        pltpu.VMEM((slots, 2, rows, half), f32),
        pltpu.VMEM((slots, 2, rows, half), f32),
        pltpu.VMEM((slots, rows, half), f32),
        pltpu.VMEM((slots, rows, half), f32),
        pltpu.VMEM((wait_z + 1, rows, width), f32),
        pltpu.VMEM((2, 3, rows, width), f32),
        dma((slots, 4)),
        dma((slots, 8)), dma((slots, 8)),
        dma((wait_z + 1,)), dma((2, 3)),
        pltpu.SemaphoreType.REGULAR((slots, 3)),
        pltpu.SemaphoreType.REGULAR((4, 2)),
    ]


class ReduceSmall:
    def __init__(self, agenda, grads, shares, own, pair, first_a, first_b, second_a, second_b, last, near, p_send, p_recv, z_send, z_recv):
        self.agenda, self.done = agenda, set()
        self.grads, self.shares, self.own, self.pair = grads, shares, own, pair
        self.first, self.second, self.last = (first_a, first_b), (second_a, second_b), last
        self.near, self.p_send, self.p_recv, self.z_send, self.z_recv = near, p_send, p_recv, z_send, z_recv
        self.flying = {}

    def start(self, p, copies, loads, k):
        size = self.own[p].shape[3] * self.own[p].shape[4] * 4
        self.agenda.launch(("s", p), copies, [(link, n * size) for link, n in loads], lambda: self.step(p, k))

    def open(self, p):
        c_at = place()[4]
        over_c = neighbours()[0]
        self.start(p, [
            far_copy(self.grads[p].at[:, :, :, 1 - c_at], self.pair[p], self.p_send.at[p, 0], self.p_recv.at[p, 0], over_c),
            pltpu.make_async_copy(self.grads[p].at[:, :, :, c_at], self.own[p], self.near.at[p]),
        ], [("c", 16)], 0)

    def step(self, p, k):
        img_at, band_at, y_at, x_at, c_at = place()
        over_c, over_x, over_y = neighbours()
        own = self.own[p]
        rows = own.shape[3]
        span = (pl.ds(0, rows // 2), pl.ds(rows // 2, rows // 2))

        def send(parts, landings, targets, slot):
            copies = [
                far_copy(parts[n], landings[n], self.p_send.at[p, slot + n], self.p_recv.at[p, slot + n], targets[n])
                for n in range(2)
            ]
            self.start(p, copies, [("x", 8 >> k), ("y", 8 >> k)], k + 1)

        if k == 0:
            own[...] += self.pair[p][...]
            send(
                (own.at[:, :, 1 - x_at, span[0]], own.at[:, 1 - y_at, :, span[1]]),
                (self.first[0][p], self.first[1][p]), (over_x, over_y), 1,
            )
        elif k == 1:
            own[:, :, x_at, span[0]] += self.first[0][p][...]
            own[:, y_at, :, span[1]] += self.first[1][p][...]
            send(
                (own.at[:, 1 - y_at, x_at, span[0]], own.at[:, y_at, 1 - x_at, span[1]]),
                (self.second[0][p], self.second[1][p]), (over_y, over_x), 3,
            )
        elif k == 2:
            own[:, y_at, x_at, span[0]] += self.second[0][p][...]
            own[:, y_at, x_at, span[1]] += self.second[1][p][...]
            copies = []
            for n in range(1, 4):
                target = (img_at + n) % 4
                copies.append(
                    far_copy(
                        own.at[target, y_at, x_at], self.last[p].at[n - 1], self.z_send.at[p, n], self.z_recv.at[p, n],
                        (target, band_at),
                    )
                )
            self.start(p, copies, z_loads(SPREAD, 2), 3)
        else:
            last = self.last[p]
            self.done.add(p)
            self.shares[p][...] = (own[img_at, y_at, x_at] + last[0]) + (last[1] + last[2])


def reduce_small_scratch(shapes):
    f32 = jnp.float32
    dma = pltpu.SemaphoreType.DMA
    count = len(shapes)
    groups = [
        [(4, 2, 2, r, w) for r, w in shapes],
        [(4, 2, 2, r, w) for r, w in shapes],
        [(4, 2, r // 2, w) for r, w in shapes],
        [(4, 2, r // 2, w) for r, w in shapes],
        [(4, r // 2, w) for r, w in shapes],
        [(4, r // 2, w) for r, w in shapes],
        [(3, r, w) for r, w in shapes],
    ]
    return [pltpu.VMEM(shape, f32) for group in groups for shape in group] + [
        dma((count,)), dma((count, 5)), dma((count, 5)), dma((count, 4)), dma((count, 4)),
    ]


def dot_nn(a, b):
    return lax.dot_general(a, b, (((1,), (0,)), ((), ())), preferred_element_type=jnp.float32)


def dot_nt(a, b):
    return lax.dot_general(a, b, (((1,), (1,)), ((), ())), preferred_element_type=jnp.float32)


def dot_tn(a, b):
    return lax.dot_general(a, b, (((0,), (0,)), ((), ())), preferred_element_type=jnp.float32)


def norm_parts(h):
    centred = h - jnp.mean(h, axis=-1, keepdims=True)
    rate = lax.rsqrt(jnp.mean(centred * centred, axis=-1, keepdims=True) + norm_eps)
    return centred * rate, rate


def norm_back(grad, h, gain):
    shape, rate = norm_parts(h)
    inner = grad * gain
    back = rate * (
        inner
        - jnp.mean(inner, axis=-1, keepdims=True)
        - shape * jnp.mean(inner * shape, axis=-1, keepdims=True)
    )
    return (
        back,
        jnp.sum(grad * shape, axis=0, keepdims=True),
        jnp.sum(grad, axis=0, keepdims=True),
    )


STEP = 256


def at(k, start=0):
    return pl.ds(pl.multiple_of(start + k * STEP, STEP), STEP)


def lanes_at(k, size, start=0):
    return pl.ds(pl.multiple_of(start + k * size, 128), size)


def loop(first, last, body):
    def step(k, carry):
        body(k)
        return carry

    lax.fori_loop(first, last, step, 0)


class Block:
    def __init__(self, base, source, first_w, small, refs):
        names = (
            "wide", "narrow", "norms", "q_extra", "k_extra", "hidden", "normed", "q_buf", "kv", "mixed_in", "wide_in",
            "middle", "second", "slope", "grad_out", "grad_low", "mid_low", "gatt", "dkv", "dkv_in", "soft", "x_send",
            "x_recv", "x_free",
        )
        for name, ref in zip(names, refs, strict=True):
            setattr(self, name, ref)
        self.base, self.source, self.first_w, self.small = base, source, first_w, small
        self.part = place()[4]
        self.total, self.own = self.kv.shape[0], self.q_buf.shape[0]
        self.width = self.q_buf.shape[1]
        self.offset = pl.multiple_of(self.part * self.own, self.own)
        self.chunks = self.own // STEP
        lane_head = lax.broadcasted_iota(jnp.int32, (1, 128), 1) // HDIM
        self.pick = [jnp.where(lane_head == k, 1.0, 0.0).astype(jnp.bfloat16) for k in range(2)]

    def slope_rows(self, f, k):
        return pl.ds(pl.multiple_of(f * self.own + k * STEP, STEP), STEP)

    def gain(self, k):
        return self.norms[pl.ds(self.base + k, 1), :]

    def add_small(self, row, value):
        self.small[pl.ds(row, 1), :] += value

    def add_loss(self, value):
        first_lane = lax.broadcasted_iota(jnp.int32, (1, self.width), 1) == 0
        self.add_small(6, jnp.where(first_lane, value, 0.0))

    def enter(self, first, last):
        def body(n):
            k = (n + self.chunks * (1 + self.part)) % (self.total // STEP)
            h = dot_nt(self.source(k), self.first_w())
            self.hidden[at(n % self.chunks)] = h
            shape, _ = norm_parts(h)
            self.normed[at(k)] = (shape * self.gain(0) + self.gain(1)).astype(jnp.bfloat16)

        loop(first, last, body)

    def make_kv(self, first, last):
        def body(k):
            self.kv[at(k)] = dot_nt(self.normed[at(k)], self.wide[self.width : 3 * self.width]).astype(jnp.bfloat16)

        loop(first, last, body)

    def make_q(self):
        def body(k):
            q = dot_nt(self.normed[at(k, self.offset)], self.wide[: self.width]).astype(jnp.bfloat16)
            self.q_buf[at(k)] = (q.astype(jnp.float32) * HDIM**-0.5).astype(jnp.bfloat16)

        loop(0, self.chunks, body)

    def scores(self, p, k, rows, k_cat):
        q_cat = jnp.concatenate([self.q_buf[rows, lanes_at(p, 128)] * self.pick[k], self.q_extra[rows]], axis=1)
        return dot_nt(q_cat, k_cat)

    def key_columns(self, p):
        return jnp.concatenate([self.kv[:, lanes_at(p, 128)], self.k_extra[...]], axis=1)

    def attend(self, first, last):
        head_lane = lax.broadcasted_iota(jnp.int32, (STEP, 128), 1)

        def pair(p):
            k_cat = self.key_columns(p)
            v_pair = self.kv[:, lanes_at(p, 128, self.width)]

            def body(j):
                rows = at(j)
                mixed = None
                for k in range(2):
                    scores = self.scores(p, k, rows, k_cat)
                    peak = jnp.max(scores, axis=-1, keepdims=True)
                    expo = jnp.exp(scores - peak)
                    total = jnp.sum(expo, axis=-1, keepdims=True)
                    prob = expo * (1.0 / total)
                    level = peak + jnp.log(total)
                    self.soft[rows] = jnp.where(head_lane == 2 * p + k, level, self.soft[rows])
                    term = dot_nn(prob.astype(jnp.bfloat16), v_pair * self.pick[k])
                    mixed = term if mixed is None else mixed + term
                self.mixed_in[rows, lanes_at(p, 128)] = mixed.astype(jnp.bfloat16)

            loop(0, self.chunks, body)

        loop(first, last, pair)

    def after_attention(self):
        def body(k):
            rows = at(k)
            mid = self.hidden[at(k)] + dot_nn(self.mixed_in[rows, : self.width], self.narrow[: self.width])
            self.middle[rows] = mid
            shape, _ = norm_parts(mid)
            self.second[rows] = (shape * self.gain(2) + self.gain(3)).astype(jnp.bfloat16)
            self.grad_out[rows] = mid

        loop(0, self.chunks, body)

    def mlp(self, first, last):
        width = self.width

        def body(n):
            f, k = n // self.chunks, n % self.chunks
            rows = at(k)
            u = dot_nt(self.second[rows], self.wide[lanes_at(3 + f, width)])
            squared = u * u
            bend = jnp.tanh(0.7978845608028654 * (u + 0.044715 * squared * u))
            low = (0.5 * u * (1.0 + bend)).astype(jnp.bfloat16)
            self.mixed_in[rows, lanes_at(1 + f, width)] = low
            self.slope[self.slope_rows(f, k)] = 0.5 * (1.0 + bend) + (0.5 * u) * (1.0 - bend * bend) * (
                0.7978845608028654 * (1.0 + (3.0 * 0.044715) * squared)
            )
            self.grad_out[rows] += dot_nn(low, self.narrow[lanes_at(1 + f, width)])

        loop(first * self.chunks, last * self.chunks, body)

    def mlp_back(self, first, last):
        width = self.width

        def body(k):
            rows = at(k)
            gy = self.grad_low[rows]

            def feature_step(f, acc):
                ga = dot_nt(gy, self.narrow[lanes_at(1 + f, width)])
                low = (ga * self.slope[self.slope_rows(f, k)]).astype(jnp.bfloat16)
                self.wide_in[rows, lanes_at(3 + f, width)] = low
                return acc + dot_nn(low, self.wide[lanes_at(3 + f, width)])

            grad_second = lax.fori_loop(0, 4, feature_step, jnp.zeros((STEP, width), jnp.float32))
            back, g_gain, g_offset = norm_back(grad_second, self.middle[rows], self.gain(2))
            self.add_small(2, g_gain)
            self.add_small(3, g_offset)
            grad_mid = back + self.grad_out[rows]
            self.grad_out[rows] = grad_mid
            low = grad_mid.astype(jnp.bfloat16)
            self.mid_low[rows] = low
            self.gatt[rows] = dot_nt(low, self.narrow[:width]).astype(jnp.bfloat16)

        loop(first, last, body)

    def attend_back(self, first, last):
        head_lane = lax.broadcasted_iota(jnp.int32, (self.own, 128), 1)
        lane_head = lax.broadcasted_iota(jnp.int32, (1, 128), 1) // HDIM
        rows, bf16 = slice(None), jnp.bfloat16

        def head(h):
            p = h // 2
            pick = jnp.where(lane_head == h % 2, 1.0, 0.0).astype(bf16)
            k_pair = self.kv[:, lanes_at(p, 128)]
            g_rows = self.gatt[rows, lanes_at(p, 128)] * pick
            q_rows = self.q_buf[rows, lanes_at(p, 128)] * pick
            level = jnp.sum(jnp.where(head_lane == h, self.soft[...], 0.0), axis=-1, keepdims=True)
            scores = dot_nt(
                jnp.concatenate([q_rows, self.q_extra[...]], axis=1), jnp.concatenate([k_pair, self.k_extra[...]], axis=1)
            )
            prob = jnp.exp(scores - level)
            d_prob = dot_nt(g_rows, self.kv[:, lanes_at(p, 128, self.width)])
            dot_row = jnp.sum(prob * d_prob, axis=-1, keepdims=True)
            d_score = (prob * (d_prob - dot_row)).astype(bf16)
            dq = (dot_nn(d_score, k_pair * pick) * HDIM**-0.5).astype(bf16)
            self.dkv[p, 0] += dot_tn(d_score, q_rows)
            self.dkv[p, 1] += dot_tn(prob.astype(bf16), g_rows)
            self.wide_in[rows, lanes_at(p, 128)] = self.wide_in[rows, lanes_at(p, 128)] + dq

        self.dkv[pl.ds(first, 2)] = jnp.zeros((2,) + self.dkv.shape[1:], jnp.float32)
        self.wide_in[:, pl.ds(pl.multiple_of(128 * first, 128), 256)] = jnp.zeros((self.own, 256), bf16)
        loop(2 * first, 2 * last, head)

    def swap(self, p):
        theirs = pl.ds(pl.multiple_of((1 - self.part) * self.own, self.own), self.own)
        return far_copy(
            self.dkv.at[p, :, theirs], self.dkv_in.at[p], self.x_send.at[p], self.x_recv.at[p], neighbours()[0]
        )

    def attend_back_all(self, opening):
        if not opening:
            pl.semaphore_wait(self.x_free, 1)

        def half(n):
            self.attend_back(2 * n, 2 * n + 2)
            for p in range(2):
                self.swap(2 * n + p).start()

        loop(0, 2, half)

    def swap_start(self, first, opening):
        if not opening and first == 0:
            pl.semaphore_wait(self.x_free, 1)
        for p in range(first, first + 2):
            self.swap(p).start()

    def swap_finish(self, closing):
        for p in range(4):
            self.swap(p).wait()

        def body(n):
            p, k = n // self.chunks, n % self.chunks
            for side in range(2):
                total = self.dkv[p, side, at(k, self.offset)] + self.dkv_in[p, side, at(k)]
                self.wide_in[at(k), lanes_at(p, 128, (1 + side) * self.width)] = total.astype(jnp.bfloat16)

        loop(0, 4 * self.chunks, body)
        if not closing:
            pl.semaphore_signal(self.x_free, inc=1, device_id=neighbours()[0], device_id_type=MESH)

    def leave_rows(self, k):
        rows = at(k)
        grad_normed = dot_nn(self.wide_in[rows, : 3 * self.width], self.wide[: 3 * self.width])
        back, g_gain, g_offset = norm_back(grad_normed, self.hidden[at(k)], self.gain(0))
        self.add_small(0, g_gain)
        self.add_small(1, g_offset)
        return (back + self.grad_out[rows]).astype(jnp.bfloat16)

    def wide_product(self, first, count):
        if first < 3 * self.width:
            right = self.normed[pl.ds(self.offset, self.own)]
        else:
            right = self.second[...]
        return dot_tn(self.wide_in[:, first : first + count], right)

    def narrow_product(self, first, count):
        right = self.mid_low if first < self.width else self.grad_low
        return dot_tn(self.mixed_in[:, first : first + count], right[...])


def pieces_of(first, count, border):
    if first < border < first + count:
        return [(first, border - first), (border, first + count - border)]
    return [(first, count)]


def block_scratch(total_rows, own_rows):
    width = 512
    f32, bf16 = jnp.float32, jnp.bfloat16
    shapes = [
        ((own_rows, width), f32),
        ((total_rows, width), bf16),
        ((own_rows, width), bf16),
        ((total_rows, 2 * width), bf16),
        ((own_rows, 5 * width), bf16),
        ((own_rows, 7 * width), bf16),
        ((own_rows, width), f32),
        ((own_rows, width), bf16),
        ((4 * own_rows, width), f32),
        ((own_rows, width), f32),
        ((own_rows, width), bf16),
        ((own_rows, width), bf16),
        ((own_rows, width), bf16),
        ((4, 2, total_rows, 128), f32),
        ((4, 2, own_rows, 128), f32),
        ((own_rows, 128), f32),
    ]
    return [pltpu.VMEM(shape, dtype) for shape, dtype in shapes] + [
        pltpu.SemaphoreType.DMA((4,)), pltpu.SemaphoreType.DMA((4,)), pltpu.SemaphoreType.REGULAR
    ]


DEC_NARROW = ((0, 80, False),)
ENC_WIDE = ((96, 16, True), (0, 96, False))
ENC_NARROW = ((0, 80, False),)
DEC_ORDER = (("n", 3), ("n", 1), ("n", 2), ("n", 0), ("w", 3), ("w", 2), ("w", 0), ("w", 1))
ENC_ORDER = (("n", 3), ("n", 1), ("n", 0), ("w", 3), ("w", 2), ("w", 0), ("w", 1), ("n", 2))


def step_kernel(slots, latent_total, *refs):
    shards, slab, code, kinds, norms = refs[:6], refs[6], refs[7], refs[8], refs[9]
    refs = refs[10:]
    share_wide_dec, share_narrow_dec, share_wide, share_narrow, share_edge, share_book, small_all = refs[:7]
    land_wide_dec, land_narrow_dec, land_wide, land_narrow = refs[7:11]
    refs = refs[11:]
    sems_dec, sems_enc, red, red_small, refs = refs[:5], refs[5:10], refs[10:25], refs[25:44], refs[44:]
    (book, edge, slab_all, code_all, tally, tally_all, t_img, t_band, e_near, e_send, e_recv, t_send, t_recv) = refs[:13]
    refs = refs[1:]
    (code_row, spread, cross, g_pixw, g_qout, g_qin, g_inw, g_edge, g_book) = refs[12:21]
    (small_dec, small_enc, small_own, s_img, s_band, s_send, s_recv, load_sem, wide, narrow) = refs[21:31]
    q_extra, k_extra = refs[31:33]
    scratch = refs[33:]
    f32, bf16 = jnp.float32, jnp.bfloat16
    img_at, band_at, y_at, x_at, c_at = place()
    chip_at = band_at // 2
    over_c = neighbours()[0]
    width = wide.shape[1]
    common = (wide, narrow, norms, q_extra, k_extra) + tuple(scratch)

    def edge_columns(first, count):
        return edge[:, :, :, :, :, first : first + count].reshape(width, count)

    def e_in():
        return edge_columns(0, 256)

    def e_pix():
        return edge_columns(256, 256)

    def e_qin():
        return edge_columns(512, 128)

    def e_qout():
        return edge_columns(640, 128)

    def pixel_rows(k, first=0, start=0):
        return slab_all[pl.ds(start + 2 * k, 2), :, first : first + 256].reshape(STEP, 256)

    own_band = 4 * c_at
    dec = Block(4, lambda k: spread[at(k)], e_qout, small_dec, common)
    enc = Block(0, pixel_rows, e_in, small_enc, common)
    agenda = Agenda()
    dec_pieces = [(shards[0], book, 0, 64, False), (shards[1], edge, 0, 16, False)]
    dec_pieces += [(shards[2], land_wide_dec, 96, 16, True)]
    dec_pieces += [(shards[2], land_wide_dec, 0, 48, False), (shards[2], land_wide_dec, 48, 48, False)]
    dec_pieces += [(shards[3], land_narrow_dec, first, count, last) for first, count, last in DEC_NARROW]
    gather = Gather("d", agenda, dec_pieces, *sems_dec)
    enc_pieces = [(shards[4], land_wide, first, count, last) for first, count, last in ENC_WIDE]
    enc_pieces += [(shards[5], land_narrow, first, count, last) for first, count, last in ENC_NARROW]
    gather_enc = Gather("e", agenda, enc_pieces, *sems_enc)
    count_all = Everywhere("n", agenda, tally, t_img, t_band, t_send, t_recv, tally_all)
    spots = lax.broadcasted_iota(jnp.int32, (1, 4), 1)
    kind = jnp.sum(jnp.where(spots == chip_at, kinds[...], 0).astype(f32), axis=1, keepdims=True)
    meet(peers())
    agenda.spend(3.0)
    gather.begin(0, 5)
    exchange = []
    for step in range(1, 4):
        chip = (chip_at + step) % 4
        target = (img_at, 2 * chip + c_at)
        here = band_at
        exchange.append(far_copy(slab.at[chip], slab_all.at[here], e_send.at[0, step], e_recv.at[0, step], target))
        exchange.append(far_copy(code.at[chip], code_all.at[here], e_send.at[1, step], e_recv.at[1, step], target))
    exchange.append(pltpu.make_async_copy(slab.at[chip_at], slab_all.at[band_at], e_near.at[0]))
    exchange.append(pltpu.make_async_copy(code.at[chip_at], code_all.at[band_at], e_near.at[1]))

    def exchange_landed():
        late = []
        for k, dst in enumerate((slab_all, code_all)):
            for chip in range(4):
                part = dst.at[2 * chip + c_at]
                late.append(far_copy(part, part, e_send.at[k, 4 + chip], e_recv.at[k, 4 + chip], over_c))
        agenda.launch("x2", late, [("c", 4e5)], lambda: arrived.append(1))

    arrived = []
    agenda.launch("x1", exchange, [("x", 4e5), ("y", 4e5)], exchange_landed)
    agenda.spend(1.0)
    segment_lane = lax.broadcasted_iota(jnp.int32, (enc.total, 128), 1)
    segment = jnp.where(kind < 0.5, 0, lax.broadcasted_iota(jnp.int32, (enc.total, 128), 0) // (enc.total // 4))
    k_extra[...] = jnp.where(segment_lane == segment, 1.0, 0.0).astype(bf16)
    segment_lane = lax.broadcasted_iota(jnp.int32, (enc.own, 128), 1)
    segment = lax.broadcasted_iota(jnp.int32, (enc.own, 128), 0) + enc.offset
    segment = jnp.where(kind < 0.5, 0, segment // (enc.total // 4))
    q_extra[...] = jnp.where((segment_lane < 4) & (segment_lane != segment), -(2.0**30), 0.0).astype(bf16)
    for ref in (small_dec, small_enc, g_pixw, g_qout, g_qin, g_inw):
        ref[...] = jnp.zeros(ref.shape, f32)
    agenda.spend(2.0)
    agenda.tick()
    agenda.until(lambda: arrived)
    def code_column(k, start=0):
        return jnp.concatenate(
            [jnp.transpose(jnp.broadcast_to(code_all[start + 2 * k + n], (8, 128)))[:, 0:1] for n in range(2)], axis=0
        )

    for n in range(4):
        code_row[:, pl.ds(128 * n, 128)] = code_all[own_band + n]

    def pick_codes(k):
        rows = at(k)
        code_here = code_column(k)
        picks = lax.broadcasted_iota(jnp.int32, (STEP, 512), 1)
        found = jnp.zeros((STEP, 128), f32)
        for z in range(4):
            hot = jnp.where(picks + 512 * z == code_here // 4, 1.0, 0.0).astype(bf16)
            found += dot_nn(hot, book[z].reshape(512, 128))
        lanes = lax.broadcasted_iota(jnp.int32, (STEP, 128), 1) // 32
        spread[rows] = jnp.where(lanes == code_here % 4, found, 0.0).astype(bf16)

    lane = lax.broadcasted_iota(jnp.int32, (4, 128, 256), 2)
    flags = slab_all[pl.ds(own_band, 4), :, 128:384].astype(f32)
    tally[...] = jnp.full(tally.shape, jnp.sum(jnp.where(lane < 64, 0.0, flags)))
    agenda.spend(1.0)
    agenda.tick()
    count_all.begin()
    gather.begin(5, len(dec_pieces))
    gather.until(0)
    agenda.tick()
    loop(0, dec.total // STEP, pick_codes)
    agenda.spend(4.0)
    agenda.tick()
    gather.until(1)
    dec.enter(0, dec.total // STEP)
    agenda.spend(1.9)
    agenda.tick()

    def fetch(landed, ref, sem):
        rows = landed.shape[4]

        def body(n):
            src = landed.at[n // 8, (n // 4) % 2, (n // 2) % 2, n % 2]
            pltpu.make_async_copy(src, ref.at[pl.ds(pl.multiple_of(n * rows, 16), rows)], sem).start()

        loop(0, 32, body)
        return pltpu.make_async_copy(ref, ref, sem)

    reduce = Reduce(agenda, *slots, *red)
    tail = ReduceSmall(
        agenda, (g_edge, g_book), (share_edge, share_book),
        *[red_small[2 * n : 2 * n + 2] for n in range(7)], *red_small[14:],
    )

    def emit_wide(blk, z, full, slot):
        values = [blk.wide_product(*span) for span in pieces_of(896 * z, 896, 3 * width)]
        value = values[0] if len(values) == 1 else jnp.concatenate(values, axis=0)
        full[slot] = value.reshape(2, 2, 2, 112, width)
        agenda.spend(0.6)

    def emit_narrow(blk, z, full, slot):
        values = [blk.narrow_product(*span) for span in pieces_of(640 * z, 640, width)]
        value = values[0] if len(values) == 1 else jnp.concatenate(values, axis=0)
        full[slot, :, :, :, :80] = value.reshape(2, 2, 2, 80, width)
        agenda.spend(0.5)

    pieces = []
    for name, blk, out_wide, out_narrow, order in (
        ("dec", dec, share_wide_dec, share_narrow_dec, DEC_ORDER), ("enc", enc, share_wide, share_narrow, ENC_ORDER)
    ):
        for kind_of, z in order:
            if kind_of == "n":
                needs = name + str(int(z == 0))
                pieces.append(dict(emit=functools.partial(emit_narrow, blk, z), z=z, rows=80, out=out_narrow, needs=needs))
                continue
            piece = dict(z=z, rows=112, out=out_wide, needs=name + str(1 + (z < 2)))
            if name == "dec" and z < 2:
                piece.update(stage=dec.slope, first=896 * z)
            else:
                piece.update(emit=functools.partial(emit_wide, blk, z))
            pieces.append(piece)
    reduce.plan(pieces)

    def spend(time):
        agenda.spend(time)
        agenda.tick()

    def decoder_head(k):
        rows = at(k)
        out = dec.grad_out[rows]
        shape, _ = norm_parts(out)
        final = (shape * norms[pl.ds(8, 1), :] + norms[pl.ds(9, 1), :]).astype(bf16)
        error = dot_nn(final, e_pix()) - pixel_rows(k, 0, own_band).astype(f32)
        lane = lax.broadcasted_iota(jnp.int32, (STEP, 256), 1)
        counted = jnp.where(lane < 192, pltpu.roll(pixel_rows(k, 128, own_band).astype(f32), 192, 1), 0.0)
        number = tally_all[0:1, 0:1]
        dec.add_loss(jnp.sum(counted * (error * error + jnp.abs(error))) / number)
        sign = jnp.where(error > 0.0, 1.0, jnp.where(error < 0.0, -1.0, 0.0))
        grad_pred = (counted * (2.0 * error + sign) / number).astype(bf16)
        g_pixw[...] += dot_tn(final, grad_pred)
        back, g_gain, g_offset = norm_back(dot_nt(grad_pred, e_pix()), out, norms[pl.ds(8, 1), :])
        dec.add_small(4, g_gain)
        dec.add_small(5, g_offset)
        dec.grad_out[rows] = back
        dec.grad_low[rows] = back.astype(bf16)

    def encoder_head(k):
        rows = at(k)
        low = enc.grad_out[rows].astype(bf16)
        lanes = lax.broadcasted_iota(jnp.int32, (STEP, 128), 1) // 32
        mine = lanes == code_column(k, own_band) % 4
        gap = jnp.where(mine, spread[at(k, enc.offset)].astype(f32) - dot_nn(low, e_qin()), 0.0)
        enc.add_loss((1.0 + commitment) * jnp.sum(gap * gap) / latent_total)
        grad_latent = jnp.where(mine, cross[rows] - 2.0 * commitment * gap / latent_total, 0.0).astype(bf16)
        g_qin[...] += dot_tn(low, grad_latent)
        back = dot_nt(grad_latent, e_qin())
        enc.grad_out[rows] = back
        enc.grad_low[rows] = back.astype(bf16)
        gap = 2.0 * gap / latent_total
        high = gap.astype(bf16)
        left = gap - high.astype(f32)
        between = left.astype(bf16)
        enc.gatt[rows, :384] = jnp.concatenate([high, between, (left - between.astype(f32)).astype(bf16)], axis=1)

    def book_rows(k):
        picks = lax.broadcasted_iota(jnp.int32, (STEP, enc.own), 0) + k * STEP
        hot = jnp.where(picks == code_row[...] // 4, 1.0, 0.0).astype(bf16)
        summed = dot_nn(hot, enc.gatt[:, :384])
        value = (summed[:, :128] + summed[:, 128:256]) + summed[:, 256:]
        g_book[k // 2, k % 2] = value.reshape(2, 2, 64, 128)

    def decoder_leave(k):
        low = dec.leave_rows(k)
        cross[at(k)] = dot_nn(low, e_qout())
        g_qout[...] += dot_tn(low, spread[at(k, dec.offset)])

    def encoder_leave(k):
        g_inw[...] += dot_tn(enc.leave_rows(k), pixel_rows(k, 0, own_band))

    gather_enc.begin(0, len(enc_pieces))
    gather.until(2, 3, 4)
    fetch(land_wide_dec, wide, load_sem.at[0]).wait()
    spend(2.0)
    dec.make_kv(0, dec.total // STEP)
    dec.make_q()
    spend(2.9)
    dec.attend(0, 4)
    spend(11.1)
    gather.until(*range(5, len(dec_pieces)))
    fetched = fetch(land_narrow_dec, narrow, load_sem.at[1])
    agenda.spend(1.0)
    fetched.wait()
    dec.after_attention()
    spend(1.1)
    dec.mlp(0, 4)
    spend(5.6)
    count_all.until()
    loop(0, dec.chunks, decoder_head)
    agenda.spend(2.0)
    reduce.allow("dec0")
    agenda.tick()
    dec.mlp_back(0, dec.chunks)
    agenda.spend(6.1)
    reduce.allow("dec1")
    agenda.tick()
    dec.attend_back_all(True)
    spend(15.8)
    gather_enc.until(*range(len(enc_pieces)))
    fetched = fetch(land_narrow, narrow, load_sem.at[1])
    dec.swap_finish(False)
    agenda.spend(2.0)
    for z in range(2):
        values = [dec.wide_product(*span) for span in pieces_of(896 * z, 896, 3 * width)]
        dec.slope[pl.ds(896 * z, 896)] = values[0] if len(values) == 1 else jnp.concatenate(values, axis=0)
    agenda.spend(1.2)
    reduce.allow("dec2")
    agenda.tick()
    loop(0, dec.chunks, decoder_leave)
    fetched_wide = fetch(land_wide, wide, load_sem.at[0])
    spend(2.0)
    emitted = 1 + max(p for p in range(8) if "emit" in pieces[p])
    staged = [p for p in range(8) if "stage" in pieces[p]]
    agenda.until(lambda: reduce.opened >= emitted)
    enc.enter(0, enc.total // STEP)
    spend(1.9)
    fetched_wide.wait()
    enc.make_kv(0, enc.total // STEP)
    enc.make_q()
    fetched.wait()
    spend(2.9)
    enc.attend(0, 4)
    spend(11.1)
    enc.after_attention()
    spend(1.1)
    agenda.until(lambda: reduce.opened > max(staged) and not any(("r", p, 0) in agenda.flying for p in staged))
    enc.mlp(0, 4)
    spend(5.6)
    loop(0, enc.chunks, encoder_head)
    agenda.spend(2.0)
    reduce.allow("enc0")
    agenda.tick()
    loop(0, 8, book_rows)
    tail.open(1)
    spend(2.0)
    enc.mlp_back(0, enc.chunks)
    agenda.spend(6.1)
    reduce.allow("enc1")
    agenda.tick()
    enc.attend_back(0, 2)
    enc.swap_start(0, False)
    spend(7.9)
    enc.attend_back(2, 4)
    enc.swap_start(2, False)
    spend(7.9)
    enc.swap_finish(True)
    agenda.spend(2.0)
    reduce.allow("enc2")
    agenda.tick()
    loop(0, enc.chunks, encoder_leave)
    agenda.spend(2.0)

    def all_groups(value):
        value = value + pltpu.roll(value, 64, 1)
        return value + pltpu.roll(value, 32, 1)

    lane = lax.broadcasted_iota(jnp.int32, (width, 128), 1)
    mixed = jnp.where(lane < 64, g_inw[:, 128:], jnp.where(lane < 96, all_groups(g_qin[...]), all_groups(g_qout[...])))
    for first, value in ((0, g_inw[:, :128]), (128, mixed), (256, g_pixw[:, :128]), (384, g_pixw[:, 128:])):
        g_edge[:, :, :, :, :, pl.ds(first, 128)] = value.reshape(4, 2, 2, 2, 16, 128)
    tail.open(0)
    agenda.until(lambda: len(reduce.ended) == len(pieces) and len(tail.done) == 2)
    shares = (share_wide_dec, share_narrow_dec, share_wide, share_narrow, share_edge, share_book)
    squares = sum(jnp.sum(share[...] * share[...]) for share in shares)
    lane = lax.broadcasted_iota(jnp.int32, (8, width), 1)
    row = lax.broadcasted_iota(jnp.int32, (8, width), 0)
    small_own[0] = small_enc[...]
    small_own[1] = jnp.where((row == 7) & (lane == 0), squares, small_dec[...])
    sum_all = Everywhere("a", agenda, small_own, s_img, s_band, s_send, s_recv, small_all)
    sum_all.begin()
    sum_all.until()


def train_step(shards, slab, code, kinds, norms, latent_total, total_rows, own_rows):
    width = 512
    slots = (4, 4)
    f32, bf16, int32 = jnp.float32, jnp.bfloat16, jnp.int32
    any_space = pl.BlockSpec(memory_space=pl.ANY)
    vmem = pl.BlockSpec(memory_space=pltpu.VMEM)
    shape = jax.ShapeDtypeStruct
    out_shape = [
        shape((112, width), f32), shape((80, width), f32), shape((112, width), f32), shape((80, width), f32),
        shape((16, width), f32), shape((64, 128), f32), shape((2, 8, width), f32),
    ]
    out_shape += [shape((4, 2, 2, 2) + s.shape, s.dtype) for s in shards[2:]]
    dma = pltpu.SemaphoreType.DMA
    mem = pltpu.VMEM
    scratch = gather_sems(5 + len(DEC_NARROW)) + gather_sems(len(ENC_WIDE) + len(ENC_NARROW))
    scratch += reduce_scratch(*slots, 112, width) + reduce_small_scratch([(16, width), (64, 128)])
    scratch += [
        mem((4, 2, 2, 2, 64, 128), bf16), mem((4, 2, 2, 2, 16, 768), bf16),
        mem((8, 128, 384), bf16), mem((8, 1, 128), int32), mem((8, 128), f32), mem((8, 128), f32),
        mem((4, 8, 128), f32), mem((8, 8, 128), f32),
        dma((2,)), dma((2, 8)), dma((2, 8)), dma((11,)), dma((11,)),
        mem((1, own_rows), int32), mem((total_rows, 128), bf16),
        mem((own_rows, 128), f32),
        mem((width, 256), f32), mem((width, 128), f32), mem((width, 128), f32), mem((width, 256), f32),
        mem((4, 2, 2, 2, 16, width), f32), mem((4, 2, 2, 2, 64, 128), f32),
        mem((8, width), f32), mem((8, width), f32), mem((2, 8, width), f32),
        mem((4, 2, 8, width), f32), mem((8, 2, 8, width), f32), dma((11,)), dma((11,)),
        dma((2,)), mem((7 * width, width), bf16), mem((5 * width, width), bf16),
        mem((own_rows, 128), bf16), mem((total_rows, 128), bf16),
    ]
    scratch += block_scratch(total_rows, own_rows)
    return pl.pallas_call(
        functools.partial(step_kernel, slots, latent_total),
        out_shape=out_shape,
        in_specs=[any_space] * 8 + [vmem] * 2,
        out_specs=[vmem] * 7 + [any_space] * 4,
        scratch_shapes=scratch,
        compiler_params=pltpu.CompilerParams(collective_id=0, has_side_effects=True, vmem_limit_bytes=(639 << 20) // 10),
        name="train_step",
    )(*shards, slab, code, kinds, norms)


def moments(gradient, first_old, second_old):
    first_new = beta_first * first_old + (1.0 - beta_first) * gradient
    second_new = beta_second * second_old + (1.0 - beta_second) * gradient * gradient
    return (first_new, second_new, first_new / (jnp.sqrt(second_new) + adam_eps))


def rotated_update(weight, gradient, first_old, second_old, basis_stack):
    turned = jnp.einsum("rld,lde->rle", gradient, basis_stack, precision=highest)
    first_new, second_new, direction = moments(turned, first_old, second_old)
    turned_back = jnp.einsum("rle,lde->rld", direction, basis_stack, precision=highest)
    return (weight - rate_matrix * (turned_back + weight_decay * weight), first_new, second_new)


def plain_update(weight, gradient, first_old, second_old):
    first_new, second_new, direction = moments(gradient, first_old, second_old)
    return (weight - rate_vector * (direction + weight_decay * weight), first_new, second_new)


def prepare_kernel(wide, narrow, edge, wide_0, wide_1, narrow_0, narrow_1, edge_low):
    low = jnp.bfloat16
    wide_0[...], wide_1[...] = wide[:, 0].astype(low), wide[:, 1].astype(low)
    narrow_0[...], narrow_1[...] = narrow[:, 0].astype(low), narrow[:, 1].astype(low)
    full = edge[...]
    gap = jnp.zeros((full.shape[0], 64), full.dtype)
    parts = [full[:, :192], gap, full[:, 192:384], gap] + [full[:, 384:416]] * 4 + [full[:, 416:448]] * 4
    edge_low[...] = jnp.concatenate(parts, axis=1).astype(low)


def prepare(w_wide, w_narrow, w_edge):
    vmem = pl.BlockSpec(memory_space=pltpu.VMEM)
    rows, width = (w_wide.shape[0], w_narrow.shape[0]), w_wide.shape[2]
    shapes = [(rows[0], width)] * 2 + [(rows[1], width)] * 2 + [(w_edge.shape[0], 768)]
    return pl.pallas_call(
        prepare_kernel,
        out_shape=[jax.ShapeDtypeStruct(shape, jnp.bfloat16) for shape in shapes],
        in_specs=[vmem] * 3,
        out_specs=[vmem] * 5,
        name="prepare",
    )(w_wide, w_narrow, w_edge)


def update_kernel(*refs):
    count = 20
    ins, refs = refs[:count], refs[count:]
    outs, held, sem = refs[:13], refs[13 : 13 + count], refs[13 + count]
    loads = {k: [pltpu.make_async_copy(ins[k], held[k], sem.at[k])] for k in range(count) if k != 18}
    loads[18] = [pltpu.make_async_copy(ins[18].at[k], held[18].at[k], sem.at[18 if k == 0 else 19 + k]) for k in range(4)]
    order = (5, 15, 16, 17, 4, 12, 13, 14, 19, 0, 1, 6, 7, 8, 18, 2, 3, 9, 10, 11)
    for k in order:
        for load in loads[k]:
            load.start()

    def need(*wanted):
        for k in wanted:
            while loads[k]:
                loads[k].pop(0).wait()

    refs = held + outs
    wide_0, wide_1, narrow_0, narrow_1, edge, small = refs[:6]
    wide, narrow, edge_set, norm_set = refs[6:9], refs[9:12], refs[12:15], refs[15:18]
    bases, basis_edge = refs[18:20]
    new_wide, new_narrow, new_edge, new_norms, scalars = refs[20:23], refs[23:26], refs[26:29], refs[29:32], refs[32]
    need(5, 15, 16, 17)
    norm_grad = jnp.concatenate([small[0, 0:4], small[1, 0:6]], axis=0)
    squares = small[1, 7:8, 0:1] + jnp.sum(norm_grad * norm_grad)
    grad_norm = jnp.sqrt(squares)
    factor = jnp.minimum(1.0, clip_level / grad_norm)
    scalars[0:1] = jnp.broadcast_to(grad_norm, (1, 128))
    scalars[1:2] = jnp.broadcast_to(factor, (1, 128))
    scalars[2:3] = jnp.broadcast_to(small[0, 6:7, 0:1] + small[1, 6:7, 0:1], (1, 128))
    scalars[3:8] = jnp.zeros((5, 128), jnp.float32)

    def halves(value):
        high = value.astype(jnp.bfloat16)
        return high, (value - high.astype(jnp.float32)).astype(jnp.bfloat16)

    def product(left, right, dot):
        (high, low), (right_high, right_low) = halves(left), right
        both = dot(jnp.concatenate([high, low], axis=0), right_high)
        rows = left.shape[0]
        return both[:rows] + (dot(high, right_low) + both[rows:])

    def turn(weight, gradient, first_old, second_old, basis):
        right = halves(basis)
        turned = product(gradient, right, dot_nn)
        first_new, second_new, direction = moments(turned, first_old, second_old)
        back = product(direction, right, dot_nt)
        return weight - rate_matrix * (back + weight_decay * weight), first_new, second_new

    need(4, 12, 13, 14, 19)
    packed = edge[...]
    grad_edge = jnp.concatenate([packed[:, :192], packed[:, 256:448], packed[:, 192:256]], axis=1)
    found = turn(edge_set[0][...], factor * grad_edge, edge_set[1][...], edge_set[2][...], basis_edge[...])
    for ref, value in zip(new_edge, found):
        ref[...] = value
    found = plain_update(norm_set[0][...], factor * norm_grad, norm_set[1][...], norm_set[2][...])
    for ref, value in zip(new_norms, found):
        ref[...] = value
    for k, (olds, news, grads) in enumerate(
        ((wide, new_wide, (wide_0, wide_1)), (narrow, new_narrow, (narrow_0, narrow_1)))
    ):
        for layer in range(2):
            need(2 * k + layer, 6 + 3 * k, 7 + 3 * k, 8 + 3 * k)
            loads[18].pop(0).wait()
            found = turn(
                olds[0][:, layer], factor * grads[layer][...], olds[1][:, layer], olds[2][:, layer], bases[2 * k + layer]
            )
            for ref, value in zip(news, found):
                ref[:, layer] = value


def update_all(grads, wide, narrow, edge, norms, bases, basis_edge):
    vmem = pl.BlockSpec(memory_space=pltpu.VMEM)
    shape = jax.ShapeDtypeStruct
    sets = wide + narrow + edge + norms
    return pl.pallas_call(
        update_kernel,
        out_shape=[shape(a.shape, a.dtype) for a in sets] + [shape((8, 128), jnp.float32)],
        in_specs=[pl.BlockSpec(memory_space=pl.ANY)] * (len(grads) + len(sets) + 2),
        out_specs=[vmem] * (len(sets) + 1),
        scratch_shapes=[pltpu.VMEM(a.shape, a.dtype) for a in (*grads, *sets, bases, basis_edge)]
        + [pltpu.SemaphoreType.DMA((len(grads) + len(sets) + 5,))],
        compiler_params=pltpu.CompilerParams(vmem_limit_bytes=63 << 20),
        name="update_all",
    )(*grads, *sets, bases, basis_edge)


def body(
    pixels,
    valid,
    codes,
    image_kind,
    w_wide,
    w_narrow,
    w_edge,
    codebook,
    norms,
    bases,
    basis_edge,
    m_wide,
    v_wide,
    m_narrow,
    v_narrow,
    m_edge,
    v_edge,
    m_code,
    v_code,
    m_norm,
    v_norm,
):
    band_count = lax.axis_size("band")
    band_index = lax.axis_index("band")
    row_count = pixels.shape[2]
    length = row_count * band_count
    batch_count = pixels.shape[0]
    group = band_count // batch_count
    row = band_index // group
    part = band_index % group
    own_rows = length // group
    groups = [[k * group + j for j in range(group)] for k in range(batch_count)]
    layer_count = w_wide.shape[1]
    code_width = codebook.shape[1]
    latent_total = batch_count * lax.axis_size("img") * length * code_width
    both = ("img", "band")

    direct = band_count == 8 and lax.axis_size("img") == 4 and batch_count == 4
    shards = [w_wide[:, l].astype(jnp.bfloat16) for l in range(layer_count)]
    shards += [w_narrow[:, l].astype(jnp.bfloat16) for l in range(layer_count)]
    shards += [w_edge.astype(jnp.bfloat16), codebook.astype(jnp.bfloat16).reshape(-1, 4 * code_width)]
    slab = jnp.concatenate([pixels[:, 0], valid[:, 0].astype(jnp.bfloat16)], axis=2)
    patch_size = pixels.shape[3]
    if direct:
        shards = list(prepare(w_wide, w_narrow, w_edge)) + shards[5:]
        out = train_step(
            [shards[k] for k in (5, 4, 1, 3, 0, 2)], slab, codes, image_kind.reshape(1, -1), norms, latent_total, length, own_rows
        )
        new = update_all(
            (out[2], out[0], out[3], out[1], out[4], out[6]), (w_wide, m_wide, v_wide), (w_narrow, m_narrow, v_narrow),
            (w_edge, m_edge, v_edge), (norms, m_norm, v_norm), bases, basis_edge,
        )
        scalars = new[12]
        grad_norm, factor, loss_total = scalars[0, 0], scalars[1, 0], scalars[2, 0]
        new_code = plain_update(codebook, factor * out[5].reshape(-1, code_width), m_code, v_code)
        return tuple(new[:9]) + new_code + tuple(new[9:12]) + (grad_norm, loss_total)
    wholes = [lax.all_gather(shard, both, axis=0, tiled=True) for shard in shards]
    count = lax.psum(jnp.sum(valid.astype(jnp.float32)), both)

    def whole_row(local):
        everywhere = lax.all_gather(local, "band", axis=0)
        chosen_row = lax.dynamic_index_in_dim(everywhere, row, axis=1, keepdims=False)
        return chosen_row.reshape((length,) + local.shape[2:])

    slab_all = whole_row(slab)
    code_all = whole_row(codes[:, 0])
    kind = lax.dynamic_index_in_dim(image_kind[:, 0], row, 0, keepdims=False)
    span = jnp.where(kind == 0, length, length // 4)
    positions = jnp.arange(length, dtype=jnp.int32)
    gathered = (wholes[:2], wholes[2:4], wholes[4], wholes[5])
    pixel_all = slab_all[:, :patch_size]
    valid_rows = lax.dynamic_slice_in_dim(slab_all, part * own_rows, own_rows, 0)[:, patch_size:]
    own_positions = part * own_rows + jnp.arange(own_rows, dtype=jnp.int32)
    allowed = (own_positions // span)[:, None] == (positions // span)[None, :]
    local_grads, norm_sum, loss_sum = row_step(
        gathered, norms, pixel_all, valid_rows, code_all, part, allowed, count, latent_total, groups
    )
    shares = [lax.psum_scatter(g, both, scatter_dimension=0, tiled=True) for g in local_grads]
    squares = sum(jnp.sum(share * share) for share in shares)
    norm_total, square_total, loss_total = lax.psum((norm_sum, squares, loss_sum), both)
    grad_sum = (
        jnp.stack([shares[0], shares[1]], axis=1),
        jnp.stack([shares[2], shares[3]], axis=1),
        shares[4],
        shares[5].reshape(-1, code_width),
    )
    grad_norm = jnp.sqrt(square_total + jnp.sum(norm_total * norm_total))
    factor = jnp.minimum(1.0, clip_level / grad_norm)
    grad_wide, grad_narrow, grad_edge, grad_book = grad_sum
    new_wide, new_m_wide, new_v_wide = rotated_update(
        w_wide, factor * grad_wide, m_wide, v_wide, bases[:layer_count]
    )
    new_narrow, new_m_narrow, new_v_narrow = rotated_update(
        w_narrow, factor * grad_narrow, m_narrow, v_narrow, bases[layer_count:]
    )
    new_edge, new_m_edge, new_v_edge = rotated_update(
        w_edge[:, None],
        factor * grad_edge[:, None],
        m_edge[:, None],
        v_edge[:, None],
        basis_edge[None],
    )
    new_book, new_m_code, new_v_code = plain_update(codebook, factor * grad_book, m_code, v_code)
    new_norms, new_m_norm, new_v_norm = plain_update(norms, factor * norm_total, m_norm, v_norm)
    return (
        new_wide,
        new_m_wide,
        new_v_wide,
        new_narrow,
        new_m_narrow,
        new_v_narrow,
        new_edge[:, 0],
        new_m_edge[:, 0],
        new_v_edge[:, 0],
        new_book,
        new_m_code,
        new_v_code,
        new_norms,
        new_m_norm,
        new_v_norm,
        grad_norm,
        loss_total,
    )


def solution(mesh):
    in_specs = (
        P(None, "img", "band", None),
        P(None, "img", "band", None),
        P(None, "img", "band"),
        P(None, "img"),
        P(("img", "band"), None, None),
        P(("img", "band"), None, None),
        P(("img", "band"), None),
        P(("img", "band"), None),
        P(),
        P(),
        P(),
        P(("img", "band"), None, None),
        P(("img", "band"), None, None),
        P(("img", "band"), None, None),
        P(("img", "band"), None, None),
        P(("img", "band"), None),
        P(("img", "band"), None),
        P(("img", "band"), None),
        P(("img", "band"), None),
        P(),
        P(),
    )
    out_specs = (
        P(("img", "band"), None, None),
        P(("img", "band"), None, None),
        P(("img", "band"), None, None),
        P(("img", "band"), None, None),
        P(("img", "band"), None, None),
        P(("img", "band"), None, None),
        P(("img", "band"), None),
        P(("img", "band"), None),
        P(("img", "band"), None),
        P(("img", "band"), None),
        P(("img", "band"), None),
        P(("img", "band"), None),
        P(),
        P(),
        P(),
        P(),
        P(),
    )
    return jax.shard_map(body, mesh=mesh, in_specs=in_specs, out_specs=out_specs, check_vma=False)
```

```python
import functools

import jax
import jax.numpy as jnp
from jax import lax
from jax.experimental import pallas as pl
from jax.experimental.pallas import tpu as pltpu
from jax.sharding import PartitionSpec as P

HEADS = 8
HDIM = 64
MESH = pl.DeviceIdType.MESH


norm_eps = 1e-05
adam_eps = 1e-08
clip_level = 0.001
beta_first = 0.5
beta_second = 0.6
rate_matrix = 0.02
rate_vector = 0.3
weight_decay = 0.01
commitment = 0.25
masked_score = -1000000000.0
highest = lax.Precision.HIGHEST


def matmul_plain(first_op, second_op):
    return jnp.dot(first_op, second_op, preferred_element_type=jnp.float32)


def matmul_trans(first_op, second_op):
    return lax.dot_general(
        first_op, second_op, (((1,), (1,)), ((), ())), preferred_element_type=jnp.float32
    )


def matmul_outer(first_op, second_op):
    return lax.dot_general(
        first_op, second_op, (((0,), (0,)), ((), ())), preferred_element_type=jnp.float32
    )


def layer_norm(hidden, scale_gain, offset):
    centred = hidden - jnp.mean(hidden, axis=-1, keepdims=True)
    spread = jnp.mean(centred * centred, axis=-1, keepdims=True)
    return centred * lax.rsqrt(spread + norm_eps) * scale_gain + offset


def gelu_tanh(inputs):
    return (
        0.5
        * inputs
        * (1.0 + jnp.tanh(0.7978845608028654 * (inputs + 0.044715 * inputs * inputs * inputs)))
    )


def split_heads(matrix):
    return matrix.reshape(matrix.shape[0], HEADS, HDIM)


def head_scores(q_heads, k_heads, allowed):
    scores = jnp.einsum(
        "qhd,khd->hqk", q_heads, k_heads, preferred_element_type=jnp.float32
    ) * HDIM ** (-0.5)
    return jnp.where(allowed[None], scores, masked_score)


def attend(queries, key_rows, value_rows, allowed):
    scores = head_scores(split_heads(queries), split_heads(key_rows), allowed)
    score_peak = jnp.max(scores, axis=-1, keepdims=True)
    expo = jnp.exp(scores - score_peak)
    total = jnp.sum(expo, axis=-1, keepdims=True)
    softmaxed = (expo / total).astype(jnp.bfloat16)
    attended = jnp.einsum(
        "hqk,khd->qhd", softmaxed, split_heads(value_rows), preferred_element_type=jnp.float32
    )
    return (
        attended.reshape(queries.shape[0], -1).astype(jnp.bfloat16),
        score_peak + jnp.log(total),
    )


def attend_back(queries, key_rows, value_rows, allowed, log_total, grad_out):
    q_heads = split_heads(queries)
    k_heads = split_heads(key_rows)
    v_heads = split_heads(value_rows)
    g_heads = split_heads(grad_out)
    softmaxed = jnp.exp(head_scores(q_heads, k_heads, allowed) - log_total)
    grad_soft = jnp.einsum("qhd,khd->hqk", g_heads, v_heads, preferred_element_type=jnp.float32)
    row_dot = jnp.sum(softmaxed * grad_soft, axis=-1, keepdims=True)
    grad_scores = (softmaxed * (grad_soft - row_dot)).astype(jnp.bfloat16)
    scale = HDIM ** (-0.5)
    grad_q = (
        jnp.einsum("hqk,khd->qhd", grad_scores, k_heads, preferred_element_type=jnp.float32) * scale
    )
    grad_k = (
        jnp.einsum("hqk,qhd->khd", grad_scores, q_heads, preferred_element_type=jnp.float32) * scale
    )
    grad_v = jnp.einsum(
        "hqk,qhd->khd", softmaxed.astype(jnp.bfloat16), g_heads, preferred_element_type=jnp.float32
    )
    return (
        grad_q.reshape(queries.shape[0], -1),
        grad_k.reshape(key_rows.shape[0], -1),
        grad_v.reshape(key_rows.shape[0], -1),
    )


def block_forward(hidden_all, part, wide_rows, narrow_rows, gain_rows, allowed):
    model_width = hidden_all.shape[1]
    own_rows = allowed.shape[0]
    normed_all = layer_norm(hidden_all, gain_rows[0], gain_rows[1]).astype(jnp.bfloat16)
    hidden = lax.dynamic_slice_in_dim(hidden_all, part * own_rows, own_rows, 0)
    normed = lax.dynamic_slice_in_dim(normed_all, part * own_rows, own_rows, 0)
    queries = matmul_trans(normed, wide_rows[:model_width]).astype(jnp.bfloat16)
    key_rows = matmul_trans(normed_all, wide_rows[model_width : 2 * model_width]).astype(jnp.bfloat16)
    value_rows = matmul_trans(normed_all, wide_rows[2 * model_width : 3 * model_width]).astype(jnp.bfloat16)
    attended, log_total = attend(queries, key_rows, value_rows, allowed)
    middle = hidden + matmul_plain(attended, narrow_rows[:model_width])
    second = layer_norm(middle, gain_rows[2], gain_rows[3]).astype(jnp.bfloat16)
    upper_in = matmul_trans(second, wide_rows[3 * model_width :])
    active = gelu_tanh(upper_in).astype(jnp.bfloat16)
    result = middle + matmul_plain(active, narrow_rows[model_width:])
    return (
        result,
        (hidden, normed, queries, key_rows, value_rows, attended, log_total, middle, second, upper_in, active),
    )


def block_backward(grad_out, wide_rows, narrow_rows, gain_rows, allowed, saved, groups):
    (hidden, normed, queries, key_rows, value_rows, attended, log_total, middle, second, upper_in, active) = saved
    model_width = hidden.shape[1]
    grad_y = grad_out.astype(jnp.bfloat16)
    grad_down = matmul_outer(active, grad_y)
    grad_active = matmul_trans(grad_y, narrow_rows[model_width:])
    grad_upper = jax.vjp(gelu_tanh, upper_in)[1](grad_active)[0].astype(jnp.bfloat16)
    grad_up = matmul_outer(grad_upper, second)
    _, second_back = jax.vjp(layer_norm, middle, gain_rows[2], gain_rows[3])
    grad_mid, gain_two, offset_two = second_back(
        matmul_plain(grad_upper, wide_rows[3 * model_width :])
    )
    grad_mid = grad_mid + grad_out
    grad_attn = grad_mid.astype(jnp.bfloat16)
    grad_outproj = matmul_outer(attended, grad_attn)
    grad_att = matmul_trans(grad_attn, narrow_rows[:model_width]).astype(jnp.bfloat16)
    grad_q, grad_keys, grad_values = attend_back(
        queries, key_rows, value_rows, allowed, log_total, grad_att
    )
    grad_k = lax.psum_scatter(grad_keys, "band", scatter_dimension=0, tiled=True, axis_index_groups=groups)
    grad_v = lax.psum_scatter(grad_values, "band", scatter_dimension=0, tiled=True, axis_index_groups=groups)
    grad_mixed = jnp.concatenate([grad_q, grad_k, grad_v], axis=1).astype(jnp.bfloat16)
    grad_qkv = matmul_outer(grad_mixed, normed)
    _, first_back = jax.vjp(layer_norm, hidden, gain_rows[0], gain_rows[1])
    grad_in, gain_one, offset_one = first_back(
        matmul_plain(grad_mixed, wide_rows[: 3 * model_width])
    )
    gain_grads = jnp.stack([gain_one, offset_one, gain_two, offset_two], axis=0)
    return (
        grad_in + grad_mid,
        jnp.concatenate([grad_qkv, grad_up], axis=0),
        jnp.concatenate([grad_outproj, grad_down], axis=0),
        gain_grads,
    )


def pick_codes(code_rows, book_wide, code_width):
    fold = book_wide.shape[1] // code_width
    one_hot = (
        (code_rows // fold)[:, None] == jnp.arange(book_wide.shape[0], dtype=jnp.int32)[None, :]
    ).astype(jnp.bfloat16)
    lane_fold = jnp.arange(book_wide.shape[1], dtype=jnp.int32)[None, :] // code_width
    lane_mask = (code_rows % fold)[:, None] == lane_fold
    spread = jnp.where(lane_mask, matmul_plain(one_hot, book_wide), 0.0)
    chosen = sum(spread[:, k * code_width : (k + 1) * code_width] for k in range(fold))
    return chosen, one_hot, lane_mask


def row_step(gathered, norms, pixel_all, valid_rows, code_all, part, allowed, count, latent_total, groups):
    wide_all, narrow_all, edge_all, book_wide = gathered
    patch_size = pixel_all.shape[1]
    code_width = edge_all.shape[1] // 2 - patch_size
    own_rows = allowed.shape[0]
    edge_in = edge_all[:, :patch_size]
    edge_pix = edge_all[:, patch_size : 2 * patch_size]
    edge_qin = edge_all[:, 2 * patch_size : 2 * patch_size + code_width]
    edge_qout = edge_all[:, 2 * patch_size + code_width :]
    pixel_rows = lax.dynamic_slice_in_dim(pixel_all, part * own_rows, own_rows, 0)
    chosen_all, one_hot_all, lane_mask_all = pick_codes(code_all, book_wide, code_width)
    chosen_low_all = chosen_all.astype(jnp.bfloat16)
    chosen = lax.dynamic_slice_in_dim(chosen_all, part * own_rows, own_rows, 0)
    one_hot = lax.dynamic_slice_in_dim(one_hot_all, part * own_rows, own_rows, 0)
    lane_mask = lax.dynamic_slice_in_dim(lane_mask_all, part * own_rows, own_rows, 0)
    chosen_low = chosen.astype(jnp.bfloat16)
    begin = matmul_trans(chosen_low_all, edge_qout)
    decoded, dec_saved = block_forward(begin, part, wide_all[1], narrow_all[1], norms[4:8], allowed)
    final = layer_norm(decoded, norms[8], norms[9]).astype(jnp.bfloat16)
    predict = matmul_plain(final, edge_pix)
    error = predict - pixel_rows.astype(jnp.float32)
    pixel_mask = valid_rows.astype(jnp.float32)
    loss_pix = jnp.sum(pixel_mask * (error * error + jnp.abs(error))) / count
    grad_pred = (pixel_mask * (2.0 * error + jnp.sign(error)) / count).astype(jnp.bfloat16)
    grad_pixw = matmul_outer(final, grad_pred)
    _, final_back = jax.vjp(layer_norm, decoded, norms[8], norms[9])
    grad_dec, gain_last, offset_last = final_back(matmul_trans(grad_pred, edge_pix))
    grad_begin, dec_wide, dec_narrow, dec_gains = block_backward(
        grad_dec, wide_all[1], narrow_all[1], norms[4:8], allowed, dec_saved, groups
    )
    grad_begin_low = grad_begin.astype(jnp.bfloat16)
    grad_qout = matmul_outer(grad_begin_low, chosen_low)
    start = matmul_trans(pixel_all, edge_in)
    encoded, enc_saved = block_forward(start, part, wide_all[0], narrow_all[0], norms[0:4], allowed)
    encoded_low = encoded.astype(jnp.bfloat16)
    latent = matmul_plain(encoded_low, edge_qin)
    gap = chosen - latent
    loss_part = loss_pix + (1.0 + commitment) * jnp.sum(gap * gap) / latent_total
    grad_latent = (
        matmul_plain(grad_begin_low, edge_qout) - 2.0 * commitment * gap / latent_total
    ).astype(jnp.bfloat16)
    fold = lane_mask.shape[1] // code_width
    gap_wide = jnp.where(lane_mask, jnp.tile(2.0 * gap / latent_total, (1, fold)), 0.0)
    gap_high = gap_wide.astype(jnp.bfloat16)
    gap_rest = gap_wide - gap_high.astype(jnp.float32)
    gap_middle = gap_rest.astype(jnp.bfloat16)
    gap_low = (gap_rest - gap_middle.astype(jnp.float32)).astype(jnp.bfloat16)
    grad_book = (
        matmul_outer(one_hot, gap_high) + matmul_outer(one_hot, gap_middle)
    ) + matmul_outer(one_hot, gap_low)
    grad_qin = matmul_outer(encoded_low, grad_latent)
    grad_start, enc_wide, enc_narrow, enc_gains = block_backward(
        matmul_trans(grad_latent, edge_qin), wide_all[0], narrow_all[0], norms[0:4], allowed, enc_saved, groups
    )
    grad_inw = matmul_outer(grad_start.astype(jnp.bfloat16), pixel_rows)
    grads = (
        enc_wide, dec_wide, enc_narrow, dec_narrow,
        jnp.concatenate([grad_inw, grad_pixw, grad_qin, grad_qout], axis=1),
        grad_book,
    )
    norm_grad = jnp.concatenate([enc_gains, dec_gains, gain_last[None], offset_last[None]], axis=0)
    return (grads, norm_grad, loss_part)


def place():
    img_at = lax.axis_index("img")
    band_at = lax.axis_index("band")
    return img_at, band_at, band_at // 4, (band_at // 2) % 2, band_at % 2


def neighbours():
    img_at, band_at, y_at, x_at, c_at = place()
    return (
        (img_at, band_at + 1 - 2 * c_at),
        (img_at, band_at + 2 - 4 * x_at),
        (img_at, band_at + 4 - 8 * y_at),
    )


def peers():
    img_at, band_at = place()[:2]
    found = [((img_at + step) % 4, band_at) for step in range(1, 4)]
    return found + [(img_at, (band_at + step) % 8) for step in range(1, 8)]


def meet(others):
    barrier = pltpu.get_barrier_semaphore()
    for other in others:
        pl.semaphore_signal(barrier, inc=1, device_id=other, device_id_type=MESH)
    pl.semaphore_wait(barrier, len(others))


def far_copy(src, dst, send, recv, target):
    return pltpu.make_async_remote_copy(
        src_ref=src, dst_ref=dst, send_sem=send, recv_sem=recv, device_id=target, device_id_type=MESH
    )


class Everywhere:
    def __init__(self, name, agenda, own_ref, img_buf, band_buf, send, recv, result_ref):
        self.name, self.agenda, self.done = name, agenda, False
        self.own, self.img_buf, self.band_buf, self.result = own_ref, img_buf, band_buf, result_ref
        self.send, self.recv = send, recv

    def begin(self):
        img_at, band_at = place()[:2]
        self.img_buf[img_at] = self.own[...]
        copies = [
            far_copy(
                self.own, self.img_buf.at[img_at], self.send.at[step], self.recv.at[step], ((img_at + step) % 4, band_at)
            )
            for step in range(1, 4)
        ]
        self.agenda.launch((self.name, 0), copies, [], self.middle)
        self.agenda.spend(0.5)

    def middle(self):
        img_at, band_at = place()[:2]
        buf = self.img_buf
        self.result[...] = (buf[0] + buf[1]) + (buf[2] + buf[3])
        self.band_buf[band_at] = self.result[...]
        copies = [
            far_copy(
                self.result, self.band_buf.at[band_at], self.send.at[3 + step], self.recv.at[3 + step],
                (img_at, (band_at + step) % 8),
            )
            for step in range(1, 8)
        ]
        self.agenda.launch((self.name, 1), copies, [], self.end)
        self.agenda.spend(1.0)

    def end(self):
        total = self.band_buf[0]
        for k in range(1, 8):
            total = total + self.band_buf[k]
        self.result[...] = total
        self.done = True

    def until(self):
        self.agenda.until(lambda: self.done)


LINK, CORE, LAG = 100e3, 500e3, 0.6
SPREAD = {"f01": 3, "f12": 4, "f23": 3, "b10": 3, "b21": 4, "b32": 3}
TOWARDS = (
    {"b10": 3, "b21": 2, "b32": 1},
    {"f01": 1, "b21": 2, "b32": 1},
    {"f01": 1, "f12": 2, "b32": 1},
    {"f01": 1, "f12": 2, "f23": 3},
)


def z_loads(table, size):
    return [(link, count * size) for link, count in table.items()]


class Agenda:
    def __init__(self):
        self.now, self.free, self.flying = 0.0, {}, {}

    def launch(self, key, copies, loads, then):
        done = self.now
        for link, size in loads:
            begin = max(self.now, self.free.get(link, 0.0))
            self.free[link] = begin + size / (CORE if link == "c" else LINK) + 0.4
            done = max(done, self.free[link])
        for copy in copies:
            copy.start()
        self.flying[key] = (done + LAG, copies, then)

    def land(self, key):
        done, copies, then = self.flying.pop(key)
        self.now = max(self.now, done) + 0.5
        for copy in copies:
            copy.wait()
        then()

    def spend(self, time):
        self.now += time

    def tick(self):
        while self.flying:
            key = min(self.flying, key=lambda name: self.flying[name][0])
            if self.flying[key][0] > self.now:
                return
            self.land(key)

    def until(self, test):
        while not test():
            self.land(min(self.flying, key=lambda name: self.flying[name][0]))


class Gather:
    def __init__(self, name, agenda, pieces, near, z_send, z_recv, p_send, p_recv):
        self.name, self.agenda, self.pieces = name, agenda, pieces
        self.near, self.z_send, self.z_recv, self.p_send, self.p_recv = near, z_send, z_recv, p_send, p_recv
        self.done = set()

    def launch(self, p, k):
        img_at, band_at, y_at, x_at, c_at = place()
        over_c, over_x, over_y = neighbours()
        shard, whole, first, count, z_last = self.pieces[p]
        rows = pl.ds(first, count)
        width = shard.shape[1]
        size = count * max(width, 128) * 2
        lanes = width // 256 * 128
        found, loads = [], []
        here, own = whole.at[img_at, y_at, x_at, c_at, rows], shard.at[rows]
        if z_last and k < 2:
            for half in range(2):
                span = pl.ds(lanes, width - lanes) if half else pl.ds(0, lanes)
                along_y = (k == 0) == (half == 0)
                if k == 0:
                    src, dst = shard.at[rows, span], whole.at[img_at, y_at, x_at, c_at, rows, span]
                elif half == 0:
                    src = dst = whole.at[img_at, :, x_at, c_at, rows, span]
                else:
                    src = dst = whole.at[img_at, y_at, :, c_at, rows, span]
                slot = 2 * k + half
                target = over_y if along_y else over_x
                found.append(far_copy(src, dst, self.p_send.at[p, slot], self.p_recv.at[p, slot], target))
                loads.append(("y" if along_y else "x", (1 + k) * size))
            if k == 0:
                found.append(pltpu.make_async_copy(own, here, self.near.at[p]))
        elif z_last and k == 2:
            part = whole.at[img_at, :, :, c_at, rows]
            found = [
                far_copy(part, part, self.z_send.at[p, step], self.z_recv.at[p, step], ((img_at + step) % 4, band_at))
                for step in range(1, 4)
            ]
            loads = z_loads(SPREAD, 8 * size)
        elif k == 0:
            found = [
                far_copy(own, here, self.z_send.at[p, step], self.z_recv.at[p, step], ((img_at + step) % 4, band_at))
                for step in range(1, 4)
            ]
            found.append(pltpu.make_async_copy(own, here, self.near.at[p]))
            loads = z_loads(SPREAD, 2 * size)
        elif k == 3:
            part = whole.at[:, :, :, c_at, rows]
            found = [far_copy(part, part, self.p_send.at[p, 4], self.p_recv.at[p, 4], over_c)]
            loads = [("c", 16 * size)]
        else:
            for half in range(2):
                span = pl.ds(lanes, width - lanes) if half else pl.ds(0, lanes)
                if lanes == 0 and half == 0:
                    continue
                if k == 1:
                    part = whole.at[:, y_at, x_at, c_at, rows, span]
                elif half == 0:
                    part = whole.at[:, :, x_at, c_at, rows, span]
                else:
                    part = whole.at[:, y_at, :, c_at, rows, span]
                slot = 2 * (k - 1) + half
                along_y = (k == 1) == (half == 0)
                target = over_y if along_y else over_x
                found.append(far_copy(part, part, self.p_send.at[p, slot], self.p_recv.at[p, slot], target))
                loads.append(("y" if along_y else "x", 4 * k * size))

        def then():
            if k < 3:
                self.launch(p, k + 1)
            else:
                self.done.add(p)

        self.agenda.launch((self.name, p), found, loads, then)

    def begin(self, first, last):
        for p in range(first, last):
            self.launch(p, 0)

    def until(self, *wanted):
        self.agenda.until(lambda: all(p in self.done for p in wanted))


def gather_sems(count):
    dma = pltpu.SemaphoreType.DMA
    return [dma((count,)), dma((count, 4)), dma((count, 4)), dma((count, 5)), dma((count, 5))]


class Reduce:
    def __init__(
        self, agenda, slots, wait_z, full, pair, first_a, first_b, second_a, second_b, ours, last,
        near, p_send, p_recv, z_send, z_recv, free, free_z,
    ):
        self.agenda, self.slots, self.wait_z = agenda, slots, wait_z
        self.full, self.pair, self.ours, self.last = full, pair, ours, last
        self.first, self.second = (first_a, first_b), (second_a, second_b)
        self.near, self.p_send, self.p_recv, self.z_send, self.z_recv = near, p_send, p_recv, z_send, z_recv
        self.free, self.free_z = free, free_z
        self.pieces, self.flying, self.events, self.at_event = [], {}, [], 0
        self.queue, self.opened = [], 0

    def plan(self, pieces):
        self.pieces = pieces
        seen = [0] * 4
        for p, piece in enumerate(pieces):
            piece["slot"] = p % self.slots
            piece["place"] = p % (self.wait_z + 1)
            piece["order"] = seen[piece["z"]]
            seen[piece["z"]] += 1
        for piece in pieces:
            piece["again"] = piece["order"] + 2 < seen[piece["z"]]
        self.opened, self.passed, self.ended = 0, set(), set()
        self.ready = {""}

    def feed(self):
        while self.opened < len(self.pieces):
            p = self.opened
            if self.pieces[p]["needs"] not in self.ready or (p >= self.slots and p - self.slots not in self.passed):
                return
            self.opened += 1
            self.open(p)

    def allow(self, name):
        self.ready.add(name)
        self.feed()

    def rows(self, p):
        return pl.ds(0, self.pieces[p]["rows"])

    def open(self, p):
        piece = self.pieces[p]
        slot, rows = piece["slot"], self.rows(p)
        c_at = place()[4]
        over_c = neighbours()[0]
        if p >= self.slots:
            for k in range(3):
                pl.semaphore_wait(self.free.at[slot, k], 1)
        landing = self.pair.at[slot, :, :, rows]
        send, recv = self.p_send.at[slot, 0], self.p_recv.at[slot, 0]
        if "stage" in piece:
            stage, first, count = piece["stage"], piece["first"], piece["rows"]
            copies = []
            for n in range(4):
                theirs = pl.ds(pl.multiple_of(first + (2 * n + 1 - c_at) * count, 8), count)
                ours = pl.ds(pl.multiple_of(first + (2 * n + c_at) * count, 8), count)
                spot = 0 if n == 0 else 4 + n
                copies.append(
                    far_copy(
                        stage.at[theirs], self.pair.at[slot, n // 2, n % 2, rows], self.p_send.at[slot, spot],
                        self.p_recv.at[slot, spot], over_c,
                    )
                )
                copies.append(
                    pltpu.make_async_copy(
                        stage.at[ours], self.full.at[slot, n // 2, n % 2, c_at, rows], self.near.at[slot, n]
                    )
                )
        else:
            piece["emit"](self.full, slot)
            copies = [far_copy(self.full.at[slot, :, :, 1 - c_at, rows], landing, send, recv, over_c)]
        size = piece["rows"] * self.full.shape[5] * 4
        self.agenda.launch(("r", p, 0), copies, [("c", 4 * size)], lambda: self.step(0, p))

    def step(self, k, p):
        piece = self.pieces[p]
        slot, rows, z = piece["slot"], self.rows(p), piece["z"]
        size = piece["rows"] * self.full.shape[5] * 4
        img_at, band_at, y_at, x_at, c_at = place()
        over_c, over_x, over_y = neighbours()
        full, half = self.full, self.full.shape[5] // 2
        low, high = pl.ds(0, half), pl.ds(half, half)
        tiles = piece["rows"] // 16

        def tile(n):
            return pl.ds(pl.multiple_of(n % tiles * 16, 16), 16)

        if k == 0:
            def add(n, carry):
                y, x = n // (2 * tiles), n // tiles % 2
                full[slot, y, x, c_at, tile(n)] += self.pair[slot, y, x, tile(n)]
                return carry
            lax.fori_loop(0, 4 * tiles, add, 0)
            parts = (full.at[slot, :, 1 - x_at, c_at, rows, low], full.at[slot, 1 - y_at, :, c_at, rows, high])
            landings = [self.first[n].at[slot, :, rows] for n in range(2)]
            targets = (over_x, over_y)
        elif k == 1:
            def add(n, carry):
                w = n // tiles
                full[slot, w, x_at, c_at, tile(n), low] += self.first[0][slot, w, tile(n)]
                full[slot, y_at, w, c_at, tile(n), high] += self.first[1][slot, w, tile(n)]
                return carry
            lax.fori_loop(0, 2 * tiles, add, 0)
            parts = (full.at[slot, 1 - y_at, x_at, c_at, rows, low], full.at[slot, y_at, 1 - x_at, c_at, rows, high])
            landings = [self.second[n].at[slot, rows] for n in range(2)]
            targets = (over_y, over_x)
        if k < 2:
            copies = [
                far_copy(
                    parts[n], landings[n], self.p_send.at[slot, 1 + 2 * k + n], self.p_recv.at[slot, 1 + 2 * k + n],
                    targets[n],
                )
                for n in range(2)
            ]
            load = 2 * size if k == 0 else size
            self.agenda.launch(("r", p, 1 + k), copies, [("x", load), ("y", load)], lambda: self.step(k + 1, p))
            return
        spot, order = piece["place"], piece["order"] % 2
        mine = self.ours.at[spot, rows]
        owner = (z, band_at)

        def hop(n):
            return far_copy(mine, self.last.at[order, n, rows], self.z_send.at[spot], self.z_recv.at[order, n], owner)

        if k == 2:
            self.agenda.until(lambda: p < self.wait_z + 1 or p - self.wait_z - 1 in self.ended)

            def add(n, carry):
                self.ours[spot, tile(n), low] = full[slot, y_at, x_at, c_at, tile(n), low] + self.second[0][slot, tile(n)]
                self.ours[spot, tile(n), high] = full[slot, y_at, x_at, c_at, tile(n), high] + self.second[1][slot, tile(n)]
                return carry
            lax.fori_loop(0, tiles, add, 0)

            assert p < self.wait_z + 1 or p - self.wait_z - 1 in self.ended

            @pl.when(img_at != z)
            def _():
                if piece["order"] >= 2:
                    pl.semaphore_wait(self.free_z.at[z, order], 1)
                hop((img_at + 3 - z) % 4).start()

            if p + self.slots < len(self.pieces):
                for n, other in enumerate((over_c, over_x, over_y)):
                    pl.semaphore_signal(self.free.at[slot, n], inc=1, device_id=other, device_id_type=MESH)
            self.passed.add(p)
            self.agenda.launch(("r", p, 3), [], z_loads(TOWARDS[z], 2 * size), lambda: self.step(3, p))
            self.feed()
            return

        @pl.when(img_at != z)
        def _():
            hop((img_at + 3 - z) % 4).wait_send()

        @pl.when(img_at == z)
        def _():
            for n in range(3):
                hop(n).wait_recv()

            def add(n, carry):
                piece["out"][tile(n)] = (self.ours[spot, tile(n)] + self.last[order, 0, tile(n)]) + (
                    self.last[order, 1, tile(n)] + self.last[order, 2, tile(n)]
                )
                return carry
            lax.fori_loop(0, tiles, add, 0)
            if piece["again"]:
                for n in range(1, 4):
                    pl.semaphore_signal(
                        self.free_z.at[z, order], inc=1, device_id=((img_at + n) % 4, band_at), device_id_type=MESH
                    )

        self.ended.add(p)


def reduce_scratch(slots, wait_z, rows, width):
    f32 = jnp.float32
    dma = pltpu.SemaphoreType.DMA
    half = width // 2
    return [
        pltpu.VMEM((slots, 2, 2, 2, rows, width), f32),
        pltpu.VMEM((slots, 2, 2, rows, width), f32),
        pltpu.VMEM((slots, 2, rows, half), f32),
        pltpu.VMEM((slots, 2, rows, half), f32),
        pltpu.VMEM((slots, rows, half), f32),
        pltpu.VMEM((slots, rows, half), f32),
        pltpu.VMEM((wait_z + 1, rows, width), f32),
        pltpu.VMEM((2, 3, rows, width), f32),
        dma((slots, 4)),
        dma((slots, 8)), dma((slots, 8)),
        dma((wait_z + 1,)), dma((2, 3)),
        pltpu.SemaphoreType.REGULAR((slots, 3)),
        pltpu.SemaphoreType.REGULAR((4, 2)),
    ]


class ReduceSmall:
    def __init__(self, agenda, grads, shares, own, pair, first_a, first_b, second_a, second_b, last, near, p_send, p_recv, z_send, z_recv):
        self.agenda, self.done = agenda, set()
        self.grads, self.shares, self.own, self.pair = grads, shares, own, pair
        self.first, self.second, self.last = (first_a, first_b), (second_a, second_b), last
        self.near, self.p_send, self.p_recv, self.z_send, self.z_recv = near, p_send, p_recv, z_send, z_recv
        self.flying = {}

    def start(self, p, copies, loads, k):
        size = self.own[p].shape[3] * self.own[p].shape[4] * 4
        self.agenda.launch(("s", p), copies, [(link, n * size) for link, n in loads], lambda: self.step(p, k))

    def open(self, p):
        c_at = place()[4]
        over_c = neighbours()[0]
        self.start(p, [
            far_copy(self.grads[p].at[:, :, :, 1 - c_at], self.pair[p], self.p_send.at[p, 0], self.p_recv.at[p, 0], over_c),
            pltpu.make_async_copy(self.grads[p].at[:, :, :, c_at], self.own[p], self.near.at[p]),
        ], [("c", 16)], 0)

    def step(self, p, k):
        img_at, band_at, y_at, x_at, c_at = place()
        over_c, over_x, over_y = neighbours()
        own = self.own[p]
        rows = own.shape[3]
        span = (pl.ds(0, rows // 2), pl.ds(rows // 2, rows // 2))

        def send(parts, landings, targets, slot):
            copies = [
                far_copy(parts[n], landings[n], self.p_send.at[p, slot + n], self.p_recv.at[p, slot + n], targets[n])
                for n in range(2)
            ]
            self.start(p, copies, [("x", 8 >> k), ("y", 8 >> k)], k + 1)

        if k == 0:
            own[...] += self.pair[p][...]
            send(
                (own.at[:, :, 1 - x_at, span[0]], own.at[:, 1 - y_at, :, span[1]]),
                (self.first[0][p], self.first[1][p]), (over_x, over_y), 1,
            )
        elif k == 1:
            own[:, :, x_at, span[0]] += self.first[0][p][...]
            own[:, y_at, :, span[1]] += self.first[1][p][...]
            send(
                (own.at[:, 1 - y_at, x_at, span[0]], own.at[:, y_at, 1 - x_at, span[1]]),
                (self.second[0][p], self.second[1][p]), (over_y, over_x), 3,
            )
        elif k == 2:
            own[:, y_at, x_at, span[0]] += self.second[0][p][...]
            own[:, y_at, x_at, span[1]] += self.second[1][p][...]
            copies = []
            for n in range(1, 4):
                target = (img_at + n) % 4
                copies.append(
                    far_copy(
                        own.at[target, y_at, x_at], self.last[p].at[n - 1], self.z_send.at[p, n], self.z_recv.at[p, n],
                        (target, band_at),
                    )
                )
            self.start(p, copies, z_loads(SPREAD, 2), 3)
        else:
            last = self.last[p]
            self.done.add(p)
            self.shares[p][...] = (own[img_at, y_at, x_at] + last[0]) + (last[1] + last[2])


def reduce_small_scratch(shapes):
    f32 = jnp.float32
    dma = pltpu.SemaphoreType.DMA
    count = len(shapes)
    groups = [
        [(4, 2, 2, r, w) for r, w in shapes],
        [(4, 2, 2, r, w) for r, w in shapes],
        [(4, 2, r // 2, w) for r, w in shapes],
        [(4, 2, r // 2, w) for r, w in shapes],
        [(4, r // 2, w) for r, w in shapes],
        [(4, r // 2, w) for r, w in shapes],
        [(3, r, w) for r, w in shapes],
    ]
    return [pltpu.VMEM(shape, f32) for group in groups for shape in group] + [
        dma((count,)), dma((count, 5)), dma((count, 5)), dma((count, 4)), dma((count, 4)),
    ]


def dot_nn(a, b):
    return lax.dot_general(a, b, (((1,), (0,)), ((), ())), preferred_element_type=jnp.float32)


def dot_nt(a, b):
    return lax.dot_general(a, b, (((1,), (1,)), ((), ())), preferred_element_type=jnp.float32)


def dot_tn(a, b):
    return lax.dot_general(a, b, (((0,), (0,)), ((), ())), preferred_element_type=jnp.float32)


def norm_parts(h):
    centred = h - jnp.mean(h, axis=-1, keepdims=True)
    rate = lax.rsqrt(jnp.mean(centred * centred, axis=-1, keepdims=True) + norm_eps)
    return centred * rate, rate


def norm_back(grad, h, gain):
    shape, rate = norm_parts(h)
    inner = grad * gain
    back = rate * (
        inner
        - jnp.mean(inner, axis=-1, keepdims=True)
        - shape * jnp.mean(inner * shape, axis=-1, keepdims=True)
    )
    return (
        back,
        jnp.sum(grad * shape, axis=0, keepdims=True),
        jnp.sum(grad, axis=0, keepdims=True),
    )


STEP = 256


def at(k, start=0):
    return pl.ds(pl.multiple_of(start + k * STEP, STEP), STEP)


def lanes_at(k, size, start=0):
    return pl.ds(pl.multiple_of(start + k * size, 128), size)


def loop(first, last, body):
    def step(k, carry):
        body(k)
        return carry

    lax.fori_loop(first, last, step, 0)


class Block:
    def __init__(self, base, source, first_w, small, refs):
        names = (
            "wide", "narrow", "norms", "q_extra", "k_extra", "hidden", "normed", "q_buf", "kv", "mixed_in", "wide_in",
            "middle", "second", "slope", "grad_out", "grad_low", "mid_low", "gatt", "dkv", "dkv_in", "soft", "x_send",
            "x_recv", "x_free",
        )
        for name, ref in zip(names, refs, strict=True):
            setattr(self, name, ref)
        self.base, self.source, self.first_w, self.small = base, source, first_w, small
        self.part = place()[4]
        self.total, self.own = self.kv.shape[0], self.q_buf.shape[0]
        self.width = self.q_buf.shape[1]
        self.offset = pl.multiple_of(self.part * self.own, self.own)
        self.chunks = self.own // STEP
        lane_head = lax.broadcasted_iota(jnp.int32, (1, 128), 1) // HDIM
        self.pick = [jnp.where(lane_head == k, 1.0, 0.0).astype(jnp.bfloat16) for k in range(2)]

    def slope_rows(self, f, k):
        return pl.ds(pl.multiple_of(f * self.own + k * STEP, STEP), STEP)

    def gain(self, k):
        return self.norms[pl.ds(self.base + k, 1), :]

    def add_small(self, row, value):
        self.small[pl.ds(row, 1), :] += value

    def add_loss(self, value):
        first_lane = lax.broadcasted_iota(jnp.int32, (1, self.width), 1) == 0
        self.add_small(6, jnp.where(first_lane, value, 0.0))

    def enter(self, first, last):
        def body(n):
            k = (n + self.chunks * (1 + self.part)) % (self.total // STEP)
            h = dot_nt(self.source(k), self.first_w())
            self.hidden[at(n % self.chunks)] = h
            shape, _ = norm_parts(h)
            self.normed[at(k)] = (shape * self.gain(0) + self.gain(1)).astype(jnp.bfloat16)

        loop(first, last, body)

    def make_kv(self, first, last):
        def body(k):
            self.kv[at(k)] = dot_nt(self.normed[at(k)], self.wide[self.width : 3 * self.width]).astype(jnp.bfloat16)

        loop(first, last, body)

    def make_q(self):
        def body(k):
            q = dot_nt(self.normed[at(k, self.offset)], self.wide[: self.width]).astype(jnp.bfloat16)
            self.q_buf[at(k)] = (q.astype(jnp.float32) * HDIM**-0.5).astype(jnp.bfloat16)

        loop(0, self.chunks, body)

    def scores(self, p, k, rows, k_cat):
        q_cat = jnp.concatenate([self.q_buf[rows, lanes_at(p, 128)] * self.pick[k], self.q_extra[rows]], axis=1)
        return dot_nt(q_cat, k_cat)

    def key_columns(self, p):
        return jnp.concatenate([self.kv[:, lanes_at(p, 128)], self.k_extra[...]], axis=1)

    def attend(self, first, last):
        head_lane = lax.broadcasted_iota(jnp.int32, (STEP, 128), 1)

        def pair(p):
            k_cat = self.key_columns(p)
            v_pair = self.kv[:, lanes_at(p, 128, self.width)]

            def body(j):
                rows = at(j)
                mixed = None
                for k in range(2):
                    scores = self.scores(p, k, rows, k_cat)
                    peak = jnp.max(scores, axis=-1, keepdims=True)
                    expo = jnp.exp(scores - peak)
                    total = jnp.sum(expo, axis=-1, keepdims=True)
                    prob = expo * (1.0 / total)
                    level = peak + jnp.log(total)
                    self.soft[rows] = jnp.where(head_lane == 2 * p + k, level, self.soft[rows])
                    term = dot_nn(prob.astype(jnp.bfloat16), v_pair * self.pick[k])
                    mixed = term if mixed is None else mixed + term
                self.mixed_in[rows, lanes_at(p, 128)] = mixed.astype(jnp.bfloat16)

            loop(0, self.chunks, body)

        loop(first, last, pair)

    def after_attention(self):
        def body(k):
            rows = at(k)
            mid = self.hidden[at(k)] + dot_nn(self.mixed_in[rows, : self.width], self.narrow[: self.width])
            self.middle[rows] = mid
            shape, _ = norm_parts(mid)
            self.second[rows] = (shape * self.gain(2) + self.gain(3)).astype(jnp.bfloat16)
            self.grad_out[rows] = mid

        loop(0, self.chunks, body)

    def mlp(self, first, last):
        width = self.width

        def body(n):
            f, k = n // self.chunks, n % self.chunks
            rows = at(k)
            u = dot_nt(self.second[rows], self.wide[lanes_at(3 + f, width)])
            squared = u * u
            bend = jnp.tanh(0.7978845608028654 * (u + 0.044715 * squared * u))
            low = (0.5 * u * (1.0 + bend)).astype(jnp.bfloat16)
            self.mixed_in[rows, lanes_at(1 + f, width)] = low
            self.slope[self.slope_rows(f, k)] = 0.5 * (1.0 + bend) + (0.5 * u) * (1.0 - bend * bend) * (
                0.7978845608028654 * (1.0 + (3.0 * 0.044715) * squared)
            )
            self.grad_out[rows] += dot_nn(low, self.narrow[lanes_at(1 + f, width)])

        loop(first * self.chunks, last * self.chunks, body)

    def mlp_back(self, first, last):
        width = self.width

        def body(k):
            rows = at(k)
            gy = self.grad_low[rows]

            def feature_step(f, acc):
                ga = dot_nt(gy, self.narrow[lanes_at(1 + f, width)])
                low = (ga * self.slope[self.slope_rows(f, k)]).astype(jnp.bfloat16)
                self.wide_in[rows, lanes_at(3 + f, width)] = low
                return acc + dot_nn(low, self.wide[lanes_at(3 + f, width)])

            grad_second = lax.fori_loop(0, 4, feature_step, jnp.zeros((STEP, width), jnp.float32))
            back, g_gain, g_offset = norm_back(grad_second, self.middle[rows], self.gain(2))
            self.add_small(2, g_gain)
            self.add_small(3, g_offset)
            grad_mid = back + self.grad_out[rows]
            self.grad_out[rows] = grad_mid
            low = grad_mid.astype(jnp.bfloat16)
            self.mid_low[rows] = low
            self.gatt[rows] = dot_nt(low, self.narrow[:width]).astype(jnp.bfloat16)

        loop(first, last, body)

    def attend_back(self, first, last):
        head_lane = lax.broadcasted_iota(jnp.int32, (self.own, 128), 1)
        lane_head = lax.broadcasted_iota(jnp.int32, (1, 128), 1) // HDIM
        rows, bf16 = slice(None), jnp.bfloat16

        def head(h):
            p = h // 2
            pick = jnp.where(lane_head == h % 2, 1.0, 0.0).astype(bf16)
            k_pair = self.kv[:, lanes_at(p, 128)]
            g_rows = self.gatt[rows, lanes_at(p, 128)] * pick
            q_rows = self.q_buf[rows, lanes_at(p, 128)] * pick
            level = jnp.sum(jnp.where(head_lane == h, self.soft[...], 0.0), axis=-1, keepdims=True)
            scores = dot_nt(
                jnp.concatenate([q_rows, self.q_extra[...]], axis=1), jnp.concatenate([k_pair, self.k_extra[...]], axis=1)
            )
            prob = jnp.exp(scores - level)
            d_prob = dot_nt(g_rows, self.kv[:, lanes_at(p, 128, self.width)])
            dot_row = jnp.sum(prob * d_prob, axis=-1, keepdims=True)
            d_score = (prob * (d_prob - dot_row)).astype(bf16)
            dq = (dot_nn(d_score, k_pair * pick) * HDIM**-0.5).astype(bf16)
            self.dkv[p, 0] += dot_tn(d_score, q_rows)
            self.dkv[p, 1] += dot_tn(prob.astype(bf16), g_rows)
            self.wide_in[rows, lanes_at(p, 128)] = self.wide_in[rows, lanes_at(p, 128)] + dq

        self.dkv[pl.ds(first, 2)] = jnp.zeros((2,) + self.dkv.shape[1:], jnp.float32)
        self.wide_in[:, pl.ds(pl.multiple_of(128 * first, 128), 256)] = jnp.zeros((self.own, 256), bf16)
        loop(2 * first, 2 * last, head)

    def swap(self, p):
        theirs = pl.ds(pl.multiple_of((1 - self.part) * self.own, self.own), self.own)
        return far_copy(
            self.dkv.at[p, :, theirs], self.dkv_in.at[p], self.x_send.at[p], self.x_recv.at[p], neighbours()[0]
        )

    def attend_back_all(self, opening):
        if not opening:
            pl.semaphore_wait(self.x_free, 1)

        def half(n):
            self.attend_back(2 * n, 2 * n + 2)
            for p in range(2):
                self.swap(2 * n + p).start()

        loop(0, 2, half)

    def swap_start(self, first, opening):
        if not opening and first == 0:
            pl.semaphore_wait(self.x_free, 1)
        for p in range(first, first + 2):
            self.swap(p).start()

    def swap_finish(self, closing):
        for p in range(4):
            self.swap(p).wait()

        def body(n):
            p, k = n // self.chunks, n % self.chunks
            for side in range(2):
                total = self.dkv[p, side, at(k, self.offset)] + self.dkv_in[p, side, at(k)]
                self.wide_in[at(k), lanes_at(p, 128, (1 + side) * self.width)] = total.astype(jnp.bfloat16)

        loop(0, 4 * self.chunks, body)
        if not closing:
            pl.semaphore_signal(self.x_free, inc=1, device_id=neighbours()[0], device_id_type=MESH)

    def leave_rows(self, k):
        rows = at(k)
        grad_normed = dot_nn(self.wide_in[rows, : 3 * self.width], self.wide[: 3 * self.width])
        back, g_gain, g_offset = norm_back(grad_normed, self.hidden[at(k)], self.gain(0))
        self.add_small(0, g_gain)
        self.add_small(1, g_offset)
        return (back + self.grad_out[rows]).astype(jnp.bfloat16)

    def wide_product(self, first, count):
        if first < 3 * self.width:
            right = self.normed[pl.ds(self.offset, self.own)]
        else:
            right = self.second[...]
        return dot_tn(self.wide_in[:, first : first + count], right)

    def narrow_product(self, first, count):
        right = self.mid_low if first < self.width else self.grad_low
        return dot_tn(self.mixed_in[:, first : first + count], right[...])


def pieces_of(first, count, border):
    if first < border < first + count:
        return [(first, border - first), (border, first + count - border)]
    return [(first, count)]


def block_scratch(total_rows, own_rows):
    width = 512
    f32, bf16 = jnp.float32, jnp.bfloat16
    shapes = [
        ((own_rows, width), f32),
        ((total_rows, width), bf16),
        ((own_rows, width), bf16),
        ((total_rows, 2 * width), bf16),
        ((own_rows, 5 * width), bf16),
        ((own_rows, 7 * width), bf16),
        ((own_rows, width), f32),
        ((own_rows, width), bf16),
        ((4 * own_rows, width), f32),
        ((own_rows, width), f32),
        ((own_rows, width), bf16),
        ((own_rows, width), bf16),
        ((own_rows, width), bf16),
        ((4, 2, total_rows, 128), f32),
        ((4, 2, own_rows, 128), f32),
        ((own_rows, 128), f32),
    ]
    return [pltpu.VMEM(shape, dtype) for shape, dtype in shapes] + [
        pltpu.SemaphoreType.DMA((4,)), pltpu.SemaphoreType.DMA((4,)), pltpu.SemaphoreType.REGULAR
    ]


DEC_NARROW = ((0, 80, False),)
ENC_WIDE = ((96, 16, True), (0, 96, False))
ENC_NARROW = ((64, 16, True), (0, 64, False))
DEC_ORDER = (("n", 3), ("n", 1), ("n", 2), ("n", 0), ("w", 3), ("w", 2), ("w", 0), ("w", 1))
ENC_ORDER = (("n", 3), ("n", 1), ("n", 0), ("w", 3), ("w", 2), ("w", 0), ("w", 1), ("n", 2))


def step_kernel(slots, latent_total, *refs):
    shards, slab, code, kinds, norms = refs[:6], refs[6], refs[7], refs[8], refs[9]
    refs = refs[10:]
    share_wide_dec, share_narrow_dec, share_wide, share_narrow, share_edge, share_book, small_all = refs[:7]
    land_wide_dec, land_narrow_dec, land_wide, land_narrow = refs[7:11]
    refs = refs[11:]
    sems_dec, sems_enc, red, red_small, refs = refs[:5], refs[5:10], refs[10:25], refs[25:44], refs[44:]
    (book, edge, slab_all, code_all, tally, tally_all, t_img, t_band, e_near, e_send, e_recv, t_send, t_recv) = refs[:13]
    refs = refs[1:]
    (code_row, spread, cross, g_pixw, g_qout, g_qin, g_inw, g_edge, g_book) = refs[12:21]
    (small_dec, small_enc, small_own, s_img, s_band, s_send, s_recv, load_sem, wide, narrow) = refs[21:31]
    q_extra, k_extra = refs[31:33]
    scratch = refs[33:]
    f32, bf16 = jnp.float32, jnp.bfloat16
    img_at, band_at, y_at, x_at, c_at = place()
    chip_at = band_at // 2
    over_c = neighbours()[0]
    width = wide.shape[1]
    common = (wide, narrow, norms, q_extra, k_extra) + tuple(scratch)

    def edge_columns(first, count):
        return edge[:, :, :, :, :, first : first + count].reshape(width, count)

    def e_in():
        return edge_columns(0, 256)

    def e_pix():
        return edge_columns(256, 256)

    def e_qin():
        return edge_columns(512, 128)

    def e_qout():
        return edge_columns(640, 128)

    def pixel_rows(k, first=0, start=0):
        return slab_all[pl.ds(start + 2 * k, 2), :, first : first + 256].reshape(STEP, 256)

    own_band = 4 * c_at
    dec = Block(4, lambda k: spread[at(k)], e_qout, small_dec, common)
    enc = Block(0, pixel_rows, e_in, small_enc, common)
    agenda = Agenda()
    dec_pieces = [(shards[0], book, 0, 64, False), (shards[1], edge, 0, 16, False)]
    dec_pieces += [(shards[2], land_wide_dec, 96, 16, True)]
    dec_pieces += [(shards[2], land_wide_dec, 0, 48, False), (shards[2], land_wide_dec, 48, 48, False)]
    dec_pieces += [(shards[3], land_narrow_dec, first, count, last) for first, count, last in DEC_NARROW]
    gather = Gather("d", agenda, dec_pieces, *sems_dec)
    enc_pieces = [(shards[4], land_wide, first, count, last) for first, count, last in ENC_WIDE]
    enc_pieces += [(shards[5], land_narrow, first, count, last) for first, count, last in ENC_NARROW]
    gather_enc = Gather("e", agenda, enc_pieces, *sems_enc)
    count_all = Everywhere("n", agenda, tally, t_img, t_band, t_send, t_recv, tally_all)
    spots = lax.broadcasted_iota(jnp.int32, (1, 4), 1)
    kind = jnp.sum(jnp.where(spots == chip_at, kinds[...], 0).astype(f32), axis=1, keepdims=True)
    meet(peers())
    agenda.spend(3.0)
    gather.begin(0, 5)
    exchange = []
    for step in range(1, 4):
        chip = (chip_at + step) % 4
        target = (img_at, 2 * chip + c_at)
        here = band_at
        exchange.append(far_copy(slab.at[chip], slab_all.at[here], e_send.at[0, step], e_recv.at[0, step], target))
        exchange.append(far_copy(code.at[chip], code_all.at[here], e_send.at[1, step], e_recv.at[1, step], target))
    exchange.append(pltpu.make_async_copy(slab.at[chip_at], slab_all.at[band_at], e_near.at[0]))
    exchange.append(pltpu.make_async_copy(code.at[chip_at], code_all.at[band_at], e_near.at[1]))

    def exchange_landed():
        late = []
        for k, dst in enumerate((slab_all, code_all)):
            for chip in range(4):
                part = dst.at[2 * chip + c_at]
                late.append(far_copy(part, part, e_send.at[k, 4 + chip], e_recv.at[k, 4 + chip], over_c))
        agenda.launch("x2", late, [("c", 4e5)], lambda: arrived.append(1))

    arrived = []
    agenda.launch("x1", exchange, [("x", 4e5), ("y", 4e5)], exchange_landed)
    agenda.spend(1.0)
    segment_lane = lax.broadcasted_iota(jnp.int32, (enc.total, 128), 1)
    segment = jnp.where(kind < 0.5, 0, lax.broadcasted_iota(jnp.int32, (enc.total, 128), 0) // (enc.total // 4))
    k_extra[...] = jnp.where(segment_lane == segment, 1.0, 0.0).astype(bf16)
    segment_lane = lax.broadcasted_iota(jnp.int32, (enc.own, 128), 1)
    segment = lax.broadcasted_iota(jnp.int32, (enc.own, 128), 0) + enc.offset
    segment = jnp.where(kind < 0.5, 0, segment // (enc.total // 4))
    q_extra[...] = jnp.where((segment_lane < 4) & (segment_lane != segment), -(2.0**30), 0.0).astype(bf16)
    for ref in (small_dec, small_enc, g_pixw, g_qout, g_qin, g_inw):
        ref[...] = jnp.zeros(ref.shape, f32)
    agenda.spend(2.0)
    agenda.tick()
    agenda.until(lambda: arrived)
    def code_column(k, start=0):
        return jnp.concatenate(
            [jnp.transpose(jnp.broadcast_to(code_all[start + 2 * k + n], (8, 128)))[:, 0:1] for n in range(2)], axis=0
        )

    for n in range(4):
        code_row[:, pl.ds(128 * n, 128)] = code_all[own_band + n]

    def pick_codes(k):
        rows = at(k)
        code_here = code_column(k)
        picks = lax.broadcasted_iota(jnp.int32, (STEP, 512), 1)
        found = jnp.zeros((STEP, 128), f32)
        for z in range(4):
            hot = jnp.where(picks + 512 * z == code_here // 4, 1.0, 0.0).astype(bf16)
            found += dot_nn(hot, book[z].reshape(512, 128))
        lanes = lax.broadcasted_iota(jnp.int32, (STEP, 128), 1) // 32
        spread[rows] = jnp.where(lanes == code_here % 4, found, 0.0).astype(bf16)

    lane = lax.broadcasted_iota(jnp.int32, (4, 128, 256), 2)
    flags = slab_all[pl.ds(own_band, 4), :, 128:384].astype(f32)
    tally[...] = jnp.full(tally.shape, jnp.sum(jnp.where(lane < 64, 0.0, flags)))
    agenda.spend(1.0)
    agenda.tick()
    count_all.begin()
    gather.begin(5, len(dec_pieces))
    gather.until(0)
    agenda.tick()
    loop(0, dec.total // STEP, pick_codes)
    agenda.spend(4.0)
    agenda.tick()
    gather.until(1)
    dec.enter(0, dec.total // STEP)
    agenda.spend(1.9)
    agenda.tick()

    def fetch(landed, ref, sem):
        rows = landed.shape[4]

        def body(n):
            src = landed.at[n // 8, (n // 4) % 2, (n // 2) % 2, n % 2]
            pltpu.make_async_copy(src, ref.at[pl.ds(pl.multiple_of(n * rows, 16), rows)], sem).start()

        loop(0, 32, body)
        return pltpu.make_async_copy(ref, ref, sem)

    reduce = Reduce(agenda, *slots, *red)
    tail = ReduceSmall(
        agenda, (g_edge, g_book), (share_edge, share_book),
        *[red_small[2 * n : 2 * n + 2] for n in range(7)], *red_small[14:],
    )

    def emit_wide(blk, z, full, slot):
        values = [blk.wide_product(*span) for span in pieces_of(896 * z, 896, 3 * width)]
        value = values[0] if len(values) == 1 else jnp.concatenate(values, axis=0)
        full[slot] = value.reshape(2, 2, 2, 112, width)
        agenda.spend(0.6)

    def emit_narrow(blk, z, full, slot):
        values = [blk.narrow_product(*span) for span in pieces_of(640 * z, 640, width)]
        value = values[0] if len(values) == 1 else jnp.concatenate(values, axis=0)
        full[slot, :, :, :, :80] = value.reshape(2, 2, 2, 80, width)
        agenda.spend(0.5)

    pieces = []
    for name, blk, out_wide, out_narrow, order in (
        ("dec", dec, share_wide_dec, share_narrow_dec, DEC_ORDER), ("enc", enc, share_wide, share_narrow, ENC_ORDER)
    ):
        for kind_of, z in order:
            if kind_of == "n":
                needs = name + str(int(z == 0))
                pieces.append(dict(emit=functools.partial(emit_narrow, blk, z), z=z, rows=80, out=out_narrow, needs=needs))
                continue
            piece = dict(z=z, rows=112, out=out_wide, needs=name + str(1 + (z < 2)))
            if name == "dec" and z < 2:
                piece.update(stage=dec.slope, first=896 * z)
            else:
                piece.update(emit=functools.partial(emit_wide, blk, z))
            pieces.append(piece)
    reduce.plan(pieces)

    def spend(time):
        agenda.spend(time)
        agenda.tick()

    def decoder_head(k):
        rows = at(k)
        out = dec.grad_out[rows]
        shape, _ = norm_parts(out)
        final = (shape * norms[pl.ds(8, 1), :] + norms[pl.ds(9, 1), :]).astype(bf16)
        error = dot_nn(final, e_pix()) - pixel_rows(k, 0, own_band).astype(f32)
        lane = lax.broadcasted_iota(jnp.int32, (STEP, 256), 1)
        counted = jnp.where(lane < 192, pltpu.roll(pixel_rows(k, 128, own_band).astype(f32), 192, 1), 0.0)
        number = tally_all[0:1, 0:1]
        dec.add_loss(jnp.sum(counted * (error * error + jnp.abs(error))) / number)
        sign = jnp.where(error > 0.0, 1.0, jnp.where(error < 0.0, -1.0, 0.0))
        grad_pred = (counted * (2.0 * error + sign) / number).astype(bf16)
        g_pixw[...] += dot_tn(final, grad_pred)
        back, g_gain, g_offset = norm_back(dot_nt(grad_pred, e_pix()), out, norms[pl.ds(8, 1), :])
        dec.add_small(4, g_gain)
        dec.add_small(5, g_offset)
        dec.grad_out[rows] = back
        dec.grad_low[rows] = back.astype(bf16)

    def encoder_head(k):
        rows = at(k)
        low = enc.grad_out[rows].astype(bf16)
        lanes = lax.broadcasted_iota(jnp.int32, (STEP, 128), 1) // 32
        mine = lanes == code_column(k, own_band) % 4
        gap = jnp.where(mine, spread[at(k, enc.offset)].astype(f32) - dot_nn(low, e_qin()), 0.0)
        enc.add_loss((1.0 + commitment) * jnp.sum(gap * gap) / latent_total)
        grad_latent = jnp.where(mine, cross[rows] - 2.0 * commitment * gap / latent_total, 0.0).astype(bf16)
        g_qin[...] += dot_tn(low, grad_latent)
        back = dot_nt(grad_latent, e_qin())
        enc.grad_out[rows] = back
        enc.grad_low[rows] = back.astype(bf16)
        gap = 2.0 * gap / latent_total
        high = gap.astype(bf16)
        left = gap - high.astype(f32)
        between = left.astype(bf16)
        enc.gatt[rows, :384] = jnp.concatenate([high, between, (left - between.astype(f32)).astype(bf16)], axis=1)

    def book_rows(k):
        picks = lax.broadcasted_iota(jnp.int32, (STEP, enc.own), 0) + k * STEP
        hot = jnp.where(picks == code_row[...] // 4, 1.0, 0.0).astype(bf16)
        summed = dot_nn(hot, enc.gatt[:, :384])
        value = (summed[:, :128] + summed[:, 128:256]) + summed[:, 256:]
        g_book[k // 2, k % 2] = value.reshape(2, 2, 64, 128)

    def decoder_leave(k):
        low = dec.leave_rows(k)
        cross[at(k)] = dot_nn(low, e_qout())
        g_qout[...] += dot_tn(low, spread[at(k, dec.offset)])

    def encoder_leave(k):
        g_inw[...] += dot_tn(enc.leave_rows(k), pixel_rows(k, 0, own_band))

    gather_enc.begin(0, len(enc_pieces))
    gather.until(2, 3, 4)
    fetch(land_wide_dec, wide, load_sem.at[0]).wait()
    spend(2.0)
    dec.make_kv(0, dec.total // STEP)
    dec.make_q()
    spend(2.9)
    dec.attend(0, 4)
    spend(11.1)
    gather.until(*range(5, len(dec_pieces)))
    fetched = fetch(land_narrow_dec, narrow, load_sem.at[1])
    agenda.spend(1.0)
    fetched.wait()
    dec.after_attention()
    spend(1.1)
    dec.mlp(0, 4)
    spend(5.6)
    count_all.until()
    loop(0, dec.chunks, decoder_head)
    agenda.spend(2.0)
    reduce.allow("dec0")
    agenda.tick()
    dec.mlp_back(0, dec.chunks)
    agenda.spend(6.1)
    reduce.allow("dec1")
    agenda.tick()
    dec.attend_back_all(True)
    spend(15.8)
    gather_enc.until(*range(len(enc_pieces)))
    fetched = fetch(land_narrow, narrow, load_sem.at[1])
    dec.swap_finish(False)
    agenda.spend(2.0)
    for z in range(2):
        values = [dec.wide_product(*span) for span in pieces_of(896 * z, 896, 3 * width)]
        dec.slope[pl.ds(896 * z, 896)] = values[0] if len(values) == 1 else jnp.concatenate(values, axis=0)
    agenda.spend(1.2)
    reduce.allow("dec2")
    agenda.tick()
    loop(0, dec.chunks, decoder_leave)
    fetched_wide = fetch(land_wide, wide, load_sem.at[0])
    spend(2.0)
    emitted = 1 + max(p for p in range(8) if "emit" in pieces[p])
    staged = [p for p in range(8) if "stage" in pieces[p]]
    agenda.until(lambda: reduce.opened >= emitted)
    enc.enter(0, enc.total // STEP)
    spend(1.9)
    fetched_wide.wait()
    enc.make_kv(0, enc.total // STEP)
    enc.make_q()
    fetched.wait()
    spend(2.9)
    enc.attend(0, 4)
    spend(11.1)
    enc.after_attention()
    spend(1.1)
    agenda.until(lambda: reduce.opened > max(staged) and not any(("r", p, 0) in agenda.flying for p in staged))
    enc.mlp(0, 4)
    spend(5.6)
    loop(0, enc.chunks, encoder_head)
    agenda.spend(2.0)
    reduce.allow("enc0")
    agenda.tick()
    loop(0, 8, book_rows)
    tail.open(1)
    spend(2.0)
    enc.mlp_back(0, enc.chunks)
    agenda.spend(6.1)
    reduce.allow("enc1")
    agenda.tick()
    enc.attend_back(0, 2)
    enc.swap_start(0, False)
    spend(7.9)
    enc.attend_back(2, 4)
    enc.swap_start(2, False)
    spend(7.9)
    enc.swap_finish(True)
    agenda.spend(2.0)
    reduce.allow("enc2")
    agenda.tick()
    loop(0, enc.chunks, encoder_leave)
    agenda.spend(2.0)

    def all_groups(value):
        value = value + pltpu.roll(value, 64, 1)
        return value + pltpu.roll(value, 32, 1)

    lane = lax.broadcasted_iota(jnp.int32, (width, 128), 1)
    mixed = jnp.where(lane < 64, g_inw[:, 128:], jnp.where(lane < 96, all_groups(g_qin[...]), all_groups(g_qout[...])))
    for first, value in ((0, g_inw[:, :128]), (128, mixed), (256, g_pixw[:, :128]), (384, g_pixw[:, 128:])):
        g_edge[:, :, :, :, :, pl.ds(first, 128)] = value.reshape(4, 2, 2, 2, 16, 128)
    tail.open(0)
    agenda.until(lambda: len(reduce.ended) == len(pieces) and len(tail.done) == 2)
    shares = (share_wide_dec, share_narrow_dec, share_wide, share_narrow, share_edge, share_book)
    squares = sum(jnp.sum(share[...] * share[...]) for share in shares)
    lane = lax.broadcasted_iota(jnp.int32, (8, width), 1)
    row = lax.broadcasted_iota(jnp.int32, (8, width), 0)
    small_own[0] = small_enc[...]
    small_own[1] = jnp.where((row == 7) & (lane == 0), squares, small_dec[...])
    sum_all = Everywhere("a", agenda, small_own, s_img, s_band, s_send, s_recv, small_all)
    sum_all.begin()
    sum_all.until()


def train_step(shards, slab, code, kinds, norms, latent_total, total_rows, own_rows):
    width = 512
    slots = (4, 4)
    f32, bf16, int32 = jnp.float32, jnp.bfloat16, jnp.int32
    any_space = pl.BlockSpec(memory_space=pl.ANY)
    vmem = pl.BlockSpec(memory_space=pltpu.VMEM)
    shape = jax.ShapeDtypeStruct
    out_shape = [
        shape((112, width), f32), shape((80, width), f32), shape((112, width), f32), shape((80, width), f32),
        shape((16, width), f32), shape((64, 128), f32), shape((2, 8, width), f32),
    ]
    out_shape += [shape((4, 2, 2, 2) + s.shape, s.dtype) for s in shards[2:]]
    dma = pltpu.SemaphoreType.DMA
    mem = pltpu.VMEM
    scratch = gather_sems(5 + len(DEC_NARROW)) + gather_sems(len(ENC_WIDE) + len(ENC_NARROW))
    scratch += reduce_scratch(*slots, 112, width) + reduce_small_scratch([(16, width), (64, 128)])
    scratch += [
        mem((4, 2, 2, 2, 64, 128), bf16), mem((4, 2, 2, 2, 16, 768), bf16),
        mem((8, 128, 384), bf16), mem((8, 1, 128), int32), mem((8, 128), f32), mem((8, 128), f32),
        mem((4, 8, 128), f32), mem((8, 8, 128), f32),
        dma((2,)), dma((2, 8)), dma((2, 8)), dma((11,)), dma((11,)),
        mem((1, own_rows), int32), mem((total_rows, 128), bf16),
        mem((own_rows, 128), f32),
        mem((width, 256), f32), mem((width, 128), f32), mem((width, 128), f32), mem((width, 256), f32),
        mem((4, 2, 2, 2, 16, width), f32), mem((4, 2, 2, 2, 64, 128), f32),
        mem((8, width), f32), mem((8, width), f32), mem((2, 8, width), f32),
        mem((4, 2, 8, width), f32), mem((8, 2, 8, width), f32), dma((11,)), dma((11,)),
        dma((2,)), mem((7 * width, width), bf16), mem((5 * width, width), bf16),
        mem((own_rows, 128), bf16), mem((total_rows, 128), bf16),
    ]
    scratch += block_scratch(total_rows, own_rows)
    return pl.pallas_call(
        functools.partial(step_kernel, slots, latent_total),
        out_shape=out_shape,
        in_specs=[any_space] * 8 + [vmem] * 2,
        out_specs=[vmem] * 7 + [any_space] * 4,
        scratch_shapes=scratch,
        compiler_params=pltpu.CompilerParams(collective_id=0, has_side_effects=True, vmem_limit_bytes=(639 << 20) // 10),
        name="train_step",
    )(*shards, slab, code, kinds, norms)


def moments(gradient, first_old, second_old):
    first_new = beta_first * first_old + (1.0 - beta_first) * gradient
    second_new = beta_second * second_old + (1.0 - beta_second) * gradient * gradient
    return (first_new, second_new, first_new / (jnp.sqrt(second_new) + adam_eps))


def rotated_update(weight, gradient, first_old, second_old, basis_stack):
    turned = jnp.einsum("rld,lde->rle", gradient, basis_stack, precision=highest)
    first_new, second_new, direction = moments(turned, first_old, second_old)
    turned_back = jnp.einsum("rle,lde->rld", direction, basis_stack, precision=highest)
    return (weight - rate_matrix * (turned_back + weight_decay * weight), first_new, second_new)


def plain_update(weight, gradient, first_old, second_old):
    first_new, second_new, direction = moments(gradient, first_old, second_old)
    return (weight - rate_vector * (direction + weight_decay * weight), first_new, second_new)


def prepare_kernel(wide, narrow, edge, wide_0, wide_1, narrow_0, narrow_1, edge_low):
    low = jnp.bfloat16
    wide_0[...], wide_1[...] = wide[:, 0].astype(low), wide[:, 1].astype(low)
    narrow_0[...], narrow_1[...] = narrow[:, 0].astype(low), narrow[:, 1].astype(low)
    full = edge[...]
    gap = jnp.zeros((full.shape[0], 64), full.dtype)
    parts = [full[:, :192], gap, full[:, 192:384], gap] + [full[:, 384:416]] * 4 + [full[:, 416:448]] * 4
    edge_low[...] = jnp.concatenate(parts, axis=1).astype(low)


def prepare(w_wide, w_narrow, w_edge):
    vmem = pl.BlockSpec(memory_space=pltpu.VMEM)
    rows, width = (w_wide.shape[0], w_narrow.shape[0]), w_wide.shape[2]
    shapes = [(rows[0], width)] * 2 + [(rows[1], width)] * 2 + [(w_edge.shape[0], 768)]
    return pl.pallas_call(
        prepare_kernel,
        out_shape=[jax.ShapeDtypeStruct(shape, jnp.bfloat16) for shape in shapes],
        in_specs=[vmem] * 3,
        out_specs=[vmem] * 5,
        name="prepare",
    )(w_wide, w_narrow, w_edge)


def update_kernel(*refs):
    count = 20
    ins, refs = refs[:count], refs[count:]
    outs, held, sem = refs[:13], refs[13 : 13 + count], refs[13 + count]
    loads = {k: [pltpu.make_async_copy(ins[k], held[k], sem.at[k])] for k in range(count) if k != 18}
    loads[18] = [pltpu.make_async_copy(ins[18].at[k], held[18].at[k], sem.at[18 if k == 0 else 19 + k]) for k in range(4)]
    order = (5, 15, 16, 17, 4, 12, 13, 14, 19, 0, 1, 6, 7, 8, 18, 2, 3, 9, 10, 11)
    for k in order:
        for load in loads[k]:
            load.start()

    def need(*wanted):
        for k in wanted:
            while loads[k]:
                loads[k].pop(0).wait()

    refs = held + outs
    wide_0, wide_1, narrow_0, narrow_1, edge, small = refs[:6]
    wide, narrow, edge_set, norm_set = refs[6:9], refs[9:12], refs[12:15], refs[15:18]
    bases, basis_edge = refs[18:20]
    new_wide, new_narrow, new_edge, new_norms, scalars = refs[20:23], refs[23:26], refs[26:29], refs[29:32], refs[32]
    need(5, 15, 16, 17)
    norm_grad = jnp.concatenate([small[0, 0:4], small[1, 0:6]], axis=0)
    squares = small[1, 7:8, 0:1] + jnp.sum(norm_grad * norm_grad)
    grad_norm = jnp.sqrt(squares)
    factor = jnp.minimum(1.0, clip_level / grad_norm)
    scalars[0:1] = jnp.broadcast_to(grad_norm, (1, 128))
    scalars[1:2] = jnp.broadcast_to(factor, (1, 128))
    scalars[2:3] = jnp.broadcast_to(small[0, 6:7, 0:1] + small[1, 6:7, 0:1], (1, 128))
    scalars[3:8] = jnp.zeros((5, 128), jnp.float32)

    def halves(value):
        high = value.astype(jnp.bfloat16)
        return high, (value - high.astype(jnp.float32)).astype(jnp.bfloat16)

    def product(left, right, dot):
        (high, low), (right_high, right_low) = halves(left), right
        both = dot(jnp.concatenate([high, low], axis=0), right_high)
        rows = left.shape[0]
        return both[:rows] + (dot(high, right_low) + both[rows:])

    def turn(weight, gradient, first_old, second_old, basis):
        right = halves(basis)
        turned = product(gradient, right, dot_nn)
        first_new, second_new, direction = moments(turned, first_old, second_old)
        back = product(direction, right, dot_nt)
        return weight - rate_matrix * (back + weight_decay * weight), first_new, second_new

    need(4, 12, 13, 14, 19)
    packed = edge[...]
    grad_edge = jnp.concatenate([packed[:, :192], packed[:, 256:448], packed[:, 192:256]], axis=1)
    found = turn(edge_set[0][...], factor * grad_edge, edge_set[1][...], edge_set[2][...], basis_edge[...])
    for ref, value in zip(new_edge, found):
        ref[...] = value
    found = plain_update(norm_set[0][...], factor * norm_grad, norm_set[1][...], norm_set[2][...])
    for ref, value in zip(new_norms, found):
        ref[...] = value
    for k, (olds, news, grads) in enumerate(
        ((wide, new_wide, (wide_0, wide_1)), (narrow, new_narrow, (narrow_0, narrow_1)))
    ):
        for layer in range(2):
            need(2 * k + layer, 6 + 3 * k, 7 + 3 * k, 8 + 3 * k)
            loads[18].pop(0).wait()
            found = turn(
                olds[0][:, layer], factor * grads[layer][...], olds[1][:, layer], olds[2][:, layer], bases[2 * k + layer]
            )
            for ref, value in zip(news, found):
                ref[:, layer] = value


def update_all(grads, wide, narrow, edge, norms, bases, basis_edge):
    vmem = pl.BlockSpec(memory_space=pltpu.VMEM)
    shape = jax.ShapeDtypeStruct
    sets = wide + narrow + edge + norms
    return pl.pallas_call(
        update_kernel,
        out_shape=[shape(a.shape, a.dtype) for a in sets] + [shape((8, 128), jnp.float32)],
        in_specs=[pl.BlockSpec(memory_space=pl.ANY)] * (len(grads) + len(sets) + 2),
        out_specs=[vmem] * (len(sets) + 1),
        scratch_shapes=[pltpu.VMEM(a.shape, a.dtype) for a in (*grads, *sets, bases, basis_edge)]
        + [pltpu.SemaphoreType.DMA((len(grads) + len(sets) + 5,))],
        compiler_params=pltpu.CompilerParams(vmem_limit_bytes=63 << 20),
        name="update_all",
    )(*grads, *sets, bases, basis_edge)


def body(
    pixels,
    valid,
    codes,
    image_kind,
    w_wide,
    w_narrow,
    w_edge,
    codebook,
    norms,
    bases,
    basis_edge,
    m_wide,
    v_wide,
    m_narrow,
    v_narrow,
    m_edge,
    v_edge,
    m_code,
    v_code,
    m_norm,
    v_norm,
):
    band_count = lax.axis_size("band")
    band_index = lax.axis_index("band")
    row_count = pixels.shape[2]
    length = row_count * band_count
    batch_count = pixels.shape[0]
    group = band_count // batch_count
    row = band_index // group
    part = band_index % group
    own_rows = length // group
    groups = [[k * group + j for j in range(group)] for k in range(batch_count)]
    layer_count = w_wide.shape[1]
    code_width = codebook.shape[1]
    latent_total = batch_count * lax.axis_size("img") * length * code_width
    both = ("img", "band")

    direct = band_count == 8 and lax.axis_size("img") == 4 and batch_count == 4
    shards = [w_wide[:, l].astype(jnp.bfloat16) for l in range(layer_count)]
    shards += [w_narrow[:, l].astype(jnp.bfloat16) for l in range(layer_count)]
    shards += [w_edge.astype(jnp.bfloat16), codebook.astype(jnp.bfloat16).reshape(-1, 4 * code_width)]
    slab = jnp.concatenate([pixels[:, 0], valid[:, 0].astype(jnp.bfloat16)], axis=2)
    patch_size = pixels.shape[3]
    if direct:
        shards = list(prepare(w_wide, w_narrow, w_edge)) + shards[5:]
        out = train_step(
            [shards[k] for k in (5, 4, 1, 3, 0, 2)], slab, codes, image_kind.reshape(1, -1), norms, latent_total, length, own_rows
        )
        new = update_all(
            (out[2], out[0], out[3], out[1], out[4], out[6]), (w_wide, m_wide, v_wide), (w_narrow, m_narrow, v_narrow),
            (w_edge, m_edge, v_edge), (norms, m_norm, v_norm), bases, basis_edge,
        )
        scalars = new[12]
        grad_norm, factor, loss_total = scalars[0, 0], scalars[1, 0], scalars[2, 0]
        new_code = plain_update(codebook, factor * out[5].reshape(-1, code_width), m_code, v_code)
        return tuple(new[:9]) + new_code + tuple(new[9:12]) + (grad_norm, loss_total)
    wholes = [lax.all_gather(shard, both, axis=0, tiled=True) for shard in shards]
    count = lax.psum(jnp.sum(valid.astype(jnp.float32)), both)

    def whole_row(local):
        everywhere = lax.all_gather(local, "band", axis=0)
        chosen_row = lax.dynamic_index_in_dim(everywhere, row, axis=1, keepdims=False)
        return chosen_row.reshape((length,) + local.shape[2:])

    slab_all = whole_row(slab)
    code_all = whole_row(codes[:, 0])
    kind = lax.dynamic_index_in_dim(image_kind[:, 0], row, 0, keepdims=False)
    span = jnp.where(kind == 0, length, length // 4)
    positions = jnp.arange(length, dtype=jnp.int32)
    gathered = (wholes[:2], wholes[2:4], wholes[4], wholes[5])
    pixel_all = slab_all[:, :patch_size]
    valid_rows = lax.dynamic_slice_in_dim(slab_all, part * own_rows, own_rows, 0)[:, patch_size:]
    own_positions = part * own_rows + jnp.arange(own_rows, dtype=jnp.int32)
    allowed = (own_positions // span)[:, None] == (positions // span)[None, :]
    local_grads, norm_sum, loss_sum = row_step(
        gathered, norms, pixel_all, valid_rows, code_all, part, allowed, count, latent_total, groups
    )
    shares = [lax.psum_scatter(g, both, scatter_dimension=0, tiled=True) for g in local_grads]
    squares = sum(jnp.sum(share * share) for share in shares)
    norm_total, square_total, loss_total = lax.psum((norm_sum, squares, loss_sum), both)
    grad_sum = (
        jnp.stack([shares[0], shares[1]], axis=1),
        jnp.stack([shares[2], shares[3]], axis=1),
        shares[4],
        shares[5].reshape(-1, code_width),
    )
    grad_norm = jnp.sqrt(square_total + jnp.sum(norm_total * norm_total))
    factor = jnp.minimum(1.0, clip_level / grad_norm)
    grad_wide, grad_narrow, grad_edge, grad_book = grad_sum
    new_wide, new_m_wide, new_v_wide = rotated_update(
        w_wide, factor * grad_wide, m_wide, v_wide, bases[:layer_count]
    )
    new_narrow, new_m_narrow, new_v_narrow = rotated_update(
        w_narrow, factor * grad_narrow, m_narrow, v_narrow, bases[layer_count:]
    )
    new_edge, new_m_edge, new_v_edge = rotated_update(
        w_edge[:, None],
        factor * grad_edge[:, None],
        m_edge[:, None],
        v_edge[:, None],
        basis_edge[None],
    )
    new_book, new_m_code, new_v_code = plain_update(codebook, factor * grad_book, m_code, v_code)
    new_norms, new_m_norm, new_v_norm = plain_update(norms, factor * norm_total, m_norm, v_norm)
    return (
        new_wide,
        new_m_wide,
        new_v_wide,
        new_narrow,
        new_m_narrow,
        new_v_narrow,
        new_edge[:, 0],
        new_m_edge[:, 0],
        new_v_edge[:, 0],
        new_book,
        new_m_code,
        new_v_code,
        new_norms,
        new_m_norm,
        new_v_norm,
        grad_norm,
        loss_total,
    )


def solution(mesh):
    in_specs = (
        P(None, "img", "band", None),
        P(None, "img", "band", None),
        P(None, "img", "band"),
        P(None, "img"),
        P(("img", "band"), None, None),
        P(("img", "band"), None, None),
        P(("img", "band"), None),
        P(("img", "band"), None),
        P(),
        P(),
        P(),
        P(("img", "band"), None, None),
        P(("img", "band"), None, None),
        P(("img", "band"), None, None),
        P(("img", "band"), None, None),
        P(("img", "band"), None),
        P(("img", "band"), None),
        P(("img", "band"), None),
        P(("img", "band"), None),
        P(),
        P(),
    )
    out_specs = (
        P(("img", "band"), None, None),
        P(("img", "band"), None, None),
        P(("img", "band"), None, None),
        P(("img", "band"), None, None),
        P(("img", "band"), None, None),
        P(("img", "band"), None, None),
        P(("img", "band"), None),
        P(("img", "band"), None),
        P(("img", "band"), None),
        P(("img", "band"), None),
        P(("img", "band"), None),
        P(("img", "band"), None),
        P(),
        P(),
        P(),
        P(),
        P(),
    )
    return jax.shard_map(body, mesh=mesh, in_specs=in_specs, out_specs=out_specs, check_vma=False)
```
